32 devices in a mesh: fsdp: 16 (over z, x, core), seq: 2 (over y).
Axes of the slice: x: 2, y: 2, z: 4, core: 2. Of those that a mesh axis runs over, the one named last changes fastest.
Arguments:
- tokens: bfloat16 [16, 256, 1024], P('fsdp', 'seq'), may hold values from -6 to 6
- visible: int32 [16], P('fsdp'), may hold values from 157 to 250, as said below
- first_gain: bfloat16 [1024], P('fsdp'), may hold values from 0.25 to 1.75
- first_shift: bfloat16 [1024], P('fsdp'), may hold values from -3 to 3
- inward_weight: bfloat16 [1024, 3072], P('fsdp'), may hold values from -0.1875 to 0.1875
- query_bias: bfloat16 [1024], P('fsdp'), may hold values from -3 to 3
- value_bias: bfloat16 [1024], P('fsdp'), may hold values from -3 to 3
- outward_weight: bfloat16 [1024, 1024], P('fsdp'), may hold values from -2 to 2
- outward_bias: bfloat16 [1024], P('fsdp'), may hold values from -3 to 3
- second_gain: bfloat16 [1024], P('fsdp'), may hold values from 0.25 to 1.75
- second_shift: bfloat16 [1024], P('fsdp'), may hold values from -3 to 3
- expand_weight: bfloat16 [1024, 4096], P('fsdp'), may hold values from -0.1875 to 0.1875
- expand_bias: bfloat16 [4096], P('fsdp'), may hold values from -3 to 3
- shrink_weight: bfloat16 [4096, 1024], P('fsdp'), may hold values from -0.09375 to 0.09375
- shrink_bias: bfloat16 [1024], P('fsdp'), may hold values from -3 to 3
- upstream: bfloat16 [16, 256, 1024], P('fsdp', 'seq'), may hold values from -6 to 6
Outputs:
- layer_out: bfloat16 [16, 256, 1024], P('fsdp', 'seq')
- tokens_grad: float32 [16, 256, 1024], P('fsdp', 'seq')
- first_gain_grad: float32 [1024], P(('fsdp', 'seq'))
- first_shift_grad: float32 [1024], P(('fsdp', 'seq'))
- inward_weight_grad: float32 [1024, 3072], P(('fsdp', 'seq'))
- query_bias_grad: float32 [1024], P(('fsdp', 'seq'))
- value_bias_grad: float32 [1024], P(('fsdp', 'seq'))
- outward_weight_grad: float32 [1024, 1024], P(('fsdp', 'seq'))
- outward_bias_grad: float32 [1024], P(('fsdp', 'seq'))
- second_gain_grad: float32 [1024], P(('fsdp', 'seq'))
- second_shift_grad: float32 [1024], P(('fsdp', 'seq'))
- expand_weight_grad: float32 [1024, 4096], P(('fsdp', 'seq'))
- expand_bias_grad: float32 [4096], P(('fsdp', 'seq'))
- shrink_weight_grad: float32 [4096, 1024], P(('fsdp', 'seq'))
- shrink_bias_grad: float32 [1024], P(('fsdp', 'seq'))
The draws below stay inside these ranges and needn't reach their ends.
Inputs may be any that keep to these rules, and one draw needn't show every extreme that they name: Clip i's visible tokens fill its first visible[i] slots; the remaining slots are padding. Some clip has exactly 250 and some exactly 157 visible tokens.
All inputs are finite; a program needn't handle non-finite values.
Results may differ from the reference program's by a relative error of at most 0.012.
Values may be sent and summed in bfloat16 or wider, within the bound.
A program may use at most 192 MiB of HBM per device.

```python
import math
import jax
import jax.numpy as jnp
from jax import lax

D = 1024
FF = 4096
HEADS = 16
SLOTS = 256
VIS_MIN = 157
VIS_MAX = 250
CLIPS = 16


def draw_visible(key, part):
    first_key, second_key = jax.random.split(jax.random.fold_in(key, 7))
    counts = jax.random.randint(first_key, (CLIPS,), VIS_MIN, VIS_MAX + 1)
    chosen = jax.random.randint(second_key, (), 0, CLIPS)
    indices = jnp.arange(CLIPS)
    counts = jnp.where(indices == chosen, VIS_MAX, counts)
    counts = jnp.where(indices == (chosen + 1) % CLIPS, VIS_MIN, counts)
    return counts.astype(jnp.int32)


def levels(key, shape, shards, least, largest):
    def one(axis_at, shards_of):
        steps = jax.random.uniform(jax.random.fold_in(jax.random.fold_in(key, 6), axis_at), (shards_of,), jnp.float32, least / len(shards), largest / len(shards))
        return jnp.repeat(jnp.exp(steps), shape[axis_at] // shards_of).reshape((-1,) + (1,) * (len(shape) - axis_at - 1))

    gain = one(*shards[0])
    for cut in shards[1:]:
        gain = gain * one(*cut)
    return gain


def scatter_about(stream_key, shape, spread, bound, pieces=(), dtype=jnp.bfloat16):
    values = spread * jax.random.normal(stream_key, shape, jnp.float32)
    if pieces:
        values = values * levels(stream_key, shape, pieces, -0.22, 0.18)
    return jnp.clip(values, -bound, bound).astype(dtype)


def setup_inputs(seed: int = 0) -> dict:
    key_of = jax.random.split(jax.random.key(seed), 17)
    tokens = scatter_about(key_of[0], (CLIPS, SLOTS, D), 1.0, 6.0, ((0, 16), (1, 2)))
    visible = draw_visible(jax.random.fold_in(key_of[16], 71), 0)
    first_gain = jnp.clip(1.0 + 0.15 * jax.random.normal(key_of[2], (D,), jnp.float32), 0.25, 1.75).astype(jnp.bfloat16)
    first_shift = scatter_about(key_of[3], (D,), 0.5, 3.0, ((0, 16),))
    inward_weight = scatter_about(key_of[4], (D, 3 * D), D ** -0.5, 0.1875, ((0, 16),))
    query_bias = scatter_about(key_of[5], (D,), 0.5, 3.0, ((0, 16),))
    value_bias = scatter_about(key_of[6], (D,), 0.5, 3.0, ((0, 16),))
    outward_weight = scatter_about(key_of[7], (D, D), (D // 128) ** -0.5, 2.0, ((0, 16),))
    outward_bias = scatter_about(key_of[8], (D,), 0.5, 3.0, ((0, 16),))
    second_gain = jnp.clip(1.0 + 0.15 * jax.random.normal(key_of[9], (D,), jnp.float32), 0.25, 1.75).astype(jnp.bfloat16)
    second_shift = scatter_about(key_of[10], (D,), 0.5, 3.0, ((0, 16),))
    expand_weight = scatter_about(key_of[11], (D, FF), D ** -0.5, 0.1875, ((0, 16),))
    expand_bias = scatter_about(key_of[12], (FF,), 0.5, 3.0, ((0, 16),))
    shrink_weight = scatter_about(key_of[13], (FF, D), FF ** -0.5, 0.09375, ((0, 16),))
    shrink_bias = scatter_about(key_of[14], (D,), 0.5, 3.0, ((0, 16),))
    upstream = scatter_about(key_of[15], (CLIPS, SLOTS, D), 1.0, 6.0, ((0, 16), (1, 2)))
    return {"tokens": tokens, "visible": visible, "first_gain": first_gain, "first_shift": first_shift, "inward_weight": inward_weight, "query_bias": query_bias, "value_bias": value_bias, "outward_weight": outward_weight, "outward_bias": outward_bias, "second_gain": second_gain, "second_shift": second_shift, "expand_weight": expand_weight, "expand_bias": expand_bias, "shrink_weight": shrink_weight, "shrink_bias": shrink_bias, "upstream": upstream}


@jax.custom_vjp
def low(v):
    return lax.optimization_barrier(v.astype(jnp.bfloat16)).astype(jnp.float32)

@jax.custom_vjp
def low_back(v):
    return v

def low_keep(v):
    return (low(v), None)

def low_pass(kept, grad):
    return (grad,)

def back_keep(v):
    return (v, None)

def back_low(kept, grad):
    return (low(grad),)
low.defvjp(low_keep, low_pass)
low_back.defvjp(back_keep, back_low)
epsilon = 1e-06
highest = lax.Precision.HIGHEST

def norm_rows(inputs, norm_gain, norm_shift):
    row_mean = lax.optimization_barrier(jnp.mean(inputs, axis=-1, keepdims=True))
    centered = inputs - row_mean
    variance = lax.optimization_barrier(jnp.mean(centered * centered, axis=-1, keepdims=True))
    return centered * lax.rsqrt(variance + epsilon) * norm_gain + norm_shift

def block_forward(params, tokens_group, counts_group):
    first_gain, first_shift, inward_weight, query_bias, value_bias, outward_weight, outward_bias, second_gain, second_shift, expand_weight, expand_bias, shrink_weight, shrink_bias = params
    group_size, slot_count, model_width = tokens_group.shape
    head_size = model_width // HEADS
    scale = head_size ** (-0.5)
    first = low(norm_rows(tokens_group, first_gain, first_shift))
    merged_bias = jnp.concatenate([query_bias, jnp.zeros_like(query_bias), value_bias])
    project = jnp.einsum('gsd,de->gse', first, inward_weight, precision=highest) + merged_bias
    shape_heads = (group_size, slot_count, HEADS, head_size)
    queries = low_back(low(project[..., :model_width])).reshape(shape_heads)
    key_rows = low_back(low(project[..., model_width:2 * model_width])).reshape(shape_heads)
    values = low_back(low(project[..., 2 * model_width:])).reshape(shape_heads)
    scores = low_back(jnp.einsum('gqhe,gkhe->ghqk', queries, key_rows, precision=highest) * scale)
    positions = jnp.arange(slot_count)
    key_valid = positions[None, :] < counts_group[:, None]
    scores = jnp.where(key_valid[:, None, None, :], scores, -1e+30)
    soft_low = low(jax.nn.softmax(scores, axis=-1))
    blended = jnp.einsum('ghqk,gkhe->gqhe', soft_low, values, precision=highest)
    blended = low_back(low(blended.reshape(group_size, slot_count, model_width)))
    branch = low_back(jnp.einsum('gsd,de->gse', blended, outward_weight, precision=highest) + outward_bias)
    middle = tokens_group + branch
    second = low(norm_rows(middle, second_gain, second_shift))
    hidden = low_back(jnp.einsum('gsd,df->gsf', second, expand_weight, precision=highest) + expand_bias)
    active = low(jax.nn.gelu(hidden, approximate=False))
    branch_second = low_back(jnp.einsum('gsf,fd->gsd', active, shrink_weight, precision=highest) + shrink_bias)
    result = middle + branch_second
    row_valid = positions[None, :, None] < counts_group[:, None, None]
    return jnp.where(row_valid, result, 0.0)

def reference(tokens, visible, first_gain, first_shift, inward_weight, query_bias, value_bias, outward_weight, outward_bias, second_gain, second_shift, expand_weight, expand_bias, shrink_weight, shrink_bias, upstream):
    params = (first_gain.astype(jnp.float32), first_shift.astype(jnp.float32), inward_weight.astype(jnp.float32), query_bias.astype(jnp.float32), value_bias.astype(jnp.float32), outward_weight.astype(jnp.float32), outward_bias.astype(jnp.float32), second_gain.astype(jnp.float32), second_shift.astype(jnp.float32), expand_weight.astype(jnp.float32), expand_bias.astype(jnp.float32), shrink_weight.astype(jnp.float32), shrink_bias.astype(jnp.float32))
    clip_count = tokens.shape[0]
    group_size = math.gcd(clip_count, 16)

    def whole(tokens_all, params_all):
        shaped = tokens_all.reshape(clip_count // group_size, group_size, SLOTS, D)
        counts_shaped = visible.reshape(clip_count // group_size, group_size)

        def block_step(bundle):
            return block_forward(params_all, bundle[0], bundle[1])
        mapped = lax.map(jax.checkpoint(block_step), (shaped, counts_shaped))
        return mapped.reshape(tokens_all.shape)
    output, pullback = jax.vjp(whole, tokens.astype(jnp.float32), params)
    tokens_grad, param_grads = pullback(upstream.astype(jnp.float32))
    return (output.astype(jnp.bfloat16), tokens_grad, param_grads[0], param_grads[1], param_grads[2], param_grads[3], param_grads[4], param_grads[5], param_grads[6], param_grads[7], param_grads[8], param_grads[9], param_grads[10], param_grads[11], param_grads[12])
```

```python
import functools

import jax
import jax.numpy as jnp
from jax import lax
from jax.experimental import pallas as pl
from jax.experimental.pallas import tpu as pltpu
from jax.sharding import PartitionSpec as P

HEADS = 16


epsilon = 1e-06


def norm_rows(inputs, norm_gain, norm_shift):
    row_mean = jnp.mean(inputs, axis=-1, keepdims=True)
    centered = inputs - row_mean
    variance = jnp.mean(centered * centered, axis=-1, keepdims=True)
    inverse = lax.rsqrt(variance + epsilon)
    normed = centered * inverse
    return (normed * norm_gain + norm_shift, normed, inverse)


def norm_back(grad_out, normed, inverse, norm_gain):
    scaled = grad_out * norm_gain
    first_mean = jnp.mean(scaled, axis=-1, keepdims=True)
    second_mean = jnp.mean(scaled * normed, axis=-1, keepdims=True)
    return inverse * (scaled - first_mean - normed * second_mean)


def gather_weights(
    first_gain,
    first_shift,
    inward_weight,
    query_bias,
    value_bias,
    outward_weight,
    outward_bias,
    second_gain,
    second_shift,
    expand_weight,
    expand_bias,
    shrink_weight,
    shrink_bias,
):
    return (
        lax.all_gather(first_gain, "fsdp", axis=0, tiled=True),
        lax.all_gather(first_shift, "fsdp", axis=0, tiled=True),
        lax.all_gather(inward_weight, "fsdp", axis=0, tiled=True),
        lax.all_gather(query_bias, "fsdp", axis=0, tiled=True),
        lax.all_gather(value_bias, "fsdp", axis=0, tiled=True),
        lax.all_gather(outward_weight, "fsdp", axis=0, tiled=True),
        lax.all_gather(outward_bias, "fsdp", axis=0, tiled=True),
        lax.all_gather(second_gain, "fsdp", axis=0, tiled=True),
        lax.all_gather(second_shift, "fsdp", axis=0, tiled=True),
        lax.all_gather(expand_weight, "fsdp", axis=0, tiled=True),
        lax.all_gather(expand_bias, "fsdp", axis=0, tiled=True),
        lax.all_gather(shrink_weight, "fsdp", axis=0, tiled=True),
        lax.all_gather(shrink_bias, "fsdp", axis=0, tiled=True),
    )


def attend_scores(query_heads, key_heads, key_valid, scale):
    scores = (
        jnp.einsum("cqhe,ckhe->chqk", query_heads, key_heads, preferred_element_type=jnp.float32)
        * scale
    )
    return jnp.where(key_valid[:, None, None, :], scores, -1e30)


def forward(tokens32, key_valid, row_valid, gathered):
    (
        first_gain,
        first_shift,
        inward_weight,
        query_bias,
        value_bias,
        outward_weight,
        outward_bias,
        second_gain,
        second_shift,
        expand_weight,
        expand_bias,
        shrink_weight,
        shrink_bias,
    ) = gathered
    clip_count, seg_rows, model_width = tokens32.shape
    head_size = model_width // HEADS
    scale = head_size ** (-0.5)
    affine_first, normed_first, inverse_first = norm_rows(
        tokens32, first_gain.astype(jnp.float32), first_shift.astype(jnp.float32)
    )
    lowered_first = affine_first.astype(jnp.bfloat16)
    merged_bias = jnp.concatenate([query_bias, jnp.zeros_like(query_bias), value_bias]).astype(
        jnp.float32
    )
    project = (
        jnp.einsum("csd,de->cse", lowered_first, inward_weight, preferred_element_type=jnp.float32)
        + merged_bias
    )
    queries = project[..., :model_width].astype(jnp.bfloat16)
    key_local = project[..., model_width : 2 * model_width].astype(jnp.bfloat16)
    value_local = project[..., 2 * model_width :].astype(jnp.bfloat16)
    key_all, value_all = (
        lax.all_gather(key_local, "seq", axis=1, tiled=True),
        lax.all_gather(value_local, "seq", axis=1, tiled=True),
    )
    slot_count = key_all.shape[1]
    query_heads = queries.reshape(clip_count, seg_rows, HEADS, head_size)
    key_heads = key_all.reshape(clip_count, slot_count, HEADS, head_size)
    value_heads = value_all.reshape(clip_count, slot_count, HEADS, head_size)
    scores = attend_scores(query_heads, key_heads, key_valid, scale)
    row_top = jnp.max(scores, axis=-1, keepdims=True)
    row_total = jnp.sum(jnp.exp(scores - row_top), axis=-1, keepdims=True)
    log_total = row_top + jnp.log(row_total)
    soft_low = jnp.exp(scores - log_total).astype(jnp.bfloat16)
    blended = jnp.einsum(
        "chqk,ckhe->cqhe", soft_low, value_heads, preferred_element_type=jnp.float32
    )
    blended = blended.reshape(clip_count, seg_rows, model_width).astype(jnp.bfloat16)
    branch = jnp.einsum(
        "csd,de->cse", blended, outward_weight, preferred_element_type=jnp.float32
    ) + outward_bias.astype(jnp.float32)
    middle = tokens32 + branch
    affine_second, normed_second, inverse_second = norm_rows(
        middle, second_gain.astype(jnp.float32), second_shift.astype(jnp.float32)
    )
    lowered_second = affine_second.astype(jnp.bfloat16)
    hidden = jnp.einsum(
        "csd,df->csf", lowered_second, expand_weight, preferred_element_type=jnp.float32
    ) + expand_bias.astype(jnp.float32)
    active = jax.nn.gelu(hidden, approximate=False).astype(jnp.bfloat16)
    branch_second = jnp.einsum(
        "csf,fd->csd", active, shrink_weight, preferred_element_type=jnp.float32
    ) + shrink_bias.astype(jnp.float32)
    result = middle + branch_second
    output = jnp.where(row_valid, result, 0.0).astype(jnp.bfloat16)
    return {
        "normed_first": normed_first,
        "inverse_first": inverse_first,
        "lowered_first": lowered_first,
        "query_heads": query_heads,
        "key_heads": key_heads,
        "value_heads": value_heads,
        "log_total": log_total,
        "blended": blended,
        "normed_second": normed_second,
        "inverse_second": inverse_second,
        "lowered_second": lowered_second,
        "hidden": hidden,
        "active": active,
        "output": output,
    }


def gelu_exact(inputs):
    return jax.nn.gelu(inputs, approximate=False)


def backward(saved, gathered, upstream32, key_valid, row_valid):
    (
        first_gain,
        first_shift,
        inward_weight,
        query_bias,
        value_bias,
        outward_weight,
        outward_bias,
        second_gain,
        second_shift,
        expand_weight,
        expand_bias,
        shrink_weight,
        shrink_bias,
    ) = gathered
    clip_count, seg_rows, model_width = upstream32.shape
    head_size = model_width // HEADS
    scale = head_size ** (-0.5)
    grad_result = jnp.where(row_valid, upstream32, 0.0)
    grad_low_second = grad_result.astype(jnp.bfloat16)
    shrink_weight_grad = jnp.einsum(
        "csf,csd->fd", saved["active"], grad_low_second, preferred_element_type=jnp.float32
    )
    shrink_bias_grad = jnp.sum(grad_low_second.astype(jnp.float32), axis=(0, 1))
    grad_active = jnp.einsum(
        "csd,fd->csf", grad_low_second, shrink_weight, preferred_element_type=jnp.float32
    )
    gelu_value, gelu_pull = jax.vjp(gelu_exact, saved["hidden"])
    grad_hidden = gelu_pull(grad_active)[0].astype(jnp.bfloat16)
    expand_weight_grad = jnp.einsum(
        "csd,csf->df", saved["lowered_second"], grad_hidden, preferred_element_type=jnp.float32
    )
    expand_bias_grad = jnp.sum(grad_hidden.astype(jnp.float32), axis=(0, 1))
    grad_second = jnp.einsum(
        "csf,df->csd", grad_hidden, expand_weight, preferred_element_type=jnp.float32
    )
    second_gain_grad = jnp.sum(grad_second * saved["normed_second"], axis=(0, 1))
    second_shift_grad = jnp.sum(grad_second, axis=(0, 1))
    grad_middle = grad_result + norm_back(
        grad_second,
        saved["normed_second"],
        saved["inverse_second"],
        second_gain.astype(jnp.float32),
    )
    grad_low_first = grad_middle.astype(jnp.bfloat16)
    outward_weight_grad = jnp.einsum(
        "csd,cse->de", saved["blended"], grad_low_first, preferred_element_type=jnp.float32
    )
    outward_bias_grad = jnp.sum(grad_low_first.astype(jnp.float32), axis=(0, 1))
    grad_blended = jnp.einsum(
        "cse,de->csd", grad_low_first, outward_weight, preferred_element_type=jnp.float32
    )
    grad_blended = grad_blended.astype(jnp.bfloat16).reshape(clip_count, seg_rows, HEADS, head_size)
    query_heads = saved["query_heads"]
    key_heads = saved["key_heads"]
    value_heads = saved["value_heads"]
    slot_count = key_heads.shape[1]
    scores = attend_scores(query_heads, key_heads, key_valid, scale)
    soft = jnp.exp(scores - saved["log_total"])
    soft_low = soft.astype(jnp.bfloat16)
    grad_soft = jnp.einsum(
        "cqhe,ckhe->chqk", grad_blended, value_heads, preferred_element_type=jnp.float32
    )
    grad_scores = soft * (grad_soft - jnp.sum(grad_soft * soft, axis=-1, keepdims=True))
    grad_scores = grad_scores.astype(jnp.bfloat16)
    grad_queries = (
        jnp.einsum("chqk,ckhe->cqhe", grad_scores, key_heads, preferred_element_type=jnp.float32)
        * scale
    )
    grad_queries = grad_queries.astype(jnp.bfloat16).reshape(clip_count, seg_rows, model_width)
    grad_keys_part = (
        jnp.einsum("chqk,cqhe->ckhe", grad_scores, query_heads, preferred_element_type=jnp.float32)
        * scale
    )
    grad_values_part = jnp.einsum(
        "chqk,cqhe->ckhe", soft_low, grad_blended, preferred_element_type=jnp.float32
    )
    grad_keys_part = grad_keys_part.reshape(clip_count, slot_count, model_width)
    grad_values_part = grad_values_part.reshape(clip_count, slot_count, model_width)
    grad_keys, grad_values = (
        lax.psum_scatter(
            grad_keys_part.astype(jnp.bfloat16), "seq", scatter_dimension=1, tiled=True
        ).astype(jnp.float32),
        lax.psum_scatter(
            grad_values_part.astype(jnp.bfloat16), "seq", scatter_dimension=1, tiled=True
        ).astype(jnp.float32),
    )
    grad_keys = grad_keys.astype(jnp.bfloat16)
    grad_values = grad_values.astype(jnp.bfloat16)
    grad_project = jnp.concatenate([grad_queries, grad_keys, grad_values], axis=-1)
    inward_weight_grad = jnp.einsum(
        "csd,cse->de", saved["lowered_first"], grad_project, preferred_element_type=jnp.float32
    )
    query_bias_grad = jnp.sum(grad_queries.astype(jnp.float32), axis=(0, 1))
    value_bias_grad = jnp.sum(grad_values.astype(jnp.float32), axis=(0, 1))
    grad_first = jnp.einsum(
        "cse,de->csd", grad_project, inward_weight, preferred_element_type=jnp.float32
    )
    first_gain_grad = jnp.sum(grad_first * saved["normed_first"], axis=(0, 1))
    first_shift_grad = jnp.sum(grad_first, axis=(0, 1))
    tokens_grad = grad_middle + norm_back(
        grad_first, saved["normed_first"], saved["inverse_first"], first_gain.astype(jnp.float32)
    )
    weight_shares = (
        lax.psum_scatter(first_gain_grad, ("fsdp", "seq"), scatter_dimension=0, tiled=True),
        lax.psum_scatter(first_shift_grad, ("fsdp", "seq"), scatter_dimension=0, tiled=True),
        lax.psum_scatter(inward_weight_grad, ("fsdp", "seq"), scatter_dimension=0, tiled=True),
        lax.psum_scatter(query_bias_grad, ("fsdp", "seq"), scatter_dimension=0, tiled=True),
        lax.psum_scatter(value_bias_grad, ("fsdp", "seq"), scatter_dimension=0, tiled=True),
        lax.psum_scatter(outward_weight_grad, ("fsdp", "seq"), scatter_dimension=0, tiled=True),
        lax.psum_scatter(outward_bias_grad, ("fsdp", "seq"), scatter_dimension=0, tiled=True),
        lax.psum_scatter(second_gain_grad, ("fsdp", "seq"), scatter_dimension=0, tiled=True),
        lax.psum_scatter(second_shift_grad, ("fsdp", "seq"), scatter_dimension=0, tiled=True),
        lax.psum_scatter(expand_weight_grad, ("fsdp", "seq"), scatter_dimension=0, tiled=True),
        lax.psum_scatter(expand_bias_grad, ("fsdp", "seq"), scatter_dimension=0, tiled=True),
        lax.psum_scatter(shrink_weight_grad, ("fsdp", "seq"), scatter_dimension=0, tiled=True),
        lax.psum_scatter(shrink_bias_grad, ("fsdp", "seq"), scatter_dimension=0, tiled=True),
    )
    return (tokens_grad, weight_shares)


def shards(
    tokens,
    visible,
    first_gain,
    first_shift,
    inward_weight,
    query_bias,
    value_bias,
    outward_weight,
    outward_bias,
    second_gain,
    second_shift,
    expand_weight,
    expand_bias,
    shrink_weight,
    shrink_bias,
    upstream,
):
    clip_count, seg_rows, model_width = tokens.shape
    slot_count = seg_rows * lax.axis_size("seq")
    local_start = lax.axis_index("seq") * seg_rows
    row_positions = local_start + jnp.arange(seg_rows, dtype=jnp.int32)
    row_valid = (row_positions[None, :] < visible[:, None])[..., None]
    key_valid = jnp.arange(slot_count, dtype=jnp.int32)[None, :] < visible[:, None]
    tokens32 = tokens.astype(jnp.float32)
    upstream32 = upstream.astype(jnp.float32)
    gathered = gather_weights(
        first_gain,
        first_shift,
        inward_weight,
        query_bias,
        value_bias,
        outward_weight,
        outward_bias,
        second_gain,
        second_shift,
        expand_weight,
        expand_bias,
        shrink_weight,
        shrink_bias,
    )
    saved = forward(tokens32, key_valid, row_valid, gathered)
    layer_out = saved["output"]
    gathered = gather_weights(
        first_gain,
        first_shift,
        inward_weight,
        query_bias,
        value_bias,
        outward_weight,
        outward_bias,
        second_gain,
        second_shift,
        expand_weight,
        expand_bias,
        shrink_weight,
        shrink_bias,
    )
    saved = forward(tokens32, key_valid, row_valid, gathered)
    tokens_grad, shares = backward(saved, gathered, upstream32, key_valid, row_valid)
    return (
        layer_out,
        tokens_grad,
        shares[0],
        shares[1],
        shares[2],
        shares[3],
        shares[4],
        shares[5],
        shares[6],
        shares[7],
        shares[8],
        shares[9],
        shares[10],
        shares[11],
        shares[12],
    )


F32 = jnp.float32
BF16 = jnp.bfloat16
MESH = pl.DeviceIdType.MESH
SLAB = 8


def matmul(a, b):
    return lax.dot_general(a, b, (((1,), (0,)), ((), ())), preferred_element_type=F32)


def matmul_bt(a, b):
    return lax.dot_general(a, b, (((1,), (1,)), ((), ())), preferred_element_type=F32)


def matmul_at(a, b):
    return lax.dot_general(a, b, (((0,), (0,)), ((), ())), preferred_element_type=F32)


def row_stats(x):
    mean = jnp.mean(x, axis=-1, keepdims=True)
    centered = x - mean
    inverse = lax.rsqrt(jnp.mean(centered * centered, axis=-1, keepdims=True) + epsilon)
    return centered * inverse, inverse


def row_norm_back(grad, normed, inverse, gain):
    scaled = grad * gain
    first_mean = jnp.mean(scaled, axis=-1, keepdims=True)
    second_mean = jnp.mean(scaled * normed, axis=-1, keepdims=True)
    return inverse * (scaled - first_mean - normed * second_mean)


class Place:
    def __init__(self, groups):
        self.groups = groups
        self.f = lax.axis_index("fsdp")
        self.y = lax.axis_index("seq")
        self.r = self.f // 4
        self.xc = self.f % 4
        self.t = self.xc * 2 + self.y
        x, c = self.xc // 2, self.xc % 2
        self.step = {4: 4 - 8 * x, 2: 2 - 4 * c, 1: 1 - 2 * self.y}

    def peer(self, mask):
        at = self.t
        for bit in (4, 2, 1):
            if mask & bit:
                at = at + self.step[bit]
        return at

    def device(self, r, t):
        return (r * 4 + t // 2, t % 2)


def rows(ref, index, size):
    return ref.at[pl.ds(pl.multiple_of(index * size, size), size), :]


def cols(ref, index, size):
    return ref.at[:, pl.ds(pl.multiple_of(index * size, size), size)]


class Wire:
    def __init__(self, place, send_sems, recv_sems, local_sems):
        self.place = place
        self.send_sems, self.recv_sems, self.local_sems = send_sems, recv_sems, local_sems
        self.sends = self.recvs = self.locals = 0
        self.open_sends = []

    def recv_slots(self, count):
        first = self.recvs
        self.recvs += count
        return [self.recv_sems.at[first + i] for i in range(count)]

    def send(self, src, dst, slot, to):
        copy = pltpu.make_async_remote_copy(
            src_ref=src,
            dst_ref=dst,
            send_sem=self.send_sems.at[self.sends],
            recv_sem=slot,
            device_id=self.place.device(*to),
            device_id_type=MESH,
        )
        self.sends += 1
        copy.start()
        self.open_sends.append(copy)

    def arrived(self, dst, slot):
        pltpu.make_async_remote_copy(
            src_ref=dst,
            dst_ref=dst,
            send_sem=self.send_sems.at[0],
            recv_sem=slot,
            device_id=self.place.device(self.place.r, self.place.peer(2)),
            device_id_type=MESH,
        ).wait_recv()

    def local(self, src, dst):
        copy = pltpu.make_async_copy(src, dst, self.local_sems.at[self.locals])
        self.locals += 1
        copy.start()
        return copy

    def finish(self):
        for copy in self.open_sends:
            copy.wait_send()


class SlabGather:
    def __init__(self, wire, at):
        self.wire, self.at = wire, at
        self.slots = wire.recv_slots(8)

    def start(self, src):
        place = self.wire.place
        for mask in (5, 4, 1, 2):
            self.wire.send(src, self.at(place.t), self.slots[mask], (place.r, place.peer(mask)))

    def forward(self):
        place = self.wire.place
        for mask in (4, 1, 5):
            block = self.at(place.peer(mask))
            self.wire.arrived(block, self.slots[mask])
            self.wire.send(block, block, self.slots[mask ^ 2], (place.r, place.peer(2)))

    def wait(self):
        place = self.wire.place
        for mask in (2, 6, 3, 7):
            self.wire.arrived(self.at(place.peer(mask)), self.slots[mask])


class SlabScatter:
    def __init__(self, wire, part, core_in, chip_in, block):
        self.wire, self.part, self.core_in, self.chip_in, self.block = wire, part, core_in, chip_in, block
        self.core_slots = wire.recv_slots(4)
        self.chip_slots = wire.recv_slots(3)
        self.order = (5, 4, 1, 0)

    def cores(self):
        place = self.wire.place
        for i, mask in enumerate(self.order):
            self.wire.send(
                rows(self.part, place.peer(mask ^ 2), self.block),
                self.core_in.at[i],
                self.core_slots[i],
                (place.r, place.peer(2)),
            )

    def chips(self):
        place = self.wire.place
        for i, mask in enumerate(self.order[:3]):
            self.wire.arrived(self.core_in.at[i], self.core_slots[i])
            mine = rows(self.part, place.peer(mask), self.block)
            mine[...] = (mine[...].astype(F32) + self.core_in[i].astype(F32)).astype(BF16)
            self.wire.send(mine, self.chip_in.at[i], self.chip_slots[i], (place.r, place.peer(mask)))
        self.wire.arrived(self.core_in.at[3], self.core_slots[3])

    def wait(self):
        for i in range(3):
            self.wire.arrived(self.chip_in.at[i], self.chip_slots[i])

    def total(self, first, size):
        mine = self.part[pl.ds(pl.multiple_of(self.wire.place.t * self.block + first, size), size), :].astype(F32)
        mine = mine + self.core_in[3, pl.ds(first, size), :].astype(F32)
        for i in range(3):
            mine = mine + self.chip_in[i, pl.ds(first, size), :].astype(F32)
        return mine


class SlabSwap:
    def __init__(self, wire, source, target):
        self.wire, self.source, self.target = wire, source, target
        self.slots = wire.recv_slots(8)

    def start(self):
        place = self.wire.place
        self.own = self.wire.local(self.source(place.t), self.target(place.t))
        for i in (4, 5, 3, 6, 2, 7, 1):
            to = (place.t + i) % SLAB
            self.wire.send(self.source(to), self.target(place.t), self.slots[i], (place.r, to))

    def wait(self):
        place = self.wire.place
        for i in range(1, SLAB):
            self.wire.arrived(self.target((place.t + SLAB - i) % SLAB), self.slots[i])
        self.own.wait()


class GroupGather:
    def __init__(self, wire, at):
        self.wire, self.at = wire, at
        self.slots = wire.recv_slots(wire.place.groups)

    def start(self, src):
        place = self.wire.place
        for i in range(1, place.groups):
            self.wire.send(src, self.at(place.r), self.slots[i], ((place.r + i) % place.groups, place.t))

    def wait(self):
        place = self.wire.place
        for i in range(1, place.groups):
            self.wire.arrived(self.at((place.r + place.groups - i) % place.groups), self.slots[i])


class GroupScatter:
    def __init__(self, wire, out, into, own):
        self.wire, self.out, self.into, self.own = wire, out, into, own
        self.slots = wire.recv_slots(wire.place.groups)

    def start(self, make):
        place = self.wire.place
        for i in range(1, place.groups):
            to = (place.r + i) % place.groups
            self.out[i - 1] = make(to).astype(BF16)
            self.wire.send(self.out.at[i - 1], self.into.at[i - 1], self.slots[i], (to, place.t))
        self.own[...] = make(place.r)

    def total(self):
        total = self.own[...]
        for i in range(1, self.wire.place.groups):
            self.wire.arrived(self.into.at[i - 1], self.slots[i])
            total = total + self.into[i - 1].astype(F32)
        return total


def layer_kernel(
    groups,
    scale,
    tokens,
    upstream,
    pack,
    w_in,
    w_out,
    w_exp,
    w_shr,
    layer_out,
    tokens_grad,
    in_grad,
    out_grad,
    exp_grad,
    shr_grad,
    vec_grad,
    packs,
    tok_all,
    first_all,
    win,
    wex,
    wsh,
    wo,
    gls,
    gls_all,
    vecs,
    ebias,
    qkv,
    gqkv,
    soft_all,
    blend_t,
    blend,
    middle,
    normed,
    inverses,
    second,
    second_all,
    active,
    ghid,
    part_a,
    part_b,
    part_c,
    part_d,
    core_a,
    core_b,
    core_c,
    core_d,
    chip_a,
    chip_b,
    chip_c,
    chip_d,
    gsec,
    glow,
    gblend,
    gblend_t,
    sh_out,
    sh_in,
    sh_own,
    ex_out,
    ex_in,
    ex_own,
    ex_sum,
    ex_all,
    in_out,
    in_in,
    in_own,
    in_sum,
    in_all,
    ou_out,
    ou_in,
    ou_own,
    gvec,
    gvec_exp,
    gvec_out,
    gvec_in,
    send_sems,
    recv_sems,
    local_sems,
):
    place = Place(groups)
    wire = Wire(place, send_sems, recv_sems, local_sems)
    f, y, r, xc, t = place.f, place.y, place.r, place.xc, place.t
    devices = groups * SLAB
    me = r * SLAB + t
    seg, width = tokens.shape
    clips = SLAB // 2
    slots = seg * 2
    total_rows = SLAB * seg
    head2 = qkv.shape[1] // 3
    own_rows = w_in.shape[0]
    slab_rows = own_rows * 4
    share = width // devices
    chunk = wsh.shape[1]

    barrier = pltpu.get_barrier_semaphore()
    for i in range(1, devices):
        to = (me + i) % devices
        pl.semaphore_signal(barrier, inc=1, device_id=place.device(to // SLAB, to % SLAB), device_id_type=MESH)
    pl.semaphore_wait(barrier, devices - 1)

    pack_slots = wire.recv_slots(groups * 4)
    for i in range(1, groups * 4):
        to = (f + i) % (groups * 4)
        wire.send(pack, packs.at[f], pack_slots[i], (to // 4, (to % 4) * 2 + y))
    own_pack = wire.local(pack, packs.at[f])

    in_slots = wire.recv_slots(12)
    ex_slots = wire.recv_slots(4 * groups)

    def in_piece(index, c):
        return win.at[pl.ds(pl.multiple_of(index * own_rows, own_rows), own_rows), pl.ds(c * head2, head2)]

    def ex_piece(index, c):
        return wex.at[pl.ds(pl.multiple_of(index * own_rows, own_rows), own_rows), pl.ds(c * chunk, chunk)]

    own_in = []
    for i in (2, 3, 1, 0):
        to = ((xc + i) % 4) * 2 + y
        for c in range(3):
            src = w_in.at[:, pl.ds(pl.multiple_of(c * width + to * head2, head2), head2)]
            if i == 0:
                own_in.append(wire.local(src, in_piece(f, c)))
            else:
                wire.send(src, in_piece(f, c), in_slots[i * 3 + c], (r, to))
    gather_tok = SlabGather(wire, lambda at: rows(tok_all, at, seg))
    gather_tok.start(tokens)
    own_tok = wire.local(tokens, rows(tok_all, t, seg))

    out_share = w_out.at[pl.ds(pl.multiple_of(y * share, share), share), :]
    own_out = wire.local(out_share, wo.at[r, t])
    group_wo = GroupGather(wire, lambda at: wo.at[at, t])
    group_wo.start(out_share)

    own_ex = []
    for i in (2, 3, 1, 0):
        to = ((xc + i) % 4) * 2 + y
        for c in range(groups):
            src = w_exp.at[:, pl.ds(pl.multiple_of((c * SLAB + to) * chunk, chunk), chunk)]
            if i == 0:
                own_ex.append(wire.local(src, ex_piece(f, c)))
            else:
                wire.send(src, ex_piece(f, c), ex_slots[i * groups + c], (r, to))

    row_at = y * seg + lax.broadcasted_iota(jnp.int32, (seg, 1), 0)
    row_valid = row_at.astype(F32) < pack[10:11, 0:1].astype(F32)
    gls[...] = jnp.where(row_valid, upstream[...].astype(F32), 0.0).astype(BF16)

    for i in range(1, 4):
        frm = r * 4 + (xc + 4 - i) % 4
        for c in range(3):
            wire.arrived(in_piece(frm, c), in_slots[i * 3 + c])
    for copy in own_in:
        copy.wait()
    group_in = GroupGather(wire, lambda at: rows(win, at, slab_rows))
    group_in.start(rows(win, r, slab_rows))

    gather_tok.forward()
    own_tok.wait()

    shr_share = w_shr.at[pl.ds(pl.multiple_of(y * chunk, chunk), chunk), :]
    own_shr = wire.local(shr_share, wsh.at[r])
    for i in range(1, 4):
        frm = r * 4 + (xc + 4 - i) % 4
        for c in range(groups):
            wire.arrived(ex_piece(frm, c), ex_slots[i * groups + c])
    for copy in own_ex:
        copy.wait()
    group_ex = GroupGather(wire, lambda at: rows(wex, at, slab_rows))
    group_ex.start(rows(wex, r, slab_rows))
    group_sh = GroupGather(wire, lambda at: wsh.at[at])
    group_sh.start(shr_share)

    own_pack.wait()
    for i in range(1, groups * 4):
        wire.arrived(packs.at[(f + groups * 4 - i) % (groups * 4)], pack_slots[i])
    per_lane = 128 // own_rows
    lane = lax.broadcasted_iota(jnp.int32, (1, 128), 1)
    for j in range(width // 128):
        piece = packs[j * per_lane].astype(F32)
        for k in range(1, per_lane):
            piece = jnp.where(lane >= k * own_rows, packs[j * per_lane + k].astype(F32), piece)
        vecs[:, j * 128 : (j + 1) * 128] = piece
    for c in range(groups):
        both = packs[c * 4 + t // 2].astype(F32)
        ebias[0:1, c * chunk : (c + 1) * chunk] = jnp.where(y == 0, both[8:9], both[9:10])

    gather_tok.wait()
    strip = 32

    def first_norm(i, carry):
        at = pl.ds(pl.multiple_of(i * strip, strip), strip)
        n, _ = row_stats(tok_all[at, :].astype(F32))
        first_all[at, :] = (n * vecs[0:1, :] + vecs[1:2, :]).astype(BF16)
        return carry

    lax.fori_loop(0, total_rows // strip, first_norm, 0)

    own_out.wait()
    group_wo.wait()
    gather_wo = SlabGather(wire, lambda at: wo.at[:, at])
    gather_wo.start(wo.at[:, t])

    group_in.wait()
    tile = 256
    at_head = pl.ds(pl.multiple_of(t * head2, head2), head2)
    bias = jnp.concatenate([vecs[2:3, at_head], jnp.zeros((1, head2), F32), vecs[3:4, at_head]], axis=1)

    def project(i, carry):
        at = pl.ds(pl.multiple_of(i * tile, tile), tile)
        qkv[at, :] = (matmul(first_all[at, :], win[...]) + bias).astype(BF16)
        return carry

    lax.fori_loop(0, total_rows // tile, project, 0)

    gather_wo.forward()

    head_size = head2 // 2
    low_half = lane < head_size
    half_masks = [low_half.astype(F32).astype(BF16), (1.0 - low_half.astype(F32)).astype(BF16)]
    key_at = lax.broadcasted_iota(jnp.int32, (1, slots), 1).astype(F32)

    def attend(i, carry):
        at = pl.ds(pl.multiple_of(i * slots, slots), slots)
        q = qkv[at, 0:head2]
        k = qkv[at, head2 : 2 * head2]
        v = qkv[at, 2 * head2 : 3 * head2]
        count = packs[r * 4 + i].astype(F32)[10:11, 0:1]
        key_valid = key_at < count
        halves = []
        for h in range(2):
            scores = matmul_bt(q * half_masks[h], k) * scale
            scores = jnp.where(key_valid, scores, -1e30)
            top = jnp.max(scores, axis=-1, keepdims=True)
            log_total = top + jnp.log(jnp.sum(jnp.exp(scores - top), axis=-1, keepdims=True))
            soft = jnp.exp(scores - log_total)
            soft_all[i * 2 + h] = soft
            halves.append(matmul(soft.astype(BF16), v))
        blend_t[at, :] = jnp.where(low_half, halves[0], halves[1]).astype(BF16)
        return carry

    lax.fori_loop(0, clips, attend, 0)

    swap_blend = SlabSwap(wire, lambda at: rows(blend_t, at, seg), lambda at: cols(blend, at, head2))
    swap_blend.start()
    gather_gls = SlabGather(wire, lambda at: rows(gls_all, at, seg))
    own_gls = wire.local(gls, rows(gls_all, t, seg))

    gather_wo.wait()
    swap_blend.wait()
    wide = 256
    for j in range(width // wide):
        at = slice(j * wide, (j + 1) * wide)
        product = matmul(blend[...], wo[:, :, :, at].reshape(width, wide))
        middle[:, at] = tokens[:, at].astype(F32) + (product + vecs[4:5, at])

    def second_norm(i, carry):
        at = pl.ds(pl.multiple_of(i * strip, strip), strip)
        n, inverse = row_stats(middle[at, :])
        normed[at, :] = n
        inverses[at, :] = jnp.broadcast_to(inverse, (strip, 128))
        second[at, :] = (n * vecs[5:6, :] + vecs[6:7, :]).astype(BF16)
        return carry

    lax.fori_loop(0, seg // strip, second_norm, 0)

    gather_second = SlabGather(wire, lambda at: rows(second_all, at, seg))
    gather_second.start(second)
    own_second = wire.local(second, rows(second_all, t, seg))
    gather_gls.start(gls)
    gather_second.forward()
    gather_gls.forward()
    gather_second.wait()
    own_second.wait()
    gather_gls.wait()
    own_gls.wait()
    for copy in (own_shr,):
        copy.wait()
    group_ex.wait()
    group_sh.wait()

    hidden_units = groups * chunk

    def feed(i, carry):
        at = pl.ds(pl.multiple_of(i * tile, tile), tile)
        hidden = matmul(second_all[at, :], wex[...]) + ebias[0:1, :]
        grad_active = matmul_bt(gls_all[at, :], wsh[...].reshape(hidden_units, width))
        cdf = 0.5 * (1.0 + lax.erf(hidden * 0.7071067811865476))
        active[at, :] = (hidden * cdf).astype(BF16)
        slope = cdf + hidden * (0.3989422804014327 * jnp.exp(-0.5 * hidden * hidden))
        grad_hidden = (grad_active * slope).astype(BF16)
        ghid[at, :] = grad_hidden
        gvec_exp[...] += jnp.sum(grad_hidden.astype(F32), axis=0, keepdims=True)
        part_a[at, :] = matmul_bt(grad_hidden, wex[...]).astype(BF16)
        return carry

    gvec_exp[...] = jnp.zeros_like(gvec_exp)
    lax.fori_loop(0, total_rows // tile, feed, 0)

    scatter_second = SlabScatter(wire, part_a, core_a, chip_a, seg)
    scatter_second.cores()

    def feed_out(i, carry):
        at = pl.ds(pl.multiple_of(i * tile, tile), tile)
        part_b[at, :] = matmul(active[at, :], wsh[...].reshape(hidden_units, width)).astype(BF16)
        return carry

    lax.fori_loop(0, total_rows // tile, feed_out, 0)
    scatter_second.chips()

    group_shr = GroupScatter(wire, sh_out, sh_in, sh_own)
    group_shr.start(
        lambda c: matmul_at(active[:, pl.ds(pl.multiple_of(c * chunk, chunk), chunk)], gls_all[...])
    )
    scatter_second.wait()

    gvec[...] = jnp.zeros_like(gvec)

    def second_back(i, carry):
        first = i * strip
        at = pl.ds(pl.multiple_of(first, strip), strip)
        grad = scatter_second.total(first, strip)
        n = normed[at, :]
        back = row_norm_back(grad, n, inverses[at, 0:1], vecs[5:6, :])
        grad_result = gls[at, :].astype(F32)
        grad_middle = grad_result + back
        gsec[at, :] = grad_middle
        low = grad_middle.astype(BF16)
        glow[at, :] = low
        gvec[4:5, :] += jnp.sum(low.astype(F32), axis=0, keepdims=True)
        gvec[5:6, :] += jnp.sum(grad * n, axis=0, keepdims=True)
        gvec[6:7, :] += jnp.sum(grad, axis=0, keepdims=True)
        gvec[7:8, :] += jnp.sum(grad_result, axis=0, keepdims=True)
        return carry

    lax.fori_loop(0, seg // strip, second_back, 0)

    for j in range(width // wide):
        rows_of = slice(j * (groups * wide // width), (j + 1) * (groups * wide // width))
        gblend[:, j * wide : (j + 1) * wide] = matmul_bt(
            glow[...], wo[rows_of].reshape(wide, width)
        ).astype(BF16)
    swap_gblend = SlabSwap(wire, lambda at: cols(gblend, at, head2), lambda at: rows(gblend_t, at, seg))
    swap_gblend.start()

    scatter_result = SlabScatter(wire, part_b, core_b, chip_b, seg)
    scatter_result.cores()
    group_exp = GroupScatter(wire, ex_out, ex_in, ex_own)
    group_exp.start(
        lambda c: matmul_at(second_all[:, pl.ds(pl.multiple_of(c * slab_rows, slab_rows), slab_rows)], ghid[...])
    )
    scatter_result.chips()

    swap_gblend.wait()

    def attend_back(i, carry):
        at = pl.ds(pl.multiple_of(i * slots, slots), slots)
        q = qkv[at, 0:head2]
        k = qkv[at, head2 : 2 * head2]
        v = qkv[at, 2 * head2 : 3 * head2]
        grad = gblend_t[at, :]
        parts = []
        for h in range(2):
            soft = soft_all[i * 2 + h]
            grad_soft = matmul_bt(grad * half_masks[h], v)
            inner = jnp.sum(grad_soft * soft, axis=-1, keepdims=True)
            grad_scores = (soft * (grad_soft - inner)).astype(BF16)
            parts.append(
                (
                    matmul(grad_scores, k) * scale,
                    matmul_at(grad_scores, q) * scale,
                    matmul_at(soft.astype(BF16), grad),
                )
            )
        for c in range(3):
            gqkv[at, c * head2 : (c + 1) * head2] = jnp.where(low_half, parts[0][c], parts[1][c]).astype(BF16)
        return carry

    lax.fori_loop(0, clips, attend_back, 0)

    def project_back(i, carry):
        at = pl.ds(pl.multiple_of(i * tile, tile), tile)
        part_c[at, :] = matmul_bt(gqkv[at, :], win[...]).astype(BF16)
        return carry

    lax.fori_loop(0, total_rows // tile, project_back, 0)
    scatter_first = SlabScatter(wire, part_c, core_c, chip_c, seg)
    scatter_first.cores()

    group_inw = GroupScatter(wire, in_out, in_in, in_own)
    group_inw.start(
        lambda c: matmul_at(first_all[:, pl.ds(pl.multiple_of(c * slab_rows, slab_rows), slab_rows)], gqkv[...])
    )
    scatter_first.chips()
    gvec[2:3, at_head] = jnp.sum(gqkv[:, 0:head2].astype(F32), axis=0, keepdims=True)
    gvec[3:4, at_head] = jnp.sum(gqkv[:, 2 * head2 :].astype(F32), axis=0, keepdims=True)

    for c in range(groups):
        product = matmul_at(blend[:, c * slab_rows : (c + 1) * slab_rows], glow[...])
        for to in range(SLAB):
            part_d[to * seg + c * share : to * seg + (c + 1) * share, :] = product[
                to * share : (to + 1) * share
            ].astype(BF16)
    scatter_out = SlabScatter(wire, part_d, core_d, chip_d, seg)
    scatter_out.cores()

    scatter_result.wait()

    def finish_out(i, carry):
        first = i * strip
        at = pl.ds(pl.multiple_of(first, strip), strip)
        result = middle[at, :] + (scatter_result.total(first, strip) + vecs[7:8, :])
        spot = y * seg + first + lax.broadcasted_iota(jnp.int32, (strip, 1), 0)
        valid = spot.astype(F32) < pack[10:11, 0:1].astype(F32)
        layer_out[at, :] = jnp.where(valid, result, 0.0).astype(BF16)
        return carry

    lax.fori_loop(0, seg // strip, finish_out, 0)
    shr_grad[...] = group_shr.total()
    ex_sum[...] = group_exp.total().astype(BF16)
    swap_exp = SlabSwap(wire, lambda at: rows(ex_sum, at, share), lambda at: ex_all.at[at])
    swap_exp.start()

    scatter_out.chips()
    scatter_first.wait()

    def first_back(i, carry):
        first = i * strip
        at = pl.ds(pl.multiple_of(first, strip), strip)
        grad = scatter_first.total(first, strip)
        n, inverse = row_stats(tokens[at, :].astype(F32))
        tokens_grad[at, :] = gsec[at, :] + row_norm_back(grad, n, inverse, vecs[0:1, :])
        gvec[0:1, :] += jnp.sum(grad * n, axis=0, keepdims=True)
        gvec[1:2, :] += jnp.sum(grad, axis=0, keepdims=True)
        return carry

    lax.fori_loop(0, seg // strip, first_back, 0)

    per_chunk = 128 // share
    for j in range(width // 128):
        gvec_out[j, 0:8, :] = gvec[:, j * 128 : (j + 1) * 128]
        c = j * per_chunk // SLAB
        gvec_out[j, 8:16, :] = jnp.broadcast_to(gvec_exp[0:1, c * chunk : (c + 1) * chunk], (8, chunk))
    vec_slots = wire.recv_slots(devices)
    for i in range(1, devices):
        to = (me + i) % devices
        wire.send(gvec_out.at[to // per_chunk], gvec_in.at[me], vec_slots[i], (to // SLAB, to % SLAB))
    own_vec = wire.local(gvec_out.at[me // per_chunk], gvec_in.at[me])

    in_sum[...] = group_inw.total().astype(BF16)
    swap_in = SlabSwap(wire, lambda at: rows(in_sum, at, share), lambda at: in_all.at[at])
    swap_in.start()

    scatter_out.wait()
    group_out = GroupScatter(wire, ou_out, ou_in, ou_own)
    group_out.start(lambda c: scatter_out.total(c * share, share))

    swap_exp.wait()
    for frm in range(SLAB):
        for c in range(groups):
            place_at = (c * SLAB + frm) * chunk
            exp_grad[:, place_at : place_at + chunk] = ex_all[frm, :, c * chunk : (c + 1) * chunk].astype(F32)
    swap_in.wait()
    for frm in range(SLAB):
        for c in range(3):
            place_at = c * width + frm * head2
            in_grad[:, place_at : place_at + head2] = in_all[frm, :, c * head2 : (c + 1) * head2].astype(F32)
    own_vec.wait()
    for i in range(1, devices):
        wire.arrived(gvec_in.at[(me + devices - i) % devices], vec_slots[i])
    summed = gvec_in[0]
    for i in range(1, devices):
        summed = summed + gvec_in[i]
    for_exp = gvec_in[t]
    for c in range(1, groups):
        for_exp = for_exp + gvec_in[c * SLAB + t]
    vec_grad[0:8, :] = pltpu.roll(summed[0:8], (128 - share * (me % per_chunk)) % 128, 1)
    vec_grad[8:16, :] = for_exp[8:16]
    out_grad[...] = group_out.total()
    wire.finish()


def fused_shards(
    tokens,
    visible,
    first_gain,
    first_shift,
    inward_weight,
    query_bias,
    value_bias,
    outward_weight,
    outward_bias,
    second_gain,
    second_shift,
    expand_weight,
    expand_bias,
    shrink_weight,
    shrink_bias,
    upstream,
):
    seg, width = tokens.shape[1:]
    groups = lax.axis_size("fsdp") // 4
    devices = groups * SLAB
    own_rows = inward_weight.shape[0]
    hidden = expand_weight.shape[1]
    share = width // devices
    chunk = hidden // devices
    units = groups * chunk
    head2 = width // SLAB
    scale = (width // HEADS) ** (-0.5)
    total_rows = SLAB * seg
    slab_rows = 4 * own_rows
    vectors = jnp.stack(
        [first_gain, first_shift, query_bias, value_bias, outward_bias, second_gain, second_shift, shrink_bias]
    )
    pack = jnp.concatenate(
        [
            jnp.concatenate([vectors] * (128 // own_rows), axis=1),
            expand_bias.reshape(2, 128),
            jnp.broadcast_to(visible.astype(BF16)[:, None], (6, 128)),
        ]
    )
    vmem = pl.BlockSpec(memory_space=pltpu.VMEM)
    anywhere = pl.BlockSpec(memory_space=pl.ANY)
    outs = pl.pallas_call(
        functools.partial(layer_kernel, groups, scale),
        out_shape=(
            jax.ShapeDtypeStruct((seg, width), BF16),
            jax.ShapeDtypeStruct((seg, width), F32),
            jax.ShapeDtypeStruct((share, 3 * width), F32),
            jax.ShapeDtypeStruct((share, width), F32),
            jax.ShapeDtypeStruct((share, hidden), F32),
            jax.ShapeDtypeStruct((chunk, width), F32),
            jax.ShapeDtypeStruct((16, 128), F32),
        ),
        in_specs=[vmem, vmem, vmem, anywhere, anywhere, anywhere, anywhere],
        out_specs=[vmem] * 7,
        scratch_shapes=[
            pltpu.VMEM((groups * 4, 16, 128), BF16),
            pltpu.VMEM((total_rows, width), BF16),
            pltpu.VMEM((total_rows, width), BF16),
            pltpu.VMEM((width, 3 * head2), BF16),
            pltpu.VMEM((width, units), BF16),
            pltpu.VMEM((groups, chunk, width), BF16),
            pltpu.VMEM((groups, SLAB, share, width), BF16),
            pltpu.VMEM((seg, width), BF16),
            pltpu.VMEM((total_rows, width), BF16),
            pltpu.VMEM((16, width), F32),
            pltpu.VMEM((8, units), F32),
            pltpu.VMEM((total_rows, 3 * head2), BF16),
            pltpu.VMEM((total_rows, 3 * head2), BF16),
            pltpu.VMEM((SLAB, 2 * seg, 2 * seg), F32),
            pltpu.VMEM((total_rows, head2), BF16),
            pltpu.VMEM((seg, width), BF16),
            pltpu.VMEM((seg, width), F32),
            pltpu.VMEM((seg, width), F32),
            pltpu.VMEM((seg, 128), F32),
            pltpu.VMEM((seg, width), BF16),
            pltpu.VMEM((total_rows, width), BF16),
            pltpu.VMEM((total_rows, units), BF16),
            pltpu.VMEM((total_rows, units), BF16),
        ]
        + [pltpu.VMEM((total_rows, width), BF16)] * 4
        + [pltpu.VMEM((4, seg, width), BF16)] * 4
        + [pltpu.VMEM((3, seg, width), BF16)] * 4
        + [
            pltpu.VMEM((seg, width), F32),
            pltpu.VMEM((seg, width), BF16),
            pltpu.VMEM((seg, width), BF16),
            pltpu.VMEM((total_rows, head2), BF16),
            pltpu.VMEM((groups - 1, chunk, width), BF16),
            pltpu.VMEM((groups - 1, chunk, width), BF16),
            pltpu.VMEM((chunk, width), F32),
            pltpu.VMEM((groups - 1, slab_rows, units), BF16),
            pltpu.VMEM((groups - 1, slab_rows, units), BF16),
            pltpu.VMEM((slab_rows, units), F32),
            pltpu.VMEM((slab_rows, units), BF16),
            pltpu.VMEM((SLAB, share, units), BF16),
            pltpu.VMEM((groups - 1, slab_rows, 3 * head2), BF16),
            pltpu.VMEM((groups - 1, slab_rows, 3 * head2), BF16),
            pltpu.VMEM((slab_rows, 3 * head2), F32),
            pltpu.VMEM((slab_rows, 3 * head2), BF16),
            pltpu.VMEM((SLAB, share, 3 * head2), BF16),
            pltpu.VMEM((groups - 1, share, width), BF16),
            pltpu.VMEM((groups - 1, share, width), BF16),
            pltpu.VMEM((share, width), F32),
            pltpu.VMEM((8, width), F32),
            pltpu.VMEM((1, units), F32),
            pltpu.VMEM((width // 128, 16, 128), F32),
            pltpu.VMEM((devices, 16, 128), F32),
            pltpu.SemaphoreType.DMA((320,)),
            pltpu.SemaphoreType.DMA((320,)),
            pltpu.SemaphoreType.DMA((40,)),
        ],
        compiler_params=pltpu.CompilerParams(
            collective_id=0, has_side_effects=True, vmem_limit_bytes=67043328
        ),
        name="layer",
    )(
        tokens.reshape(seg, width),
        upstream.reshape(seg, width),
        pack,
        inward_weight,
        outward_weight,
        expand_weight,
        shrink_weight,
    )
    layer_out, tokens_grad, in_grad, out_grad, exp_grad, shr_grad, vec = outs

    def vector(k):
        return vec[k, :share]

    return (
        layer_out.reshape(1, seg, width),
        tokens_grad.reshape(1, seg, width),
        vector(0),
        vector(1),
        in_grad,
        vector(2),
        vector(3),
        out_grad,
        vector(4),
        vector(5),
        vector(6),
        exp_grad,
        vec[8],
        shr_grad,
        vector(7),
    )


def fits_fused(mesh, tokens, inward_weight, expand_weight):
    fsdp, seq = mesh.shape["fsdp"], mesh.shape["seq"]
    clips, slots, width = tokens.shape
    devices = fsdp * seq
    return (
        seq == 2
        and clips == fsdp
        and fsdp % 4 == 0
        and width // HEADS * 2 == 128
        and width == SLAB * 128
        and slots % 64 == 0
        and width % (16 * devices) == 0
        and 128 % (width // fsdp) == 0
        and expand_weight.shape[1] == 128 * devices
    )


def solution(mesh):
    in_specs = (
        P("fsdp", "seq", None),
        P("fsdp"),
        P("fsdp"),
        P("fsdp"),
        P("fsdp", None),
        P("fsdp"),
        P("fsdp"),
        P("fsdp", None),
        P("fsdp"),
        P("fsdp"),
        P("fsdp"),
        P("fsdp", None),
        P("fsdp"),
        P("fsdp", None),
        P("fsdp"),
        P("fsdp", "seq", None),
    )
    out_specs = (
        P("fsdp", "seq", None),
        P("fsdp", "seq", None),
        P(("fsdp", "seq")),
        P(("fsdp", "seq")),
        P(("fsdp", "seq"), None),
        P(("fsdp", "seq")),
        P(("fsdp", "seq")),
        P(("fsdp", "seq"), None),
        P(("fsdp", "seq")),
        P(("fsdp", "seq")),
        P(("fsdp", "seq")),
        P(("fsdp", "seq"), None),
        P(("fsdp", "seq")),
        P(("fsdp", "seq"), None),
        P(("fsdp", "seq")),
    )

    def step(*args):
        body = fused_shards if fits_fused(mesh, args[0], args[4], args[11]) else shards
        return jax.shard_map(body, mesh=mesh, in_specs=in_specs, out_specs=out_specs, check_vma=False)(*args)

    return step
```

```python
import functools

import jax
import jax.numpy as jnp
from jax import lax
from jax.experimental import pallas as pl
from jax.experimental.pallas import tpu as pltpu
from jax.sharding import PartitionSpec as P

HEADS = 16


epsilon = 1e-06


def norm_rows(inputs, norm_gain, norm_shift):
    row_mean = jnp.mean(inputs, axis=-1, keepdims=True)
    centered = inputs - row_mean
    variance = jnp.mean(centered * centered, axis=-1, keepdims=True)
    inverse = lax.rsqrt(variance + epsilon)
    normed = centered * inverse
    return (normed * norm_gain + norm_shift, normed, inverse)


def norm_back(grad_out, normed, inverse, norm_gain):
    scaled = grad_out * norm_gain
    first_mean = jnp.mean(scaled, axis=-1, keepdims=True)
    second_mean = jnp.mean(scaled * normed, axis=-1, keepdims=True)
    return inverse * (scaled - first_mean - normed * second_mean)


def gather_weights(
    first_gain,
    first_shift,
    inward_weight,
    query_bias,
    value_bias,
    outward_weight,
    outward_bias,
    second_gain,
    second_shift,
    expand_weight,
    expand_bias,
    shrink_weight,
    shrink_bias,
):
    return (
        lax.all_gather(first_gain, "fsdp", axis=0, tiled=True),
        lax.all_gather(first_shift, "fsdp", axis=0, tiled=True),
        lax.all_gather(inward_weight, "fsdp", axis=0, tiled=True),
        lax.all_gather(query_bias, "fsdp", axis=0, tiled=True),
        lax.all_gather(value_bias, "fsdp", axis=0, tiled=True),
        lax.all_gather(outward_weight, "fsdp", axis=0, tiled=True),
        lax.all_gather(outward_bias, "fsdp", axis=0, tiled=True),
        lax.all_gather(second_gain, "fsdp", axis=0, tiled=True),
        lax.all_gather(second_shift, "fsdp", axis=0, tiled=True),
        lax.all_gather(expand_weight, "fsdp", axis=0, tiled=True),
        lax.all_gather(expand_bias, "fsdp", axis=0, tiled=True),
        lax.all_gather(shrink_weight, "fsdp", axis=0, tiled=True),
        lax.all_gather(shrink_bias, "fsdp", axis=0, tiled=True),
    )


def attend_scores(query_heads, key_heads, key_valid, scale):
    scores = (
        jnp.einsum("cqhe,ckhe->chqk", query_heads, key_heads, preferred_element_type=jnp.float32)
        * scale
    )
    return jnp.where(key_valid[:, None, None, :], scores, -1e30)


def forward(tokens32, key_valid, row_valid, gathered):
    (
        first_gain,
        first_shift,
        inward_weight,
        query_bias,
        value_bias,
        outward_weight,
        outward_bias,
        second_gain,
        second_shift,
        expand_weight,
        expand_bias,
        shrink_weight,
        shrink_bias,
    ) = gathered
    clip_count, seg_rows, model_width = tokens32.shape
    head_size = model_width // HEADS
    scale = head_size ** (-0.5)
    affine_first, normed_first, inverse_first = norm_rows(
        tokens32, first_gain.astype(jnp.float32), first_shift.astype(jnp.float32)
    )
    lowered_first = affine_first.astype(jnp.bfloat16)
    merged_bias = jnp.concatenate([query_bias, jnp.zeros_like(query_bias), value_bias]).astype(
        jnp.float32
    )
    project = (
        jnp.einsum("csd,de->cse", lowered_first, inward_weight, preferred_element_type=jnp.float32)
        + merged_bias
    )
    queries = project[..., :model_width].astype(jnp.bfloat16)
    key_local = project[..., model_width : 2 * model_width].astype(jnp.bfloat16)
    value_local = project[..., 2 * model_width :].astype(jnp.bfloat16)
    key_all, value_all = (
        lax.all_gather(key_local, "seq", axis=1, tiled=True),
        lax.all_gather(value_local, "seq", axis=1, tiled=True),
    )
    slot_count = key_all.shape[1]
    query_heads = queries.reshape(clip_count, seg_rows, HEADS, head_size)
    key_heads = key_all.reshape(clip_count, slot_count, HEADS, head_size)
    value_heads = value_all.reshape(clip_count, slot_count, HEADS, head_size)
    scores = attend_scores(query_heads, key_heads, key_valid, scale)
    row_top = jnp.max(scores, axis=-1, keepdims=True)
    row_total = jnp.sum(jnp.exp(scores - row_top), axis=-1, keepdims=True)
    log_total = row_top + jnp.log(row_total)
    soft_low = jnp.exp(scores - log_total).astype(jnp.bfloat16)
    blended = jnp.einsum(
        "chqk,ckhe->cqhe", soft_low, value_heads, preferred_element_type=jnp.float32
    )
    blended = blended.reshape(clip_count, seg_rows, model_width).astype(jnp.bfloat16)
    branch = jnp.einsum(
        "csd,de->cse", blended, outward_weight, preferred_element_type=jnp.float32
    ) + outward_bias.astype(jnp.float32)
    middle = tokens32 + branch
    affine_second, normed_second, inverse_second = norm_rows(
        middle, second_gain.astype(jnp.float32), second_shift.astype(jnp.float32)
    )
    lowered_second = affine_second.astype(jnp.bfloat16)
    hidden = jnp.einsum(
        "csd,df->csf", lowered_second, expand_weight, preferred_element_type=jnp.float32
    ) + expand_bias.astype(jnp.float32)
    active = jax.nn.gelu(hidden, approximate=False).astype(jnp.bfloat16)
    branch_second = jnp.einsum(
        "csf,fd->csd", active, shrink_weight, preferred_element_type=jnp.float32
    ) + shrink_bias.astype(jnp.float32)
    result = middle + branch_second
    output = jnp.where(row_valid, result, 0.0).astype(jnp.bfloat16)
    return {
        "normed_first": normed_first,
        "inverse_first": inverse_first,
        "lowered_first": lowered_first,
        "query_heads": query_heads,
        "key_heads": key_heads,
        "value_heads": value_heads,
        "log_total": log_total,
        "blended": blended,
        "normed_second": normed_second,
        "inverse_second": inverse_second,
        "lowered_second": lowered_second,
        "hidden": hidden,
        "active": active,
        "output": output,
    }


def gelu_exact(inputs):
    return jax.nn.gelu(inputs, approximate=False)


def backward(saved, gathered, upstream32, key_valid, row_valid):
    (
        first_gain,
        first_shift,
        inward_weight,
        query_bias,
        value_bias,
        outward_weight,
        outward_bias,
        second_gain,
        second_shift,
        expand_weight,
        expand_bias,
        shrink_weight,
        shrink_bias,
    ) = gathered
    clip_count, seg_rows, model_width = upstream32.shape
    head_size = model_width // HEADS
    scale = head_size ** (-0.5)
    grad_result = jnp.where(row_valid, upstream32, 0.0)
    grad_low_second = grad_result.astype(jnp.bfloat16)
    shrink_weight_grad = jnp.einsum(
        "csf,csd->fd", saved["active"], grad_low_second, preferred_element_type=jnp.float32
    )
    shrink_bias_grad = jnp.sum(grad_low_second.astype(jnp.float32), axis=(0, 1))
    grad_active = jnp.einsum(
        "csd,fd->csf", grad_low_second, shrink_weight, preferred_element_type=jnp.float32
    )
    gelu_value, gelu_pull = jax.vjp(gelu_exact, saved["hidden"])
    grad_hidden = gelu_pull(grad_active)[0].astype(jnp.bfloat16)
    expand_weight_grad = jnp.einsum(
        "csd,csf->df", saved["lowered_second"], grad_hidden, preferred_element_type=jnp.float32
    )
    expand_bias_grad = jnp.sum(grad_hidden.astype(jnp.float32), axis=(0, 1))
    grad_second = jnp.einsum(
        "csf,df->csd", grad_hidden, expand_weight, preferred_element_type=jnp.float32
    )
    second_gain_grad = jnp.sum(grad_second * saved["normed_second"], axis=(0, 1))
    second_shift_grad = jnp.sum(grad_second, axis=(0, 1))
    grad_middle = grad_result + norm_back(
        grad_second,
        saved["normed_second"],
        saved["inverse_second"],
        second_gain.astype(jnp.float32),
    )
    grad_low_first = grad_middle.astype(jnp.bfloat16)
    outward_weight_grad = jnp.einsum(
        "csd,cse->de", saved["blended"], grad_low_first, preferred_element_type=jnp.float32
    )
    outward_bias_grad = jnp.sum(grad_low_first.astype(jnp.float32), axis=(0, 1))
    grad_blended = jnp.einsum(
        "cse,de->csd", grad_low_first, outward_weight, preferred_element_type=jnp.float32
    )
    grad_blended = grad_blended.astype(jnp.bfloat16).reshape(clip_count, seg_rows, HEADS, head_size)
    query_heads = saved["query_heads"]
    key_heads = saved["key_heads"]
    value_heads = saved["value_heads"]
    slot_count = key_heads.shape[1]
    scores = attend_scores(query_heads, key_heads, key_valid, scale)
    soft = jnp.exp(scores - saved["log_total"])
    soft_low = soft.astype(jnp.bfloat16)
    grad_soft = jnp.einsum(
        "cqhe,ckhe->chqk", grad_blended, value_heads, preferred_element_type=jnp.float32
    )
    grad_scores = soft * (grad_soft - jnp.sum(grad_soft * soft, axis=-1, keepdims=True))
    grad_scores = grad_scores.astype(jnp.bfloat16)
    grad_queries = (
        jnp.einsum("chqk,ckhe->cqhe", grad_scores, key_heads, preferred_element_type=jnp.float32)
        * scale
    )
    grad_queries = grad_queries.astype(jnp.bfloat16).reshape(clip_count, seg_rows, model_width)
    grad_keys_part = (
        jnp.einsum("chqk,cqhe->ckhe", grad_scores, query_heads, preferred_element_type=jnp.float32)
        * scale
    )
    grad_values_part = jnp.einsum(
        "chqk,cqhe->ckhe", soft_low, grad_blended, preferred_element_type=jnp.float32
    )
    grad_keys_part = grad_keys_part.reshape(clip_count, slot_count, model_width)
    grad_values_part = grad_values_part.reshape(clip_count, slot_count, model_width)
    grad_keys, grad_values = (
        lax.psum_scatter(
            grad_keys_part.astype(jnp.bfloat16), "seq", scatter_dimension=1, tiled=True
        ).astype(jnp.float32),
        lax.psum_scatter(
            grad_values_part.astype(jnp.bfloat16), "seq", scatter_dimension=1, tiled=True
        ).astype(jnp.float32),
    )
    grad_keys = grad_keys.astype(jnp.bfloat16)
    grad_values = grad_values.astype(jnp.bfloat16)
    grad_project = jnp.concatenate([grad_queries, grad_keys, grad_values], axis=-1)
    inward_weight_grad = jnp.einsum(
        "csd,cse->de", saved["lowered_first"], grad_project, preferred_element_type=jnp.float32
    )
    query_bias_grad = jnp.sum(grad_queries.astype(jnp.float32), axis=(0, 1))
    value_bias_grad = jnp.sum(grad_values.astype(jnp.float32), axis=(0, 1))
    grad_first = jnp.einsum(
        "cse,de->csd", grad_project, inward_weight, preferred_element_type=jnp.float32
    )
    first_gain_grad = jnp.sum(grad_first * saved["normed_first"], axis=(0, 1))
    first_shift_grad = jnp.sum(grad_first, axis=(0, 1))
    tokens_grad = grad_middle + norm_back(
        grad_first, saved["normed_first"], saved["inverse_first"], first_gain.astype(jnp.float32)
    )
    weight_shares = (
        lax.psum_scatter(first_gain_grad, ("fsdp", "seq"), scatter_dimension=0, tiled=True),
        lax.psum_scatter(first_shift_grad, ("fsdp", "seq"), scatter_dimension=0, tiled=True),
        lax.psum_scatter(inward_weight_grad, ("fsdp", "seq"), scatter_dimension=0, tiled=True),
        lax.psum_scatter(query_bias_grad, ("fsdp", "seq"), scatter_dimension=0, tiled=True),
        lax.psum_scatter(value_bias_grad, ("fsdp", "seq"), scatter_dimension=0, tiled=True),
        lax.psum_scatter(outward_weight_grad, ("fsdp", "seq"), scatter_dimension=0, tiled=True),
        lax.psum_scatter(outward_bias_grad, ("fsdp", "seq"), scatter_dimension=0, tiled=True),
        lax.psum_scatter(second_gain_grad, ("fsdp", "seq"), scatter_dimension=0, tiled=True),
        lax.psum_scatter(second_shift_grad, ("fsdp", "seq"), scatter_dimension=0, tiled=True),
        lax.psum_scatter(expand_weight_grad, ("fsdp", "seq"), scatter_dimension=0, tiled=True),
        lax.psum_scatter(expand_bias_grad, ("fsdp", "seq"), scatter_dimension=0, tiled=True),
        lax.psum_scatter(shrink_weight_grad, ("fsdp", "seq"), scatter_dimension=0, tiled=True),
        lax.psum_scatter(shrink_bias_grad, ("fsdp", "seq"), scatter_dimension=0, tiled=True),
    )
    return (tokens_grad, weight_shares)


def shards(
    tokens,
    visible,
    first_gain,
    first_shift,
    inward_weight,
    query_bias,
    value_bias,
    outward_weight,
    outward_bias,
    second_gain,
    second_shift,
    expand_weight,
    expand_bias,
    shrink_weight,
    shrink_bias,
    upstream,
):
    clip_count, seg_rows, model_width = tokens.shape
    slot_count = seg_rows * lax.axis_size("seq")
    local_start = lax.axis_index("seq") * seg_rows
    row_positions = local_start + jnp.arange(seg_rows, dtype=jnp.int32)
    row_valid = (row_positions[None, :] < visible[:, None])[..., None]
    key_valid = jnp.arange(slot_count, dtype=jnp.int32)[None, :] < visible[:, None]
    tokens32 = tokens.astype(jnp.float32)
    upstream32 = upstream.astype(jnp.float32)
    gathered = gather_weights(
        first_gain,
        first_shift,
        inward_weight,
        query_bias,
        value_bias,
        outward_weight,
        outward_bias,
        second_gain,
        second_shift,
        expand_weight,
        expand_bias,
        shrink_weight,
        shrink_bias,
    )
    saved = forward(tokens32, key_valid, row_valid, gathered)
    layer_out = saved["output"]
    gathered = gather_weights(
        first_gain,
        first_shift,
        inward_weight,
        query_bias,
        value_bias,
        outward_weight,
        outward_bias,
        second_gain,
        second_shift,
        expand_weight,
        expand_bias,
        shrink_weight,
        shrink_bias,
    )
    saved = forward(tokens32, key_valid, row_valid, gathered)
    tokens_grad, shares = backward(saved, gathered, upstream32, key_valid, row_valid)
    return (
        layer_out,
        tokens_grad,
        shares[0],
        shares[1],
        shares[2],
        shares[3],
        shares[4],
        shares[5],
        shares[6],
        shares[7],
        shares[8],
        shares[9],
        shares[10],
        shares[11],
        shares[12],
    )


F32 = jnp.float32
BF16 = jnp.bfloat16
MESH = pl.DeviceIdType.MESH
SENDS, RECVS, LOCALS = 200, 138, 22
SLAB = 8


def matmul(a, b):
    return lax.dot_general(a, b, (((1,), (0,)), ((), ())), preferred_element_type=F32)


def matmul_bt(a, b):
    return lax.dot_general(a, b, (((1,), (1,)), ((), ())), preferred_element_type=F32)


def matmul_at(a, b):
    return lax.dot_general(a, b, (((0,), (0,)), ((), ())), preferred_element_type=F32)


def row_stats(x):
    mean = jnp.mean(x, axis=-1, keepdims=True)
    centered = x - mean
    inverse = lax.rsqrt(jnp.mean(centered * centered, axis=-1, keepdims=True) + epsilon)
    return centered * inverse, inverse


def row_norm_back(grad, normed, inverse, gain):
    scaled = grad * gain
    first_mean = jnp.mean(scaled, axis=-1, keepdims=True)
    second_mean = jnp.mean(scaled * normed, axis=-1, keepdims=True)
    return inverse * (scaled - first_mean - normed * second_mean)


class Place:
    def __init__(self, groups):
        self.groups = groups
        self.f = lax.axis_index("fsdp")
        self.y = lax.axis_index("seq")
        self.r = self.f // 4
        self.xc = self.f % 4
        self.t = self.xc * 2 + self.y
        x, c = self.xc // 2, self.xc % 2
        self.step = {4: 4 - 8 * x, 2: 2 - 4 * c, 1: 1 - 2 * self.y}

    def peer(self, mask):
        at = self.t
        for bit in (4, 2, 1):
            if mask & bit:
                at = at + self.step[bit]
        return at

    def device(self, r, t):
        return (r * 4 + t // 2, t % 2)


def rows(ref, index, size):
    return ref.at[pl.ds(pl.multiple_of(index * size, size), size), :]


def cols(ref, index, size):
    return ref.at[:, pl.ds(pl.multiple_of(index * size, size), size)]


class Wire:
    def __init__(self, place, send_sems, recv_sems, local_sems):
        self.place = place
        self.send_sems, self.recv_sems, self.local_sems = send_sems, recv_sems, local_sems
        self.sends = self.recvs = self.locals = 0
        self.free, self.open_sends = [], []

    def recv_slots(self, count):
        first = self.recvs
        self.recvs += count
        return [self.recv_sems.at[first + i] for i in range(count)]

    def send(self, src, dst, slot, to, when=None):
        if not self.free:
            self.free.append(self.sends)
            self.sends += 1
        spot = self.free.pop()
        send_sem = self.send_sems.at[spot]

        def make():
            return pltpu.make_async_remote_copy(
                src_ref=src,
                dst_ref=dst,
                send_sem=send_sem,
                recv_sem=slot,
                device_id=self.place.device(*to),
                device_id_type=MESH,
            )

        if when is None:
            make().start()
        else:
            pl.when(when)(lambda: make().start())
        self.open_sends.append((make, when, spot))

    def settle(self, count=None):
        count = len(self.open_sends) if count is None else count
        for make, when, spot in self.open_sends[:count]:
            if when is None:
                make().wait_send()
            else:
                pl.when(when)(lambda make=make: make().wait_send())
            self.free.append(spot)
        self.open_sends = self.open_sends[count:]

    def arrived(self, dst, slot, when=None):
        def wait():
            pltpu.make_async_remote_copy(
                src_ref=dst,
                dst_ref=dst,
                send_sem=self.send_sems.at[0],
                recv_sem=slot,
                device_id=self.place.device(self.place.r, self.place.peer(2)),
                device_id_type=MESH,
            ).wait_recv()

        if when is None:
            wait()
        else:
            pl.when(when)(wait)

    def local(self, src, dst):
        copy = pltpu.make_async_copy(src, dst, self.local_sems.at[self.locals])
        self.locals += 1
        copy.start()
        return copy


class SlabGather:
    def __init__(self, wire, at, half):
        self.wire, self.at, self.half = wire, at, half
        self.slots = wire.recv_slots(11)

    def start(self, whole, halves):
        wire, place, slots = self.wire, self.wire.place, self.slots
        t, r = place.t, place.r
        wire.send(halves[0], self.half(t, 0), slots[0], (r, place.peer(4)))
        wire.send(halves[1], self.half(t, 1), slots[3], (r, place.peer(1)))
        wire.send(halves[1], self.half(t, 1), slots[1], (r, place.peer(4)))
        wire.send(halves[0], self.half(t, 0), slots[2], (r, place.peer(1)))
        wire.send(whole, self.at(t), slots[6], (r, place.peer(2)))

    def relay(self):
        wire, place, slots = self.wire, self.wire.place, self.slots
        r, far, near = place.r, place.peer(4), place.peer(1)
        wire.arrived(self.half(far, 0), slots[0])
        wire.send(self.half(far, 0), self.half(far, 0), slots[4], (r, near))
        wire.arrived(self.half(near, 1), slots[3])
        wire.send(self.half(near, 1), self.half(near, 1), slots[5], (r, far))
        wire.arrived(self.half(far, 1), slots[1])
        wire.send(self.at(far), self.at(far), slots[7], (r, place.peer(2)))
        wire.arrived(self.half(near, 0), slots[2])
        wire.send(self.at(near), self.at(near), slots[8], (r, place.peer(2)))

    def forward(self):
        wire, place, slots = self.wire, self.wire.place, self.slots
        across = place.peer(5)
        for h in range(2):
            block = self.half(across, h)
            wire.arrived(block, slots[4 + h])
            wire.send(block, block, slots[9 + h], (place.r, place.peer(2)))

    def wait_block(self, mask):
        wire, place, slots = self.wire, self.wire.place, self.slots
        if mask == 7:
            for h in range(2):
                wire.arrived(self.half(place.peer(7), h), slots[9 + h])
        else:
            wire.arrived(self.at(place.peer(mask)), slots[{2: 6, 6: 7, 3: 8}[mask]])

    def wait(self):
        for mask in (2, 6, 3, 7):
            self.wait_block(mask)


class SlabScatter:
    def __init__(self, wire, part, core_in, chip_in, block):
        self.wire, self.part, self.core_in, self.chip_in, self.block = wire, part, core_in, chip_in, block
        self.core_slots = wire.recv_slots(4)
        self.slots = wire.recv_slots(6)
        self.order = (5, 4, 1, 0)

    def cores(self):
        place = self.wire.place
        for i, mask in enumerate(self.order):
            self.wire.send(
                rows(self.part, place.peer(mask ^ 2), self.block),
                self.core_in.at[i],
                self.core_slots[i],
                (place.r, place.peer(2)),
            )

    def half(self, mask, h):
        return rows(self.part, self.wire.place.peer(mask) * 2 + h, self.block // 2)

    def add_core(self, i):
        mask = self.order[i]
        self.wire.arrived(self.core_in.at[i], self.core_slots[i])
        mine = rows(self.part, self.wire.place.peer(mask), self.block)
        mine[...] = (mine[...].astype(F32) + self.core_in[i].astype(F32)).astype(BF16)

    def chips(self):
        wire, place = self.wire, self.wire.place
        far, near = (place.r, place.peer(4)), (place.r, place.peer(1))
        self.add_core(0)
        wire.send(self.half(5, 0), self.chip_in.at[0], self.slots[0], far)
        wire.send(self.half(5, 1), self.chip_in.at[1], self.slots[1], near)
        self.add_core(1)
        wire.send(self.half(4, 0), self.chip_in.at[2], self.slots[2], far)
        self.add_core(2)
        wire.send(self.half(1, 1), self.chip_in.at[3], self.slots[3], near)
        wire.arrived(self.core_in.at[3], self.core_slots[3])

    def relay(self):
        wire, place = self.wire, self.wire.place
        far, near = (place.r, place.peer(4)), (place.r, place.peer(1))
        for i, (block, to) in enumerate(((self.half(1, 0), near), (self.half(4, 1), far))):
            wire.arrived(self.chip_in.at[i], self.slots[i])
            block[...] = (block[...].astype(F32) + self.chip_in[i].astype(F32)).astype(BF16)
            wire.send(block, self.chip_in.at[4 + i], self.slots[4 + i], to)

    def wait(self):
        for i in range(2, 6):
            self.wire.arrived(self.chip_in.at[i], self.slots[i])

    def total(self, first, size):
        mine = self.part[pl.ds(pl.multiple_of(self.wire.place.t * self.block + first, size), size), :].astype(F32)
        mine = mine + self.core_in[3, pl.ds(pl.multiple_of(first, size), size), :].astype(F32)
        h = first // (self.block // 2)
        at = pl.ds(pl.multiple_of(first % (self.block // 2), size), size)
        return mine + self.chip_in[2 + h, at, :].astype(F32) + self.chip_in[4 + h, at, :].astype(F32)


class SlabSwap:
    def __init__(self, wire, source, target, seven):
        self.wire, self.source, self.target, self.seven = wire, source, target, seven
        (self.slot,) = wire.recv_slots(1)

    def start(self):
        place = self.wire.place
        self.own = self.wire.local(self.source(place.t), self.target(place.t))
        for i in (4, 5, 3, 6, 2, 7, 1):
            to = (place.t + i) % SLAB
            self.wire.send(self.source(to), self.target(place.t), self.slot, (place.r, to))

    def wait(self):
        self.wire.arrived(self.seven, self.slot)
        self.own.wait()


class GroupGather:
    def __init__(self, wire, at):
        self.wire, self.at = wire, at
        self.slots = wire.recv_slots(4)
        self.first = wire.recvs - 4
        r = wire.place.r
        self.inner, self.outer = (r + 1) // 2 == 1, (r + 1) // 2 != 1

    def start(self, src):
        wire, place = self.wire, self.wire.place
        r = place.r
        wire.send(src, self.at(r), self.slots[1], ((r + 1) % 4, place.t), r != 3)
        wire.send(src, self.at(r), self.slots[3], ((r + 3) % 4, place.t), r != 0)

    def pass_on(self):
        wire, place = self.wire, self.wire.place
        r = place.r
        below, above = (r + 3) % 4, (r + 1) % 4
        for block, slot, to in ((self.at(below), self.slots[1], above), (self.at(above), self.slots[3], below)):
            wire.arrived(block, slot, self.inner)
            wire.send(block, block, self.slots[2], (to, place.t), self.inner)

    def pass_far(self):
        wire, place = self.wire, self.wire.place
        r = place.r
        block = self.at((r + 2) % 4)
        wire.arrived(block, self.slots[2], self.inner)
        slot = wire.recv_sems.at[self.first + (2 * r + 3) % 4]
        wire.send(block, block, slot, ((3 * r + 1) % 4, place.t), self.inner)

    def wait(self):
        wire, r = self.wire, self.wire.place.r
        for i in (1, 2, 3):
            wire.arrived(self.at((r + 4 - i) % 4), self.slots[i], self.outer)


class GroupScatter:
    def __init__(self, wire, out, into, own, passing):
        self.wire, self.out, self.into, self.own, self.passing = wire, out, into, own, passing
        self.slots = wire.recv_slots(5)
        self.first = wire.recvs - 5
        r = wire.place.r

        @pl.when(r == 0)
        def _():
            into[0] = jnp.zeros_like(into[0])

        @pl.when(r == 3)
        def _():
            into[2] = jnp.zeros_like(into[2])

    def start(self, make):
        wire, place = self.wire, self.wire.place
        r, t = place.r, place.t
        inner = (r + 1) // 2 == 1
        outer = (r + 1) // 2 != 1
        low = 1 - r // 2
        pair = r + 1 - 2 * (r % 2)
        first, last = 1 + 2 * low, 3 - 2 * low
        self.out[0] = make((r + first) % 4).astype(BF16)
        wire.send(self.out.at[0], self.passing, self.slots[0], (pair, t), outer)
        wire.send(self.out.at[0], self.into.at[first - 1], wire.recv_sems.at[self.first + first], (pair, t), inner)
        self.out[1] = make((r + 2) % 4).astype(BF16)
        wire.send(self.out.at[1], self.into.at[1], self.slots[2], ((r + 2) % 4, t), outer)
        self.out[2] = make((r + last) % 4).astype(BF16)
        wire.send(
            self.out.at[2], self.into.at[last - 1], wire.recv_sems.at[self.first + last], ((r + last) % 4, t)
        )
        self.own[...] = make(r)

    def relay(self):
        wire, place = self.wire, self.wire.place
        r = place.r
        inner = (r + 1) // 2 == 1
        wire.arrived(self.passing, self.slots[0], inner)

        @pl.when(inner)
        def _():
            self.out[1] = (self.out[1].astype(F32) + self.passing[...].astype(F32)).astype(BF16)

        wire.send(self.out.at[1], self.into.at[1], self.slots[2], ((r + 2) % 4, place.t), inner)

    def total(self):
        wire, r = self.wire, self.wire.place.r
        wire.arrived(self.into.at[1], self.slots[2])
        wire.arrived(self.into.at[0], self.slots[1], r != 0)
        wire.arrived(self.into.at[2], self.slots[3], r != 3)
        total = self.own[...]
        for i in range(3):
            total = total + self.into[i].astype(F32)
        return total


def layer_kernel(
    groups,
    scale,
    tokens,
    upstream,
    pack,
    w_in,
    w_out,
    w_exp,
    w_shr,
    layer_hbm,
    tokens_hbm,
    in_hbm,
    out_hbm,
    exp_hbm,
    shr_hbm,
    vec_hbm,
    layer_out,
    tokens_grad,
    out_grad,
    shr_grad,
    vec_grad,
    packs,
    tok_all,
    first_all,
    win,
    wex,
    wsh,
    wo,
    gls,
    gls_all,
    vecs,
    ebias,
    qkv,
    gqkv,
    soft_all,
    blend_t,
    blend,
    middle,
    normed,
    inverses,
    second,
    second_all,
    active,
    ghid,
    part_a,
    part_b,
    part_c,
    part_d,
    core_a,
    core_b,
    core_c,
    core_d,
    chip_a,
    chip_b,
    chip_c,
    chip_d,
    gsec,
    glow,
    gblend,
    gblend_t,
    sh_out,
    sh_in,
    sh_own,
    sh_pass,
    ex_out,
    ex_in,
    ex_own,
    ex_pass,
    ex_sum,
    ex_all,
    in_out,
    in_in,
    in_own,
    in_pass,
    in_sum,
    in_all,
    ou_out,
    ou_in,
    ou_own,
    ou_pass,
    gvec,
    gvec_exp,
    gvec_out,
    gvec_in,
    send_sems,
    recv_sems,
    local_sems,
):
    place = Place(groups)
    wire = Wire(place, send_sems, recv_sems, local_sems)
    f, y, r, xc, t = place.f, place.y, place.r, place.xc, place.t
    devices = groups * SLAB
    me = r * SLAB + t
    seg, width = tokens.shape
    clips = SLAB // 2
    slots = seg * 2
    total_rows = SLAB * seg
    head2 = qkv.shape[1] // 3
    own_rows = w_in.shape[0]
    slab_rows = own_rows * 4
    share = width // devices
    chunk = wsh.shape[1]
    strip = 32
    tile = 256

    barrier = pltpu.get_barrier_semaphore()
    for i in range(1, devices):
        to = (me + i) % devices
        pl.semaphore_signal(barrier, inc=1, device_id=place.device(to // SLAB, to % SLAB), device_id_type=MESH)
    pl.semaphore_wait(barrier, devices - 1)

    (pack_slot,) = wire.recv_slots(1)
    for i in range(1, groups * 4):
        to = (f + i) % (groups * 4)
        wire.send(pack, packs.at[f], pack_slot, (to // 4, (to % 4) * 2 + y))
    own_pack = wire.local(pack, packs.at[f])

    in_slots = wire.recv_slots(4)
    ex_slots = wire.recv_slots(4)

    def in_piece(index, c):
        return win.at[pl.ds(pl.multiple_of(index * own_rows, own_rows), own_rows), pl.ds(c * head2, head2)]

    def ex_piece(index, c):
        return wex.at[pl.ds(pl.multiple_of(index * own_rows, own_rows), own_rows), pl.ds(c * chunk, chunk)]

    own_in = []
    for i in (2, 3, 1, 0):
        to = ((xc + i) % 4) * 2 + y
        for c in range(3):
            src = w_in.at[:, pl.ds(pl.multiple_of(c * width + to * head2, head2), head2)]
            if i == 0:
                own_in.append(wire.local(src, in_piece(f, c)))
            else:
                wire.send(src, in_piece(f, c), in_slots[i], (r, to))

    out_share = w_out.at[pl.ds(pl.multiple_of(y * share, share), share), :]
    own_out = wire.local(out_share, wo.at[r, t])
    group_wo = GroupGather(wire, lambda at: wo.at[at, t])
    group_wo.start(out_share)
    shr_share = w_shr.at[pl.ds(pl.multiple_of(y * chunk, chunk), chunk), :]
    own_shr = wire.local(shr_share, wsh.at[r])
    group_sh = GroupGather(wire, lambda at: wsh.at[at])
    group_sh.start(shr_share)

    def slab_gather(ref):
        return SlabGather(wire, lambda at: rows(ref, at, seg), lambda at, h: rows(ref, at * 2 + h, seg // 2))

    gather_tok = slab_gather(tok_all)
    gather_tok.start(tokens, [rows(tokens, h, seg // 2) for h in range(2)])

    own_ex = []
    for i in (2, 3, 1, 0):
        to = ((xc + i) % 4) * 2 + y
        for c in range(groups):
            src = w_exp.at[:, pl.ds(pl.multiple_of((c * SLAB + to) * chunk, chunk), chunk)]
            if i == 0:
                own_ex.append(wire.local(src, ex_piece(f, c)))
            else:
                wire.send(src, ex_piece(f, c), ex_slots[i], (r, to))

    row_at = y * seg + lax.broadcasted_iota(jnp.int32, (seg, 1), 0)
    row_valid = row_at.astype(F32) < pack[10:11, 0:1].astype(F32)
    gls[...] = jnp.where(row_valid, upstream[...].astype(F32), 0.0).astype(BF16)
    gls_all[pl.ds(pl.multiple_of(t * seg, seg), seg), :] = gls[...]
    gvec[...] = jnp.zeros_like(gvec)
    gvec_exp[...] = jnp.zeros_like(gvec_exp)
    group_shr = GroupScatter(wire, sh_out, sh_in, sh_own, sh_pass)
    group_exp = GroupScatter(wire, ex_out, ex_in, ex_own, ex_pass)
    group_inw = GroupScatter(wire, in_out, in_in, in_own, in_pass)
    group_out = GroupScatter(wire, ou_out, ou_in, ou_own, ou_pass)

    for i in range(1, 4):
        frm = r * 4 + (xc + 4 - i) % 4
        wire.arrived(rows(win, frm, own_rows), in_slots[i])
    for copy in own_in:
        copy.wait()
    own_out.wait()
    group_wo.pass_on()
    group_in = GroupGather(wire, lambda at: rows(win, at, slab_rows))
    group_in.start(rows(win, r, slab_rows))
    group_wo.pass_far()

    own_pack.wait()
    wire.arrived(packs.at[pl.ds(0, groups * 4 - 1)], pack_slot)
    per_lane = 128 // own_rows
    lane = lax.broadcasted_iota(jnp.int32, (1, 128), 1)
    for j in range(width // 128):
        piece = packs[j * per_lane].astype(F32)
        for k in range(1, per_lane):
            piece = jnp.where(lane >= k * own_rows, packs[j * per_lane + k].astype(F32), piece)
        vecs[:, j * 128 : (j + 1) * 128] = piece
    for c in range(groups):
        both = packs[c * 4 + t // 2].astype(F32)
        ebias[0:1, c * chunk : (c + 1) * chunk] = jnp.where(y == 0, both[8:9], both[9:10])

    def first_norm(src, offset, block):
        def strip_norm(i, carry):
            at = pl.multiple_of(i * strip, strip)
            n, _ = row_stats(src[pl.ds(offset + at, strip), :].astype(F32))
            to = pl.multiple_of(block * seg + at, strip)
            first_all[pl.ds(to, strip), :] = (n * vecs[0:1, :] + vecs[1:2, :]).astype(BF16)
            return carry

        lax.fori_loop(0, seg // strip, strip_norm, 0)

    first_norm(tokens, 0, t)

    def norm_block(mask):
        block = place.peer(mask)
        first_norm(tok_all, pl.multiple_of(block * seg, seg), block)

    gather_tok.relay()
    group_in.pass_on()
    norm_block(4)
    norm_block(1)

    gather_tok.forward()

    norm_block(5)
    group_in.pass_far()
    group_sh.pass_on()
    for i in range(1, 4):
        frm = r * 4 + (xc + 4 - i) % 4
        wire.arrived(rows(wex, frm, own_rows), ex_slots[i])
    for copy in own_ex:
        copy.wait()
    group_ex = GroupGather(wire, lambda at: rows(wex, at, slab_rows))
    group_ex.start(rows(wex, r, slab_rows))

    group_wo.wait()
    gather_wo = SlabGather(wire, lambda at: wo.at[:, at], lambda at, h: wo.at[pl.ds(h * (groups // 2), groups // 2), at])
    gather_wo.start(wo.at[:, t], [wo.at[pl.ds(h * (groups // 2), groups // 2), t] for h in range(2)])
    gather_gls = slab_gather(gls_all)
    gather_gls.start(gls, [rows(gls, h, seg // 2) for h in range(2)])

    for mask in (2, 6, 3, 7):
        gather_tok.wait_block(mask)
        norm_block(mask)

    gather_wo.relay()
    group_in.wait()
    at_head = pl.ds(pl.multiple_of(t * head2, head2), head2)
    bias = jnp.concatenate([vecs[2:3, at_head], jnp.zeros((1, head2), F32), vecs[3:4, at_head]], axis=1)

    def project(i, carry):
        at = pl.ds(pl.multiple_of(i * tile, tile), tile)
        qkv[at, :] = (matmul(first_all[at, :], win[...]) + bias).astype(BF16)
        return carry

    lax.fori_loop(0, total_rows // tile, project, 0)

    gather_wo.forward()

    head_size = head2 // 2
    low_half = lane < head_size
    half_masks = [low_half.astype(F32).astype(BF16), (1.0 - low_half.astype(F32)).astype(BF16)]
    key_at = lax.broadcasted_iota(jnp.int32, (1, slots), 1).astype(F32)

    def attend(i, carry):
        at = pl.ds(pl.multiple_of(i * slots, slots), slots)
        q = qkv[at, 0:head2]
        k = qkv[at, head2 : 2 * head2]
        v = qkv[at, 2 * head2 : 3 * head2]
        count = packs[r * 4 + i].astype(F32)[10:11, 0:1]
        key_valid = key_at < count
        halves = []
        for h in range(2):
            scores = matmul_bt(q * half_masks[h], k) * scale
            scores = jnp.where(key_valid, scores, -1e30)
            top = jnp.max(scores, axis=-1, keepdims=True)
            log_total = top + jnp.log(jnp.sum(jnp.exp(scores - top), axis=-1, keepdims=True))
            soft = jnp.exp(scores - log_total)
            soft_all[i * 2 + h] = soft
            halves.append(matmul(soft.astype(BF16), v))
        blend_t[at, :] = jnp.where(low_half, halves[0], halves[1]).astype(BF16)
        return carry

    lax.fori_loop(0, clips, attend, 0)

    group_sh.pass_far()
    swap_blend = SlabSwap(wire, lambda at: rows(blend_t, at, seg), lambda at: cols(blend, at, head2), blend.at[:, 0 : 7 * head2])
    swap_blend.start()
    gather_gls.relay()
    gather_wo.wait()
    swap_blend.wait()
    group_ex.pass_on()
    wide = 256
    for j in range(width // wide):
        at = slice(j * wide, (j + 1) * wide)
        product = matmul(blend[...], wo[:, :, :, at].reshape(width, wide))
        middle[:, at] = tokens[:, at].astype(F32) + (product + vecs[4:5, at])

    own_second_rows = pl.multiple_of(t * seg, seg)

    def second_norm(i, carry):
        at = pl.ds(pl.multiple_of(i * strip, strip), strip)
        n, inverse = row_stats(middle[at, :])
        normed[at, :] = n
        inverses[at, :] = jnp.broadcast_to(inverse, (strip, 128))
        low = (n * vecs[5:6, :] + vecs[6:7, :]).astype(BF16)
        second[at, :] = low
        second_all[pl.ds(pl.multiple_of(own_second_rows + i * strip, strip), strip), :] = low
        return carry

    lax.fori_loop(0, seg // strip, second_norm, 0)

    gather_second = slab_gather(second_all)
    gather_second.start(second, [rows(second, h, seg // 2) for h in range(2)])
    gather_gls.forward()
    gather_second.relay()
    group_ex.pass_far()
    gather_second.forward()
    gather_gls.wait()
    gather_second.wait()
    group_ex.wait()
    group_sh.wait()
    own_shr.wait()

    front_sends = len(wire.open_sends)

    hidden_units = groups * chunk

    def feed(i, carry):
        at = pl.ds(pl.multiple_of(i * tile, tile), tile)
        hidden = matmul(second_all[at, :], wex[...]) + ebias[0:1, :]
        grad_active = matmul_bt(gls_all[at, :], wsh[...].reshape(hidden_units, width))
        cdf = 0.5 * (1.0 + lax.erf(hidden * 0.7071067811865476))
        active[at, :] = (hidden * cdf).astype(BF16)
        slope = cdf + hidden * (0.3989422804014327 * jnp.exp(-0.5 * hidden * hidden))
        grad_hidden = (grad_active * slope).astype(BF16)
        ghid[at, :] = grad_hidden
        gvec_exp[...] += jnp.sum(grad_hidden.astype(F32), axis=0, keepdims=True)
        part_a[at, :] = matmul_bt(grad_hidden, wex[...]).astype(BF16)
        return carry

    lax.fori_loop(0, total_rows // tile, feed, 0)

    scatter_second = SlabScatter(wire, part_a, core_a, chip_a, seg)
    scatter_second.cores()
    group_shr.start(
        lambda c: matmul_at(active[:, pl.ds(pl.multiple_of(c * chunk, chunk), chunk)], gls_all[...])
    )
    scatter_second.chips()
    group_exp.start(
        lambda c: matmul_at(second_all[:, pl.ds(pl.multiple_of(c * slab_rows, slab_rows), slab_rows)], ghid[...])
    )
    scatter_second.relay()

    def feed_out(i, carry):
        at = pl.ds(pl.multiple_of(i * tile, tile), tile)
        part_b[at, :] = matmul(active[at, :], wsh[...].reshape(hidden_units, width)).astype(BF16)
        return carry

    lax.fori_loop(0, total_rows // tile, feed_out, 0)
    scatter_result = SlabScatter(wire, part_b, core_b, chip_b, seg)
    scatter_result.cores()

    scatter_second.wait()
    wire.settle(front_sends)

    feed_sends = len(wire.open_sends)

    def second_back(i, carry):
        first = i * strip
        at = pl.ds(pl.multiple_of(first, strip), strip)
        grad = scatter_second.total(first, strip)
        n = normed[at, :]
        back = row_norm_back(grad, n, inverses[at, 0:1], vecs[5:6, :])
        grad_result = gls[at, :].astype(F32)
        grad_middle = grad_result + back
        gsec[at, :] = grad_middle
        low = grad_middle.astype(BF16)
        glow[at, :] = low
        gvec[4:5, :] += jnp.sum(low.astype(F32), axis=0, keepdims=True)
        gvec[5:6, :] += jnp.sum(grad * n, axis=0, keepdims=True)
        gvec[6:7, :] += jnp.sum(grad, axis=0, keepdims=True)
        gvec[7:8, :] += jnp.sum(grad_result, axis=0, keepdims=True)
        return carry

    lax.fori_loop(0, seg // strip, second_back, 0)

    for j in range(width // wide):
        rows_of = slice(j * (groups * wide // width), (j + 1) * (groups * wide // width))
        gblend[:, j * wide : (j + 1) * wide] = matmul_bt(
            glow[...], wo[rows_of].reshape(wide, width)
        ).astype(BF16)
    swap_gblend = SlabSwap(wire, lambda at: cols(gblend, at, head2), lambda at: rows(gblend_t, at, seg), gblend_t.at[pl.ds(0, 7 * seg), :])
    swap_gblend.start()
    scatter_result.chips()
    group_shr.relay()

    for c in range(groups):
        product = matmul_at(blend[:, c * slab_rows : (c + 1) * slab_rows], glow[...])
        for to in range(SLAB):
            part_d[to * seg + c * share : to * seg + (c + 1) * share, :] = product[
                to * share : (to + 1) * share
            ].astype(BF16)
    scatter_out = SlabScatter(wire, part_d, core_d, chip_d, seg)
    scatter_out.cores()

    swap_gblend.wait()

    def attend_back(i, carry):
        at = pl.ds(pl.multiple_of(i * slots, slots), slots)
        q = qkv[at, 0:head2]
        k = qkv[at, head2 : 2 * head2]
        v = qkv[at, 2 * head2 : 3 * head2]
        grad = gblend_t[at, :]
        parts = []
        for h in range(2):
            soft = soft_all[i * 2 + h]
            grad_soft = matmul_bt(grad * half_masks[h], v)
            inner = jnp.sum(grad_soft * soft, axis=-1, keepdims=True)
            grad_scores = (soft * (grad_soft - inner)).astype(BF16)
            parts.append(
                (
                    matmul(grad_scores, k) * scale,
                    matmul_at(grad_scores, q) * scale,
                    matmul_at(soft.astype(BF16), grad),
                )
            )
        for c in range(3):
            gqkv[at, c * head2 : (c + 1) * head2] = jnp.where(low_half, parts[0][c], parts[1][c]).astype(BF16)
        return carry

    lax.fori_loop(0, clips, attend_back, 0)

    def project_back(i, carry):
        at = pl.ds(pl.multiple_of(i * tile, tile), tile)
        part_c[at, :] = matmul_bt(gqkv[at, :], win[...]).astype(BF16)
        return carry

    lax.fori_loop(0, total_rows // tile, project_back, 0)
    scatter_first = SlabScatter(wire, part_c, core_c, chip_c, seg)
    scatter_first.cores()

    group_inw.start(
        lambda c: matmul_at(first_all[:, pl.ds(pl.multiple_of(c * slab_rows, slab_rows), slab_rows)], gqkv[...])
    )
    scatter_first.chips()
    gvec[2:3, at_head] = jnp.sum(gqkv[:, 0:head2].astype(F32), axis=0, keepdims=True)
    gvec[3:4, at_head] = jnp.sum(gqkv[:, 2 * head2 :].astype(F32), axis=0, keepdims=True)

    scatter_result.relay()
    group_exp.relay()
    scatter_first.relay()
    scatter_out.chips()
    scatter_result.wait()

    def finish_out(i, carry):
        first = i * strip
        at = pl.ds(pl.multiple_of(first, strip), strip)
        result = middle[at, :] + (scatter_result.total(first, strip) + vecs[7:8, :])
        spot = y * seg + first + lax.broadcasted_iota(jnp.int32, (strip, 1), 0)
        valid = spot.astype(F32) < pack[10:11, 0:1].astype(F32)
        layer_out[at, :] = jnp.where(valid, result, 0.0).astype(BF16)
        return carry

    lax.fori_loop(0, seg // strip, finish_out, 0)
    stores = [wire.local(layer_out, layer_hbm)]

    scatter_first.wait()
    wire.settle(feed_sends)

    def first_back(i, carry):
        first = i * strip
        at = pl.ds(pl.multiple_of(first, strip), strip)
        grad = scatter_first.total(first, strip)
        n, inverse = row_stats(tokens[at, :].astype(F32))
        tokens_grad[at, :] = gsec[at, :] + row_norm_back(grad, n, inverse, vecs[0:1, :])
        gvec[0:1, :] += jnp.sum(grad * n, axis=0, keepdims=True)
        gvec[1:2, :] += jnp.sum(grad, axis=0, keepdims=True)
        return carry

    lax.fori_loop(0, seg // strip, first_back, 0)
    stores.append(wire.local(tokens_grad, tokens_hbm))

    per_chunk = 128 // share
    for j in range(width // 128):
        gvec_out[j, 0:8, :] = gvec[:, j * 128 : (j + 1) * 128]
        c = j * per_chunk // SLAB
        gvec_out[j, 8:16, :] = jnp.broadcast_to(gvec_exp[0:1, c * chunk : (c + 1) * chunk], (8, chunk))
    (vec_slot,) = wire.recv_slots(1)
    for i in range(1, devices):
        to = (me + i) % devices
        wire.send(gvec_out.at[to // per_chunk], gvec_in.at[me], vec_slot, (to // SLAB, to % SLAB))
    own_vec = wire.local(gvec_out.at[me // per_chunk], gvec_in.at[me])

    scatter_out.relay()
    scatter_out.wait()
    group_out.start(lambda c: scatter_out.total(c * share, share))
    shr_grad[...] = group_shr.total()
    stores.append(wire.local(shr_grad, shr_hbm))
    group_inw.relay()
    group_out.relay()
    ex_sum[...] = group_exp.total().astype(BF16)
    swap_exp = SlabSwap(wire, lambda at: rows(ex_sum, at, share), lambda at: ex_all.at[at], ex_all.at[pl.ds(0, 7)])
    swap_exp.start()
    own_vec.wait()
    wire.arrived(gvec_in.at[pl.ds(0, devices - 1)], vec_slot)
    summed = gvec_in[0]
    for i in range(1, devices):
        summed = summed + gvec_in[i]
    for_exp = gvec_in[t]
    for c in range(1, groups):
        for_exp = for_exp + gvec_in[c * SLAB + t]
    vec_grad[0:8, :] = pltpu.roll(summed[0:8], (128 - share * (me % per_chunk)) % 128, 1)
    vec_grad[8:16, :] = for_exp[8:16]
    stores.append(wire.local(vec_grad, vec_hbm))

    in_sum[...] = group_inw.total().astype(BF16)
    swap_in = SlabSwap(wire, lambda at: rows(in_sum, at, share), lambda at: in_all.at[at], in_all.at[pl.ds(0, 7)])
    swap_in.start()
    out_grad[...] = group_out.total()
    stores.append(wire.local(out_grad, out_hbm))
    swap_exp.wait()
    stores.append(wire.local(ex_all, exp_hbm))
    swap_in.wait()
    stores.append(wire.local(in_all, in_hbm))
    for copy in stores:
        copy.wait()
    wire.settle()
    assert wire.sends <= SENDS and wire.recvs <= RECVS and wire.locals <= LOCALS


def output_kernel(
    groups,
    layer_in,
    tokens_in,
    in_pieces,
    out_in,
    exp_pieces,
    shr_in,
    vec_in,
    layer_out,
    tokens_grad,
    first_gain_grad,
    first_shift_grad,
    in_grad,
    query_bias_grad,
    value_bias_grad,
    out_grad,
    outward_bias_grad,
    second_gain_grad,
    second_shift_grad,
    exp_grad,
    expand_bias_grad,
    shr_grad,
    shrink_bias_grad,
    layer_buf,
    tokens_buf,
    in_buf,
    out_buf,
    exp_buf,
    shr_buf,
    vec_buf,
    in_wide,
    exp_wide,
    load_sems,
    store_sems,
):
    share, width = out_buf.shape
    head2, chunk = in_buf.shape[2] // 3, exp_buf.shape[2] // groups
    loads = [
        pltpu.make_async_copy(src, dst, load_sems.at[i])
        for i, (src, dst) in enumerate(
            (
                (vec_in, vec_buf),
                (exp_pieces, exp_buf),
                (in_pieces, in_buf),
                (shr_in, shr_buf),
                (tokens_in, tokens_buf),
                (layer_in, layer_buf),
                (out_in, out_buf),
            )
        )
    ]
    for copy in loads:
        copy.start()
    stores = []

    def store(src, dst):
        stores.append(pltpu.make_async_copy(src, dst, store_sems.at[len(stores)]))
        stores[-1].start()

    loads[0].wait()
    vectors = (
        first_gain_grad,
        first_shift_grad,
        query_bias_grad,
        value_bias_grad,
        outward_bias_grad,
        second_gain_grad,
        second_shift_grad,
        shrink_bias_grad,
    )
    for k, ref in enumerate(vectors):
        ref[...] = vec_buf[k, 0:share]
    expand_bias_grad[...] = vec_buf[8, :]
    loads[1].wait()
    for frm in range(SLAB):
        for c in range(groups):
            at = (c * SLAB + frm) * chunk
            exp_wide[:, at : at + chunk] = exp_buf[frm, :, c * chunk : (c + 1) * chunk].astype(F32)
    store(exp_wide, exp_grad)
    loads[2].wait()
    for frm in range(SLAB):
        for c in range(3):
            at = c * width + frm * head2
            in_wide[:, at : at + head2] = in_buf[frm, :, c * head2 : (c + 1) * head2].astype(F32)
    store(in_wide, in_grad)
    for copy, src, dst in (
        (loads[3], shr_buf, shr_grad),
        (loads[4], tokens_buf, tokens_grad.at[0]),
        (loads[5], layer_buf, layer_out.at[0]),
        (loads[6], out_buf, out_grad),
    ):
        copy.wait()
        store(src, dst)
    for copy in stores:
        copy.wait()


def fused_shards(
    tokens,
    visible,
    first_gain,
    first_shift,
    inward_weight,
    query_bias,
    value_bias,
    outward_weight,
    outward_bias,
    second_gain,
    second_shift,
    expand_weight,
    expand_bias,
    shrink_weight,
    shrink_bias,
    upstream,
):
    seg, width = tokens.shape[1:]
    groups = lax.axis_size("fsdp") // 4
    devices = groups * SLAB
    own_rows = inward_weight.shape[0]
    hidden = expand_weight.shape[1]
    share = width // devices
    chunk = hidden // devices
    units = groups * chunk
    head2 = width // SLAB
    scale = (width // HEADS) ** (-0.5)
    total_rows = SLAB * seg
    slab_rows = 4 * own_rows
    vectors = jnp.stack(
        [first_gain, first_shift, query_bias, value_bias, outward_bias, second_gain, second_shift, shrink_bias]
    )
    pack = jnp.concatenate(
        [
            jnp.concatenate([vectors] * (128 // own_rows), axis=1),
            expand_bias.reshape(2, 128),
            jnp.broadcast_to(visible.astype(BF16)[:, None], (6, 128)),
        ]
    )
    vmem = pl.BlockSpec(memory_space=pltpu.VMEM)
    anywhere = pl.BlockSpec(memory_space=pl.ANY)
    outs = pl.pallas_call(
        functools.partial(layer_kernel, groups, scale),
        out_shape=(
            jax.ShapeDtypeStruct((seg, width), BF16),
            jax.ShapeDtypeStruct((seg, width), F32),
            jax.ShapeDtypeStruct((SLAB, share, 3 * head2), BF16),
            jax.ShapeDtypeStruct((share, width), F32),
            jax.ShapeDtypeStruct((SLAB, share, units), BF16),
            jax.ShapeDtypeStruct((chunk, width), F32),
            jax.ShapeDtypeStruct((16, 128), F32),
        ),
        in_specs=[vmem, vmem, vmem, anywhere, anywhere, anywhere, anywhere],
        out_specs=[anywhere] * 7,
        scratch_shapes=[
            pltpu.VMEM((seg, width), BF16),
            pltpu.VMEM((seg, width), F32),
            pltpu.VMEM((share, width), F32),
            pltpu.VMEM((chunk, width), F32),
            pltpu.VMEM((16, 128), F32),
            pltpu.VMEM((groups * 4, 16, 128), BF16),
            pltpu.VMEM((total_rows, width), BF16),
            pltpu.VMEM((total_rows, width), BF16),
            pltpu.VMEM((width, 3 * head2), BF16),
            pltpu.VMEM((width, units), BF16),
            pltpu.VMEM((groups, chunk, width), BF16),
            pltpu.VMEM((groups, SLAB, share, width), BF16),
            pltpu.VMEM((seg, width), BF16),
            pltpu.VMEM((total_rows, width), BF16),
            pltpu.VMEM((16, width), F32),
            pltpu.VMEM((8, units), F32),
            pltpu.VMEM((total_rows, 3 * head2), BF16),
            pltpu.VMEM((total_rows, 3 * head2), BF16),
            pltpu.VMEM((SLAB, 2 * seg, 2 * seg), F32),
            pltpu.VMEM((total_rows, head2), BF16),
            pltpu.VMEM((seg, width), BF16),
            pltpu.VMEM((seg, width), F32),
            pltpu.VMEM((seg, width), F32),
            pltpu.VMEM((seg, 128), F32),
            pltpu.VMEM((seg, width), BF16),
            pltpu.VMEM((total_rows, width), BF16),
            pltpu.VMEM((total_rows, units), BF16),
            pltpu.VMEM((total_rows, units), BF16),
        ]
        + [pltpu.VMEM((total_rows, width), BF16)] * 4
        + [pltpu.VMEM((4, seg, width), BF16)] * 4
        + [pltpu.VMEM((6, seg // 2, width), BF16)] * 4
        + [
            pltpu.VMEM((seg, width), F32),
            pltpu.VMEM((seg, width), BF16),
            pltpu.VMEM((seg, width), BF16),
            pltpu.VMEM((total_rows, head2), BF16),
            pltpu.VMEM((groups - 1, chunk, width), BF16),
            pltpu.VMEM((groups - 1, chunk, width), BF16),
            pltpu.VMEM((chunk, width), F32),
            pltpu.VMEM((chunk, width), BF16),
            pltpu.VMEM((groups - 1, slab_rows, units), BF16),
            pltpu.VMEM((groups - 1, slab_rows, units), BF16),
            pltpu.VMEM((slab_rows, units), F32),
            pltpu.VMEM((slab_rows, units), BF16),
            pltpu.VMEM((slab_rows, units), BF16),
            pltpu.VMEM((SLAB, share, units), BF16),
            pltpu.VMEM((groups - 1, slab_rows, 3 * head2), BF16),
            pltpu.VMEM((groups - 1, slab_rows, 3 * head2), BF16),
            pltpu.VMEM((slab_rows, 3 * head2), F32),
            pltpu.VMEM((slab_rows, 3 * head2), BF16),
            pltpu.VMEM((slab_rows, 3 * head2), BF16),
            pltpu.VMEM((SLAB, share, 3 * head2), BF16),
            pltpu.VMEM((groups - 1, share, width), BF16),
            pltpu.VMEM((groups - 1, share, width), BF16),
            pltpu.VMEM((share, width), F32),
            pltpu.VMEM((share, width), BF16),
            pltpu.VMEM((8, width), F32),
            pltpu.VMEM((1, units), F32),
            pltpu.VMEM((width // 128, 16, 128), F32),
            pltpu.VMEM((devices, 16, 128), F32),
            pltpu.SemaphoreType.DMA((SENDS,)),
            pltpu.SemaphoreType.DMA((RECVS,)),
            pltpu.SemaphoreType.DMA((LOCALS,)),
        ],
        compiler_params=pltpu.CompilerParams(
            collective_id=0, has_side_effects=True, vmem_limit_bytes=67043328
        ),
        name="layer",
    )(
        tokens.reshape(seg, width),
        upstream.reshape(seg, width),
        pack,
        inward_weight,
        outward_weight,
        expand_weight,
        shrink_weight,
    )
    vector = jax.ShapeDtypeStruct((share,), F32)
    return pl.pallas_call(
        functools.partial(output_kernel, groups),
        out_shape=(
            jax.ShapeDtypeStruct((1, seg, width), BF16),
            jax.ShapeDtypeStruct((1, seg, width), F32),
            vector,
            vector,
            jax.ShapeDtypeStruct((share, 3 * width), F32),
            vector,
            vector,
            jax.ShapeDtypeStruct((share, width), F32),
            vector,
            vector,
            vector,
            jax.ShapeDtypeStruct((share, hidden), F32),
            jax.ShapeDtypeStruct((chunk,), F32),
            jax.ShapeDtypeStruct((chunk, width), F32),
            vector,
        ),
        in_specs=[anywhere] * 7,
        out_specs=[vmem if k in (2, 3, 5, 6, 8, 9, 10, 12, 14) else anywhere for k in range(15)],
        scratch_shapes=[
            pltpu.VMEM((seg, width), BF16),
            pltpu.VMEM((seg, width), F32),
            pltpu.VMEM((SLAB, share, 3 * head2), BF16),
            pltpu.VMEM((share, width), F32),
            pltpu.VMEM((SLAB, share, units), BF16),
            pltpu.VMEM((chunk, width), F32),
            pltpu.VMEM((16, 128), F32),
            pltpu.VMEM((share, 3 * width), F32),
            pltpu.VMEM((share, hidden), F32),
            pltpu.SemaphoreType.DMA((7,)),
            pltpu.SemaphoreType.DMA((15,)),
        ],
        name="outputs",
    )(*outs)


def fits_fused(mesh, tokens, inward_weight, expand_weight):
    fsdp, seq = mesh.shape["fsdp"], mesh.shape["seq"]
    clips, slots, width = tokens.shape
    devices = fsdp * seq
    return (
        seq == 2
        and clips == fsdp
        and fsdp == 16
        and width // HEADS * 2 == 128
        and width == SLAB * 128
        and slots % 64 == 0
        and width % (16 * devices) == 0
        and 128 % (width // fsdp) == 0
        and expand_weight.shape[1] == 128 * devices
    )


def solution(mesh):
    in_specs = (
        P("fsdp", "seq", None),
        P("fsdp"),
        P("fsdp"),
        P("fsdp"),
        P("fsdp", None),
        P("fsdp"),
        P("fsdp"),
        P("fsdp", None),
        P("fsdp"),
        P("fsdp"),
        P("fsdp"),
        P("fsdp", None),
        P("fsdp"),
        P("fsdp", None),
        P("fsdp"),
        P("fsdp", "seq", None),
    )
    out_specs = (
        P("fsdp", "seq", None),
        P("fsdp", "seq", None),
        P(("fsdp", "seq")),
        P(("fsdp", "seq")),
        P(("fsdp", "seq"), None),
        P(("fsdp", "seq")),
        P(("fsdp", "seq")),
        P(("fsdp", "seq"), None),
        P(("fsdp", "seq")),
        P(("fsdp", "seq")),
        P(("fsdp", "seq")),
        P(("fsdp", "seq"), None),
        P(("fsdp", "seq")),
        P(("fsdp", "seq"), None),
        P(("fsdp", "seq")),
    )

    def step(*args):
        body = fused_shards if fits_fused(mesh, args[0], args[4], args[11]) else shards
        return jax.shard_map(body, mesh=mesh, in_specs=in_specs, out_specs=out_specs, check_vma=False)(*args)

    return step
```

```python
import functools

import jax
import jax.numpy as jnp
from jax import lax
from jax.experimental import pallas as pl
from jax.experimental.pallas import tpu as pltpu
from jax.sharding import PartitionSpec as P

HEADS = 16


epsilon = 1e-06


def norm_rows(inputs, norm_gain, norm_shift):
    row_mean = jnp.mean(inputs, axis=-1, keepdims=True)
    centered = inputs - row_mean
    variance = jnp.mean(centered * centered, axis=-1, keepdims=True)
    inverse = lax.rsqrt(variance + epsilon)
    normed = centered * inverse
    return (normed * norm_gain + norm_shift, normed, inverse)


def norm_back(grad_out, normed, inverse, norm_gain):
    scaled = grad_out * norm_gain
    first_mean = jnp.mean(scaled, axis=-1, keepdims=True)
    second_mean = jnp.mean(scaled * normed, axis=-1, keepdims=True)
    return inverse * (scaled - first_mean - normed * second_mean)


def gather_weights(
    first_gain,
    first_shift,
    inward_weight,
    query_bias,
    value_bias,
    outward_weight,
    outward_bias,
    second_gain,
    second_shift,
    expand_weight,
    expand_bias,
    shrink_weight,
    shrink_bias,
):
    return (
        lax.all_gather(first_gain, "fsdp", axis=0, tiled=True),
        lax.all_gather(first_shift, "fsdp", axis=0, tiled=True),
        lax.all_gather(inward_weight, "fsdp", axis=0, tiled=True),
        lax.all_gather(query_bias, "fsdp", axis=0, tiled=True),
        lax.all_gather(value_bias, "fsdp", axis=0, tiled=True),
        lax.all_gather(outward_weight, "fsdp", axis=0, tiled=True),
        lax.all_gather(outward_bias, "fsdp", axis=0, tiled=True),
        lax.all_gather(second_gain, "fsdp", axis=0, tiled=True),
        lax.all_gather(second_shift, "fsdp", axis=0, tiled=True),
        lax.all_gather(expand_weight, "fsdp", axis=0, tiled=True),
        lax.all_gather(expand_bias, "fsdp", axis=0, tiled=True),
        lax.all_gather(shrink_weight, "fsdp", axis=0, tiled=True),
        lax.all_gather(shrink_bias, "fsdp", axis=0, tiled=True),
    )


def attend_scores(query_heads, key_heads, key_valid, scale):
    scores = (
        jnp.einsum("cqhe,ckhe->chqk", query_heads, key_heads, preferred_element_type=jnp.float32)
        * scale
    )
    return jnp.where(key_valid[:, None, None, :], scores, -1e30)


def forward(tokens32, key_valid, row_valid, gathered):
    (
        first_gain,
        first_shift,
        inward_weight,
        query_bias,
        value_bias,
        outward_weight,
        outward_bias,
        second_gain,
        second_shift,
        expand_weight,
        expand_bias,
        shrink_weight,
        shrink_bias,
    ) = gathered
    clip_count, seg_rows, model_width = tokens32.shape
    head_size = model_width // HEADS
    scale = head_size ** (-0.5)
    affine_first, normed_first, inverse_first = norm_rows(
        tokens32, first_gain.astype(jnp.float32), first_shift.astype(jnp.float32)
    )
    lowered_first = affine_first.astype(jnp.bfloat16)
    merged_bias = jnp.concatenate([query_bias, jnp.zeros_like(query_bias), value_bias]).astype(
        jnp.float32
    )
    project = (
        jnp.einsum("csd,de->cse", lowered_first, inward_weight, preferred_element_type=jnp.float32)
        + merged_bias
    )
    queries = project[..., :model_width].astype(jnp.bfloat16)
    key_local = project[..., model_width : 2 * model_width].astype(jnp.bfloat16)
    value_local = project[..., 2 * model_width :].astype(jnp.bfloat16)
    key_all, value_all = (
        lax.all_gather(key_local, "seq", axis=1, tiled=True),
        lax.all_gather(value_local, "seq", axis=1, tiled=True),
    )
    slot_count = key_all.shape[1]
    query_heads = queries.reshape(clip_count, seg_rows, HEADS, head_size)
    key_heads = key_all.reshape(clip_count, slot_count, HEADS, head_size)
    value_heads = value_all.reshape(clip_count, slot_count, HEADS, head_size)
    scores = attend_scores(query_heads, key_heads, key_valid, scale)
    row_top = jnp.max(scores, axis=-1, keepdims=True)
    row_total = jnp.sum(jnp.exp(scores - row_top), axis=-1, keepdims=True)
    log_total = row_top + jnp.log(row_total)
    soft_low = jnp.exp(scores - log_total).astype(jnp.bfloat16)
    blended = jnp.einsum(
        "chqk,ckhe->cqhe", soft_low, value_heads, preferred_element_type=jnp.float32
    )
    blended = blended.reshape(clip_count, seg_rows, model_width).astype(jnp.bfloat16)
    branch = jnp.einsum(
        "csd,de->cse", blended, outward_weight, preferred_element_type=jnp.float32
    ) + outward_bias.astype(jnp.float32)
    middle = tokens32 + branch
    affine_second, normed_second, inverse_second = norm_rows(
        middle, second_gain.astype(jnp.float32), second_shift.astype(jnp.float32)
    )
    lowered_second = affine_second.astype(jnp.bfloat16)
    hidden = jnp.einsum(
        "csd,df->csf", lowered_second, expand_weight, preferred_element_type=jnp.float32
    ) + expand_bias.astype(jnp.float32)
    active = jax.nn.gelu(hidden, approximate=False).astype(jnp.bfloat16)
    branch_second = jnp.einsum(
        "csf,fd->csd", active, shrink_weight, preferred_element_type=jnp.float32
    ) + shrink_bias.astype(jnp.float32)
    result = middle + branch_second
    output = jnp.where(row_valid, result, 0.0).astype(jnp.bfloat16)
    return {
        "normed_first": normed_first,
        "inverse_first": inverse_first,
        "lowered_first": lowered_first,
        "query_heads": query_heads,
        "key_heads": key_heads,
        "value_heads": value_heads,
        "log_total": log_total,
        "blended": blended,
        "normed_second": normed_second,
        "inverse_second": inverse_second,
        "lowered_second": lowered_second,
        "hidden": hidden,
        "active": active,
        "output": output,
    }


def gelu_exact(inputs):
    return jax.nn.gelu(inputs, approximate=False)


def backward(saved, gathered, upstream32, key_valid, row_valid):
    (
        first_gain,
        first_shift,
        inward_weight,
        query_bias,
        value_bias,
        outward_weight,
        outward_bias,
        second_gain,
        second_shift,
        expand_weight,
        expand_bias,
        shrink_weight,
        shrink_bias,
    ) = gathered
    clip_count, seg_rows, model_width = upstream32.shape
    head_size = model_width // HEADS
    scale = head_size ** (-0.5)
    grad_result = jnp.where(row_valid, upstream32, 0.0)
    grad_low_second = grad_result.astype(jnp.bfloat16)
    shrink_weight_grad = jnp.einsum(
        "csf,csd->fd", saved["active"], grad_low_second, preferred_element_type=jnp.float32
    )
    shrink_bias_grad = jnp.sum(grad_low_second.astype(jnp.float32), axis=(0, 1))
    grad_active = jnp.einsum(
        "csd,fd->csf", grad_low_second, shrink_weight, preferred_element_type=jnp.float32
    )
    gelu_value, gelu_pull = jax.vjp(gelu_exact, saved["hidden"])
    grad_hidden = gelu_pull(grad_active)[0].astype(jnp.bfloat16)
    expand_weight_grad = jnp.einsum(
        "csd,csf->df", saved["lowered_second"], grad_hidden, preferred_element_type=jnp.float32
    )
    expand_bias_grad = jnp.sum(grad_hidden.astype(jnp.float32), axis=(0, 1))
    grad_second = jnp.einsum(
        "csf,df->csd", grad_hidden, expand_weight, preferred_element_type=jnp.float32
    )
    second_gain_grad = jnp.sum(grad_second * saved["normed_second"], axis=(0, 1))
    second_shift_grad = jnp.sum(grad_second, axis=(0, 1))
    grad_middle = grad_result + norm_back(
        grad_second,
        saved["normed_second"],
        saved["inverse_second"],
        second_gain.astype(jnp.float32),
    )
    grad_low_first = grad_middle.astype(jnp.bfloat16)
    outward_weight_grad = jnp.einsum(
        "csd,cse->de", saved["blended"], grad_low_first, preferred_element_type=jnp.float32
    )
    outward_bias_grad = jnp.sum(grad_low_first.astype(jnp.float32), axis=(0, 1))
    grad_blended = jnp.einsum(
        "cse,de->csd", grad_low_first, outward_weight, preferred_element_type=jnp.float32
    )
    grad_blended = grad_blended.astype(jnp.bfloat16).reshape(clip_count, seg_rows, HEADS, head_size)
    query_heads = saved["query_heads"]
    key_heads = saved["key_heads"]
    value_heads = saved["value_heads"]
    slot_count = key_heads.shape[1]
    scores = attend_scores(query_heads, key_heads, key_valid, scale)
    soft = jnp.exp(scores - saved["log_total"])
    soft_low = soft.astype(jnp.bfloat16)
    grad_soft = jnp.einsum(
        "cqhe,ckhe->chqk", grad_blended, value_heads, preferred_element_type=jnp.float32
    )
    grad_scores = soft * (grad_soft - jnp.sum(grad_soft * soft, axis=-1, keepdims=True))
    grad_scores = grad_scores.astype(jnp.bfloat16)
    grad_queries = (
        jnp.einsum("chqk,ckhe->cqhe", grad_scores, key_heads, preferred_element_type=jnp.float32)
        * scale
    )
    grad_queries = grad_queries.astype(jnp.bfloat16).reshape(clip_count, seg_rows, model_width)
    grad_keys_part = (
        jnp.einsum("chqk,cqhe->ckhe", grad_scores, query_heads, preferred_element_type=jnp.float32)
        * scale
    )
    grad_values_part = jnp.einsum(
        "chqk,cqhe->ckhe", soft_low, grad_blended, preferred_element_type=jnp.float32
    )
    grad_keys_part = grad_keys_part.reshape(clip_count, slot_count, model_width)
    grad_values_part = grad_values_part.reshape(clip_count, slot_count, model_width)
    grad_keys, grad_values = (
        lax.psum_scatter(
            grad_keys_part.astype(jnp.bfloat16), "seq", scatter_dimension=1, tiled=True
        ).astype(jnp.float32),
        lax.psum_scatter(
            grad_values_part.astype(jnp.bfloat16), "seq", scatter_dimension=1, tiled=True
        ).astype(jnp.float32),
    )
    grad_keys = grad_keys.astype(jnp.bfloat16)
    grad_values = grad_values.astype(jnp.bfloat16)
    grad_project = jnp.concatenate([grad_queries, grad_keys, grad_values], axis=-1)
    inward_weight_grad = jnp.einsum(
        "csd,cse->de", saved["lowered_first"], grad_project, preferred_element_type=jnp.float32
    )
    query_bias_grad = jnp.sum(grad_queries.astype(jnp.float32), axis=(0, 1))
    value_bias_grad = jnp.sum(grad_values.astype(jnp.float32), axis=(0, 1))
    grad_first = jnp.einsum(
        "cse,de->csd", grad_project, inward_weight, preferred_element_type=jnp.float32
    )
    first_gain_grad = jnp.sum(grad_first * saved["normed_first"], axis=(0, 1))
    first_shift_grad = jnp.sum(grad_first, axis=(0, 1))
    tokens_grad = grad_middle + norm_back(
        grad_first, saved["normed_first"], saved["inverse_first"], first_gain.astype(jnp.float32)
    )
    weight_shares = (
        lax.psum_scatter(first_gain_grad, ("fsdp", "seq"), scatter_dimension=0, tiled=True),
        lax.psum_scatter(first_shift_grad, ("fsdp", "seq"), scatter_dimension=0, tiled=True),
        lax.psum_scatter(inward_weight_grad, ("fsdp", "seq"), scatter_dimension=0, tiled=True),
        lax.psum_scatter(query_bias_grad, ("fsdp", "seq"), scatter_dimension=0, tiled=True),
        lax.psum_scatter(value_bias_grad, ("fsdp", "seq"), scatter_dimension=0, tiled=True),
        lax.psum_scatter(outward_weight_grad, ("fsdp", "seq"), scatter_dimension=0, tiled=True),
        lax.psum_scatter(outward_bias_grad, ("fsdp", "seq"), scatter_dimension=0, tiled=True),
        lax.psum_scatter(second_gain_grad, ("fsdp", "seq"), scatter_dimension=0, tiled=True),
        lax.psum_scatter(second_shift_grad, ("fsdp", "seq"), scatter_dimension=0, tiled=True),
        lax.psum_scatter(expand_weight_grad, ("fsdp", "seq"), scatter_dimension=0, tiled=True),
        lax.psum_scatter(expand_bias_grad, ("fsdp", "seq"), scatter_dimension=0, tiled=True),
        lax.psum_scatter(shrink_weight_grad, ("fsdp", "seq"), scatter_dimension=0, tiled=True),
        lax.psum_scatter(shrink_bias_grad, ("fsdp", "seq"), scatter_dimension=0, tiled=True),
    )
    return (tokens_grad, weight_shares)


def shards(
    tokens,
    visible,
    first_gain,
    first_shift,
    inward_weight,
    query_bias,
    value_bias,
    outward_weight,
    outward_bias,
    second_gain,
    second_shift,
    expand_weight,
    expand_bias,
    shrink_weight,
    shrink_bias,
    upstream,
):
    clip_count, seg_rows, model_width = tokens.shape
    slot_count = seg_rows * lax.axis_size("seq")
    local_start = lax.axis_index("seq") * seg_rows
    row_positions = local_start + jnp.arange(seg_rows, dtype=jnp.int32)
    row_valid = (row_positions[None, :] < visible[:, None])[..., None]
    key_valid = jnp.arange(slot_count, dtype=jnp.int32)[None, :] < visible[:, None]
    tokens32 = tokens.astype(jnp.float32)
    upstream32 = upstream.astype(jnp.float32)
    gathered = gather_weights(
        first_gain,
        first_shift,
        inward_weight,
        query_bias,
        value_bias,
        outward_weight,
        outward_bias,
        second_gain,
        second_shift,
        expand_weight,
        expand_bias,
        shrink_weight,
        shrink_bias,
    )
    saved = forward(tokens32, key_valid, row_valid, gathered)
    layer_out = saved["output"]
    gathered = gather_weights(
        first_gain,
        first_shift,
        inward_weight,
        query_bias,
        value_bias,
        outward_weight,
        outward_bias,
        second_gain,
        second_shift,
        expand_weight,
        expand_bias,
        shrink_weight,
        shrink_bias,
    )
    saved = forward(tokens32, key_valid, row_valid, gathered)
    tokens_grad, shares = backward(saved, gathered, upstream32, key_valid, row_valid)
    return (
        layer_out,
        tokens_grad,
        shares[0],
        shares[1],
        shares[2],
        shares[3],
        shares[4],
        shares[5],
        shares[6],
        shares[7],
        shares[8],
        shares[9],
        shares[10],
        shares[11],
        shares[12],
    )


F32 = jnp.float32
BF16 = jnp.bfloat16
MESH = pl.DeviceIdType.MESH
SENDS, RECVS, LOCALS = 90, 134, 31
SLAB = 8


def matmul(a, b):
    return lax.dot_general(a, b, (((1,), (0,)), ((), ())), preferred_element_type=F32)


def matmul_bt(a, b):
    return lax.dot_general(a, b, (((1,), (1,)), ((), ())), preferred_element_type=F32)


def matmul_at(a, b):
    return lax.dot_general(a, b, (((0,), (0,)), ((), ())), preferred_element_type=F32)


def row_stats(x):
    mean = jnp.mean(x, axis=-1, keepdims=True)
    centered = x - mean
    inverse = lax.rsqrt(jnp.mean(centered * centered, axis=-1, keepdims=True) + epsilon)
    return centered * inverse, inverse


def row_norm_back(grad, normed, inverse, gain):
    scaled = grad * gain
    first_mean = jnp.mean(scaled, axis=-1, keepdims=True)
    second_mean = jnp.mean(scaled * normed, axis=-1, keepdims=True)
    return inverse * (scaled - first_mean - normed * second_mean)


class Place:
    def __init__(self, groups):
        self.groups = groups
        self.f = lax.axis_index("fsdp")
        self.y = lax.axis_index("seq")
        self.r = self.f // 4
        self.xc = self.f % 4
        self.t = self.xc * 2 + self.y
        x, c = self.xc // 2, self.xc % 2
        self.step = {4: 4 - 8 * x, 2: 2 - 4 * c, 1: 1 - 2 * self.y}

    def peer(self, mask):
        at = self.t
        for bit in (4, 2, 1):
            if mask & bit:
                at = at + self.step[bit]
        return at

    def device(self, r, t):
        return (r * 4 + t // 2, t % 2)


def rows(ref, index, size):
    return ref.at[pl.ds(pl.multiple_of(index * size, size), size), :]


def cols(ref, index, size):
    return ref.at[:, pl.ds(pl.multiple_of(index * size, size), size)]


class Wire:
    def __init__(self, place, send_sems, recv_sems, local_sems):
        self.place = place
        self.send_sems, self.recv_sems, self.local_sems = send_sems, recv_sems, local_sems
        self.sends = self.recvs = self.locals = 0
        self.free, self.open_sends = [], []

    def recv_slots(self, count):
        first = self.recvs
        self.recvs += count
        return [self.recv_sems.at[first + i] for i in range(count)]

    def batch(self, whole):
        spot = self.take()
        self.open_sends.append((lambda: self.describe(whole, whole, spot, self.recv_sems.at[0], self.near()), None, spot, False))
        return spot

    def near(self):
        return (self.place.r, self.place.peer(2))

    def take(self):
        if not self.free:
            self.free.append(self.sends)
            self.sends += 1
        return self.free.pop()

    def describe(self, src, dst, spot, slot, to):
        return pltpu.make_async_remote_copy(
            src_ref=src,
            dst_ref=dst,
            send_sem=self.send_sems.at[spot],
            recv_sem=slot,
            device_id=self.place.device(*to),
            device_id_type=MESH,
        )

    def send(self, src, dst, slot, to, when=None, batch=None):
        spot = self.take() if batch is None else batch

        def make():
            return self.describe(src, dst, spot, slot, to)

        if when is None:
            make().start()
        else:
            pl.when(when)(lambda: make().start())
        if batch is None:
            self.open_sends.append((make, when, spot, to[0] is not self.place.r))

    def settle(self, count=None, slab_only=False):
        count = len(self.open_sends) if count is None else count
        kept = []
        for item in self.open_sends[:count]:
            make, when, spot, far = item
            if slab_only and far:
                kept.append(item)
                continue
            if when is None:
                make().wait_send()
            else:
                pl.when(when)(lambda make=make: make().wait_send())
            self.free.append(spot)
        self.open_sends = kept + self.open_sends[count:]

    def arrived(self, dst, slot, when=None):
        def wait():
            self.describe(dst, dst, 0, slot, self.near()).wait_recv()

        if when is None:
            wait()
        else:
            pl.when(when)(wait)

    def local(self, src, dst):
        copy = pltpu.make_async_copy(src, dst, self.local_sems.at[self.locals])
        self.locals += 1
        copy.start()
        return copy


class SlabGather:
    def __init__(self, wire, at, half):
        self.wire, self.at, self.half = wire, at, half
        self.slots = wire.recv_slots(11)

    def start(self, whole, halves):
        wire, place, slots = self.wire, self.wire.place, self.slots
        t, r = place.t, place.r
        wire.send(halves[0], self.half(t, 0), slots[0], (r, place.peer(4)))
        wire.send(halves[1], self.half(t, 1), slots[3], (r, place.peer(1)))
        wire.send(halves[1], self.half(t, 1), slots[1], (r, place.peer(4)))
        wire.send(halves[0], self.half(t, 0), slots[2], (r, place.peer(1)))
        wire.send(whole, self.at(t), slots[6], (r, place.peer(2)))

    def relay(self):
        wire, place, slots = self.wire, self.wire.place, self.slots
        r, far, near = place.r, place.peer(4), place.peer(1)
        wire.arrived(self.half(far, 0), slots[0])
        wire.send(self.half(far, 0), self.half(far, 0), slots[4], (r, near))
        wire.arrived(self.half(near, 1), slots[3])
        wire.send(self.half(near, 1), self.half(near, 1), slots[5], (r, far))
        wire.arrived(self.half(far, 1), slots[1])
        wire.send(self.at(far), self.at(far), slots[7], (r, place.peer(2)))
        wire.arrived(self.half(near, 0), slots[2])
        wire.send(self.at(near), self.at(near), slots[8], (r, place.peer(2)))

    def forward(self):
        wire, place, slots = self.wire, self.wire.place, self.slots
        across = place.peer(5)
        for h in range(2):
            block = self.half(across, h)
            wire.arrived(block, slots[4 + h])
            wire.send(block, block, slots[9 + h], (place.r, place.peer(2)))

    def wait_block(self, mask):
        wire, place, slots = self.wire, self.wire.place, self.slots
        if mask == 7:
            for h in range(2):
                wire.arrived(self.half(place.peer(7), h), slots[9 + h])
        else:
            wire.arrived(self.at(place.peer(mask)), slots[{2: 6, 6: 7, 3: 8}[mask]])

    def wait(self):
        for mask in (2, 6, 3, 7):
            self.wait_block(mask)


class SlabScatter:
    def __init__(self, wire, part, core_in, chip_in, block):
        self.wire, self.part, self.core_in, self.chip_in, self.block = wire, part, core_in, chip_in, block
        self.core_slots = wire.recv_slots(4)
        self.slots = wire.recv_slots(6)
        self.order = (5, 4, 1, 0)

    def cores(self):
        place = self.wire.place
        for i, mask in enumerate(self.order):
            self.wire.send(
                rows(self.part, place.peer(mask ^ 2), self.block),
                self.core_in.at[i],
                self.core_slots[i],
                (place.r, place.peer(2)),
            )

    def half(self, mask, h):
        return rows(self.part, self.wire.place.peer(mask) * 2 + h, self.block // 2)

    def add_core(self, i):
        mask = self.order[i]
        self.wire.arrived(self.core_in.at[i], self.core_slots[i])
        mine = rows(self.part, self.wire.place.peer(mask), self.block)
        mine[...] = (mine[...].astype(F32) + self.core_in[i].astype(F32)).astype(BF16)

    def chips(self):
        wire, place = self.wire, self.wire.place
        far, near = (place.r, place.peer(4)), (place.r, place.peer(1))
        self.add_core(0)
        wire.send(self.half(5, 0), self.chip_in.at[0], self.slots[0], far)
        wire.send(self.half(5, 1), self.chip_in.at[1], self.slots[1], near)
        self.add_core(1)
        wire.send(self.half(4, 0), self.chip_in.at[2], self.slots[2], far)
        self.add_core(2)
        wire.send(self.half(1, 1), self.chip_in.at[3], self.slots[3], near)
        wire.arrived(self.core_in.at[3], self.core_slots[3])

    def relay(self):
        wire, place = self.wire, self.wire.place
        far, near = (place.r, place.peer(4)), (place.r, place.peer(1))
        for i, (block, to) in enumerate(((self.half(1, 0), near), (self.half(4, 1), far))):
            wire.arrived(self.chip_in.at[i], self.slots[i])
            block[...] = (block[...].astype(F32) + self.chip_in[i].astype(F32)).astype(BF16)
            wire.send(block, self.chip_in.at[4 + i], self.slots[4 + i], to)

    def wait(self):
        for i in range(2, 6):
            self.wire.arrived(self.chip_in.at[i], self.slots[i])

    def total(self, first, size):
        mine = self.part[pl.ds(pl.multiple_of(self.wire.place.t * self.block + first, size), size), :].astype(F32)
        mine = mine + self.core_in[3, pl.ds(pl.multiple_of(first, size), size), :].astype(F32)
        h = first // (self.block // 2)
        at = pl.ds(pl.multiple_of(first % (self.block // 2), size), size)
        return mine + self.chip_in[2 + h, at, :].astype(F32) + self.chip_in[4 + h, at, :].astype(F32)


class SlabSwap:
    def __init__(self, wire, source, target, seven):
        self.wire, self.source, self.target, self.seven = wire, source, target, seven
        (self.slot,) = wire.recv_slots(1)

    def start(self):
        place = self.wire.place
        self.own = self.wire.local(self.source(place.t), self.target(place.t))
        batch = self.wire.batch(self.seven)
        for i in (4, 5, 3, 6, 2, 7, 1):
            to = (place.t + i) % SLAB
            self.wire.send(self.source(to), self.target(place.t), self.slot, (place.r, to), batch=batch)

    def wait(self):
        self.wire.arrived(self.seven, self.slot)
        self.own.wait()


class GroupGather:
    def __init__(self, wire, at):
        self.wire, self.at = wire, at
        self.slots = wire.recv_slots(4)
        self.first = wire.recvs - 4
        r = wire.place.r
        self.inner, self.outer = (r + 1) // 2 == 1, (r + 1) // 2 != 1

    def start(self, src):
        wire, place = self.wire, self.wire.place
        r = place.r
        wire.send(src, self.at(r), self.slots[1], ((r + 1) % 4, place.t), r != 3)
        wire.send(src, self.at(r), self.slots[3], ((r + 3) % 4, place.t), r != 0)

    def pass_on(self):
        wire, place = self.wire, self.wire.place
        r = place.r
        below, above = (r + 3) % 4, (r + 1) % 4
        for block, slot, to in ((self.at(below), self.slots[1], above), (self.at(above), self.slots[3], below)):
            wire.arrived(block, slot, self.inner)
            wire.send(block, block, self.slots[2], (to, place.t), self.inner)

    def pass_far(self):
        wire, place = self.wire, self.wire.place
        r = place.r
        block = self.at((r + 2) % 4)
        wire.arrived(block, self.slots[2], self.inner)
        slot = wire.recv_sems.at[self.first + (2 * r + 3) % 4]
        wire.send(block, block, slot, ((3 * r + 1) % 4, place.t), self.inner)

    def wait(self):
        wire, r = self.wire, self.wire.place.r
        for i in (1, 2, 3):
            wire.arrived(self.at((r + 4 - i) % 4), self.slots[i], self.outer)


class GroupScatter:
    def __init__(self, wire, out, into, own, passing):
        self.wire, self.out, self.into, self.own, self.passing = wire, out, into, own, passing
        self.slots = wire.recv_slots(5)
        self.first = wire.recvs - 5
        r = wire.place.r

        @pl.when(r == 0)
        def _():
            into[0] = jnp.zeros_like(into[0])

        @pl.when(r == 3)
        def _():
            into[2] = jnp.zeros_like(into[2])

    def start(self, make):
        wire, place = self.wire, self.wire.place
        r, t = place.r, place.t
        inner = (r + 1) // 2 == 1
        outer = (r + 1) // 2 != 1
        low = 1 - r // 2
        pair = r + 1 - 2 * (r % 2)
        first, last = 1 + 2 * low, 3 - 2 * low
        self.out[0] = make((r + first) % 4).astype(BF16)
        wire.send(self.out.at[0], self.passing, self.slots[0], (pair, t), outer)
        wire.send(self.out.at[0], self.into.at[first - 1], wire.recv_sems.at[self.first + first], (pair, t), inner)
        self.out[1] = make((r + 2) % 4).astype(BF16)
        wire.send(self.out.at[1], self.into.at[1], self.slots[2], ((r + 2) % 4, t), outer)
        self.out[2] = make((r + last) % 4).astype(BF16)
        wire.send(
            self.out.at[2], self.into.at[last - 1], wire.recv_sems.at[self.first + last], ((r + last) % 4, t)
        )
        self.own[...] = make(r)

    def relay(self):
        wire, place = self.wire, self.wire.place
        r = place.r
        inner = (r + 1) // 2 == 1
        wire.arrived(self.passing, self.slots[0], inner)

        @pl.when(inner)
        def _():
            self.out[1] = (self.out[1].astype(F32) + self.passing[...].astype(F32)).astype(BF16)

        wire.send(self.out.at[1], self.into.at[1], self.slots[2], ((r + 2) % 4, place.t), inner)

    def total(self):
        wire, r = self.wire, self.wire.place.r
        wire.arrived(self.into.at[1], self.slots[2])
        wire.arrived(self.into.at[0], self.slots[1], r != 0)
        wire.arrived(self.into.at[2], self.slots[3], r != 3)
        total = self.own[...]
        for i in range(3):
            total = total + self.into[i].astype(F32)
        return total


def layer_kernel(
    groups,
    scale,
    tokens,
    upstream,
    visible,
    first_gain,
    first_shift,
    query_bias,
    value_bias,
    outward_bias,
    second_gain,
    second_shift,
    shrink_bias,
    expand_bias,
    w_in,
    w_out,
    w_exp,
    w_shr,
    layer_hbm,
    tokens_hbm,
    in_hbm,
    out_hbm,
    exp_hbm,
    shr_hbm,
    vec_hbm,
    layer_out,
    tokens_grad,
    out_grad,
    shr_grad,
    vec_grad,
    pack,
    small,
    wide_small,
    packs,
    tok_all,
    first_all,
    win,
    wex,
    wsh,
    wo,
    gls,
    gls_all,
    vecs,
    ebias,
    qkv,
    gqkv,
    soft_all,
    blend_t,
    blend,
    middle,
    normed,
    inverses,
    second,
    second_all,
    active,
    ghid,
    slopes,
    part_a,
    part_b,
    part_c,
    part_d,
    core_a,
    core_b,
    core_c,
    core_d,
    chip_a,
    chip_b,
    chip_c,
    chip_d,
    gsec,
    glow,
    gblend,
    gblend_t,
    sh_out,
    sh_in,
    sh_own,
    sh_pass,
    ex_out,
    ex_in,
    ex_own,
    ex_pass,
    ex_sum,
    ex_all,
    in_out,
    in_in,
    in_own,
    in_pass,
    in_sum,
    in_all,
    ou_out,
    ou_in,
    ou_own,
    ou_pass,
    gvec,
    gvec_exp,
    gvec_out,
    gvec_in,
    send_sems,
    recv_sems,
    local_sems,
):
    place = Place(groups)
    wire = Wire(place, send_sems, recv_sems, local_sems)
    f, y, r, xc, t = place.f, place.y, place.r, place.xc, place.t
    devices = groups * SLAB
    me = r * SLAB + t
    seg, width = tokens.shape
    clips = SLAB // 2
    slots = seg * 2
    total_rows = SLAB * seg
    head2 = qkv.shape[1] // 3
    own_rows = w_in.shape[0]
    slab_rows = own_rows * 4
    share = width // devices
    chunk = wsh.shape[1]
    strip = 32
    tile = 256

    vectors = (
        first_gain,
        first_shift,
        query_bias,
        value_bias,
        outward_bias,
        second_gain,
        second_shift,
        shrink_bias,
    )
    loads = [wire.local(ref, small.at[k]) for k, ref in enumerate(vectors)]
    loads.append(wire.local(expand_bias, wide_small))
    barrier = pltpu.get_barrier_semaphore()
    for i in range(1, devices):
        to = (me + i) % devices
        pl.semaphore_signal(barrier, inc=1, device_id=place.device(to // SLAB, to % SLAB), device_id_type=MESH)
    for copy in loads:
        copy.wait()
    per_lane = 128 // own_rows
    lines = [jnp.concatenate([small[k].astype(F32)] * per_lane, axis=1) for k in range(8)]
    lines.append(wide_small[...].astype(F32))
    count_here = jnp.full((6, 128), visible[0], jnp.int32).astype(F32)
    pack[...] = jnp.concatenate(lines + [count_here], axis=0).astype(BF16)
    pl.semaphore_wait(barrier, devices - 1)

    (pack_slot,) = wire.recv_slots(1)
    pack_batch = wire.batch(packs.at[pl.ds(0, groups * 4 - 1)])
    for i in range(1, groups * 4):
        to = (f + i) % (groups * 4)
        wire.send(pack, packs.at[f], pack_slot, (to // 4, (to % 4) * 2 + y), batch=pack_batch)
    own_pack = wire.local(pack, packs.at[f])

    in_slots = wire.recv_slots(4)
    ex_slots = wire.recv_slots(4)

    def in_piece(index, c):
        return win.at[pl.ds(pl.multiple_of(index * own_rows, own_rows), own_rows), pl.ds(c * head2, head2)]

    def ex_piece(index, c):
        return wex.at[pl.ds(pl.multiple_of(index * own_rows, own_rows), own_rows), pl.ds(c * chunk, chunk)]

    own_in = []
    in_batch = wire.batch(win.at[pl.ds(0, 3 * own_rows), :])
    for i in (2, 3, 1, 0):
        to = ((xc + i) % 4) * 2 + y
        for c in range(3):
            src = w_in.at[:, pl.ds(pl.multiple_of(c * width + to * head2, head2), head2)]
            if i == 0:
                own_in.append(wire.local(src, in_piece(f, c)))
            else:
                wire.send(src, in_piece(f, c), in_slots[i], (r, to), batch=in_batch)

    out_share = w_out.at[pl.ds(pl.multiple_of(y * share, share), share), :]
    own_out = wire.local(out_share, wo.at[r, t])
    group_wo = GroupGather(wire, lambda at: wo.at[at, t])
    group_wo.start(out_share)
    shr_share = w_shr.at[pl.ds(pl.multiple_of(y * chunk, chunk), chunk), :]
    own_shr = wire.local(shr_share, wsh.at[r])
    group_sh = GroupGather(wire, lambda at: wsh.at[at])

    def slab_gather(ref):
        return SlabGather(wire, lambda at: rows(ref, at, seg), lambda at, h: rows(ref, at * 2 + h, seg // 2))

    gather_tok = slab_gather(tok_all)
    gather_tok.start(tokens, [rows(tokens, h, seg // 2) for h in range(2)])

    own_ex = []
    ex_batch = wire.batch(wex.at[pl.ds(0, 3 * own_rows), :])
    for i in (2, 3, 1, 0):
        to = ((xc + i) % 4) * 2 + y
        for c in range(groups):
            src = w_exp.at[:, pl.ds(pl.multiple_of((c * SLAB + to) * chunk, chunk), chunk)]
            if i == 0:
                own_ex.append(wire.local(src, ex_piece(f, c)))
            else:
                wire.send(src, ex_piece(f, c), ex_slots[i], (r, to), batch=ex_batch)

    row_at = y * seg + lax.broadcasted_iota(jnp.int32, (seg, 1), 0)
    row_valid = row_at.astype(F32) < pack[10:11, 0:1].astype(F32)
    gls[...] = jnp.where(row_valid, upstream[...].astype(F32), 0.0).astype(BF16)
    gls_all[pl.ds(pl.multiple_of(t * seg, seg), seg), :] = gls[...]
    gvec[...] = jnp.zeros_like(gvec)
    gvec_exp[...] = jnp.zeros_like(gvec_exp)
    group_shr = GroupScatter(wire, sh_out, sh_in, sh_own, sh_pass)
    group_exp = GroupScatter(wire, ex_out, ex_in, ex_own, ex_pass)
    group_inw = GroupScatter(wire, in_out, in_in, in_own, in_pass)
    group_out = GroupScatter(wire, ou_out, ou_in, ou_own, ou_pass)

    for i in range(1, 4):
        frm = r * 4 + (xc + 4 - i) % 4
        wire.arrived(rows(win, frm, own_rows), in_slots[i])
    for copy in own_in:
        copy.wait()
    own_out.wait()
    group_wo.pass_on()
    group_in = GroupGather(wire, lambda at: rows(win, at, slab_rows))
    group_in.start(rows(win, r, slab_rows))
    group_wo.pass_far()

    own_pack.wait()
    wire.arrived(packs.at[pl.ds(0, groups * 4 - 1)], pack_slot)
    lane = lax.broadcasted_iota(jnp.int32, (1, 128), 1)
    for j in range(width // 128):
        piece = packs[j * per_lane].astype(F32)
        for k in range(1, per_lane):
            piece = jnp.where(lane >= k * own_rows, packs[j * per_lane + k].astype(F32), piece)
        vecs[:, j * 128 : (j + 1) * 128] = piece
    for c in range(groups):
        both = packs[c * 4 + t // 2].astype(F32)
        ebias[0:1, c * chunk : (c + 1) * chunk] = jnp.where(y == 0, both[8:9], both[9:10])

    def first_norm(src, offset, block):
        def strip_norm(i, carry):
            at = pl.multiple_of(i * strip, strip)
            n, _ = row_stats(src[pl.ds(offset + at, strip), :].astype(F32))
            to = pl.multiple_of(block * seg + at, strip)
            first_all[pl.ds(to, strip), :] = (n * vecs[0:1, :] + vecs[1:2, :]).astype(BF16)
            return carry

        lax.fori_loop(0, seg // strip, strip_norm, 0)

    first_norm(tokens, 0, t)

    def norm_block(mask):
        block = place.peer(mask)
        first_norm(tok_all, pl.multiple_of(block * seg, seg), block)

    gather_tok.relay()
    group_in.pass_on()
    norm_block(4)
    norm_block(1)

    gather_tok.forward()

    norm_block(5)
    group_in.pass_far()
    for i in range(1, 4):
        frm = r * 4 + (xc + 4 - i) % 4
        wire.arrived(rows(wex, frm, own_rows), ex_slots[i])
    for copy in own_ex:
        copy.wait()
    group_ex = GroupGather(wire, lambda at: rows(wex, at, slab_rows))
    group_ex.start(rows(wex, r, slab_rows))
    group_sh.start(shr_share)

    group_wo.wait()
    gather_wo = SlabGather(wire, lambda at: wo.at[:, at], lambda at, h: wo.at[pl.ds(h * (groups // 2), groups // 2), at])
    gather_wo.start(wo.at[:, t], [wo.at[pl.ds(h * (groups // 2), groups // 2), t] for h in range(2)])

    for mask in (2, 6, 3, 7):
        gather_tok.wait_block(mask)
        norm_block(mask)

    gather_wo.relay()
    gather_gls = slab_gather(gls_all)
    gather_gls.start(gls, [rows(gls, h, seg // 2) for h in range(2)])
    group_in.wait()
    at_head = pl.ds(pl.multiple_of(t * head2, head2), head2)
    bias = jnp.concatenate([vecs[2:3, at_head], jnp.zeros((1, head2), F32), vecs[3:4, at_head]], axis=1)

    def project(i, carry):
        at = pl.ds(pl.multiple_of(i * tile, tile), tile)
        qkv[at, :] = (matmul(first_all[at, :], win[...]) + bias).astype(BF16)
        return carry

    lax.fori_loop(0, total_rows // tile, project, 0)

    head_size = head2 // 2
    low_half = lane < head_size
    half_masks = [low_half.astype(F32).astype(BF16), (1.0 - low_half.astype(F32)).astype(BF16)]
    key_at = lax.broadcasted_iota(jnp.int32, (1, slots), 1).astype(F32)

    def attend(i, carry):
        at = pl.ds(pl.multiple_of(i * slots, slots), slots)
        q = qkv[at, 0:head2]
        k = qkv[at, head2 : 2 * head2]
        v = qkv[at, 2 * head2 : 3 * head2]
        count = packs[r * 4 + i].astype(F32)[10:11, 0:1]
        key_valid = key_at < count
        halves = []
        for h in range(2):
            scores = matmul_bt(q * half_masks[h], k) * scale
            scores = jnp.where(key_valid, scores, -1e30)
            top = jnp.max(scores, axis=-1, keepdims=True)
            log_total = top + jnp.log(jnp.sum(jnp.exp(scores - top), axis=-1, keepdims=True))
            soft = jnp.exp(scores - log_total)
            soft_all[i * 2 + h] = soft
            halves.append(matmul(soft.astype(BF16), v))
        blend_t[at, :] = jnp.where(low_half, halves[0], halves[1]).astype(BF16)
        return carry

    lax.fori_loop(0, clips, attend, 0)

    group_ex.pass_on()
    swap_blend = SlabSwap(wire, lambda at: rows(blend_t, at, seg), lambda at: cols(blend, at, head2), blend.at[:, 0 : 7 * head2])
    swap_blend.start()
    gather_wo.forward()

    gather_gls.relay()
    gather_wo.wait()
    swap_blend.wait()
    group_ex.pass_far()
    wide = 256
    for j in range(width // wide):
        at = slice(j * wide, (j + 1) * wide)
        product = matmul(blend[...], wo[:, :, :, at].reshape(width, wide))
        middle[:, at] = tokens[:, at].astype(F32) + (product + vecs[4:5, at])

    own_second_rows = pl.multiple_of(t * seg, seg)

    def second_norm(i, carry):
        at = pl.ds(pl.multiple_of(i * strip, strip), strip)
        n, inverse = row_stats(middle[at, :])
        normed[at, :] = n
        inverses[at, :] = jnp.broadcast_to(inverse, (strip, 128))
        low = (n * vecs[5:6, :] + vecs[6:7, :]).astype(BF16)
        second[at, :] = low
        second_all[pl.ds(pl.multiple_of(own_second_rows + i * strip, strip), strip), :] = low
        return carry

    lax.fori_loop(0, seg // strip, second_norm, 0)

    gather_second = slab_gather(second_all)
    gather_second.start(second, [rows(second, h, seg // 2) for h in range(2)])
    group_sh.pass_on()
    gather_gls.forward()
    gather_second.relay()
    group_sh.pass_far()
    gather_second.forward()
    gather_gls.wait()
    gather_second.wait()
    group_ex.wait()
    front_sends = len(wire.open_sends)

    hidden_units = groups * chunk

    def feed(i, carry):
        at = pl.ds(pl.multiple_of(i * tile, tile), tile)
        hidden = matmul(second_all[at, :], wex[...]) + ebias[0:1, :]
        cdf = 0.5 * (1.0 + lax.erf(hidden * 0.7071067811865476))
        active[at, :] = (hidden * cdf).astype(BF16)
        slopes[at, :] = cdf + hidden * (0.3989422804014327 * jnp.exp(-0.5 * hidden * hidden))
        return carry

    lax.fori_loop(0, total_rows // tile, feed, 0)
    group_shr.start(
        lambda c: matmul_at(active[:, pl.ds(pl.multiple_of(c * chunk, chunk), chunk)], gls_all[...])
    )
    group_sh.wait()
    own_shr.wait()

    def feed_back(i, carry):
        at = pl.ds(pl.multiple_of(i * tile, tile), tile)
        grad_active = matmul_bt(gls_all[at, :], wsh[...].reshape(hidden_units, width))
        grad_hidden = (grad_active * slopes[at, :]).astype(BF16)
        ghid[at, :] = grad_hidden
        gvec_exp[...] += jnp.sum(grad_hidden.astype(F32), axis=0, keepdims=True)
        part_a[at, :] = matmul_bt(grad_hidden, wex[...]).astype(BF16)
        return carry

    lax.fori_loop(0, total_rows // tile, feed_back, 0)

    scatter_second = SlabScatter(wire, part_a, core_a, chip_a, seg)
    scatter_second.cores()
    scatter_second.chips()
    group_exp.start(
        lambda c: matmul_at(second_all[:, pl.ds(pl.multiple_of(c * slab_rows, slab_rows), slab_rows)], ghid[...])
    )
    scatter_second.relay()

    def feed_out(i, carry):
        at = pl.ds(pl.multiple_of(i * tile, tile), tile)
        part_b[at, :] = matmul(active[at, :], wsh[...].reshape(hidden_units, width)).astype(BF16)
        return carry

    lax.fori_loop(0, total_rows // tile, feed_out, 0)
    scatter_result = SlabScatter(wire, part_b, core_b, chip_b, seg)
    scatter_result.cores()

    scatter_second.wait()
    wire.settle(front_sends)

    feed_sends = len(wire.open_sends)

    def second_back(i, carry):
        first = i * strip
        at = pl.ds(pl.multiple_of(first, strip), strip)
        grad = scatter_second.total(first, strip)
        n = normed[at, :]
        back = row_norm_back(grad, n, inverses[at, 0:1], vecs[5:6, :])
        grad_result = gls[at, :].astype(F32)
        grad_middle = grad_result + back
        gsec[at, :] = grad_middle
        low = grad_middle.astype(BF16)
        glow[at, :] = low
        gvec[4:5, :] += jnp.sum(low.astype(F32), axis=0, keepdims=True)
        gvec[5:6, :] += jnp.sum(grad * n, axis=0, keepdims=True)
        gvec[6:7, :] += jnp.sum(grad, axis=0, keepdims=True)
        gvec[7:8, :] += jnp.sum(grad_result, axis=0, keepdims=True)
        return carry

    lax.fori_loop(0, seg // strip, second_back, 0)

    for j in range(width // wide):
        rows_of = slice(j * (groups * wide // width), (j + 1) * (groups * wide // width))
        gblend[:, j * wide : (j + 1) * wide] = matmul_bt(
            glow[...], wo[rows_of].reshape(wide, width)
        ).astype(BF16)
    swap_gblend = SlabSwap(wire, lambda at: cols(gblend, at, head2), lambda at: rows(gblend_t, at, seg), gblend_t.at[pl.ds(0, 7 * seg), :])
    swap_gblend.start()
    group_shr.relay()

    for c in range(groups):
        product = matmul_at(blend[:, c * slab_rows : (c + 1) * slab_rows], glow[...])
        for to in range(SLAB):
            part_d[to * seg + c * share : to * seg + (c + 1) * share, :] = product[
                to * share : (to + 1) * share
            ].astype(BF16)
    scatter_out = SlabScatter(wire, part_d, core_d, chip_d, seg)
    scatter_out.cores()

    swap_gblend.wait()

    scatter_out.chips()
    def attend_back(i, carry):
        at = pl.ds(pl.multiple_of(i * slots, slots), slots)
        q = qkv[at, 0:head2]
        k = qkv[at, head2 : 2 * head2]
        v = qkv[at, 2 * head2 : 3 * head2]
        grad = gblend_t[at, :]
        parts = []
        for h in range(2):
            soft = soft_all[i * 2 + h]
            grad_soft = matmul_bt(grad * half_masks[h], v)
            inner = jnp.sum(grad_soft * soft, axis=-1, keepdims=True)
            grad_scores = (soft * (grad_soft - inner)).astype(BF16)
            parts.append(
                (
                    matmul(grad_scores, k) * scale,
                    matmul_at(grad_scores, q) * scale,
                    matmul_at(soft.astype(BF16), grad),
                )
            )
        for c in range(3):
            gqkv[at, c * head2 : (c + 1) * head2] = jnp.where(low_half, parts[0][c], parts[1][c]).astype(BF16)
        return carry

    lax.fori_loop(0, clips, attend_back, 0)

    scatter_out.relay()
    def project_back(i, carry):
        at = pl.ds(pl.multiple_of(i * tile, tile), tile)
        part_c[at, :] = matmul_bt(gqkv[at, :], win[...]).astype(BF16)
        return carry

    lax.fori_loop(0, total_rows // tile, project_back, 0)
    scatter_first = SlabScatter(wire, part_c, core_c, chip_c, seg)
    scatter_first.cores()

    group_inw.start(
        lambda c: matmul_at(first_all[:, pl.ds(pl.multiple_of(c * slab_rows, slab_rows), slab_rows)], gqkv[...])
    )
    scatter_first.chips()
    gvec[2:3, at_head] = jnp.sum(gqkv[:, 0:head2].astype(F32), axis=0, keepdims=True)
    gvec[3:4, at_head] = jnp.sum(gqkv[:, 2 * head2 :].astype(F32), axis=0, keepdims=True)

    scatter_out.wait()
    group_out.start(lambda c: scatter_out.total(c * share, share))
    group_exp.relay()
    scatter_first.relay()
    scatter_result.chips()
    scatter_first.wait()
    wire.settle(feed_sends, slab_only=True)

    def first_back(i, carry):
        first = i * strip
        at = pl.ds(pl.multiple_of(first, strip), strip)
        grad = scatter_first.total(first, strip)
        n, inverse = row_stats(tokens[at, :].astype(F32))
        tokens_grad[at, :] = gsec[at, :] + row_norm_back(grad, n, inverse, vecs[0:1, :])
        gvec[0:1, :] += jnp.sum(grad * n, axis=0, keepdims=True)
        gvec[1:2, :] += jnp.sum(grad, axis=0, keepdims=True)
        return carry

    lax.fori_loop(0, seg // strip, first_back, 0)
    stores = [wire.local(tokens_grad, tokens_hbm)]

    per_chunk = 128 // share
    for j in range(width // 128):
        gvec_out[j, 0:8, :] = gvec[:, j * 128 : (j + 1) * 128]
        c = j * per_chunk // SLAB
        gvec_out[j, 8:16, :] = jnp.broadcast_to(gvec_exp[0:1, c * chunk : (c + 1) * chunk], (8, chunk))
    (vec_slot,) = wire.recv_slots(1)
    vec_batch = wire.batch(gvec_in.at[pl.ds(0, devices - 1)])
    for i in range(1, devices):
        to = (me + i) % devices
        wire.send(gvec_out.at[to // per_chunk], gvec_in.at[me], vec_slot, (to // SLAB, to % SLAB), batch=vec_batch)
    own_vec = wire.local(gvec_out.at[me // per_chunk], gvec_in.at[me])

    group_inw.relay()
    scatter_result.relay()
    group_out.relay()
    scatter_result.wait()

    def finish_out(i, carry):
        first = i * strip
        at = pl.ds(pl.multiple_of(first, strip), strip)
        result = middle[at, :] + (scatter_result.total(first, strip) + vecs[7:8, :])
        spot = y * seg + first + lax.broadcasted_iota(jnp.int32, (strip, 1), 0)
        valid = spot.astype(F32) < pack[10:11, 0:1].astype(F32)
        layer_out[at, :] = jnp.where(valid, result, 0.0).astype(BF16)
        return carry

    lax.fori_loop(0, seg // strip, finish_out, 0)
    stores.append(wire.local(layer_out, layer_hbm))

    shr_grad[...] = group_shr.total()
    stores.append(wire.local(shr_grad, shr_hbm))
    ex_sum[...] = group_exp.total().astype(BF16)
    swap_exp = SlabSwap(wire, lambda at: rows(ex_sum, at, share), lambda at: ex_all.at[at], ex_all.at[pl.ds(0, 7)])
    swap_exp.start()
    own_vec.wait()
    wire.arrived(gvec_in.at[pl.ds(0, devices - 1)], vec_slot)
    summed = gvec_in[0]
    for i in range(1, devices):
        summed = summed + gvec_in[i]
    for_exp = gvec_in[t]
    for c in range(1, groups):
        for_exp = for_exp + gvec_in[c * SLAB + t]
    vec_grad[0:8, :] = pltpu.roll(summed[0:8], (128 - share * (me % per_chunk)) % 128, 1)
    vec_grad[8:16, :] = for_exp[8:16]
    stores.append(wire.local(vec_grad, vec_hbm))

    in_sum[...] = group_inw.total().astype(BF16)
    swap_in = SlabSwap(wire, lambda at: rows(in_sum, at, share), lambda at: in_all.at[at], in_all.at[pl.ds(0, 7)])
    swap_in.start()
    out_grad[...] = group_out.total()
    stores.append(wire.local(out_grad, out_hbm))
    swap_exp.wait()
    stores.append(wire.local(ex_all, exp_hbm))
    swap_in.wait()
    stores.append(wire.local(in_all, in_hbm))
    for copy in stores:
        copy.wait()
    wire.settle()
    assert wire.sends <= SENDS and wire.recvs <= RECVS and wire.locals <= LOCALS


def output_kernel(
    groups,
    layer_in,
    tokens_in,
    in_pieces,
    out_in,
    exp_pieces,
    shr_in,
    vec_in,
    layer_out,
    tokens_grad,
    first_gain_grad,
    first_shift_grad,
    in_grad,
    query_bias_grad,
    value_bias_grad,
    out_grad,
    outward_bias_grad,
    second_gain_grad,
    second_shift_grad,
    exp_grad,
    expand_bias_grad,
    shr_grad,
    shrink_bias_grad,
    layer_buf,
    tokens_buf,
    in_buf,
    out_buf,
    exp_buf,
    shr_buf,
    vec_buf,
    in_wide,
    exp_wide,
    lines,
    wide_line,
    load_sems,
    store_sems,
):
    share, width = out_buf.shape
    head2, chunk = in_buf.shape[2] // 3, exp_buf.shape[2] // groups
    loads = [
        pltpu.make_async_copy(src, dst, load_sems.at[i])
        for i, (src, dst) in enumerate(
            (
                (vec_in, vec_buf),
                (exp_pieces, exp_buf),
                (in_pieces, in_buf),
                (shr_in, shr_buf),
                (tokens_in, tokens_buf),
                (layer_in, layer_buf),
                (out_in, out_buf),
            )
        )
    ]
    for copy in loads:
        copy.start()
    stores = []

    def store(src, dst):
        stores.append(pltpu.make_async_copy(src, dst, store_sems.at[len(stores)]))
        stores[-1].start()

    loads[0].wait()
    vectors = (
        first_gain_grad,
        first_shift_grad,
        query_bias_grad,
        value_bias_grad,
        outward_bias_grad,
        second_gain_grad,
        second_shift_grad,
        shrink_bias_grad,
    )
    for k, ref in enumerate(vectors):
        lines[k] = vec_buf[k, 0:share]
        store(lines.at[k], ref)
    wide_line[...] = vec_buf[8, :]
    store(wide_line, expand_bias_grad)
    loads[1].wait()
    for frm in range(SLAB):
        for c in range(groups):
            at = (c * SLAB + frm) * chunk
            exp_wide[:, at : at + chunk] = exp_buf[frm, :, c * chunk : (c + 1) * chunk].astype(F32)
    store(exp_wide, exp_grad)
    loads[2].wait()
    for frm in range(SLAB):
        for c in range(3):
            at = c * width + frm * head2
            in_wide[:, at : at + head2] = in_buf[frm, :, c * head2 : (c + 1) * head2].astype(F32)
    store(in_wide, in_grad)
    for copy, src, dst in (
        (loads[3], shr_buf, shr_grad),
        (loads[4], tokens_buf, tokens_grad.at[0]),
        (loads[5], layer_buf, layer_out.at[0]),
        (loads[6], out_buf, out_grad),
    ):
        copy.wait()
        store(src, dst)
    for copy in stores:
        copy.wait()


def fused_shards(
    tokens,
    visible,
    first_gain,
    first_shift,
    inward_weight,
    query_bias,
    value_bias,
    outward_weight,
    outward_bias,
    second_gain,
    second_shift,
    expand_weight,
    expand_bias,
    shrink_weight,
    shrink_bias,
    upstream,
):
    seg, width = tokens.shape[1:]
    groups = lax.axis_size("fsdp") // 4
    devices = groups * SLAB
    own_rows = inward_weight.shape[0]
    hidden = expand_weight.shape[1]
    share = width // devices
    chunk = hidden // devices
    units = groups * chunk
    head2 = width // SLAB
    scale = (width // HEADS) ** (-0.5)
    total_rows = SLAB * seg
    slab_rows = 4 * own_rows
    vmem = pl.BlockSpec(memory_space=pltpu.VMEM)
    anywhere = pl.BlockSpec(memory_space=pl.ANY)
    outs = pl.pallas_call(
        functools.partial(layer_kernel, groups, scale),
        out_shape=(
            jax.ShapeDtypeStruct((seg, width), BF16),
            jax.ShapeDtypeStruct((seg, width), F32),
            jax.ShapeDtypeStruct((SLAB, share, 3 * head2), BF16),
            jax.ShapeDtypeStruct((share, width), F32),
            jax.ShapeDtypeStruct((SLAB, share, units), BF16),
            jax.ShapeDtypeStruct((chunk, width), F32),
            jax.ShapeDtypeStruct((16, 128), F32),
        ),
        in_specs=[vmem, vmem, pl.BlockSpec(memory_space=pltpu.SMEM)] + [anywhere] * 13,
        out_specs=[anywhere] * 7,
        scratch_shapes=[
            pltpu.VMEM((seg, width), BF16),
            pltpu.VMEM((seg, width), F32),
            pltpu.VMEM((share, width), F32),
            pltpu.VMEM((chunk, width), F32),
            pltpu.VMEM((16, 128), F32),
            pltpu.VMEM((16, 128), BF16),
            pltpu.VMEM((8, 1, own_rows), BF16),
            pltpu.VMEM((2, 128), BF16),
            pltpu.VMEM((groups * 4, 16, 128), BF16),
            pltpu.VMEM((total_rows, width), BF16),
            pltpu.VMEM((total_rows, width), BF16),
            pltpu.VMEM((width, 3 * head2), BF16),
            pltpu.VMEM((width, units), BF16),
            pltpu.VMEM((groups, chunk, width), BF16),
            pltpu.VMEM((groups, SLAB, share, width), BF16),
            pltpu.VMEM((seg, width), BF16),
            pltpu.VMEM((total_rows, width), BF16),
            pltpu.VMEM((16, width), F32),
            pltpu.VMEM((8, units), F32),
            pltpu.VMEM((total_rows, 3 * head2), BF16),
            pltpu.VMEM((total_rows, 3 * head2), BF16),
            pltpu.VMEM((SLAB, 2 * seg, 2 * seg), F32),
            pltpu.VMEM((total_rows, head2), BF16),
            pltpu.VMEM((seg, width), BF16),
            pltpu.VMEM((seg, width), F32),
            pltpu.VMEM((seg, width), F32),
            pltpu.VMEM((seg, 128), F32),
            pltpu.VMEM((seg, width), BF16),
            pltpu.VMEM((total_rows, width), BF16),
            pltpu.VMEM((total_rows, units), BF16),
            pltpu.VMEM((total_rows, units), BF16),
            pltpu.VMEM((total_rows, units), F32),
        ]
        + [pltpu.VMEM((total_rows, width), BF16)] * 4
        + [pltpu.VMEM((4, seg, width), BF16)] * 4
        + [pltpu.VMEM((6, seg // 2, width), BF16)] * 4
        + [
            pltpu.VMEM((seg, width), F32),
            pltpu.VMEM((seg, width), BF16),
            pltpu.VMEM((seg, width), BF16),
            pltpu.VMEM((total_rows, head2), BF16),
            pltpu.VMEM((groups - 1, chunk, width), BF16),
            pltpu.VMEM((groups - 1, chunk, width), BF16),
            pltpu.VMEM((chunk, width), F32),
            pltpu.VMEM((chunk, width), BF16),
            pltpu.VMEM((groups - 1, slab_rows, units), BF16),
            pltpu.VMEM((groups - 1, slab_rows, units), BF16),
            pltpu.VMEM((slab_rows, units), F32),
            pltpu.VMEM((slab_rows, units), BF16),
            pltpu.VMEM((slab_rows, units), BF16),
            pltpu.VMEM((SLAB, share, units), BF16),
            pltpu.VMEM((groups - 1, slab_rows, 3 * head2), BF16),
            pltpu.VMEM((groups - 1, slab_rows, 3 * head2), BF16),
            pltpu.VMEM((slab_rows, 3 * head2), F32),
            pltpu.VMEM((slab_rows, 3 * head2), BF16),
            pltpu.VMEM((slab_rows, 3 * head2), BF16),
            pltpu.VMEM((SLAB, share, 3 * head2), BF16),
            pltpu.VMEM((groups - 1, share, width), BF16),
            pltpu.VMEM((groups - 1, share, width), BF16),
            pltpu.VMEM((share, width), F32),
            pltpu.VMEM((share, width), BF16),
            pltpu.VMEM((8, width), F32),
            pltpu.VMEM((1, units), F32),
            pltpu.VMEM((width // 128, 16, 128), F32),
            pltpu.VMEM((devices, 16, 128), F32),
            pltpu.SemaphoreType.DMA((SENDS,)),
            pltpu.SemaphoreType.DMA((RECVS,)),
            pltpu.SemaphoreType.DMA((LOCALS,)),
        ],
        compiler_params=pltpu.CompilerParams(
            collective_id=0, has_side_effects=True, vmem_limit_bytes=67043328
        ),
        name="layer",
    )(
        tokens.reshape(seg, width),
        upstream.reshape(seg, width),
        visible,
        *(
            vector.reshape(1, own_rows)
            for vector in (
                first_gain,
                first_shift,
                query_bias,
                value_bias,
                outward_bias,
                second_gain,
                second_shift,
                shrink_bias,
            )
        ),
        expand_bias.reshape(2, 128),
        inward_weight,
        outward_weight,
        expand_weight,
        shrink_weight,
    )
    vector = jax.ShapeDtypeStruct((share,), F32)
    return pl.pallas_call(
        functools.partial(output_kernel, groups),
        out_shape=(
            jax.ShapeDtypeStruct((1, seg, width), BF16),
            jax.ShapeDtypeStruct((1, seg, width), F32),
            vector,
            vector,
            jax.ShapeDtypeStruct((share, 3 * width), F32),
            vector,
            vector,
            jax.ShapeDtypeStruct((share, width), F32),
            vector,
            vector,
            vector,
            jax.ShapeDtypeStruct((share, hidden), F32),
            jax.ShapeDtypeStruct((chunk,), F32),
            jax.ShapeDtypeStruct((chunk, width), F32),
            vector,
        ),
        in_specs=[anywhere] * 7,
        out_specs=[anywhere] * 15,
        scratch_shapes=[
            pltpu.VMEM((seg, width), BF16),
            pltpu.VMEM((seg, width), F32),
            pltpu.VMEM((SLAB, share, 3 * head2), BF16),
            pltpu.VMEM((share, width), F32),
            pltpu.VMEM((SLAB, share, units), BF16),
            pltpu.VMEM((chunk, width), F32),
            pltpu.VMEM((16, 128), F32),
            pltpu.VMEM((share, 3 * width), F32),
            pltpu.VMEM((share, hidden), F32),
            pltpu.VMEM((8, share), F32),
            pltpu.VMEM((chunk,), F32),
            pltpu.SemaphoreType.DMA((7,)),
            pltpu.SemaphoreType.DMA((15,)),
        ],
        name="outputs",
    )(*outs)


def fits_fused(mesh, tokens, inward_weight, expand_weight):
    fsdp, seq = mesh.shape["fsdp"], mesh.shape["seq"]
    clips, slots, width = tokens.shape
    devices = fsdp * seq
    return (
        seq == 2
        and clips == fsdp
        and fsdp == 16
        and width // HEADS * 2 == 128
        and width == SLAB * 128
        and slots % 64 == 0
        and width % (16 * devices) == 0
        and 128 % (width // fsdp) == 0
        and expand_weight.shape[1] == 128 * devices
    )


def solution(mesh):
    in_specs = (
        P("fsdp", "seq", None),
        P("fsdp"),
        P("fsdp"),
        P("fsdp"),
        P("fsdp", None),
        P("fsdp"),
        P("fsdp"),
        P("fsdp", None),
        P("fsdp"),
        P("fsdp"),
        P("fsdp"),
        P("fsdp", None),
        P("fsdp"),
        P("fsdp", None),
        P("fsdp"),
        P("fsdp", "seq", None),
    )
    out_specs = (
        P("fsdp", "seq", None),
        P("fsdp", "seq", None),
        P(("fsdp", "seq")),
        P(("fsdp", "seq")),
        P(("fsdp", "seq"), None),
        P(("fsdp", "seq")),
        P(("fsdp", "seq")),
        P(("fsdp", "seq"), None),
        P(("fsdp", "seq")),
        P(("fsdp", "seq")),
        P(("fsdp", "seq")),
        P(("fsdp", "seq"), None),
        P(("fsdp", "seq")),
        P(("fsdp", "seq"), None),
        P(("fsdp", "seq")),
    )

    def step(*args):
        body = fused_shards if fits_fused(mesh, args[0], args[4], args[11]) else shards
        return jax.shard_map(body, mesh=mesh, in_specs=in_specs, out_specs=out_specs, check_vma=False)(*args)

    return step
```

```python
import functools

import jax
import jax.numpy as jnp
from jax import lax
from jax.experimental import pallas as pl
from jax.experimental.pallas import tpu as pltpu
from jax.sharding import PartitionSpec as P

HEADS = 16


epsilon = 1e-06


def norm_rows(inputs, norm_gain, norm_shift):
    row_mean = jnp.mean(inputs, axis=-1, keepdims=True)
    centered = inputs - row_mean
    variance = jnp.mean(centered * centered, axis=-1, keepdims=True)
    inverse = lax.rsqrt(variance + epsilon)
    normed = centered * inverse
    return (normed * norm_gain + norm_shift, normed, inverse)


def norm_back(grad_out, normed, inverse, norm_gain):
    scaled = grad_out * norm_gain
    first_mean = jnp.mean(scaled, axis=-1, keepdims=True)
    second_mean = jnp.mean(scaled * normed, axis=-1, keepdims=True)
    return inverse * (scaled - first_mean - normed * second_mean)


def gather_weights(
    first_gain,
    first_shift,
    inward_weight,
    query_bias,
    value_bias,
    outward_weight,
    outward_bias,
    second_gain,
    second_shift,
    expand_weight,
    expand_bias,
    shrink_weight,
    shrink_bias,
):
    return (
        lax.all_gather(first_gain, "fsdp", axis=0, tiled=True),
        lax.all_gather(first_shift, "fsdp", axis=0, tiled=True),
        lax.all_gather(inward_weight, "fsdp", axis=0, tiled=True),
        lax.all_gather(query_bias, "fsdp", axis=0, tiled=True),
        lax.all_gather(value_bias, "fsdp", axis=0, tiled=True),
        lax.all_gather(outward_weight, "fsdp", axis=0, tiled=True),
        lax.all_gather(outward_bias, "fsdp", axis=0, tiled=True),
        lax.all_gather(second_gain, "fsdp", axis=0, tiled=True),
        lax.all_gather(second_shift, "fsdp", axis=0, tiled=True),
        lax.all_gather(expand_weight, "fsdp", axis=0, tiled=True),
        lax.all_gather(expand_bias, "fsdp", axis=0, tiled=True),
        lax.all_gather(shrink_weight, "fsdp", axis=0, tiled=True),
        lax.all_gather(shrink_bias, "fsdp", axis=0, tiled=True),
    )


def attend_scores(query_heads, key_heads, key_valid, scale):
    scores = (
        jnp.einsum("cqhe,ckhe->chqk", query_heads, key_heads, preferred_element_type=jnp.float32)
        * scale
    )
    return jnp.where(key_valid[:, None, None, :], scores, -1e30)


def forward(tokens32, key_valid, row_valid, gathered):
    (
        first_gain,
        first_shift,
        inward_weight,
        query_bias,
        value_bias,
        outward_weight,
        outward_bias,
        second_gain,
        second_shift,
        expand_weight,
        expand_bias,
        shrink_weight,
        shrink_bias,
    ) = gathered
    clip_count, seg_rows, model_width = tokens32.shape
    head_size = model_width // HEADS
    scale = head_size ** (-0.5)
    affine_first, normed_first, inverse_first = norm_rows(
        tokens32, first_gain.astype(jnp.float32), first_shift.astype(jnp.float32)
    )
    lowered_first = affine_first.astype(jnp.bfloat16)
    merged_bias = jnp.concatenate([query_bias, jnp.zeros_like(query_bias), value_bias]).astype(
        jnp.float32
    )
    project = (
        jnp.einsum("csd,de->cse", lowered_first, inward_weight, preferred_element_type=jnp.float32)
        + merged_bias
    )
    queries = project[..., :model_width].astype(jnp.bfloat16)
    key_local = project[..., model_width : 2 * model_width].astype(jnp.bfloat16)
    value_local = project[..., 2 * model_width :].astype(jnp.bfloat16)
    key_all, value_all = (
        lax.all_gather(key_local, "seq", axis=1, tiled=True),
        lax.all_gather(value_local, "seq", axis=1, tiled=True),
    )
    slot_count = key_all.shape[1]
    query_heads = queries.reshape(clip_count, seg_rows, HEADS, head_size)
    key_heads = key_all.reshape(clip_count, slot_count, HEADS, head_size)
    value_heads = value_all.reshape(clip_count, slot_count, HEADS, head_size)
    scores = attend_scores(query_heads, key_heads, key_valid, scale)
    row_top = jnp.max(scores, axis=-1, keepdims=True)
    row_total = jnp.sum(jnp.exp(scores - row_top), axis=-1, keepdims=True)
    log_total = row_top + jnp.log(row_total)
    soft_low = jnp.exp(scores - log_total).astype(jnp.bfloat16)
    blended = jnp.einsum(
        "chqk,ckhe->cqhe", soft_low, value_heads, preferred_element_type=jnp.float32
    )
    blended = blended.reshape(clip_count, seg_rows, model_width).astype(jnp.bfloat16)
    branch = jnp.einsum(
        "csd,de->cse", blended, outward_weight, preferred_element_type=jnp.float32
    ) + outward_bias.astype(jnp.float32)
    middle = tokens32 + branch
    affine_second, normed_second, inverse_second = norm_rows(
        middle, second_gain.astype(jnp.float32), second_shift.astype(jnp.float32)
    )
    lowered_second = affine_second.astype(jnp.bfloat16)
    hidden = jnp.einsum(
        "csd,df->csf", lowered_second, expand_weight, preferred_element_type=jnp.float32
    ) + expand_bias.astype(jnp.float32)
    active = jax.nn.gelu(hidden, approximate=False).astype(jnp.bfloat16)
    branch_second = jnp.einsum(
        "csf,fd->csd", active, shrink_weight, preferred_element_type=jnp.float32
    ) + shrink_bias.astype(jnp.float32)
    result = middle + branch_second
    output = jnp.where(row_valid, result, 0.0).astype(jnp.bfloat16)
    return {
        "normed_first": normed_first,
        "inverse_first": inverse_first,
        "lowered_first": lowered_first,
        "query_heads": query_heads,
        "key_heads": key_heads,
        "value_heads": value_heads,
        "log_total": log_total,
        "blended": blended,
        "normed_second": normed_second,
        "inverse_second": inverse_second,
        "lowered_second": lowered_second,
        "hidden": hidden,
        "active": active,
        "output": output,
    }


def gelu_exact(inputs):
    return jax.nn.gelu(inputs, approximate=False)


def backward(saved, gathered, upstream32, key_valid, row_valid):
    (
        first_gain,
        first_shift,
        inward_weight,
        query_bias,
        value_bias,
        outward_weight,
        outward_bias,
        second_gain,
        second_shift,
        expand_weight,
        expand_bias,
        shrink_weight,
        shrink_bias,
    ) = gathered
    clip_count, seg_rows, model_width = upstream32.shape
    head_size = model_width // HEADS
    scale = head_size ** (-0.5)
    grad_result = jnp.where(row_valid, upstream32, 0.0)
    grad_low_second = grad_result.astype(jnp.bfloat16)
    shrink_weight_grad = jnp.einsum(
        "csf,csd->fd", saved["active"], grad_low_second, preferred_element_type=jnp.float32
    )
    shrink_bias_grad = jnp.sum(grad_low_second.astype(jnp.float32), axis=(0, 1))
    grad_active = jnp.einsum(
        "csd,fd->csf", grad_low_second, shrink_weight, preferred_element_type=jnp.float32
    )
    gelu_value, gelu_pull = jax.vjp(gelu_exact, saved["hidden"])
    grad_hidden = gelu_pull(grad_active)[0].astype(jnp.bfloat16)
    expand_weight_grad = jnp.einsum(
        "csd,csf->df", saved["lowered_second"], grad_hidden, preferred_element_type=jnp.float32
    )
    expand_bias_grad = jnp.sum(grad_hidden.astype(jnp.float32), axis=(0, 1))
    grad_second = jnp.einsum(
        "csf,df->csd", grad_hidden, expand_weight, preferred_element_type=jnp.float32
    )
    second_gain_grad = jnp.sum(grad_second * saved["normed_second"], axis=(0, 1))
    second_shift_grad = jnp.sum(grad_second, axis=(0, 1))
    grad_middle = grad_result + norm_back(
        grad_second,
        saved["normed_second"],
        saved["inverse_second"],
        second_gain.astype(jnp.float32),
    )
    grad_low_first = grad_middle.astype(jnp.bfloat16)
    outward_weight_grad = jnp.einsum(
        "csd,cse->de", saved["blended"], grad_low_first, preferred_element_type=jnp.float32
    )
    outward_bias_grad = jnp.sum(grad_low_first.astype(jnp.float32), axis=(0, 1))
    grad_blended = jnp.einsum(
        "cse,de->csd", grad_low_first, outward_weight, preferred_element_type=jnp.float32
    )
    grad_blended = grad_blended.astype(jnp.bfloat16).reshape(clip_count, seg_rows, HEADS, head_size)
    query_heads = saved["query_heads"]
    key_heads = saved["key_heads"]
    value_heads = saved["value_heads"]
    slot_count = key_heads.shape[1]
    scores = attend_scores(query_heads, key_heads, key_valid, scale)
    soft = jnp.exp(scores - saved["log_total"])
    soft_low = soft.astype(jnp.bfloat16)
    grad_soft = jnp.einsum(
        "cqhe,ckhe->chqk", grad_blended, value_heads, preferred_element_type=jnp.float32
    )
    grad_scores = soft * (grad_soft - jnp.sum(grad_soft * soft, axis=-1, keepdims=True))
    grad_scores = grad_scores.astype(jnp.bfloat16)
    grad_queries = (
        jnp.einsum("chqk,ckhe->cqhe", grad_scores, key_heads, preferred_element_type=jnp.float32)
        * scale
    )
    grad_queries = grad_queries.astype(jnp.bfloat16).reshape(clip_count, seg_rows, model_width)
    grad_keys_part = (
        jnp.einsum("chqk,cqhe->ckhe", grad_scores, query_heads, preferred_element_type=jnp.float32)
        * scale
    )
    grad_values_part = jnp.einsum(
        "chqk,cqhe->ckhe", soft_low, grad_blended, preferred_element_type=jnp.float32
    )
    grad_keys_part = grad_keys_part.reshape(clip_count, slot_count, model_width)
    grad_values_part = grad_values_part.reshape(clip_count, slot_count, model_width)
    grad_keys, grad_values = (
        lax.psum_scatter(
            grad_keys_part.astype(jnp.bfloat16), "seq", scatter_dimension=1, tiled=True
        ).astype(jnp.float32),
        lax.psum_scatter(
            grad_values_part.astype(jnp.bfloat16), "seq", scatter_dimension=1, tiled=True
        ).astype(jnp.float32),
    )
    grad_keys = grad_keys.astype(jnp.bfloat16)
    grad_values = grad_values.astype(jnp.bfloat16)
    grad_project = jnp.concatenate([grad_queries, grad_keys, grad_values], axis=-1)
    inward_weight_grad = jnp.einsum(
        "csd,cse->de", saved["lowered_first"], grad_project, preferred_element_type=jnp.float32
    )
    query_bias_grad = jnp.sum(grad_queries.astype(jnp.float32), axis=(0, 1))
    value_bias_grad = jnp.sum(grad_values.astype(jnp.float32), axis=(0, 1))
    grad_first = jnp.einsum(
        "cse,de->csd", grad_project, inward_weight, preferred_element_type=jnp.float32
    )
    first_gain_grad = jnp.sum(grad_first * saved["normed_first"], axis=(0, 1))
    first_shift_grad = jnp.sum(grad_first, axis=(0, 1))
    tokens_grad = grad_middle + norm_back(
        grad_first, saved["normed_first"], saved["inverse_first"], first_gain.astype(jnp.float32)
    )
    weight_shares = (
        lax.psum_scatter(first_gain_grad, ("fsdp", "seq"), scatter_dimension=0, tiled=True),
        lax.psum_scatter(first_shift_grad, ("fsdp", "seq"), scatter_dimension=0, tiled=True),
        lax.psum_scatter(inward_weight_grad, ("fsdp", "seq"), scatter_dimension=0, tiled=True),
        lax.psum_scatter(query_bias_grad, ("fsdp", "seq"), scatter_dimension=0, tiled=True),
        lax.psum_scatter(value_bias_grad, ("fsdp", "seq"), scatter_dimension=0, tiled=True),
        lax.psum_scatter(outward_weight_grad, ("fsdp", "seq"), scatter_dimension=0, tiled=True),
        lax.psum_scatter(outward_bias_grad, ("fsdp", "seq"), scatter_dimension=0, tiled=True),
        lax.psum_scatter(second_gain_grad, ("fsdp", "seq"), scatter_dimension=0, tiled=True),
        lax.psum_scatter(second_shift_grad, ("fsdp", "seq"), scatter_dimension=0, tiled=True),
        lax.psum_scatter(expand_weight_grad, ("fsdp", "seq"), scatter_dimension=0, tiled=True),
        lax.psum_scatter(expand_bias_grad, ("fsdp", "seq"), scatter_dimension=0, tiled=True),
        lax.psum_scatter(shrink_weight_grad, ("fsdp", "seq"), scatter_dimension=0, tiled=True),
        lax.psum_scatter(shrink_bias_grad, ("fsdp", "seq"), scatter_dimension=0, tiled=True),
    )
    return (tokens_grad, weight_shares)


def shards(
    tokens,
    visible,
    first_gain,
    first_shift,
    inward_weight,
    query_bias,
    value_bias,
    outward_weight,
    outward_bias,
    second_gain,
    second_shift,
    expand_weight,
    expand_bias,
    shrink_weight,
    shrink_bias,
    upstream,
):
    clip_count, seg_rows, model_width = tokens.shape
    slot_count = seg_rows * lax.axis_size("seq")
    local_start = lax.axis_index("seq") * seg_rows
    row_positions = local_start + jnp.arange(seg_rows, dtype=jnp.int32)
    row_valid = (row_positions[None, :] < visible[:, None])[..., None]
    key_valid = jnp.arange(slot_count, dtype=jnp.int32)[None, :] < visible[:, None]
    tokens32 = tokens.astype(jnp.float32)
    upstream32 = upstream.astype(jnp.float32)
    gathered = gather_weights(
        first_gain,
        first_shift,
        inward_weight,
        query_bias,
        value_bias,
        outward_weight,
        outward_bias,
        second_gain,
        second_shift,
        expand_weight,
        expand_bias,
        shrink_weight,
        shrink_bias,
    )
    saved = forward(tokens32, key_valid, row_valid, gathered)
    layer_out = saved["output"]
    gathered = gather_weights(
        first_gain,
        first_shift,
        inward_weight,
        query_bias,
        value_bias,
        outward_weight,
        outward_bias,
        second_gain,
        second_shift,
        expand_weight,
        expand_bias,
        shrink_weight,
        shrink_bias,
    )
    saved = forward(tokens32, key_valid, row_valid, gathered)
    tokens_grad, shares = backward(saved, gathered, upstream32, key_valid, row_valid)
    return (
        layer_out,
        tokens_grad,
        shares[0],
        shares[1],
        shares[2],
        shares[3],
        shares[4],
        shares[5],
        shares[6],
        shares[7],
        shares[8],
        shares[9],
        shares[10],
        shares[11],
        shares[12],
    )


F32 = jnp.float32
BF16 = jnp.bfloat16
MESH = pl.DeviceIdType.MESH
SENDS, RECVS, LOCALS = 93, 137, 31
SLAB = 8


def matmul(a, b):
    return lax.dot_general(a, b, (((1,), (0,)), ((), ())), preferred_element_type=F32)


def matmul_bt(a, b):
    return lax.dot_general(a, b, (((1,), (1,)), ((), ())), preferred_element_type=F32)


def matmul_at(a, b):
    return lax.dot_general(a, b, (((0,), (0,)), ((), ())), preferred_element_type=F32)


def row_stats(x):
    mean = jnp.mean(x, axis=-1, keepdims=True)
    centered = x - mean
    inverse = lax.rsqrt(jnp.mean(centered * centered, axis=-1, keepdims=True) + epsilon)
    return centered * inverse, inverse


def row_norm_back(grad, normed, inverse, gain):
    scaled = grad * gain
    first_mean = jnp.mean(scaled, axis=-1, keepdims=True)
    second_mean = jnp.mean(scaled * normed, axis=-1, keepdims=True)
    return inverse * (scaled - first_mean - normed * second_mean)


class Place:
    def __init__(self, groups):
        self.groups = groups
        self.f = lax.axis_index("fsdp")
        self.y = lax.axis_index("seq")
        self.r = self.f // 4
        self.xc = self.f % 4
        self.t = self.xc * 2 + self.y
        x, c = self.xc // 2, self.xc % 2
        self.step = {4: 4 - 8 * x, 2: 2 - 4 * c, 1: 1 - 2 * self.y}

    def peer(self, mask):
        at = self.t
        for bit in (4, 2, 1):
            if mask & bit:
                at = at + self.step[bit]
        return at

    def device(self, r, t):
        return (r * 4 + t // 2, t % 2)


def rows(ref, index, size):
    return ref.at[pl.ds(pl.multiple_of(index * size, size), size), :]


def cols(ref, index, size):
    return ref.at[:, pl.ds(pl.multiple_of(index * size, size), size)]


class Wire:
    def __init__(self, place, send_sems, recv_sems, local_sems):
        self.place = place
        self.send_sems, self.recv_sems, self.local_sems = send_sems, recv_sems, local_sems
        self.sends = self.recvs = self.locals = 0
        self.free, self.open_sends = [], []

    def recv_slots(self, count):
        first = self.recvs
        self.recvs += count
        return [self.recv_sems.at[first + i] for i in range(count)]

    def batch(self, whole):
        spot = self.take()
        self.open_sends.append((lambda: self.describe(whole, whole, spot, self.recv_sems.at[0], self.near()), None, spot, False))
        return spot

    def near(self):
        return (self.place.r, self.place.peer(2))

    def take(self):
        if not self.free:
            self.free.append(self.sends)
            self.sends += 1
        return self.free.pop()

    def describe(self, src, dst, spot, slot, to):
        return pltpu.make_async_remote_copy(
            src_ref=src,
            dst_ref=dst,
            send_sem=self.send_sems.at[spot],
            recv_sem=slot,
            device_id=self.place.device(*to),
            device_id_type=MESH,
        )

    def send(self, src, dst, slot, to, when=None, batch=None):
        spot = self.take() if batch is None else batch

        def make():
            return self.describe(src, dst, spot, slot, to)

        if when is None:
            make().start()
        else:
            pl.when(when)(lambda: make().start())
        if batch is None:
            self.open_sends.append((make, when, spot, to[0] is not self.place.r))

    def settle(self, count=None, slab_only=False):
        count = len(self.open_sends) if count is None else count
        kept = []
        for item in self.open_sends[:count]:
            make, when, spot, far = item
            if slab_only and far:
                kept.append(item)
                continue
            if when is None:
                make().wait_send()
            else:
                pl.when(when)(lambda make=make: make().wait_send())
            self.free.append(spot)
        self.open_sends = kept + self.open_sends[count:]

    def arrived(self, dst, slot, when=None):
        def wait():
            self.describe(dst, dst, 0, slot, self.near()).wait_recv()

        if when is None:
            wait()
        else:
            pl.when(when)(wait)

    def local(self, src, dst):
        copy = pltpu.make_async_copy(src, dst, self.local_sems.at[self.locals])
        self.locals += 1
        copy.start()
        return copy


class SlabGather:
    def __init__(self, wire, at, half):
        self.wire, self.at, self.half = wire, at, half
        self.slots = wire.recv_slots(11)

    def start(self, whole, halves):
        wire, place, slots = self.wire, self.wire.place, self.slots
        t, r = place.t, place.r
        wire.send(halves[0], self.half(t, 0), slots[0], (r, place.peer(4)))
        wire.send(halves[1], self.half(t, 1), slots[3], (r, place.peer(1)))
        wire.send(halves[1], self.half(t, 1), slots[1], (r, place.peer(4)))
        wire.send(halves[0], self.half(t, 0), slots[2], (r, place.peer(1)))
        wire.send(whole, self.at(t), slots[6], (r, place.peer(2)))

    def relay(self):
        wire, place, slots = self.wire, self.wire.place, self.slots
        r, far, near = place.r, place.peer(4), place.peer(1)
        wire.arrived(self.half(far, 0), slots[0])
        wire.send(self.half(far, 0), self.half(far, 0), slots[4], (r, near))
        wire.arrived(self.half(near, 1), slots[3])
        wire.send(self.half(near, 1), self.half(near, 1), slots[5], (r, far))
        wire.arrived(self.half(far, 1), slots[1])
        wire.send(self.at(far), self.at(far), slots[7], (r, place.peer(2)))
        wire.arrived(self.half(near, 0), slots[2])
        wire.send(self.at(near), self.at(near), slots[8], (r, place.peer(2)))

    def forward(self):
        wire, place, slots = self.wire, self.wire.place, self.slots
        across = place.peer(5)
        for h in range(2):
            block = self.half(across, h)
            wire.arrived(block, slots[4 + h])
            wire.send(block, block, slots[9 + h], (place.r, place.peer(2)))

    def wait_block(self, mask):
        wire, place, slots = self.wire, self.wire.place, self.slots
        if mask == 7:
            for h in range(2):
                wire.arrived(self.half(place.peer(7), h), slots[9 + h])
        else:
            wire.arrived(self.at(place.peer(mask)), slots[{2: 6, 6: 7, 3: 8}[mask]])

    def wait(self):
        for mask in (2, 6, 3, 7):
            self.wait_block(mask)


class SlabScatter:
    def __init__(self, wire, part, core_in, chip_in, block):
        self.wire, self.part, self.core_in, self.chip_in, self.block = wire, part, core_in, chip_in, block
        self.core_slots = wire.recv_slots(4)
        self.slots = wire.recv_slots(6)
        self.order = (5, 4, 1, 0)

    def cores(self):
        place = self.wire.place
        for i, mask in enumerate(self.order):
            self.wire.send(
                rows(self.part, place.peer(mask ^ 2), self.block),
                self.core_in.at[i],
                self.core_slots[i],
                (place.r, place.peer(2)),
            )

    def half(self, mask, h):
        return rows(self.part, self.wire.place.peer(mask) * 2 + h, self.block // 2)

    def add_core(self, i):
        mask = self.order[i]
        self.wire.arrived(self.core_in.at[i], self.core_slots[i])
        mine = rows(self.part, self.wire.place.peer(mask), self.block)
        mine[...] = (mine[...].astype(F32) + self.core_in[i].astype(F32)).astype(BF16)

    def chips(self):
        wire, place = self.wire, self.wire.place
        far, near = (place.r, place.peer(4)), (place.r, place.peer(1))
        self.add_core(0)
        wire.send(self.half(5, 0), self.chip_in.at[0], self.slots[0], far)
        wire.send(self.half(5, 1), self.chip_in.at[1], self.slots[1], near)
        self.add_core(1)
        wire.send(self.half(4, 0), self.chip_in.at[2], self.slots[2], far)
        self.add_core(2)
        wire.send(self.half(1, 1), self.chip_in.at[3], self.slots[3], near)
        wire.arrived(self.core_in.at[3], self.core_slots[3])

    def relay(self):
        wire, place = self.wire, self.wire.place
        far, near = (place.r, place.peer(4)), (place.r, place.peer(1))
        for i, (block, to) in enumerate(((self.half(1, 0), near), (self.half(4, 1), far))):
            wire.arrived(self.chip_in.at[i], self.slots[i])
            block[...] = (block[...].astype(F32) + self.chip_in[i].astype(F32)).astype(BF16)
            wire.send(block, self.chip_in.at[4 + i], self.slots[4 + i], to)

    def wait(self):
        for i in range(2, 6):
            self.wire.arrived(self.chip_in.at[i], self.slots[i])

    def total(self, first, size):
        mine = self.part[pl.ds(pl.multiple_of(self.wire.place.t * self.block + first, size), size), :].astype(F32)
        mine = mine + self.core_in[3, pl.ds(pl.multiple_of(first, size), size), :].astype(F32)
        h = first // (self.block // 2)
        at = pl.ds(pl.multiple_of(first % (self.block // 2), size), size)
        return mine + self.chip_in[2 + h, at, :].astype(F32) + self.chip_in[4 + h, at, :].astype(F32)


class SlabSwap:
    def __init__(self, wire, source, target, seven):
        self.wire, self.source, self.target, self.seven = wire, source, target, seven
        (self.slot,) = wire.recv_slots(1)

    def start(self):
        place = self.wire.place
        self.own = self.wire.local(self.source(place.t), self.target(place.t))
        batch = self.wire.batch(self.seven)
        for i in (4, 5, 3, 6, 2, 7, 1):
            to = (place.t + i) % SLAB
            self.wire.send(self.source(to), self.target(place.t), self.slot, (place.r, to), batch=batch)

    def wait(self):
        self.wire.arrived(self.seven, self.slot)
        self.own.wait()


class GroupGather:
    def __init__(self, wire, at):
        self.wire, self.at = wire, at
        self.slots = wire.recv_slots(4)
        self.first = wire.recvs - 4
        r = wire.place.r
        self.inner, self.outer = (r + 1) // 2 == 1, (r + 1) // 2 != 1

    def start(self, src, dst=None):
        wire, place = self.wire, self.wire.place
        r = place.r
        dst = self.at(r) if dst is None else dst
        wire.send(src, dst, self.slots[1], ((r + 1) % 4, place.t), r != 3)
        wire.send(src, dst, self.slots[3], ((r + 3) % 4, place.t), r != 0)

    def pass_on(self):
        wire, place = self.wire, self.wire.place
        r = place.r
        below, above = (r + 3) % 4, (r + 1) % 4
        for block, slot, to in ((self.at(below), self.slots[1], above), (self.at(above), self.slots[3], below)):
            wire.arrived(block, slot, self.inner)
            wire.send(block, block, self.slots[2], (to, place.t), self.inner)

    def pass_far(self):
        wire, place = self.wire, self.wire.place
        r = place.r
        block = self.at((r + 2) % 4)
        wire.arrived(block, self.slots[2], self.inner)
        slot = wire.recv_sems.at[self.first + (2 * r + 3) % 4]
        wire.send(block, block, slot, ((3 * r + 1) % 4, place.t), self.inner)

    def wait(self):
        wire, r = self.wire, self.wire.place.r
        for i in (1, 2, 3):
            wire.arrived(self.at((r + 4 - i) % 4), self.slots[i], self.outer)


class GroupScatter:
    def __init__(self, wire, out, into, own, passing):
        self.wire, self.out, self.into, self.own, self.passing = wire, out, into, own, passing
        self.slots = wire.recv_slots(5)
        self.first = wire.recvs - 5
        r = wire.place.r

        @pl.when(r == 0)
        def _():
            into[0] = jnp.zeros_like(into[0])

        @pl.when(r == 3)
        def _():
            into[2] = jnp.zeros_like(into[2])

    def start(self, make):
        wire, place = self.wire, self.wire.place
        r, t = place.r, place.t
        inner = (r + 1) // 2 == 1
        outer = (r + 1) // 2 != 1
        low = 1 - r // 2
        pair = r + 1 - 2 * (r % 2)
        first, last = 1 + 2 * low, 3 - 2 * low
        self.out[0] = make((r + first) % 4).astype(BF16)
        wire.send(self.out.at[0], self.passing, self.slots[0], (pair, t), outer)
        wire.send(self.out.at[0], self.into.at[first - 1], wire.recv_sems.at[self.first + first], (pair, t), inner)
        self.out[1] = make((r + 2) % 4).astype(BF16)
        wire.send(self.out.at[1], self.into.at[1], self.slots[2], ((r + 2) % 4, t), outer)
        self.out[2] = make((r + last) % 4).astype(BF16)
        wire.send(
            self.out.at[2], self.into.at[last - 1], wire.recv_sems.at[self.first + last], ((r + last) % 4, t)
        )
        self.own[...] = make(r)

    def relay(self):
        wire, place = self.wire, self.wire.place
        r = place.r
        inner = (r + 1) // 2 == 1
        wire.arrived(self.passing, self.slots[0], inner)

        @pl.when(inner)
        def _():
            self.out[1] = (self.out[1].astype(F32) + self.passing[...].astype(F32)).astype(BF16)

        wire.send(self.out.at[1], self.into.at[1], self.slots[2], ((r + 2) % 4, place.t), inner)

    def total(self):
        wire, r = self.wire, self.wire.place.r
        wire.arrived(self.into.at[1], self.slots[2])
        wire.arrived(self.into.at[0], self.slots[1], r != 0)
        wire.arrived(self.into.at[2], self.slots[3], r != 3)
        total = self.own[...]
        for i in range(3):
            total = total + self.into[i].astype(F32)
        return total


def layer_kernel(
    groups,
    scale,
    tokens,
    upstream,
    visible,
    first_gain,
    first_shift,
    query_bias,
    value_bias,
    outward_bias,
    second_gain,
    second_shift,
    shrink_bias,
    expand_bias,
    w_in,
    w_out,
    w_exp,
    w_shr,
    layer_hbm,
    tokens_hbm,
    in_hbm,
    out_hbm,
    exp_hbm,
    shr_hbm,
    vec_hbm,
    layer_out,
    tokens_grad,
    out_grad,
    shr_grad,
    vec_grad,
    pack,
    small,
    wide_small,
    packs,
    tok_all,
    first_all,
    win,
    wex,
    wsh,
    wo,
    gls,
    gls_all,
    vecs,
    ebias,
    qkv,
    gqkv,
    soft_all,
    blend_t,
    blend,
    middle,
    normed,
    inverses,
    second,
    second_all,
    active,
    ghid,
    slopes,
    part_a,
    part_b,
    part_c,
    part_d,
    core_a,
    core_b,
    core_c,
    core_d,
    chip_a,
    chip_b,
    chip_c,
    chip_d,
    gsec,
    glow,
    gblend,
    gblend_t,
    sh_out,
    sh_in,
    sh_own,
    sh_pass,
    ex_out,
    ex_in,
    ex_own,
    ex_pass,
    ex_sum,
    ex_all,
    in_out,
    in_in,
    in_own,
    in_pass,
    in_sum,
    in_all,
    ou_out,
    ou_in,
    ou_own,
    ou_pass,
    gvec,
    gvec_exp,
    gvec_out,
    gvec_in,
    gvec_sum,
    gvec_far,
    send_sems,
    recv_sems,
    local_sems,
):
    place = Place(groups)
    wire = Wire(place, send_sems, recv_sems, local_sems)
    f, y, r, xc, t = place.f, place.y, place.r, place.xc, place.t
    devices = groups * SLAB
    me = r * SLAB + t
    seg, width = tokens.shape
    clips = SLAB // 2
    slots = seg * 2
    total_rows = SLAB * seg
    head2 = qkv.shape[1] // 3
    own_rows = w_in.shape[0]
    slab_rows = own_rows * 4
    share = width // devices
    chunk = wsh.shape[1]
    strip = 32
    tile = 256

    vectors = (
        first_gain,
        first_shift,
        query_bias,
        value_bias,
        outward_bias,
        second_gain,
        second_shift,
        shrink_bias,
    )
    loads = [wire.local(ref, small.at[k]) for k, ref in enumerate(vectors)]
    loads.append(wire.local(expand_bias, wide_small))
    barrier = pltpu.get_barrier_semaphore()
    for i in range(1, devices):
        to = (me + i) % devices
        pl.semaphore_signal(barrier, inc=1, device_id=place.device(to // SLAB, to % SLAB), device_id_type=MESH)
    for copy in loads:
        copy.wait()
    per_lane = 128 // own_rows
    lines = [jnp.concatenate([small[k].astype(F32)] * per_lane, axis=1) for k in range(8)]
    lines.append(wide_small[...].astype(F32))
    count_here = jnp.full((6, 128), visible[0], jnp.int32).astype(F32)
    pack[...] = jnp.concatenate(lines + [count_here], axis=0).astype(BF16)
    pl.semaphore_wait(barrier, devices - 1)

    (pack_slot,) = wire.recv_slots(1)
    pack_batch = wire.batch(packs.at[pl.ds(0, groups * 4 - 1)])
    for i in range(1, groups * 4):
        to = (f + i) % (groups * 4)
        wire.send(pack, packs.at[f], pack_slot, (to // 4, (to % 4) * 2 + y), batch=pack_batch)
    own_pack = wire.local(pack, packs.at[f])

    in_slots = wire.recv_slots(4)
    ex_slots = wire.recv_slots(4)

    def in_piece(index, c):
        return win.at[pl.ds(pl.multiple_of(index * own_rows, own_rows), own_rows), pl.ds(c * head2, head2)]

    def ex_piece(index, c):
        return wex.at[pl.ds(pl.multiple_of(index * own_rows, own_rows), own_rows), pl.ds(c * chunk, chunk)]

    own_in = []
    in_batch = wire.batch(win.at[pl.ds(0, 3 * own_rows), :])
    for i in (2, 3, 1, 0):
        to = ((xc + i) % 4) * 2 + y
        for c in range(3):
            src = w_in.at[:, pl.ds(pl.multiple_of(c * width + to * head2, head2), head2)]
            if i == 0:
                own_in.append(wire.local(src, in_piece(f, c)))
            else:
                wire.send(src, in_piece(f, c), in_slots[i], (r, to), batch=in_batch)

    out_share = w_out.at[pl.ds(pl.multiple_of(y * share, share), share), :]
    own_out = wire.local(out_share, wo.at[r, t])
    group_wo = GroupGather(wire, lambda at: wo.at[at, t])
    group_wo.start(out_share)
    shr_share = w_shr.at[pl.ds(pl.multiple_of(y * chunk, chunk), chunk), :]
    own_shr = wire.local(shr_share, wsh.at[r])
    group_sh = GroupGather(wire, lambda at: wsh.at[at])

    def shr_half(h):
        at = pl.ds(h * (chunk // 2), chunk // 2)
        src = w_shr.at[pl.ds(pl.multiple_of(y * chunk + h * (chunk // 2), chunk // 2), chunk // 2), :]
        group_sh.start(src, wsh.at[r, at])

    shr_half(0)

    def slab_gather(ref):
        return SlabGather(wire, lambda at: rows(ref, at, seg), lambda at, h: rows(ref, at * 2 + h, seg // 2))

    gather_tok = slab_gather(tok_all)
    gather_tok.start(tokens, [rows(tokens, h, seg // 2) for h in range(2)])

    own_ex = []
    ex_batch = wire.batch(wex.at[pl.ds(0, 3 * own_rows), :])
    for i in (2, 3, 1, 0):
        to = ((xc + i) % 4) * 2 + y
        for c in range(groups):
            src = w_exp.at[:, pl.ds(pl.multiple_of((c * SLAB + to) * chunk, chunk), chunk)]
            if i == 0:
                own_ex.append(wire.local(src, ex_piece(f, c)))
            else:
                wire.send(src, ex_piece(f, c), ex_slots[i], (r, to), batch=ex_batch)

    row_at = y * seg + lax.broadcasted_iota(jnp.int32, (seg, 1), 0)
    row_valid = row_at.astype(F32) < pack[10:11, 0:1].astype(F32)
    gls[...] = jnp.where(row_valid, upstream[...].astype(F32), 0.0).astype(BF16)
    gls_all[pl.ds(pl.multiple_of(t * seg, seg), seg), :] = gls[...]
    gvec[...] = jnp.zeros_like(gvec)
    gvec_exp[...] = jnp.zeros_like(gvec_exp)
    group_shr = GroupScatter(wire, sh_out, sh_in, sh_own, sh_pass)
    group_exp = GroupScatter(wire, ex_out, ex_in, ex_own, ex_pass)
    group_inw = GroupScatter(wire, in_out, in_in, in_own, in_pass)
    group_out = GroupScatter(wire, ou_out, ou_in, ou_own, ou_pass)

    for i in range(1, 4):
        frm = r * 4 + (xc + 4 - i) % 4
        wire.arrived(rows(win, frm, own_rows), in_slots[i])
    for copy in own_in:
        copy.wait()
    own_out.wait()
    group_wo.pass_on()
    group_in = GroupGather(wire, lambda at: rows(win, at, slab_rows))
    group_in.start(rows(win, r, slab_rows))
    shr_half(1)
    group_wo.pass_far()

    own_pack.wait()
    wire.arrived(packs.at[pl.ds(0, groups * 4 - 1)], pack_slot)
    lane = lax.broadcasted_iota(jnp.int32, (1, 128), 1)
    for j in range(width // 128):
        piece = packs[j * per_lane].astype(F32)
        for k in range(1, per_lane):
            piece = jnp.where(lane >= k * own_rows, packs[j * per_lane + k].astype(F32), piece)
        vecs[:, j * 128 : (j + 1) * 128] = piece
    for c in range(groups):
        both = packs[c * 4 + t // 2].astype(F32)
        ebias[0:1, c * chunk : (c + 1) * chunk] = jnp.where(y == 0, both[8:9], both[9:10])

    def first_norm(src, offset, block):
        def strip_norm(i, carry):
            at = pl.multiple_of(i * strip, strip)
            n, _ = row_stats(src[pl.ds(offset + at, strip), :].astype(F32))
            to = pl.multiple_of(block * seg + at, strip)
            first_all[pl.ds(to, strip), :] = (n * vecs[0:1, :] + vecs[1:2, :]).astype(BF16)
            return carry

        lax.fori_loop(0, seg // strip, strip_norm, 0)

    first_norm(tokens, 0, t)

    def norm_block(mask):
        block = place.peer(mask)
        first_norm(tok_all, pl.multiple_of(block * seg, seg), block)

    gather_tok.relay()
    group_wo.wait()
    gather_wo = SlabGather(wire, lambda at: wo.at[:, at], lambda at, h: wo.at[pl.ds(h * (groups // 2), groups // 2), at])
    gather_wo.start(wo.at[:, t], [wo.at[pl.ds(h * (groups // 2), groups // 2), t] for h in range(2)])
    group_in.pass_on()
    norm_block(4)
    norm_block(1)

    gather_tok.forward()

    norm_block(5)
    group_in.pass_far()
    for i in range(1, 4):
        frm = r * 4 + (xc + 4 - i) % 4
        wire.arrived(rows(wex, frm, own_rows), ex_slots[i])
    for copy in own_ex:
        copy.wait()
    group_ex = GroupGather(wire, lambda at: rows(wex, at, slab_rows))
    group_ex.start(rows(wex, r, slab_rows))


    for mask in (2, 6, 3, 7):
        gather_tok.wait_block(mask)
        norm_block(mask)

    gather_wo.relay()
    gather_gls = slab_gather(gls_all)
    gather_gls.start(gls, [rows(gls, h, seg // 2) for h in range(2)])
    group_in.wait()
    at_head = pl.ds(pl.multiple_of(t * head2, head2), head2)
    bias = jnp.concatenate([vecs[2:3, at_head], jnp.zeros((1, head2), F32), vecs[3:4, at_head]], axis=1)

    def project(i, carry):
        at = pl.ds(pl.multiple_of(i * tile, tile), tile)
        qkv[at, :] = (matmul(first_all[at, :], win[...]) + bias).astype(BF16)
        return carry

    lax.fori_loop(0, total_rows // tile, project, 0)

    head_size = head2 // 2
    low_half = lane < head_size
    half_masks = [low_half.astype(F32).astype(BF16), (1.0 - low_half.astype(F32)).astype(BF16)]
    key_at = lax.broadcasted_iota(jnp.int32, (1, slots), 1).astype(F32)

    def attend(i, carry):
        at = pl.ds(pl.multiple_of(i * slots, slots), slots)
        q = qkv[at, 0:head2]
        k = qkv[at, head2 : 2 * head2]
        v = qkv[at, 2 * head2 : 3 * head2]
        count = packs[r * 4 + i].astype(F32)[10:11, 0:1]
        key_valid = key_at < count
        halves = []
        for h in range(2):
            scores = matmul_bt(q * half_masks[h], k) * scale
            scores = jnp.where(key_valid, scores, -1e30)
            top = jnp.max(scores, axis=-1, keepdims=True)
            log_total = top + jnp.log(jnp.sum(jnp.exp(scores - top), axis=-1, keepdims=True))
            soft = jnp.exp(scores - log_total)
            soft_all[i * 2 + h] = soft
            halves.append(matmul(soft.astype(BF16), v))
        blend_t[at, :] = jnp.where(low_half, halves[0], halves[1]).astype(BF16)
        return carry

    lax.fori_loop(0, clips, attend, 0)

    group_ex.pass_on()
    swap_blend = SlabSwap(wire, lambda at: rows(blend_t, at, seg), lambda at: cols(blend, at, head2), blend.at[:, 0 : 7 * head2])
    swap_blend.start()
    gather_wo.forward()

    gather_gls.relay()
    gather_wo.wait()
    swap_blend.wait()
    group_ex.pass_far()
    wide = 256
    for j in range(width // wide):
        at = slice(j * wide, (j + 1) * wide)
        product = matmul(blend[...], wo[:, :, :, at].reshape(width, wide))
        middle[:, at] = tokens[:, at].astype(F32) + (product + vecs[4:5, at])

    own_second_rows = pl.multiple_of(t * seg, seg)

    def second_norm(i, carry):
        at = pl.ds(pl.multiple_of(i * strip, strip), strip)
        n, inverse = row_stats(middle[at, :])
        normed[at, :] = n
        inverses[at, :] = jnp.broadcast_to(inverse, (strip, 128))
        low = (n * vecs[5:6, :] + vecs[6:7, :]).astype(BF16)
        second[at, :] = low
        second_all[pl.ds(pl.multiple_of(own_second_rows + i * strip, strip), strip), :] = low
        return carry

    lax.fori_loop(0, seg // strip, second_norm, 0)

    gather_second = slab_gather(second_all)
    gather_second.start(second, [rows(second, h, seg // 2) for h in range(2)])
    group_sh.pass_on()
    gather_gls.forward()
    gather_second.relay()
    group_sh.pass_far()
    gather_second.forward()
    gather_gls.wait()
    gather_second.wait()
    group_ex.wait()
    front_sends = len(wire.open_sends)

    hidden_units = groups * chunk

    def feed(i, carry):
        at = pl.ds(pl.multiple_of(i * tile, tile), tile)
        hidden = matmul(second_all[at, :], wex[...]) + ebias[0:1, :]
        cdf = 0.5 * (1.0 + lax.erf(hidden * 0.7071067811865476))
        active[at, :] = (hidden * cdf).astype(BF16)
        slopes[at, :] = cdf + hidden * (0.3989422804014327 * jnp.exp(-0.5 * hidden * hidden))
        return carry

    lax.fori_loop(0, total_rows // tile, feed, 0)
    group_shr.start(
        lambda c: matmul_at(active[:, pl.ds(pl.multiple_of(c * chunk, chunk), chunk)], gls_all[...])
    )
    group_sh.wait()
    own_shr.wait()

    def feed_back(i, carry):
        at = pl.ds(pl.multiple_of(i * tile, tile), tile)
        grad_active = matmul_bt(gls_all[at, :], wsh[...].reshape(hidden_units, width))
        grad_hidden = (grad_active * slopes[at, :]).astype(BF16)
        ghid[at, :] = grad_hidden
        gvec_exp[...] += jnp.sum(grad_hidden.astype(F32), axis=0, keepdims=True)
        part_a[at, :] = matmul_bt(grad_hidden, wex[...]).astype(BF16)
        return carry

    core = xc % 2
    scatter_second = SlabScatter(wire, part_a, core_a, chip_a, seg)
    lax.fori_loop(0, 2, lambda k, carry: feed_back(1 - core + 2 * k, carry), 0)
    scatter_second.cores()
    lax.fori_loop(0, 2, lambda k, carry: feed_back(core + 2 * k, carry), 0)

    scatter_second.chips()
    group_exp.start(
        lambda c: matmul_at(second_all[:, pl.ds(pl.multiple_of(c * slab_rows, slab_rows), slab_rows)], ghid[...])
    )
    scatter_second.relay()
    group_shr.relay()

    def feed_out(i, carry):
        at = pl.ds(pl.multiple_of(i * tile, tile), tile)
        part_b[at, :] = matmul(active[at, :], wsh[...].reshape(hidden_units, width)).astype(BF16)
        return carry

    lax.fori_loop(0, total_rows // tile, feed_out, 0)
    scatter_result = SlabScatter(wire, part_b, core_b, chip_b, seg)
    scatter_result.cores()

    scatter_second.wait()
    wire.settle(front_sends)

    feed_sends = len(wire.open_sends)

    def second_back(i, carry):
        first = i * strip
        at = pl.ds(pl.multiple_of(first, strip), strip)
        grad = scatter_second.total(first, strip)
        n = normed[at, :]
        back = row_norm_back(grad, n, inverses[at, 0:1], vecs[5:6, :])
        grad_result = gls[at, :].astype(F32)
        grad_middle = grad_result + back
        gsec[at, :] = grad_middle
        low = grad_middle.astype(BF16)
        glow[at, :] = low
        gvec[4:5, :] += jnp.sum(low.astype(F32), axis=0, keepdims=True)
        gvec[5:6, :] += jnp.sum(grad * n, axis=0, keepdims=True)
        gvec[6:7, :] += jnp.sum(grad, axis=0, keepdims=True)
        gvec[7:8, :] += jnp.sum(grad_result, axis=0, keepdims=True)
        return carry

    lax.fori_loop(0, seg // strip, second_back, 0)

    for j in range(width // wide):
        rows_of = slice(j * (groups * wide // width), (j + 1) * (groups * wide // width))
        gblend[:, j * wide : (j + 1) * wide] = matmul_bt(
            glow[...], wo[rows_of].reshape(wide, width)
        ).astype(BF16)
    swap_gblend = SlabSwap(wire, lambda at: cols(gblend, at, head2), lambda at: rows(gblend_t, at, seg), gblend_t.at[pl.ds(0, 7 * seg), :])
    swap_gblend.start()

    for c in range(groups):
        product = matmul_at(blend[:, c * slab_rows : (c + 1) * slab_rows], glow[...])
        for to in range(SLAB):
            part_d[to * seg + c * share : to * seg + (c + 1) * share, :] = product[
                to * share : (to + 1) * share
            ].astype(BF16)
    scatter_out = SlabScatter(wire, part_d, core_d, chip_d, seg)
    scatter_out.cores()

    scatter_out.chips()
    swap_gblend.wait()

    def attend_back(i, carry):
        at = pl.ds(pl.multiple_of(i * slots, slots), slots)
        q = qkv[at, 0:head2]
        k = qkv[at, head2 : 2 * head2]
        v = qkv[at, 2 * head2 : 3 * head2]
        grad = gblend_t[at, :]
        parts = []
        for h in range(2):
            soft = soft_all[i * 2 + h]
            grad_soft = matmul_bt(grad * half_masks[h], v)
            inner = jnp.sum(grad_soft * soft, axis=-1, keepdims=True)
            grad_scores = (soft * (grad_soft - inner)).astype(BF16)
            parts.append(
                (
                    matmul(grad_scores, k) * scale,
                    matmul_at(grad_scores, q) * scale,
                    matmul_at(soft.astype(BF16), grad),
                )
            )
        for c in range(3):
            gqkv[at, c * head2 : (c + 1) * head2] = jnp.where(low_half, parts[0][c], parts[1][c]).astype(BF16)
        return carry

    lax.fori_loop(0, clips, attend_back, 0)

    scatter_out.relay()
    group_exp.relay()
    def project_back(i, carry):
        at = pl.ds(pl.multiple_of(i * tile, tile), tile)
        part_c[at, :] = matmul_bt(gqkv[at, :], win[...]).astype(BF16)
        return carry

    scatter_first = SlabScatter(wire, part_c, core_c, chip_c, seg)
    lax.fori_loop(0, 2, lambda k, carry: project_back(1 - core + 2 * k, carry), 0)
    scatter_first.cores()
    lax.fori_loop(0, 2, lambda k, carry: project_back(core + 2 * k, carry), 0)

    group_inw.start(
        lambda c: matmul_at(first_all[:, pl.ds(pl.multiple_of(c * slab_rows, slab_rows), slab_rows)], gqkv[...])
    )
    scatter_first.chips()
    gvec[2:3, at_head] = jnp.sum(gqkv[:, 0:head2].astype(F32), axis=0, keepdims=True)
    gvec[3:4, at_head] = jnp.sum(gqkv[:, 2 * head2 :].astype(F32), axis=0, keepdims=True)

    scatter_out.wait()
    group_out.start(lambda c: scatter_out.total(c * share, share))
    scatter_first.relay()
    scatter_result.chips()
    scatter_first.wait()
    wire.settle(feed_sends, slab_only=True)

    group_inw.relay()
    def first_back(i, carry):
        first = i * strip
        at = pl.ds(pl.multiple_of(first, strip), strip)
        grad = scatter_first.total(first, strip)
        n, inverse = row_stats(tokens[at, :].astype(F32))
        tokens_grad[at, :] = gsec[at, :] + row_norm_back(grad, n, inverse, vecs[0:1, :])
        gvec[0:1, :] += jnp.sum(grad * n, axis=0, keepdims=True)
        gvec[1:2, :] += jnp.sum(grad, axis=0, keepdims=True)
        return carry

    lax.fori_loop(0, seg // strip, first_back, 0)
    stores = [wire.local(tokens_grad, tokens_hbm)]

    for to in range(SLAB):
        gvec_out[to] = jnp.concatenate(
            [gvec[:, (c * SLAB + to) * share : (c * SLAB + to + 1) * share] for c in range(groups)], axis=1
        )
    swap_vec = SlabSwap(wire, lambda at: gvec_out.at[at], lambda at: gvec_in.at[at], gvec_in.at[pl.ds(0, 7)])
    swap_vec.start()

    scatter_result.relay()
    swap_vec.wait()
    summed = gvec_in[0]
    for i in range(1, SLAB):
        summed = summed + gvec_in[i]
    gvec_sum[0:8] = summed
    for c in range(groups):
        gvec_sum[8 + c : 9 + c] = gvec_exp[0:1, c * chunk : (c + 1) * chunk]
    gvec_sum[8 + groups : 16] = jnp.zeros((8 - groups, 128), F32)
    vec_slots = wire.recv_slots(groups - 1)
    for i in range(1, groups):
        wire.send(gvec_sum, gvec_far.at[i - 1], vec_slots[i - 1], ((r + i) % groups, t))
    scatter_result.wait()

    def finish_out(i, carry):
        first = i * strip
        at = pl.ds(pl.multiple_of(first, strip), strip)
        result = middle[at, :] + (scatter_result.total(first, strip) + vecs[7:8, :])
        spot = y * seg + first + lax.broadcasted_iota(jnp.int32, (strip, 1), 0)
        valid = spot.astype(F32) < pack[10:11, 0:1].astype(F32)
        layer_out[at, :] = jnp.where(valid, result, 0.0).astype(BF16)
        return carry

    lax.fori_loop(0, seg // strip, finish_out, 0)
    stores.append(wire.local(layer_out, layer_hbm))

    group_out.relay()
    ex_sum[...] = group_exp.total().astype(BF16)
    swap_exp = SlabSwap(wire, lambda at: rows(ex_sum, at, share), lambda at: ex_all.at[at], ex_all.at[pl.ds(0, 7)])
    swap_exp.start()
    shr_grad[...] = group_shr.total()
    stores.append(wire.local(shr_grad, shr_hbm))
    in_sum[...] = group_inw.total().astype(BF16)
    swap_in = SlabSwap(wire, lambda at: rows(in_sum, at, share), lambda at: in_all.at[at], in_all.at[pl.ds(0, 7)])
    swap_in.start()
    out_grad[...] = group_out.total()
    stores.append(wire.local(out_grad, out_hbm))
    for i in range(1, groups):
        wire.arrived(gvec_far.at[i - 1], vec_slots[i - 1])
    total = gvec_sum[...]
    for i in range(1, groups):
        total = total + gvec_far[i - 1]
    vec_grad[0:8, :] = pltpu.roll(total[0:8], (128 - share * r) % 128, 1)
    line = total[8:9]
    for c in range(1, groups):
        line = jnp.where(r == c, total[8 + c : 9 + c], line)
    vec_grad[8:16, :] = jnp.broadcast_to(line, (8, 128))
    stores.append(wire.local(vec_grad, vec_hbm))
    swap_exp.wait()
    stores.append(wire.local(ex_all, exp_hbm))
    swap_in.wait()
    stores.append(wire.local(in_all, in_hbm))
    for copy in stores:
        copy.wait()
    wire.settle()
    assert (wire.sends, wire.recvs, wire.locals) == (SENDS, RECVS, LOCALS), (wire.sends, wire.recvs, wire.locals)


def output_kernel(
    groups,
    layer_in,
    tokens_in,
    in_pieces,
    out_in,
    exp_pieces,
    shr_in,
    vec_in,
    layer_out,
    tokens_grad,
    first_gain_grad,
    first_shift_grad,
    in_grad,
    query_bias_grad,
    value_bias_grad,
    out_grad,
    outward_bias_grad,
    second_gain_grad,
    second_shift_grad,
    exp_grad,
    expand_bias_grad,
    shr_grad,
    shrink_bias_grad,
    layer_buf,
    tokens_buf,
    in_buf,
    out_buf,
    exp_buf,
    shr_buf,
    vec_buf,
    in_wide,
    exp_wide,
    lines,
    wide_line,
    load_sems,
    store_sems,
):
    share, width = out_buf.shape
    head2, chunk = in_buf.shape[2] // 3, exp_buf.shape[2] // groups
    loads = [
        pltpu.make_async_copy(src, dst, load_sems.at[i])
        for i, (src, dst) in enumerate(
            (
                (vec_in, vec_buf),
                (exp_pieces, exp_buf),
                (in_pieces, in_buf),
                (shr_in, shr_buf),
                (tokens_in, tokens_buf),
                (layer_in, layer_buf),
                (out_in, out_buf),
            )
        )
    ]
    for copy in loads:
        copy.start()
    stores = []

    def store(src, dst):
        stores.append(pltpu.make_async_copy(src, dst, store_sems.at[len(stores)]))
        stores[-1].start()

    loads[0].wait()
    vectors = (
        first_gain_grad,
        first_shift_grad,
        query_bias_grad,
        value_bias_grad,
        outward_bias_grad,
        second_gain_grad,
        second_shift_grad,
        shrink_bias_grad,
    )
    for k, ref in enumerate(vectors):
        lines[k] = vec_buf[k, 0:share]
        store(lines.at[k], ref)
    wide_line[...] = vec_buf[8, :]
    store(wide_line, expand_bias_grad)
    loads[1].wait()
    for frm in range(SLAB):
        for c in range(groups):
            at = (c * SLAB + frm) * chunk
            exp_wide[:, at : at + chunk] = exp_buf[frm, :, c * chunk : (c + 1) * chunk].astype(F32)
    store(exp_wide, exp_grad)
    loads[2].wait()
    for frm in range(SLAB):
        for c in range(3):
            at = c * width + frm * head2
            in_wide[:, at : at + head2] = in_buf[frm, :, c * head2 : (c + 1) * head2].astype(F32)
    store(in_wide, in_grad)
    for copy, src, dst in (
        (loads[3], shr_buf, shr_grad),
        (loads[4], tokens_buf, tokens_grad.at[0]),
        (loads[5], layer_buf, layer_out.at[0]),
        (loads[6], out_buf, out_grad),
    ):
        copy.wait()
        store(src, dst)
    for copy in stores:
        copy.wait()


def fused_shards(
    tokens,
    visible,
    first_gain,
    first_shift,
    inward_weight,
    query_bias,
    value_bias,
    outward_weight,
    outward_bias,
    second_gain,
    second_shift,
    expand_weight,
    expand_bias,
    shrink_weight,
    shrink_bias,
    upstream,
):
    seg, width = tokens.shape[1:]
    groups = lax.axis_size("fsdp") // 4
    devices = groups * SLAB
    own_rows = inward_weight.shape[0]
    hidden = expand_weight.shape[1]
    share = width // devices
    chunk = hidden // devices
    units = groups * chunk
    head2 = width // SLAB
    scale = (width // HEADS) ** (-0.5)
    total_rows = SLAB * seg
    slab_rows = 4 * own_rows
    vmem = pl.BlockSpec(memory_space=pltpu.VMEM)
    anywhere = pl.BlockSpec(memory_space=pl.ANY)
    outs = pl.pallas_call(
        functools.partial(layer_kernel, groups, scale),
        out_shape=(
            jax.ShapeDtypeStruct((seg, width), BF16),
            jax.ShapeDtypeStruct((seg, width), F32),
            jax.ShapeDtypeStruct((SLAB, share, 3 * head2), BF16),
            jax.ShapeDtypeStruct((share, width), F32),
            jax.ShapeDtypeStruct((SLAB, share, units), BF16),
            jax.ShapeDtypeStruct((chunk, width), F32),
            jax.ShapeDtypeStruct((16, 128), F32),
        ),
        in_specs=[vmem, vmem, pl.BlockSpec(memory_space=pltpu.SMEM)] + [anywhere] * 13,
        out_specs=[anywhere] * 7,
        scratch_shapes=[
            pltpu.VMEM((seg, width), BF16),
            pltpu.VMEM((seg, width), F32),
            pltpu.VMEM((share, width), F32),
            pltpu.VMEM((chunk, width), F32),
            pltpu.VMEM((16, 128), F32),
            pltpu.VMEM((16, 128), BF16),
            pltpu.VMEM((8, 1, own_rows), BF16),
            pltpu.VMEM((2, 128), BF16),
            pltpu.VMEM((groups * 4, 16, 128), BF16),
            pltpu.VMEM((total_rows, width), BF16),
            pltpu.VMEM((total_rows, width), BF16),
            pltpu.VMEM((width, 3 * head2), BF16),
            pltpu.VMEM((width, units), BF16),
            pltpu.VMEM((groups, chunk, width), BF16),
            pltpu.VMEM((groups, SLAB, share, width), BF16),
            pltpu.VMEM((seg, width), BF16),
            pltpu.VMEM((total_rows, width), BF16),
            pltpu.VMEM((16, width), F32),
            pltpu.VMEM((8, units), F32),
            pltpu.VMEM((total_rows, 3 * head2), BF16),
            pltpu.VMEM((total_rows, 3 * head2), BF16),
            pltpu.VMEM((SLAB, 2 * seg, 2 * seg), F32),
            pltpu.VMEM((total_rows, head2), BF16),
            pltpu.VMEM((seg, width), BF16),
            pltpu.VMEM((seg, width), F32),
            pltpu.VMEM((seg, width), F32),
            pltpu.VMEM((seg, 128), F32),
            pltpu.VMEM((seg, width), BF16),
            pltpu.VMEM((total_rows, width), BF16),
            pltpu.VMEM((total_rows, units), BF16),
            pltpu.VMEM((total_rows, units), BF16),
            pltpu.VMEM((total_rows, units), F32),
        ]
        + [pltpu.VMEM((total_rows, width), BF16)] * 4
        + [pltpu.VMEM((4, seg, width), BF16)] * 4
        + [pltpu.VMEM((6, seg // 2, width), BF16)] * 4
        + [
            pltpu.VMEM((seg, width), F32),
            pltpu.VMEM((seg, width), BF16),
            pltpu.VMEM((seg, width), BF16),
            pltpu.VMEM((total_rows, head2), BF16),
            pltpu.VMEM((groups - 1, chunk, width), BF16),
            pltpu.VMEM((groups - 1, chunk, width), BF16),
            pltpu.VMEM((chunk, width), F32),
            pltpu.VMEM((chunk, width), BF16),
            pltpu.VMEM((groups - 1, slab_rows, units), BF16),
            pltpu.VMEM((groups - 1, slab_rows, units), BF16),
            pltpu.VMEM((slab_rows, units), F32),
            pltpu.VMEM((slab_rows, units), BF16),
            pltpu.VMEM((slab_rows, units), BF16),
            pltpu.VMEM((SLAB, share, units), BF16),
            pltpu.VMEM((groups - 1, slab_rows, 3 * head2), BF16),
            pltpu.VMEM((groups - 1, slab_rows, 3 * head2), BF16),
            pltpu.VMEM((slab_rows, 3 * head2), F32),
            pltpu.VMEM((slab_rows, 3 * head2), BF16),
            pltpu.VMEM((slab_rows, 3 * head2), BF16),
            pltpu.VMEM((SLAB, share, 3 * head2), BF16),
            pltpu.VMEM((groups - 1, share, width), BF16),
            pltpu.VMEM((groups - 1, share, width), BF16),
            pltpu.VMEM((share, width), F32),
            pltpu.VMEM((share, width), BF16),
            pltpu.VMEM((8, width), F32),
            pltpu.VMEM((1, units), F32),
            pltpu.VMEM((SLAB, 8, 128), F32),
            pltpu.VMEM((SLAB, 8, 128), F32),
            pltpu.VMEM((16, 128), F32),
            pltpu.VMEM((groups - 1, 16, 128), F32),
            pltpu.SemaphoreType.DMA((SENDS,)),
            pltpu.SemaphoreType.DMA((RECVS,)),
            pltpu.SemaphoreType.DMA((LOCALS,)),
        ],
        compiler_params=pltpu.CompilerParams(
            collective_id=0, has_side_effects=True, vmem_limit_bytes=67043328
        ),
        name="layer",
    )(
        tokens.reshape(seg, width),
        upstream.reshape(seg, width),
        visible,
        *(
            vector.reshape(1, own_rows)
            for vector in (
                first_gain,
                first_shift,
                query_bias,
                value_bias,
                outward_bias,
                second_gain,
                second_shift,
                shrink_bias,
            )
        ),
        expand_bias.reshape(2, 128),
        inward_weight,
        outward_weight,
        expand_weight,
        shrink_weight,
    )
    vector = jax.ShapeDtypeStruct((share,), F32)
    return pl.pallas_call(
        functools.partial(output_kernel, groups),
        out_shape=(
            jax.ShapeDtypeStruct((1, seg, width), BF16),
            jax.ShapeDtypeStruct((1, seg, width), F32),
            vector,
            vector,
            jax.ShapeDtypeStruct((share, 3 * width), F32),
            vector,
            vector,
            jax.ShapeDtypeStruct((share, width), F32),
            vector,
            vector,
            vector,
            jax.ShapeDtypeStruct((share, hidden), F32),
            jax.ShapeDtypeStruct((chunk,), F32),
            jax.ShapeDtypeStruct((chunk, width), F32),
            vector,
        ),
        in_specs=[anywhere] * 7,
        out_specs=[anywhere] * 15,
        scratch_shapes=[
            pltpu.VMEM((seg, width), BF16),
            pltpu.VMEM((seg, width), F32),
            pltpu.VMEM((SLAB, share, 3 * head2), BF16),
            pltpu.VMEM((share, width), F32),
            pltpu.VMEM((SLAB, share, units), BF16),
            pltpu.VMEM((chunk, width), F32),
            pltpu.VMEM((16, 128), F32),
            pltpu.VMEM((share, 3 * width), F32),
            pltpu.VMEM((share, hidden), F32),
            pltpu.VMEM((8, share), F32),
            pltpu.VMEM((chunk,), F32),
            pltpu.SemaphoreType.DMA((7,)),
            pltpu.SemaphoreType.DMA((15,)),
        ],
        name="outputs",
    )(*outs)


def fits_fused(mesh, tokens, inward_weight, expand_weight):
    fsdp, seq = mesh.shape["fsdp"], mesh.shape["seq"]
    clips, slots, width = tokens.shape
    devices = fsdp * seq
    return (
        seq == 2
        and clips == fsdp
        and fsdp == 16
        and width // HEADS * 2 == 128
        and width == SLAB * 128
        and slots % 64 == 0
        and width % (16 * devices) == 0
        and 128 % (width // fsdp) == 0
        and width // devices * 4 == 128
        and expand_weight.shape[1] == 128 * devices
    )


def solution(mesh):
    in_specs = (
        P("fsdp", "seq", None),
        P("fsdp"),
        P("fsdp"),
        P("fsdp"),
        P("fsdp", None),
        P("fsdp"),
        P("fsdp"),
        P("fsdp", None),
        P("fsdp"),
        P("fsdp"),
        P("fsdp"),
        P("fsdp", None),
        P("fsdp"),
        P("fsdp", None),
        P("fsdp"),
        P("fsdp", "seq", None),
    )
    out_specs = (
        P("fsdp", "seq", None),
        P("fsdp", "seq", None),
        P(("fsdp", "seq")),
        P(("fsdp", "seq")),
        P(("fsdp", "seq"), None),
        P(("fsdp", "seq")),
        P(("fsdp", "seq")),
        P(("fsdp", "seq"), None),
        P(("fsdp", "seq")),
        P(("fsdp", "seq")),
        P(("fsdp", "seq")),
        P(("fsdp", "seq"), None),
        P(("fsdp", "seq")),
        P(("fsdp", "seq"), None),
        P(("fsdp", "seq")),
    )

    def step(*args):
        body = fused_shards if fits_fused(mesh, args[0], args[4], args[11]) else shards
        return jax.shard_map(body, mesh=mesh, in_specs=in_specs, out_specs=out_specs, check_vma=False)(*args)

    return step
```

```python
import functools

import jax
import jax.numpy as jnp
from jax import lax
from jax.experimental import pallas as pl
from jax.experimental.pallas import tpu as pltpu
from jax.sharding import PartitionSpec as P

HEADS = 16


epsilon = 1e-06


def norm_rows(inputs, norm_gain, norm_shift):
    row_mean = jnp.mean(inputs, axis=-1, keepdims=True)
    centered = inputs - row_mean
    variance = jnp.mean(centered * centered, axis=-1, keepdims=True)
    inverse = lax.rsqrt(variance + epsilon)
    normed = centered * inverse
    return (normed * norm_gain + norm_shift, normed, inverse)


def norm_back(grad_out, normed, inverse, norm_gain):
    scaled = grad_out * norm_gain
    first_mean = jnp.mean(scaled, axis=-1, keepdims=True)
    second_mean = jnp.mean(scaled * normed, axis=-1, keepdims=True)
    return inverse * (scaled - first_mean - normed * second_mean)


def gather_weights(
    first_gain,
    first_shift,
    inward_weight,
    query_bias,
    value_bias,
    outward_weight,
    outward_bias,
    second_gain,
    second_shift,
    expand_weight,
    expand_bias,
    shrink_weight,
    shrink_bias,
):
    return (
        lax.all_gather(first_gain, "fsdp", axis=0, tiled=True),
        lax.all_gather(first_shift, "fsdp", axis=0, tiled=True),
        lax.all_gather(inward_weight, "fsdp", axis=0, tiled=True),
        lax.all_gather(query_bias, "fsdp", axis=0, tiled=True),
        lax.all_gather(value_bias, "fsdp", axis=0, tiled=True),
        lax.all_gather(outward_weight, "fsdp", axis=0, tiled=True),
        lax.all_gather(outward_bias, "fsdp", axis=0, tiled=True),
        lax.all_gather(second_gain, "fsdp", axis=0, tiled=True),
        lax.all_gather(second_shift, "fsdp", axis=0, tiled=True),
        lax.all_gather(expand_weight, "fsdp", axis=0, tiled=True),
        lax.all_gather(expand_bias, "fsdp", axis=0, tiled=True),
        lax.all_gather(shrink_weight, "fsdp", axis=0, tiled=True),
        lax.all_gather(shrink_bias, "fsdp", axis=0, tiled=True),
    )


def attend_scores(query_heads, key_heads, key_valid, scale):
    scores = (
        jnp.einsum("cqhe,ckhe->chqk", query_heads, key_heads, preferred_element_type=jnp.float32)
        * scale
    )
    return jnp.where(key_valid[:, None, None, :], scores, -1e30)


def forward(tokens32, key_valid, row_valid, gathered):
    (
        first_gain,
        first_shift,
        inward_weight,
        query_bias,
        value_bias,
        outward_weight,
        outward_bias,
        second_gain,
        second_shift,
        expand_weight,
        expand_bias,
        shrink_weight,
        shrink_bias,
    ) = gathered
    clip_count, seg_rows, model_width = tokens32.shape
    head_size = model_width // HEADS
    scale = head_size ** (-0.5)
    affine_first, normed_first, inverse_first = norm_rows(
        tokens32, first_gain.astype(jnp.float32), first_shift.astype(jnp.float32)
    )
    lowered_first = affine_first.astype(jnp.bfloat16)
    merged_bias = jnp.concatenate([query_bias, jnp.zeros_like(query_bias), value_bias]).astype(
        jnp.float32
    )
    project = (
        jnp.einsum("csd,de->cse", lowered_first, inward_weight, preferred_element_type=jnp.float32)
        + merged_bias
    )
    queries = project[..., :model_width].astype(jnp.bfloat16)
    key_local = project[..., model_width : 2 * model_width].astype(jnp.bfloat16)
    value_local = project[..., 2 * model_width :].astype(jnp.bfloat16)
    key_all, value_all = (
        lax.all_gather(key_local, "seq", axis=1, tiled=True),
        lax.all_gather(value_local, "seq", axis=1, tiled=True),
    )
    slot_count = key_all.shape[1]
    query_heads = queries.reshape(clip_count, seg_rows, HEADS, head_size)
    key_heads = key_all.reshape(clip_count, slot_count, HEADS, head_size)
    value_heads = value_all.reshape(clip_count, slot_count, HEADS, head_size)
    scores = attend_scores(query_heads, key_heads, key_valid, scale)
    row_top = jnp.max(scores, axis=-1, keepdims=True)
    row_total = jnp.sum(jnp.exp(scores - row_top), axis=-1, keepdims=True)
    log_total = row_top + jnp.log(row_total)
    soft_low = jnp.exp(scores - log_total).astype(jnp.bfloat16)
    blended = jnp.einsum(
        "chqk,ckhe->cqhe", soft_low, value_heads, preferred_element_type=jnp.float32
    )
    blended = blended.reshape(clip_count, seg_rows, model_width).astype(jnp.bfloat16)
    branch = jnp.einsum(
        "csd,de->cse", blended, outward_weight, preferred_element_type=jnp.float32
    ) + outward_bias.astype(jnp.float32)
    middle = tokens32 + branch
    affine_second, normed_second, inverse_second = norm_rows(
        middle, second_gain.astype(jnp.float32), second_shift.astype(jnp.float32)
    )
    lowered_second = affine_second.astype(jnp.bfloat16)
    hidden = jnp.einsum(
        "csd,df->csf", lowered_second, expand_weight, preferred_element_type=jnp.float32
    ) + expand_bias.astype(jnp.float32)
    active = jax.nn.gelu(hidden, approximate=False).astype(jnp.bfloat16)
    branch_second = jnp.einsum(
        "csf,fd->csd", active, shrink_weight, preferred_element_type=jnp.float32
    ) + shrink_bias.astype(jnp.float32)
    result = middle + branch_second
    output = jnp.where(row_valid, result, 0.0).astype(jnp.bfloat16)
    return {
        "normed_first": normed_first,
        "inverse_first": inverse_first,
        "lowered_first": lowered_first,
        "query_heads": query_heads,
        "key_heads": key_heads,
        "value_heads": value_heads,
        "log_total": log_total,
        "blended": blended,
        "normed_second": normed_second,
        "inverse_second": inverse_second,
        "lowered_second": lowered_second,
        "hidden": hidden,
        "active": active,
        "output": output,
    }


def gelu_exact(inputs):
    return jax.nn.gelu(inputs, approximate=False)


def backward(saved, gathered, upstream32, key_valid, row_valid):
    (
        first_gain,
        first_shift,
        inward_weight,
        query_bias,
        value_bias,
        outward_weight,
        outward_bias,
        second_gain,
        second_shift,
        expand_weight,
        expand_bias,
        shrink_weight,
        shrink_bias,
    ) = gathered
    clip_count, seg_rows, model_width = upstream32.shape
    head_size = model_width // HEADS
    scale = head_size ** (-0.5)
    grad_result = jnp.where(row_valid, upstream32, 0.0)
    grad_low_second = grad_result.astype(jnp.bfloat16)
    shrink_weight_grad = jnp.einsum(
        "csf,csd->fd", saved["active"], grad_low_second, preferred_element_type=jnp.float32
    )
    shrink_bias_grad = jnp.sum(grad_low_second.astype(jnp.float32), axis=(0, 1))
    grad_active = jnp.einsum(
        "csd,fd->csf", grad_low_second, shrink_weight, preferred_element_type=jnp.float32
    )
    gelu_value, gelu_pull = jax.vjp(gelu_exact, saved["hidden"])
    grad_hidden = gelu_pull(grad_active)[0].astype(jnp.bfloat16)
    expand_weight_grad = jnp.einsum(
        "csd,csf->df", saved["lowered_second"], grad_hidden, preferred_element_type=jnp.float32
    )
    expand_bias_grad = jnp.sum(grad_hidden.astype(jnp.float32), axis=(0, 1))
    grad_second = jnp.einsum(
        "csf,df->csd", grad_hidden, expand_weight, preferred_element_type=jnp.float32
    )
    second_gain_grad = jnp.sum(grad_second * saved["normed_second"], axis=(0, 1))
    second_shift_grad = jnp.sum(grad_second, axis=(0, 1))
    grad_middle = grad_result + norm_back(
        grad_second,
        saved["normed_second"],
        saved["inverse_second"],
        second_gain.astype(jnp.float32),
    )
    grad_low_first = grad_middle.astype(jnp.bfloat16)
    outward_weight_grad = jnp.einsum(
        "csd,cse->de", saved["blended"], grad_low_first, preferred_element_type=jnp.float32
    )
    outward_bias_grad = jnp.sum(grad_low_first.astype(jnp.float32), axis=(0, 1))
    grad_blended = jnp.einsum(
        "cse,de->csd", grad_low_first, outward_weight, preferred_element_type=jnp.float32
    )
    grad_blended = grad_blended.astype(jnp.bfloat16).reshape(clip_count, seg_rows, HEADS, head_size)
    query_heads = saved["query_heads"]
    key_heads = saved["key_heads"]
    value_heads = saved["value_heads"]
    slot_count = key_heads.shape[1]
    scores = attend_scores(query_heads, key_heads, key_valid, scale)
    soft = jnp.exp(scores - saved["log_total"])
    soft_low = soft.astype(jnp.bfloat16)
    grad_soft = jnp.einsum(
        "cqhe,ckhe->chqk", grad_blended, value_heads, preferred_element_type=jnp.float32
    )
    grad_scores = soft * (grad_soft - jnp.sum(grad_soft * soft, axis=-1, keepdims=True))
    grad_scores = grad_scores.astype(jnp.bfloat16)
    grad_queries = (
        jnp.einsum("chqk,ckhe->cqhe", grad_scores, key_heads, preferred_element_type=jnp.float32)
        * scale
    )
    grad_queries = grad_queries.astype(jnp.bfloat16).reshape(clip_count, seg_rows, model_width)
    grad_keys_part = (
        jnp.einsum("chqk,cqhe->ckhe", grad_scores, query_heads, preferred_element_type=jnp.float32)
        * scale
    )
    grad_values_part = jnp.einsum(
        "chqk,cqhe->ckhe", soft_low, grad_blended, preferred_element_type=jnp.float32
    )
    grad_keys_part = grad_keys_part.reshape(clip_count, slot_count, model_width)
    grad_values_part = grad_values_part.reshape(clip_count, slot_count, model_width)
    grad_keys, grad_values = (
        lax.psum_scatter(
            grad_keys_part.astype(jnp.bfloat16), "seq", scatter_dimension=1, tiled=True
        ).astype(jnp.float32),
        lax.psum_scatter(
            grad_values_part.astype(jnp.bfloat16), "seq", scatter_dimension=1, tiled=True
        ).astype(jnp.float32),
    )
    grad_keys = grad_keys.astype(jnp.bfloat16)
    grad_values = grad_values.astype(jnp.bfloat16)
    grad_project = jnp.concatenate([grad_queries, grad_keys, grad_values], axis=-1)
    inward_weight_grad = jnp.einsum(
        "csd,cse->de", saved["lowered_first"], grad_project, preferred_element_type=jnp.float32
    )
    query_bias_grad = jnp.sum(grad_queries.astype(jnp.float32), axis=(0, 1))
    value_bias_grad = jnp.sum(grad_values.astype(jnp.float32), axis=(0, 1))
    grad_first = jnp.einsum(
        "cse,de->csd", grad_project, inward_weight, preferred_element_type=jnp.float32
    )
    first_gain_grad = jnp.sum(grad_first * saved["normed_first"], axis=(0, 1))
    first_shift_grad = jnp.sum(grad_first, axis=(0, 1))
    tokens_grad = grad_middle + norm_back(
        grad_first, saved["normed_first"], saved["inverse_first"], first_gain.astype(jnp.float32)
    )
    weight_shares = (
        lax.psum_scatter(first_gain_grad, ("fsdp", "seq"), scatter_dimension=0, tiled=True),
        lax.psum_scatter(first_shift_grad, ("fsdp", "seq"), scatter_dimension=0, tiled=True),
        lax.psum_scatter(inward_weight_grad, ("fsdp", "seq"), scatter_dimension=0, tiled=True),
        lax.psum_scatter(query_bias_grad, ("fsdp", "seq"), scatter_dimension=0, tiled=True),
        lax.psum_scatter(value_bias_grad, ("fsdp", "seq"), scatter_dimension=0, tiled=True),
        lax.psum_scatter(outward_weight_grad, ("fsdp", "seq"), scatter_dimension=0, tiled=True),
        lax.psum_scatter(outward_bias_grad, ("fsdp", "seq"), scatter_dimension=0, tiled=True),
        lax.psum_scatter(second_gain_grad, ("fsdp", "seq"), scatter_dimension=0, tiled=True),
        lax.psum_scatter(second_shift_grad, ("fsdp", "seq"), scatter_dimension=0, tiled=True),
        lax.psum_scatter(expand_weight_grad, ("fsdp", "seq"), scatter_dimension=0, tiled=True),
        lax.psum_scatter(expand_bias_grad, ("fsdp", "seq"), scatter_dimension=0, tiled=True),
        lax.psum_scatter(shrink_weight_grad, ("fsdp", "seq"), scatter_dimension=0, tiled=True),
        lax.psum_scatter(shrink_bias_grad, ("fsdp", "seq"), scatter_dimension=0, tiled=True),
    )
    return (tokens_grad, weight_shares)


def shards(
    tokens,
    visible,
    first_gain,
    first_shift,
    inward_weight,
    query_bias,
    value_bias,
    outward_weight,
    outward_bias,
    second_gain,
    second_shift,
    expand_weight,
    expand_bias,
    shrink_weight,
    shrink_bias,
    upstream,
):
    clip_count, seg_rows, model_width = tokens.shape
    slot_count = seg_rows * lax.axis_size("seq")
    local_start = lax.axis_index("seq") * seg_rows
    row_positions = local_start + jnp.arange(seg_rows, dtype=jnp.int32)
    row_valid = (row_positions[None, :] < visible[:, None])[..., None]
    key_valid = jnp.arange(slot_count, dtype=jnp.int32)[None, :] < visible[:, None]
    tokens32 = tokens.astype(jnp.float32)
    upstream32 = upstream.astype(jnp.float32)
    gathered = gather_weights(
        first_gain,
        first_shift,
        inward_weight,
        query_bias,
        value_bias,
        outward_weight,
        outward_bias,
        second_gain,
        second_shift,
        expand_weight,
        expand_bias,
        shrink_weight,
        shrink_bias,
    )
    saved = forward(tokens32, key_valid, row_valid, gathered)
    layer_out = saved["output"]
    gathered = gather_weights(
        first_gain,
        first_shift,
        inward_weight,
        query_bias,
        value_bias,
        outward_weight,
        outward_bias,
        second_gain,
        second_shift,
        expand_weight,
        expand_bias,
        shrink_weight,
        shrink_bias,
    )
    saved = forward(tokens32, key_valid, row_valid, gathered)
    tokens_grad, shares = backward(saved, gathered, upstream32, key_valid, row_valid)
    return (
        layer_out,
        tokens_grad,
        shares[0],
        shares[1],
        shares[2],
        shares[3],
        shares[4],
        shares[5],
        shares[6],
        shares[7],
        shares[8],
        shares[9],
        shares[10],
        shares[11],
        shares[12],
    )


F32 = jnp.float32
BF16 = jnp.bfloat16
MESH = pl.DeviceIdType.MESH
SENDS, RECVS, LOCALS = 93, 137, 31
SLAB = 8


def matmul(a, b):
    return lax.dot_general(a, b, (((1,), (0,)), ((), ())), preferred_element_type=F32)


def matmul_bt(a, b):
    return lax.dot_general(a, b, (((1,), (1,)), ((), ())), preferred_element_type=F32)


def matmul_at(a, b):
    return lax.dot_general(a, b, (((0,), (0,)), ((), ())), preferred_element_type=F32)


def row_stats(x):
    mean = jnp.mean(x, axis=-1, keepdims=True)
    centered = x - mean
    inverse = lax.rsqrt(jnp.mean(centered * centered, axis=-1, keepdims=True) + epsilon)
    return centered * inverse, inverse


def row_norm_back(grad, normed, inverse, gain):
    scaled = grad * gain
    first_mean = jnp.mean(scaled, axis=-1, keepdims=True)
    second_mean = jnp.mean(scaled * normed, axis=-1, keepdims=True)
    return inverse * (scaled - first_mean - normed * second_mean)


class Place:
    def __init__(self, groups):
        self.groups = groups
        self.f = lax.axis_index("fsdp")
        self.y = lax.axis_index("seq")
        self.r = self.f // 4
        self.xc = self.f % 4
        self.t = self.xc * 2 + self.y
        x, c = self.xc // 2, self.xc % 2
        self.step = {4: 4 - 8 * x, 2: 2 - 4 * c, 1: 1 - 2 * self.y}

    def peer(self, mask):
        at = self.t
        for bit in (4, 2, 1):
            if mask & bit:
                at = at + self.step[bit]
        return at

    def device(self, r, t):
        return (r * 4 + t // 2, t % 2)


def rows(ref, index, size):
    return ref.at[pl.ds(pl.multiple_of(index * size, size), size), :]


def cols(ref, index, size):
    return ref.at[:, pl.ds(pl.multiple_of(index * size, size), size)]


class Wire:
    def __init__(self, place, send_sems, recv_sems, local_sems):
        self.place = place
        self.send_sems, self.recv_sems, self.local_sems = send_sems, recv_sems, local_sems
        self.sends = self.recvs = self.locals = 0
        self.free, self.open_sends = [], []

    def recv_slots(self, count):
        first = self.recvs
        self.recvs += count
        return [self.recv_sems.at[first + i] for i in range(count)]

    def batch(self, whole):
        spot = self.take()
        self.open_sends.append((lambda: self.describe(whole, whole, spot, self.recv_sems.at[0], self.near()), None, spot, False))
        return spot

    def near(self):
        return (self.place.r, self.place.peer(2))

    def take(self):
        if not self.free:
            self.free.append(self.sends)
            self.sends += 1
        return self.free.pop()

    def describe(self, src, dst, spot, slot, to):
        return pltpu.make_async_remote_copy(
            src_ref=src,
            dst_ref=dst,
            send_sem=self.send_sems.at[spot],
            recv_sem=slot,
            device_id=self.place.device(*to),
            device_id_type=MESH,
        )

    def send(self, src, dst, slot, to, when=None, batch=None):
        spot = self.take() if batch is None else batch

        def make():
            return self.describe(src, dst, spot, slot, to)

        if when is None:
            make().start()
        else:
            pl.when(when)(lambda: make().start())
        if batch is None:
            self.open_sends.append((make, when, spot, to[0] is not self.place.r))

    def settle(self, count=None, slab_only=False):
        count = len(self.open_sends) if count is None else count
        kept = []
        for item in self.open_sends[:count]:
            make, when, spot, far = item
            if slab_only and far:
                kept.append(item)
                continue
            if when is None:
                make().wait_send()
            else:
                pl.when(when)(lambda make=make: make().wait_send())
            self.free.append(spot)
        self.open_sends = kept + self.open_sends[count:]

    def arrived(self, dst, slot, when=None):
        def wait():
            self.describe(dst, dst, 0, slot, self.near()).wait_recv()

        if when is None:
            wait()
        else:
            pl.when(when)(wait)

    def local(self, src, dst):
        copy = pltpu.make_async_copy(src, dst, self.local_sems.at[self.locals])
        self.locals += 1
        copy.start()
        return copy


class SlabGather:
    def __init__(self, wire, at, half):
        self.wire, self.at, self.half = wire, at, half
        self.slots = wire.recv_slots(11)

    def start(self, whole, halves):
        wire, place, slots = self.wire, self.wire.place, self.slots
        t, r = place.t, place.r
        wire.send(halves[0], self.half(t, 0), slots[0], (r, place.peer(4)))
        wire.send(halves[1], self.half(t, 1), slots[3], (r, place.peer(1)))
        wire.send(halves[1], self.half(t, 1), slots[1], (r, place.peer(4)))
        wire.send(halves[0], self.half(t, 0), slots[2], (r, place.peer(1)))
        wire.send(whole, self.at(t), slots[6], (r, place.peer(2)))

    def relay(self):
        wire, place, slots = self.wire, self.wire.place, self.slots
        r, far, near = place.r, place.peer(4), place.peer(1)
        wire.arrived(self.half(far, 0), slots[0])
        wire.send(self.half(far, 0), self.half(far, 0), slots[4], (r, near))
        wire.arrived(self.half(near, 1), slots[3])
        wire.send(self.half(near, 1), self.half(near, 1), slots[5], (r, far))
        wire.arrived(self.half(far, 1), slots[1])
        wire.send(self.at(far), self.at(far), slots[7], (r, place.peer(2)))
        wire.arrived(self.half(near, 0), slots[2])
        wire.send(self.at(near), self.at(near), slots[8], (r, place.peer(2)))

    def forward(self):
        wire, place, slots = self.wire, self.wire.place, self.slots
        across = place.peer(5)
        for h in range(2):
            block = self.half(across, h)
            wire.arrived(block, slots[4 + h])
            wire.send(block, block, slots[9 + h], (place.r, place.peer(2)))

    def wait_block(self, mask):
        wire, place, slots = self.wire, self.wire.place, self.slots
        if mask == 7:
            for h in range(2):
                wire.arrived(self.half(place.peer(7), h), slots[9 + h])
        else:
            wire.arrived(self.at(place.peer(mask)), slots[{2: 6, 6: 7, 3: 8}[mask]])

    def wait(self):
        for mask in (2, 6, 3, 7):
            self.wait_block(mask)


class SlabScatter:
    def __init__(self, wire, part, core_in, chip_in, block):
        self.wire, self.part, self.core_in, self.chip_in, self.block = wire, part, core_in, chip_in, block
        self.core_slots = wire.recv_slots(4)
        self.slots = wire.recv_slots(6)
        self.order = (5, 4, 1, 0)

    def cores(self):
        place = self.wire.place
        for i, mask in enumerate(self.order):
            self.wire.send(
                rows(self.part, place.peer(mask ^ 2), self.block),
                self.core_in.at[i],
                self.core_slots[i],
                (place.r, place.peer(2)),
            )

    def half(self, mask, h):
        return rows(self.part, self.wire.place.peer(mask) * 2 + h, self.block // 2)

    def add_core(self, i):
        mask = self.order[i]
        self.wire.arrived(self.core_in.at[i], self.core_slots[i])
        mine = rows(self.part, self.wire.place.peer(mask), self.block)
        mine[...] = (mine[...].astype(F32) + self.core_in[i].astype(F32)).astype(BF16)

    def chips(self):
        wire, place = self.wire, self.wire.place
        far, near = (place.r, place.peer(4)), (place.r, place.peer(1))
        self.add_core(0)
        wire.send(self.half(5, 0), self.chip_in.at[0], self.slots[0], far)
        wire.send(self.half(5, 1), self.chip_in.at[1], self.slots[1], near)
        self.add_core(1)
        wire.send(self.half(4, 0), self.chip_in.at[2], self.slots[2], far)
        self.add_core(2)
        wire.send(self.half(1, 1), self.chip_in.at[3], self.slots[3], near)
        wire.arrived(self.core_in.at[3], self.core_slots[3])

    def relay(self):
        wire, place = self.wire, self.wire.place
        far, near = (place.r, place.peer(4)), (place.r, place.peer(1))
        for i, (block, to) in enumerate(((self.half(1, 0), near), (self.half(4, 1), far))):
            wire.arrived(self.chip_in.at[i], self.slots[i])
            block[...] = (block[...].astype(F32) + self.chip_in[i].astype(F32)).astype(BF16)
            wire.send(block, self.chip_in.at[4 + i], self.slots[4 + i], to)

    def wait(self):
        for i in range(2, 6):
            self.wire.arrived(self.chip_in.at[i], self.slots[i])

    def total(self, first, size):
        mine = self.part[pl.ds(pl.multiple_of(self.wire.place.t * self.block + first, size), size), :].astype(F32)
        mine = mine + self.core_in[3, pl.ds(pl.multiple_of(first, size), size), :].astype(F32)
        h = first // (self.block // 2)
        at = pl.ds(pl.multiple_of(first % (self.block // 2), size), size)
        return mine + self.chip_in[2 + h, at, :].astype(F32) + self.chip_in[4 + h, at, :].astype(F32)


class SlabSwap:
    def __init__(self, wire, source, target, seven):
        self.wire, self.source, self.target, self.seven = wire, source, target, seven
        (self.slot,) = wire.recv_slots(1)

    def start(self):
        place = self.wire.place
        self.own = self.wire.local(self.source(place.t), self.target(place.t))
        batch = self.wire.batch(self.seven)
        for i in (4, 5, 3, 6, 2, 7, 1):
            to = (place.t + i) % SLAB
            self.wire.send(self.source(to), self.target(place.t), self.slot, (place.r, to), batch=batch)

    def wait(self):
        self.wire.arrived(self.seven, self.slot)
        self.own.wait()


class GroupGather:
    def __init__(self, wire, at):
        self.wire, self.at = wire, at
        self.slots = wire.recv_slots(4)
        self.first = wire.recvs - 4
        r = wire.place.r
        self.inner, self.outer = (r + 1) // 2 == 1, (r + 1) // 2 != 1

    def start(self, src, dst=None):
        wire, place = self.wire, self.wire.place
        r = place.r
        dst = self.at(r) if dst is None else dst
        wire.send(src, dst, self.slots[1], ((r + 1) % 4, place.t), r != 3)
        wire.send(src, dst, self.slots[3], ((r + 3) % 4, place.t), r != 0)

    def pass_on(self):
        wire, place = self.wire, self.wire.place
        r = place.r
        below, above = (r + 3) % 4, (r + 1) % 4
        for block, slot, to in ((self.at(below), self.slots[1], above), (self.at(above), self.slots[3], below)):
            wire.arrived(block, slot, self.inner)
            wire.send(block, block, self.slots[2], (to, place.t), self.inner)

    def pass_far(self):
        wire, place = self.wire, self.wire.place
        r = place.r
        block = self.at((r + 2) % 4)
        wire.arrived(block, self.slots[2], self.inner)
        slot = wire.recv_sems.at[self.first + (2 * r + 3) % 4]
        wire.send(block, block, slot, ((3 * r + 1) % 4, place.t), self.inner)

    def wait(self):
        wire, r = self.wire, self.wire.place.r
        for i in (1, 2, 3):
            wire.arrived(self.at((r + 4 - i) % 4), self.slots[i], self.outer)


class GroupScatter:
    def __init__(self, wire, out, into, own, passing):
        self.wire, self.out, self.into, self.own, self.passing = wire, out, into, own, passing
        self.slots = wire.recv_slots(5)
        self.first = wire.recvs - 5
        r = wire.place.r

        @pl.when(r == 0)
        def _():
            into[0] = jnp.zeros_like(into[0])

        @pl.when(r == 3)
        def _():
            into[2] = jnp.zeros_like(into[2])

    def start(self, make, hold=None):
        wire, place = self.wire, self.wire.place
        r, t = place.r, place.t
        inner = (r + 1) // 2 == 1
        outer = (r + 1) // 2 != 1
        low = 1 - r // 2
        pair = r + 1 - 2 * (r % 2)
        first, last = 1 + 2 * low, 3 - 2 * low
        self.out[0] = make((r + first) % 4).astype(BF16)
        wire.send(self.out.at[0], self.passing, self.slots[0], (pair, t), outer)
        wire.send(self.out.at[0], self.into.at[first - 1], wire.recv_sems.at[self.first + first], (pair, t), inner)
        self.out[1] = make((r + 2) % 4).astype(BF16)
        wire.send(self.out.at[1], self.into.at[1], self.slots[2], ((r + 2) % 4, t), outer)
        self.out[2] = make((r + last) % 4).astype(BF16)
        self.last = last
        if not hold:
            self.start_last()
        elif hold == "outer":
            self.start_last(inner)
        self.own[...] = make(r)

    def start_last(self, when=None):
        wire, place = self.wire, self.wire.place
        to = (place.r + self.last) % 4
        slot = wire.recv_sems.at[self.first + self.last]
        wire.send(self.out.at[2], self.into.at[self.last - 1], slot, (to, place.t), when)

    def relay(self):
        wire, place = self.wire, self.wire.place
        r = place.r
        inner = (r + 1) // 2 == 1
        wire.arrived(self.passing, self.slots[0], inner)

        @pl.when(inner)
        def _():
            self.out[1] = (self.out[1].astype(F32) + self.passing[...].astype(F32)).astype(BF16)

        wire.send(self.out.at[1], self.into.at[1], self.slots[2], ((r + 2) % 4, place.t), inner)

    def total(self):
        wire, r = self.wire, self.wire.place.r
        wire.arrived(self.into.at[1], self.slots[2])
        wire.arrived(self.into.at[0], self.slots[1], r != 0)
        wire.arrived(self.into.at[2], self.slots[3], r != 3)
        total = self.own[...]
        for i in range(3):
            total = total + self.into[i].astype(F32)
        return total


def layer_kernel(
    groups,
    scale,
    tokens,
    upstream,
    visible,
    first_gain,
    first_shift,
    query_bias,
    value_bias,
    outward_bias,
    second_gain,
    second_shift,
    shrink_bias,
    expand_bias,
    w_in,
    w_out,
    w_exp,
    w_shr,
    layer_hbm,
    tokens_hbm,
    in_hbm,
    out_hbm,
    exp_hbm,
    shr_hbm,
    vec_hbm,
    layer_out,
    tokens_grad,
    out_grad,
    shr_grad,
    vec_grad,
    pack,
    small,
    wide_small,
    packs,
    tok_all,
    first_all,
    win,
    wex,
    wsh,
    wo,
    gls,
    gls_all,
    vecs,
    ebias,
    qkv,
    gqkv,
    soft_all,
    blend_t,
    blend,
    middle,
    normed,
    inverses,
    second,
    second_all,
    active,
    ghid,
    slopes,
    part_a,
    part_b,
    part_c,
    part_d,
    core_a,
    core_b,
    core_c,
    core_d,
    chip_a,
    chip_b,
    chip_c,
    chip_d,
    gsec,
    glow,
    gblend,
    gblend_t,
    sh_out,
    sh_in,
    sh_own,
    sh_pass,
    ex_out,
    ex_in,
    ex_own,
    ex_pass,
    ex_sum,
    ex_all,
    in_out,
    in_in,
    in_own,
    in_pass,
    in_sum,
    in_all,
    ou_out,
    ou_in,
    ou_own,
    ou_pass,
    gvec,
    gvec_exp,
    gvec_out,
    gvec_in,
    gvec_sum,
    gvec_far,
    send_sems,
    recv_sems,
    local_sems,
):
    place = Place(groups)
    wire = Wire(place, send_sems, recv_sems, local_sems)
    f, y, r, xc, t = place.f, place.y, place.r, place.xc, place.t
    devices = groups * SLAB
    me = r * SLAB + t
    seg, width = tokens.shape
    clips = SLAB // 2
    slots = seg * 2
    total_rows = SLAB * seg
    head2 = qkv.shape[1] // 3
    own_rows = w_in.shape[0]
    slab_rows = own_rows * 4
    share = width // devices
    chunk = wsh.shape[1]
    strip = 32
    tile = 256

    vectors = (
        first_gain,
        first_shift,
        query_bias,
        value_bias,
        outward_bias,
        second_gain,
        second_shift,
        shrink_bias,
    )
    loads = [wire.local(ref, small.at[k]) for k, ref in enumerate(vectors)]
    loads.append(wire.local(expand_bias, wide_small))
    barrier = pltpu.get_barrier_semaphore()
    for i in range(1, devices):
        to = (me + i) % devices
        pl.semaphore_signal(barrier, inc=1, device_id=place.device(to // SLAB, to % SLAB), device_id_type=MESH)
    for copy in loads:
        copy.wait()
    per_lane = 128 // own_rows
    lines = [jnp.concatenate([small[k].astype(F32)] * per_lane, axis=1) for k in range(8)]
    lines.append(wide_small[...].astype(F32))
    count_here = jnp.full((6, 128), visible[0], jnp.int32).astype(F32)
    pack[...] = jnp.concatenate(lines + [count_here], axis=0).astype(BF16)
    pl.semaphore_wait(barrier, devices - 1)

    (pack_slot,) = wire.recv_slots(1)
    pack_batch = wire.batch(packs.at[pl.ds(0, groups * 4 - 1)])
    for i in range(1, groups * 4):
        to = (f + i) % (groups * 4)
        wire.send(pack, packs.at[f], pack_slot, (to // 4, (to % 4) * 2 + y), batch=pack_batch)
    own_pack = wire.local(pack, packs.at[f])

    in_slots = wire.recv_slots(4)
    ex_slots = wire.recv_slots(4)

    def in_piece(index, c):
        return win.at[pl.ds(pl.multiple_of(index * own_rows, own_rows), own_rows), pl.ds(c * head2, head2)]

    def ex_piece(index, c):
        return wex.at[pl.ds(pl.multiple_of(index * own_rows, own_rows), own_rows), pl.ds(c * chunk, chunk)]

    own_in = []
    in_batch = wire.batch(win.at[pl.ds(0, 3 * own_rows), :])
    for i in (2, 3, 1, 0):
        to = ((xc + i) % 4) * 2 + y
        for c in range(3):
            src = w_in.at[:, pl.ds(pl.multiple_of(c * width + to * head2, head2), head2)]
            if i == 0:
                own_in.append(wire.local(src, in_piece(f, c)))
            else:
                wire.send(src, in_piece(f, c), in_slots[i], (r, to), batch=in_batch)

    out_share = w_out.at[pl.ds(pl.multiple_of(y * share, share), share), :]
    own_out = wire.local(out_share, wo.at[r, t])
    group_wo = GroupGather(wire, lambda at: wo.at[at, t])
    group_wo.start(out_share)
    shr_share = w_shr.at[pl.ds(pl.multiple_of(y * chunk, chunk), chunk), :]
    own_shr = wire.local(shr_share, wsh.at[r])
    group_sh = GroupGather(wire, lambda at: wsh.at[at])

    def shr_half(h):
        at = pl.ds(h * (chunk // 2), chunk // 2)
        src = w_shr.at[pl.ds(pl.multiple_of(y * chunk + h * (chunk // 2), chunk // 2), chunk // 2), :]
        group_sh.start(src, wsh.at[r, at])

    shr_half(0)

    def slab_gather(ref):
        return SlabGather(wire, lambda at: rows(ref, at, seg), lambda at, h: rows(ref, at * 2 + h, seg // 2))

    gather_tok = slab_gather(tok_all)
    gather_tok.start(tokens, [rows(tokens, h, seg // 2) for h in range(2)])

    own_ex = []
    ex_batch = wire.batch(wex.at[pl.ds(0, 3 * own_rows), :])
    for i in (2, 3, 1, 0):
        to = ((xc + i) % 4) * 2 + y
        for c in range(groups):
            src = w_exp.at[:, pl.ds(pl.multiple_of((c * SLAB + to) * chunk, chunk), chunk)]
            if i == 0:
                own_ex.append(wire.local(src, ex_piece(f, c)))
            else:
                wire.send(src, ex_piece(f, c), ex_slots[i], (r, to), batch=ex_batch)

    row_at = y * seg + lax.broadcasted_iota(jnp.int32, (seg, 1), 0)
    row_valid = row_at.astype(F32) < pack[10:11, 0:1].astype(F32)
    gls[...] = jnp.where(row_valid, upstream[...].astype(F32), 0.0).astype(BF16)
    gls_all[pl.ds(pl.multiple_of(t * seg, seg), seg), :] = gls[...]
    gvec[...] = jnp.zeros_like(gvec)
    gvec_exp[...] = jnp.zeros_like(gvec_exp)
    group_shr = GroupScatter(wire, sh_out, sh_in, sh_own, sh_pass)
    group_exp = GroupScatter(wire, ex_out, ex_in, ex_own, ex_pass)
    group_inw = GroupScatter(wire, in_out, in_in, in_own, in_pass)
    group_out = GroupScatter(wire, ou_out, ou_in, ou_own, ou_pass)

    for i in range(1, 4):
        frm = r * 4 + (xc + 4 - i) % 4
        wire.arrived(rows(win, frm, own_rows), in_slots[i])
    for copy in own_in:
        copy.wait()
    own_out.wait()
    group_wo.pass_on()
    group_in = GroupGather(wire, lambda at: rows(win, at, slab_rows))
    group_in.start(rows(win, r, slab_rows))
    shr_half(1)
    group_wo.pass_far()

    own_pack.wait()
    wire.arrived(packs.at[pl.ds(0, groups * 4 - 1)], pack_slot)
    lane = lax.broadcasted_iota(jnp.int32, (1, 128), 1)
    for j in range(width // 128):
        piece = packs[j * per_lane].astype(F32)
        for k in range(1, per_lane):
            piece = jnp.where(lane >= k * own_rows, packs[j * per_lane + k].astype(F32), piece)
        vecs[:, j * 128 : (j + 1) * 128] = piece
    for c in range(groups):
        both = packs[c * 4 + t // 2].astype(F32)
        ebias[0:1, c * chunk : (c + 1) * chunk] = jnp.where(y == 0, both[8:9], both[9:10])

    def first_norm(src, offset, block):
        def strip_norm(i, carry):
            at = pl.multiple_of(i * strip, strip)
            n, _ = row_stats(src[pl.ds(offset + at, strip), :].astype(F32))
            to = pl.multiple_of(block * seg + at, strip)
            first_all[pl.ds(to, strip), :] = (n * vecs[0:1, :] + vecs[1:2, :]).astype(BF16)
            return carry

        lax.fori_loop(0, seg // strip, strip_norm, 0)

    first_norm(tokens, 0, t)

    def norm_block(mask):
        block = place.peer(mask)
        first_norm(tok_all, pl.multiple_of(block * seg, seg), block)

    gather_tok.relay()
    group_wo.wait()
    gather_wo = SlabGather(wire, lambda at: wo.at[:, at], lambda at, h: wo.at[pl.ds(h * (groups // 2), groups // 2), at])
    gather_wo.start(wo.at[:, t], [wo.at[pl.ds(h * (groups // 2), groups // 2), t] for h in range(2)])
    group_in.pass_on()
    norm_block(4)
    norm_block(1)

    gather_tok.forward()

    norm_block(5)
    group_in.pass_far()
    for i in range(1, 4):
        frm = r * 4 + (xc + 4 - i) % 4
        wire.arrived(rows(wex, frm, own_rows), ex_slots[i])
    for copy in own_ex:
        copy.wait()
    group_ex = GroupGather(wire, lambda at: rows(wex, at, slab_rows))
    group_ex.start(rows(wex, r, slab_rows))


    for mask in (2, 6, 3, 7):
        gather_tok.wait_block(mask)
        norm_block(mask)

    gather_wo.relay()
    gather_gls = slab_gather(gls_all)
    gather_gls.start(gls, [rows(gls, h, seg // 2) for h in range(2)])
    group_in.wait()
    at_head = pl.ds(pl.multiple_of(t * head2, head2), head2)
    bias = jnp.concatenate([vecs[2:3, at_head], jnp.zeros((1, head2), F32), vecs[3:4, at_head]], axis=1)

    def project(i, carry):
        at = pl.ds(pl.multiple_of(i * tile, tile), tile)
        qkv[at, :] = (matmul(first_all[at, :], win[...]) + bias).astype(BF16)
        return carry

    lax.fori_loop(0, total_rows // tile, project, 0)

    group_sh.pass_on()
    head_size = head2 // 2
    low_half = lane < head_size
    half_masks = [low_half.astype(F32).astype(BF16), (1.0 - low_half.astype(F32)).astype(BF16)]
    key_at = lax.broadcasted_iota(jnp.int32, (1, slots), 1).astype(F32)

    def attend(i, carry):
        at = pl.ds(pl.multiple_of(i * slots, slots), slots)
        q = qkv[at, 0:head2]
        k = qkv[at, head2 : 2 * head2]
        v = qkv[at, 2 * head2 : 3 * head2]
        count = packs[r * 4 + i].astype(F32)[10:11, 0:1]
        key_valid = key_at < count
        halves = []
        for h in range(2):
            scores = matmul_bt(q * half_masks[h], k) * scale
            scores = jnp.where(key_valid, scores, -1e30)
            top = jnp.max(scores, axis=-1, keepdims=True)
            soft = jnp.exp(scores - top)
            soft = soft * (1.0 / jnp.sum(soft, axis=-1, keepdims=True))
            soft_all[i * 2 + h] = soft
            halves.append(matmul(soft.astype(BF16), v))
        blend_t[at, :] = jnp.where(low_half, halves[0], halves[1]).astype(BF16)
        return carry

    lax.fori_loop(0, clips, attend, 0)

    group_ex.pass_on()
    swap_blend = SlabSwap(wire, lambda at: rows(blend_t, at, seg), lambda at: cols(blend, at, head2), blend.at[:, 0 : 7 * head2])
    swap_blend.start()
    gather_wo.forward()

    gather_gls.relay()
    gather_wo.wait()
    swap_blend.wait()
    group_ex.pass_far()
    wide = 256
    for j in range(width // wide):
        at = slice(j * wide, (j + 1) * wide)
        product = matmul(blend[...], wo[:, :, :, at].reshape(width, wide))
        middle[:, at] = tokens[:, at].astype(F32) + (product + vecs[4:5, at])

    own_second_rows = pl.multiple_of(t * seg, seg)

    def second_norm(i, carry):
        at = pl.ds(pl.multiple_of(i * strip, strip), strip)
        n, inverse = row_stats(middle[at, :])
        normed[at, :] = n
        inverses[at, :] = jnp.broadcast_to(inverse, (strip, 128))
        low = (n * vecs[5:6, :] + vecs[6:7, :]).astype(BF16)
        second[at, :] = low
        second_all[pl.ds(pl.multiple_of(own_second_rows + i * strip, strip), strip), :] = low
        return carry

    lax.fori_loop(0, seg // strip, second_norm, 0)

    gather_second = slab_gather(second_all)
    gather_second.start(second, [rows(second, h, seg // 2) for h in range(2)])
    gather_gls.forward()
    hidden_units = groups * chunk

    def feed(i, carry):
        at = pl.ds(pl.multiple_of(i * tile, tile), tile)
        hidden = matmul(second_all[at, :], wex[...]) + ebias[0:1, :]
        cdf = 0.5 * (1.0 + lax.erf(hidden * 0.7071067811865476))
        active[at, :] = (hidden * cdf).astype(BF16)
        slopes[at, :] = cdf + hidden * (0.3989422804014327 * jnp.exp(-0.5 * hidden * hidden))
        return carry

    gather_second.relay()
    group_sh.pass_far()
    group_ex.wait()
    core = xc % 2
    beside = xc + 1 - 2 * core
    across = (xc + 2) % 4
    feed(xc, 0)
    gather_second.forward()
    feed(across, 0)
    gather_second.wait_block(2)
    gather_second.wait_block(3)
    feed(beside, 0)
    gather_second.wait_block(6)
    gather_second.wait_block(7)
    feed((beside + 2) % 4, 0)
    gather_gls.wait()
    front_sends = len(wire.open_sends)

    group_shr.start(
        lambda c: matmul_at(active[:, pl.ds(pl.multiple_of(c * chunk, chunk), chunk)], gls_all[...]),
        hold="outer",
    )
    group_sh.wait()
    own_shr.wait()

    def feed_back(i, carry):
        at = pl.ds(pl.multiple_of(i * tile, tile), tile)
        grad_active = matmul_bt(gls_all[at, :], wsh[...].reshape(hidden_units, width))
        grad_hidden = (grad_active * slopes[at, :]).astype(BF16)
        ghid[at, :] = grad_hidden
        gvec_exp[...] += jnp.sum(grad_hidden.astype(F32), axis=0, keepdims=True)
        part_a[at, :] = matmul_bt(grad_hidden, wex[...]).astype(BF16)
        return carry

    scatter_second = SlabScatter(wire, part_a, core_a, chip_a, seg)
    lax.fori_loop(0, 2, lambda k, carry: feed_back(1 - core + 2 * k, carry), 0)
    scatter_second.cores()
    lax.fori_loop(0, 2, lambda k, carry: feed_back(core + 2 * k, carry), 0)

    scatter_second.chips()
    group_exp.start(
        lambda c: matmul_at(second_all[:, pl.ds(pl.multiple_of(c * slab_rows, slab_rows), slab_rows)], ghid[...])
    )
    scatter_second.relay()
    group_shr.relay()

    def feed_out(i, carry):
        at = pl.ds(pl.multiple_of(i * tile, tile), tile)
        part_b[at, :] = matmul(active[at, :], wsh[...].reshape(hidden_units, width)).astype(BF16)
        return carry

    lax.fori_loop(0, total_rows // tile, feed_out, 0)
    scatter_result = SlabScatter(wire, part_b, core_b, chip_b, seg)
    scatter_result.cores()

    scatter_second.wait()
    wire.settle(front_sends)

    feed_sends = len(wire.open_sends)

    def second_back(i, carry):
        first = i * strip
        at = pl.ds(pl.multiple_of(first, strip), strip)
        grad = scatter_second.total(first, strip)
        n = normed[at, :]
        back = row_norm_back(grad, n, inverses[at, 0:1], vecs[5:6, :])
        grad_result = gls[at, :].astype(F32)
        grad_middle = grad_result + back
        gsec[at, :] = grad_middle
        low = grad_middle.astype(BF16)
        glow[at, :] = low
        gvec[4:5, :] += jnp.sum(low.astype(F32), axis=0, keepdims=True)
        gvec[5:6, :] += jnp.sum(grad * n, axis=0, keepdims=True)
        gvec[6:7, :] += jnp.sum(grad, axis=0, keepdims=True)
        gvec[7:8, :] += jnp.sum(grad_result, axis=0, keepdims=True)
        return carry

    lax.fori_loop(0, seg // strip, second_back, 0)

    for j in range(width // wide):
        rows_of = slice(j * (groups * wide // width), (j + 1) * (groups * wide // width))
        gblend[:, j * wide : (j + 1) * wide] = matmul_bt(
            glow[...], wo[rows_of].reshape(wide, width)
        ).astype(BF16)
    swap_gblend = SlabSwap(wire, lambda at: cols(gblend, at, head2), lambda at: rows(gblend_t, at, seg), gblend_t.at[pl.ds(0, 7 * seg), :])
    swap_gblend.start()

    for c in range(groups):
        product = matmul_at(blend[:, c * slab_rows : (c + 1) * slab_rows], glow[...])
        for to in range(SLAB):
            part_d[to * seg + c * share : to * seg + (c + 1) * share, :] = product[
                to * share : (to + 1) * share
            ].astype(BF16)
    scatter_out = SlabScatter(wire, part_d, core_d, chip_d, seg)
    scatter_out.cores()

    scatter_out.chips()
    swap_gblend.wait()

    def attend_back(i, carry):
        at = pl.ds(pl.multiple_of(i * slots, slots), slots)
        q = qkv[at, 0:head2]
        k = qkv[at, head2 : 2 * head2]
        v = qkv[at, 2 * head2 : 3 * head2]
        grad = gblend_t[at, :]
        parts = []
        for h in range(2):
            soft = soft_all[i * 2 + h]
            grad_soft = matmul_bt(grad * half_masks[h], v)
            inner = jnp.sum(grad_soft * soft, axis=-1, keepdims=True)
            grad_scores = (soft * (grad_soft - inner)).astype(BF16)
            parts.append(
                (
                    matmul(grad_scores, k) * scale,
                    matmul_at(grad_scores, q) * scale,
                    matmul_at(soft.astype(BF16), grad),
                )
            )
        for c in range(3):
            gqkv[at, c * head2 : (c + 1) * head2] = jnp.where(low_half, parts[0][c], parts[1][c]).astype(BF16)
        return carry

    lax.fori_loop(0, clips, attend_back, 0)

    scatter_out.relay()
    group_exp.relay()
    def project_back(i, carry):
        at = pl.ds(pl.multiple_of(i * tile, tile), tile)
        part_c[at, :] = matmul_bt(gqkv[at, :], win[...]).astype(BF16)
        return carry

    scatter_first = SlabScatter(wire, part_c, core_c, chip_c, seg)
    lax.fori_loop(0, 2, lambda k, carry: project_back(1 - core + 2 * k, carry), 0)
    scatter_first.cores()
    lax.fori_loop(0, 2, lambda k, carry: project_back(core + 2 * k, carry), 0)

    group_inw.start(
        lambda c: matmul_at(first_all[:, pl.ds(pl.multiple_of(c * slab_rows, slab_rows), slab_rows)], gqkv[...]),
        hold="all",
    )
    scatter_first.chips()
    gvec[2:3, at_head] = jnp.sum(gqkv[:, 0:head2].astype(F32), axis=0, keepdims=True)
    gvec[3:4, at_head] = jnp.sum(gqkv[:, 2 * head2 :].astype(F32), axis=0, keepdims=True)

    scatter_out.wait()
    group_out.start(lambda c: scatter_out.total(c * share, share), hold="outer")
    outer = (r + 1) // 2 != 1
    group_inw.start_last(outer)
    group_out.start_last(outer)
    group_shr.start_last(outer)
    scatter_first.relay()
    scatter_result.chips()
    group_inw.relay()
    group_inw.start_last((r + 1) // 2 == 1)
    scatter_first.wait()
    wire.settle(feed_sends, slab_only=True)

    def first_back(i, carry):
        first = i * strip
        at = pl.ds(pl.multiple_of(first, strip), strip)
        grad = scatter_first.total(first, strip)
        n, inverse = row_stats(tokens[at, :].astype(F32))
        tokens_grad[at, :] = gsec[at, :] + row_norm_back(grad, n, inverse, vecs[0:1, :])
        gvec[0:1, :] += jnp.sum(grad * n, axis=0, keepdims=True)
        gvec[1:2, :] += jnp.sum(grad, axis=0, keepdims=True)
        return carry

    lax.fori_loop(0, seg // strip, first_back, 0)
    stores = [wire.local(tokens_grad, tokens_hbm)]

    group_out.relay()
    for to in range(SLAB):
        gvec_out[to] = jnp.concatenate(
            [gvec[:, (c * SLAB + to) * share : (c * SLAB + to + 1) * share] for c in range(groups)], axis=1
        )
    swap_vec = SlabSwap(wire, lambda at: gvec_out.at[at], lambda at: gvec_in.at[at], gvec_in.at[pl.ds(0, 7)])
    swap_vec.start()

    scatter_result.relay()
    ex_sum[...] = group_exp.total().astype(BF16)
    swap_exp = SlabSwap(wire, lambda at: rows(ex_sum, at, share), lambda at: ex_all.at[at], ex_all.at[pl.ds(0, 7)])
    swap_exp.start()
    swap_vec.wait()
    summed = gvec_in[0]
    for i in range(1, SLAB):
        summed = summed + gvec_in[i]
    gvec_sum[0:8] = summed
    for c in range(groups):
        gvec_sum[8 + c : 9 + c] = gvec_exp[0:1, c * chunk : (c + 1) * chunk]
    gvec_sum[8 + groups : 16] = jnp.zeros((8 - groups, 128), F32)
    vec_slots = wire.recv_slots(groups - 1)
    for i in range(1, groups):
        wire.send(gvec_sum, gvec_far.at[i - 1], vec_slots[i - 1], ((r + i) % groups, t))
    in_sum[...] = group_inw.total().astype(BF16)
    swap_in = SlabSwap(wire, lambda at: rows(in_sum, at, share), lambda at: in_all.at[at], in_all.at[pl.ds(0, 7)])
    swap_in.start()
    scatter_result.wait()

    def finish_out(i, carry):
        first = i * strip
        at = pl.ds(pl.multiple_of(first, strip), strip)
        result = middle[at, :] + (scatter_result.total(first, strip) + vecs[7:8, :])
        spot = y * seg + first + lax.broadcasted_iota(jnp.int32, (strip, 1), 0)
        valid = spot.astype(F32) < pack[10:11, 0:1].astype(F32)
        layer_out[at, :] = jnp.where(valid, result, 0.0).astype(BF16)
        return carry

    lax.fori_loop(0, seg // strip, finish_out, 0)
    stores.append(wire.local(layer_out, layer_hbm))

    out_grad[...] = group_out.total()
    stores.append(wire.local(out_grad, out_hbm))
    shr_grad[...] = group_shr.total()
    stores.append(wire.local(shr_grad, shr_hbm))
    for i in range(1, groups):
        wire.arrived(gvec_far.at[i - 1], vec_slots[i - 1])
    total = gvec_sum[...]
    for i in range(1, groups):
        total = total + gvec_far[i - 1]
    vec_grad[0:8, :] = pltpu.roll(total[0:8], (128 - share * r) % 128, 1)
    line = total[8:9]
    for c in range(1, groups):
        line = jnp.where(r == c, total[8 + c : 9 + c], line)
    vec_grad[8:16, :] = jnp.broadcast_to(line, (8, 128))
    stores.append(wire.local(vec_grad, vec_hbm))
    swap_exp.wait()
    stores.append(wire.local(ex_all, exp_hbm))
    swap_in.wait()
    stores.append(wire.local(in_all, in_hbm))
    for copy in stores:
        copy.wait()
    wire.settle()
    assert (wire.sends, wire.recvs, wire.locals) == (SENDS, RECVS, LOCALS), (wire.sends, wire.recvs, wire.locals)


def output_kernel(
    groups,
    layer_in,
    tokens_in,
    in_pieces,
    out_in,
    exp_pieces,
    shr_in,
    vec_in,
    layer_out,
    tokens_grad,
    first_gain_grad,
    first_shift_grad,
    in_grad,
    query_bias_grad,
    value_bias_grad,
    out_grad,
    outward_bias_grad,
    second_gain_grad,
    second_shift_grad,
    exp_grad,
    expand_bias_grad,
    shr_grad,
    shrink_bias_grad,
    layer_buf,
    tokens_buf,
    in_buf,
    out_buf,
    exp_buf,
    shr_buf,
    vec_buf,
    in_wide,
    exp_wide,
    lines,
    wide_line,
    load_sems,
    store_sems,
):
    share, width = out_buf.shape
    head2, chunk = in_buf.shape[2] // 3, exp_buf.shape[2] // groups
    loads = [
        pltpu.make_async_copy(src, dst, load_sems.at[i])
        for i, (src, dst) in enumerate(
            (
                (vec_in, vec_buf),
                (exp_pieces, exp_buf),
                (in_pieces, in_buf),
                (shr_in, shr_buf),
                (tokens_in, tokens_buf),
                (layer_in, layer_buf),
                (out_in, out_buf),
            )
        )
    ]
    for copy in loads:
        copy.start()
    stores = []

    def store(src, dst):
        stores.append(pltpu.make_async_copy(src, dst, store_sems.at[len(stores)]))
        stores[-1].start()

    loads[0].wait()
    vectors = (
        first_gain_grad,
        first_shift_grad,
        query_bias_grad,
        value_bias_grad,
        outward_bias_grad,
        second_gain_grad,
        second_shift_grad,
        shrink_bias_grad,
    )
    for k, ref in enumerate(vectors):
        lines[k] = vec_buf[k, 0:share]
        store(lines.at[k], ref)
    wide_line[...] = vec_buf[8, :]
    store(wide_line, expand_bias_grad)
    loads[1].wait()
    for frm in range(SLAB):
        for c in range(groups):
            at = (c * SLAB + frm) * chunk
            exp_wide[:, at : at + chunk] = exp_buf[frm, :, c * chunk : (c + 1) * chunk].astype(F32)
    store(exp_wide, exp_grad)
    loads[2].wait()
    for frm in range(SLAB):
        for c in range(3):
            at = c * width + frm * head2
            in_wide[:, at : at + head2] = in_buf[frm, :, c * head2 : (c + 1) * head2].astype(F32)
    store(in_wide, in_grad)
    for copy, src, dst in (
        (loads[3], shr_buf, shr_grad),
        (loads[4], tokens_buf, tokens_grad.at[0]),
        (loads[5], layer_buf, layer_out.at[0]),
        (loads[6], out_buf, out_grad),
    ):
        copy.wait()
        store(src, dst)
    for copy in stores:
        copy.wait()


def fused_shards(
    tokens,
    visible,
    first_gain,
    first_shift,
    inward_weight,
    query_bias,
    value_bias,
    outward_weight,
    outward_bias,
    second_gain,
    second_shift,
    expand_weight,
    expand_bias,
    shrink_weight,
    shrink_bias,
    upstream,
):
    seg, width = tokens.shape[1:]
    groups = lax.axis_size("fsdp") // 4
    devices = groups * SLAB
    own_rows = inward_weight.shape[0]
    hidden = expand_weight.shape[1]
    share = width // devices
    chunk = hidden // devices
    units = groups * chunk
    head2 = width // SLAB
    scale = (width // HEADS) ** (-0.5)
    total_rows = SLAB * seg
    slab_rows = 4 * own_rows
    vmem = pl.BlockSpec(memory_space=pltpu.VMEM)
    anywhere = pl.BlockSpec(memory_space=pl.ANY)
    outs = pl.pallas_call(
        functools.partial(layer_kernel, groups, scale),
        out_shape=(
            jax.ShapeDtypeStruct((seg, width), BF16),
            jax.ShapeDtypeStruct((seg, width), F32),
            jax.ShapeDtypeStruct((SLAB, share, 3 * head2), BF16),
            jax.ShapeDtypeStruct((share, width), F32),
            jax.ShapeDtypeStruct((SLAB, share, units), BF16),
            jax.ShapeDtypeStruct((chunk, width), F32),
            jax.ShapeDtypeStruct((16, 128), F32),
        ),
        in_specs=[vmem, vmem, pl.BlockSpec(memory_space=pltpu.SMEM)] + [anywhere] * 13,
        out_specs=[anywhere] * 7,
        scratch_shapes=[
            pltpu.VMEM((seg, width), BF16),
            pltpu.VMEM((seg, width), F32),
            pltpu.VMEM((share, width), F32),
            pltpu.VMEM((chunk, width), F32),
            pltpu.VMEM((16, 128), F32),
            pltpu.VMEM((16, 128), BF16),
            pltpu.VMEM((8, 1, own_rows), BF16),
            pltpu.VMEM((2, 128), BF16),
            pltpu.VMEM((groups * 4, 16, 128), BF16),
            pltpu.VMEM((total_rows, width), BF16),
            pltpu.VMEM((total_rows, width), BF16),
            pltpu.VMEM((width, 3 * head2), BF16),
            pltpu.VMEM((width, units), BF16),
            pltpu.VMEM((groups, chunk, width), BF16),
            pltpu.VMEM((groups, SLAB, share, width), BF16),
            pltpu.VMEM((seg, width), BF16),
            pltpu.VMEM((total_rows, width), BF16),
            pltpu.VMEM((16, width), F32),
            pltpu.VMEM((8, units), F32),
            pltpu.VMEM((total_rows, 3 * head2), BF16),
            pltpu.VMEM((total_rows, 3 * head2), BF16),
            pltpu.VMEM((SLAB, 2 * seg, 2 * seg), F32),
            pltpu.VMEM((total_rows, head2), BF16),
            pltpu.VMEM((seg, width), BF16),
            pltpu.VMEM((seg, width), F32),
            pltpu.VMEM((seg, width), F32),
            pltpu.VMEM((seg, 128), F32),
            pltpu.VMEM((seg, width), BF16),
            pltpu.VMEM((total_rows, width), BF16),
            pltpu.VMEM((total_rows, units), BF16),
            pltpu.VMEM((total_rows, units), BF16),
            pltpu.VMEM((total_rows, units), F32),
        ]
        + [pltpu.VMEM((total_rows, width), BF16)] * 4
        + [pltpu.VMEM((4, seg, width), BF16)] * 4
        + [pltpu.VMEM((6, seg // 2, width), BF16)] * 4
        + [
            pltpu.VMEM((seg, width), F32),
            pltpu.VMEM((seg, width), BF16),
            pltpu.VMEM((seg, width), BF16),
            pltpu.VMEM((total_rows, head2), BF16),
            pltpu.VMEM((groups - 1, chunk, width), BF16),
            pltpu.VMEM((groups - 1, chunk, width), BF16),
            pltpu.VMEM((chunk, width), F32),
            pltpu.VMEM((chunk, width), BF16),
            pltpu.VMEM((groups - 1, slab_rows, units), BF16),
            pltpu.VMEM((groups - 1, slab_rows, units), BF16),
            pltpu.VMEM((slab_rows, units), F32),
            pltpu.VMEM((slab_rows, units), BF16),
            pltpu.VMEM((slab_rows, units), BF16),
            pltpu.VMEM((SLAB, share, units), BF16),
            pltpu.VMEM((groups - 1, slab_rows, 3 * head2), BF16),
            pltpu.VMEM((groups - 1, slab_rows, 3 * head2), BF16),
            pltpu.VMEM((slab_rows, 3 * head2), F32),
            pltpu.VMEM((slab_rows, 3 * head2), BF16),
            pltpu.VMEM((slab_rows, 3 * head2), BF16),
            pltpu.VMEM((SLAB, share, 3 * head2), BF16),
            pltpu.VMEM((groups - 1, share, width), BF16),
            pltpu.VMEM((groups - 1, share, width), BF16),
            pltpu.VMEM((share, width), F32),
            pltpu.VMEM((share, width), BF16),
            pltpu.VMEM((8, width), F32),
            pltpu.VMEM((1, units), F32),
            pltpu.VMEM((SLAB, 8, 128), F32),
            pltpu.VMEM((SLAB, 8, 128), F32),
            pltpu.VMEM((16, 128), F32),
            pltpu.VMEM((groups - 1, 16, 128), F32),
            pltpu.SemaphoreType.DMA((SENDS,)),
            pltpu.SemaphoreType.DMA((RECVS,)),
            pltpu.SemaphoreType.DMA((LOCALS,)),
        ],
        compiler_params=pltpu.CompilerParams(
            collective_id=0, has_side_effects=True, vmem_limit_bytes=67043328
        ),
        name="layer",
    )(
        tokens.reshape(seg, width),
        upstream.reshape(seg, width),
        visible,
        *(
            vector.reshape(1, own_rows)
            for vector in (
                first_gain,
                first_shift,
                query_bias,
                value_bias,
                outward_bias,
                second_gain,
                second_shift,
                shrink_bias,
            )
        ),
        expand_bias.reshape(2, 128),
        inward_weight,
        outward_weight,
        expand_weight,
        shrink_weight,
    )
    vector = jax.ShapeDtypeStruct((share,), F32)
    return pl.pallas_call(
        functools.partial(output_kernel, groups),
        out_shape=(
            jax.ShapeDtypeStruct((1, seg, width), BF16),
            jax.ShapeDtypeStruct((1, seg, width), F32),
            vector,
            vector,
            jax.ShapeDtypeStruct((share, 3 * width), F32),
            vector,
            vector,
            jax.ShapeDtypeStruct((share, width), F32),
            vector,
            vector,
            vector,
            jax.ShapeDtypeStruct((share, hidden), F32),
            jax.ShapeDtypeStruct((chunk,), F32),
            jax.ShapeDtypeStruct((chunk, width), F32),
            vector,
        ),
        in_specs=[anywhere] * 7,
        out_specs=[anywhere] * 15,
        scratch_shapes=[
            pltpu.VMEM((seg, width), BF16),
            pltpu.VMEM((seg, width), F32),
            pltpu.VMEM((SLAB, share, 3 * head2), BF16),
            pltpu.VMEM((share, width), F32),
            pltpu.VMEM((SLAB, share, units), BF16),
            pltpu.VMEM((chunk, width), F32),
            pltpu.VMEM((16, 128), F32),
            pltpu.VMEM((share, 3 * width), F32),
            pltpu.VMEM((share, hidden), F32),
            pltpu.VMEM((8, share), F32),
            pltpu.VMEM((chunk,), F32),
            pltpu.SemaphoreType.DMA((7,)),
            pltpu.SemaphoreType.DMA((15,)),
        ],
        name="outputs",
    )(*outs)


def fits_fused(mesh, tokens, inward_weight, expand_weight):
    fsdp, seq = mesh.shape["fsdp"], mesh.shape["seq"]
    clips, slots, width = tokens.shape
    devices = fsdp * seq
    return (
        seq == 2
        and clips == fsdp
        and fsdp == 16
        and width // HEADS * 2 == 128
        and width == SLAB * 128
        and slots % 64 == 0
        and width % (16 * devices) == 0
        and 128 % (width // fsdp) == 0
        and width // devices * 4 == 128
        and expand_weight.shape[1] == 128 * devices
    )


def solution(mesh):
    in_specs = (
        P("fsdp", "seq", None),
        P("fsdp"),
        P("fsdp"),
        P("fsdp"),
        P("fsdp", None),
        P("fsdp"),
        P("fsdp"),
        P("fsdp", None),
        P("fsdp"),
        P("fsdp"),
        P("fsdp"),
        P("fsdp", None),
        P("fsdp"),
        P("fsdp", None),
        P("fsdp"),
        P("fsdp", "seq", None),
    )
    out_specs = (
        P("fsdp", "seq", None),
        P("fsdp", "seq", None),
        P(("fsdp", "seq")),
        P(("fsdp", "seq")),
        P(("fsdp", "seq"), None),
        P(("fsdp", "seq")),
        P(("fsdp", "seq")),
        P(("fsdp", "seq"), None),
        P(("fsdp", "seq")),
        P(("fsdp", "seq")),
        P(("fsdp", "seq")),
        P(("fsdp", "seq"), None),
        P(("fsdp", "seq")),
        P(("fsdp", "seq"), None),
        P(("fsdp", "seq")),
    )

    def step(*args):
        body = fused_shards if fits_fused(mesh, args[0], args[4], args[11]) else shards
        return jax.shard_map(body, mesh=mesh, in_specs=in_specs, out_specs=out_specs, check_vma=False)(*args)

    return step
```

```python
import functools

import jax
import jax.numpy as jnp
from jax import lax
from jax.experimental import pallas as pl
from jax.experimental.pallas import tpu as pltpu
from jax.sharding import PartitionSpec as P

HEADS = 16


epsilon = 1e-06


def norm_rows(inputs, norm_gain, norm_shift):
    row_mean = jnp.mean(inputs, axis=-1, keepdims=True)
    centered = inputs - row_mean
    variance = jnp.mean(centered * centered, axis=-1, keepdims=True)
    inverse = lax.rsqrt(variance + epsilon)
    normed = centered * inverse
    return (normed * norm_gain + norm_shift, normed, inverse)


def norm_back(grad_out, normed, inverse, norm_gain):
    scaled = grad_out * norm_gain
    first_mean = jnp.mean(scaled, axis=-1, keepdims=True)
    second_mean = jnp.mean(scaled * normed, axis=-1, keepdims=True)
    return inverse * (scaled - first_mean - normed * second_mean)


def gather_weights(
    first_gain,
    first_shift,
    inward_weight,
    query_bias,
    value_bias,
    outward_weight,
    outward_bias,
    second_gain,
    second_shift,
    expand_weight,
    expand_bias,
    shrink_weight,
    shrink_bias,
):
    return (
        lax.all_gather(first_gain, "fsdp", axis=0, tiled=True),
        lax.all_gather(first_shift, "fsdp", axis=0, tiled=True),
        lax.all_gather(inward_weight, "fsdp", axis=0, tiled=True),
        lax.all_gather(query_bias, "fsdp", axis=0, tiled=True),
        lax.all_gather(value_bias, "fsdp", axis=0, tiled=True),
        lax.all_gather(outward_weight, "fsdp", axis=0, tiled=True),
        lax.all_gather(outward_bias, "fsdp", axis=0, tiled=True),
        lax.all_gather(second_gain, "fsdp", axis=0, tiled=True),
        lax.all_gather(second_shift, "fsdp", axis=0, tiled=True),
        lax.all_gather(expand_weight, "fsdp", axis=0, tiled=True),
        lax.all_gather(expand_bias, "fsdp", axis=0, tiled=True),
        lax.all_gather(shrink_weight, "fsdp", axis=0, tiled=True),
        lax.all_gather(shrink_bias, "fsdp", axis=0, tiled=True),
    )


def attend_scores(query_heads, key_heads, key_valid, scale):
    scores = (
        jnp.einsum("cqhe,ckhe->chqk", query_heads, key_heads, preferred_element_type=jnp.float32)
        * scale
    )
    return jnp.where(key_valid[:, None, None, :], scores, -1e30)


def forward(tokens32, key_valid, row_valid, gathered):
    (
        first_gain,
        first_shift,
        inward_weight,
        query_bias,
        value_bias,
        outward_weight,
        outward_bias,
        second_gain,
        second_shift,
        expand_weight,
        expand_bias,
        shrink_weight,
        shrink_bias,
    ) = gathered
    clip_count, seg_rows, model_width = tokens32.shape
    head_size = model_width // HEADS
    scale = head_size ** (-0.5)
    affine_first, normed_first, inverse_first = norm_rows(
        tokens32, first_gain.astype(jnp.float32), first_shift.astype(jnp.float32)
    )
    lowered_first = affine_first.astype(jnp.bfloat16)
    merged_bias = jnp.concatenate([query_bias, jnp.zeros_like(query_bias), value_bias]).astype(
        jnp.float32
    )
    project = (
        jnp.einsum("csd,de->cse", lowered_first, inward_weight, preferred_element_type=jnp.float32)
        + merged_bias
    )
    queries = project[..., :model_width].astype(jnp.bfloat16)
    key_local = project[..., model_width : 2 * model_width].astype(jnp.bfloat16)
    value_local = project[..., 2 * model_width :].astype(jnp.bfloat16)
    key_all, value_all = (
        lax.all_gather(key_local, "seq", axis=1, tiled=True),
        lax.all_gather(value_local, "seq", axis=1, tiled=True),
    )
    slot_count = key_all.shape[1]
    query_heads = queries.reshape(clip_count, seg_rows, HEADS, head_size)
    key_heads = key_all.reshape(clip_count, slot_count, HEADS, head_size)
    value_heads = value_all.reshape(clip_count, slot_count, HEADS, head_size)
    scores = attend_scores(query_heads, key_heads, key_valid, scale)
    row_top = jnp.max(scores, axis=-1, keepdims=True)
    row_total = jnp.sum(jnp.exp(scores - row_top), axis=-1, keepdims=True)
    log_total = row_top + jnp.log(row_total)
    soft_low = jnp.exp(scores - log_total).astype(jnp.bfloat16)
    blended = jnp.einsum(
        "chqk,ckhe->cqhe", soft_low, value_heads, preferred_element_type=jnp.float32
    )
    blended = blended.reshape(clip_count, seg_rows, model_width).astype(jnp.bfloat16)
    branch = jnp.einsum(
        "csd,de->cse", blended, outward_weight, preferred_element_type=jnp.float32
    ) + outward_bias.astype(jnp.float32)
    middle = tokens32 + branch
    affine_second, normed_second, inverse_second = norm_rows(
        middle, second_gain.astype(jnp.float32), second_shift.astype(jnp.float32)
    )
    lowered_second = affine_second.astype(jnp.bfloat16)
    hidden = jnp.einsum(
        "csd,df->csf", lowered_second, expand_weight, preferred_element_type=jnp.float32
    ) + expand_bias.astype(jnp.float32)
    active = jax.nn.gelu(hidden, approximate=False).astype(jnp.bfloat16)
    branch_second = jnp.einsum(
        "csf,fd->csd", active, shrink_weight, preferred_element_type=jnp.float32
    ) + shrink_bias.astype(jnp.float32)
    result = middle + branch_second
    output = jnp.where(row_valid, result, 0.0).astype(jnp.bfloat16)
    return {
        "normed_first": normed_first,
        "inverse_first": inverse_first,
        "lowered_first": lowered_first,
        "query_heads": query_heads,
        "key_heads": key_heads,
        "value_heads": value_heads,
        "log_total": log_total,
        "blended": blended,
        "normed_second": normed_second,
        "inverse_second": inverse_second,
        "lowered_second": lowered_second,
        "hidden": hidden,
        "active": active,
        "output": output,
    }


def gelu_exact(inputs):
    return jax.nn.gelu(inputs, approximate=False)


def backward(saved, gathered, upstream32, key_valid, row_valid):
    (
        first_gain,
        first_shift,
        inward_weight,
        query_bias,
        value_bias,
        outward_weight,
        outward_bias,
        second_gain,
        second_shift,
        expand_weight,
        expand_bias,
        shrink_weight,
        shrink_bias,
    ) = gathered
    clip_count, seg_rows, model_width = upstream32.shape
    head_size = model_width // HEADS
    scale = head_size ** (-0.5)
    grad_result = jnp.where(row_valid, upstream32, 0.0)
    grad_low_second = grad_result.astype(jnp.bfloat16)
    shrink_weight_grad = jnp.einsum(
        "csf,csd->fd", saved["active"], grad_low_second, preferred_element_type=jnp.float32
    )
    shrink_bias_grad = jnp.sum(grad_low_second.astype(jnp.float32), axis=(0, 1))
    grad_active = jnp.einsum(
        "csd,fd->csf", grad_low_second, shrink_weight, preferred_element_type=jnp.float32
    )
    gelu_value, gelu_pull = jax.vjp(gelu_exact, saved["hidden"])
    grad_hidden = gelu_pull(grad_active)[0].astype(jnp.bfloat16)
    expand_weight_grad = jnp.einsum(
        "csd,csf->df", saved["lowered_second"], grad_hidden, preferred_element_type=jnp.float32
    )
    expand_bias_grad = jnp.sum(grad_hidden.astype(jnp.float32), axis=(0, 1))
    grad_second = jnp.einsum(
        "csf,df->csd", grad_hidden, expand_weight, preferred_element_type=jnp.float32
    )
    second_gain_grad = jnp.sum(grad_second * saved["normed_second"], axis=(0, 1))
    second_shift_grad = jnp.sum(grad_second, axis=(0, 1))
    grad_middle = grad_result + norm_back(
        grad_second,
        saved["normed_second"],
        saved["inverse_second"],
        second_gain.astype(jnp.float32),
    )
    grad_low_first = grad_middle.astype(jnp.bfloat16)
    outward_weight_grad = jnp.einsum(
        "csd,cse->de", saved["blended"], grad_low_first, preferred_element_type=jnp.float32
    )
    outward_bias_grad = jnp.sum(grad_low_first.astype(jnp.float32), axis=(0, 1))
    grad_blended = jnp.einsum(
        "cse,de->csd", grad_low_first, outward_weight, preferred_element_type=jnp.float32
    )
    grad_blended = grad_blended.astype(jnp.bfloat16).reshape(clip_count, seg_rows, HEADS, head_size)
    query_heads = saved["query_heads"]
    key_heads = saved["key_heads"]
    value_heads = saved["value_heads"]
    slot_count = key_heads.shape[1]
    scores = attend_scores(query_heads, key_heads, key_valid, scale)
    soft = jnp.exp(scores - saved["log_total"])
    soft_low = soft.astype(jnp.bfloat16)
    grad_soft = jnp.einsum(
        "cqhe,ckhe->chqk", grad_blended, value_heads, preferred_element_type=jnp.float32
    )
    grad_scores = soft * (grad_soft - jnp.sum(grad_soft * soft, axis=-1, keepdims=True))
    grad_scores = grad_scores.astype(jnp.bfloat16)
    grad_queries = (
        jnp.einsum("chqk,ckhe->cqhe", grad_scores, key_heads, preferred_element_type=jnp.float32)
        * scale
    )
    grad_queries = grad_queries.astype(jnp.bfloat16).reshape(clip_count, seg_rows, model_width)
    grad_keys_part = (
        jnp.einsum("chqk,cqhe->ckhe", grad_scores, query_heads, preferred_element_type=jnp.float32)
        * scale
    )
    grad_values_part = jnp.einsum(
        "chqk,cqhe->ckhe", soft_low, grad_blended, preferred_element_type=jnp.float32
    )
    grad_keys_part = grad_keys_part.reshape(clip_count, slot_count, model_width)
    grad_values_part = grad_values_part.reshape(clip_count, slot_count, model_width)
    grad_keys, grad_values = (
        lax.psum_scatter(
            grad_keys_part.astype(jnp.bfloat16), "seq", scatter_dimension=1, tiled=True
        ).astype(jnp.float32),
        lax.psum_scatter(
            grad_values_part.astype(jnp.bfloat16), "seq", scatter_dimension=1, tiled=True
        ).astype(jnp.float32),
    )
    grad_keys = grad_keys.astype(jnp.bfloat16)
    grad_values = grad_values.astype(jnp.bfloat16)
    grad_project = jnp.concatenate([grad_queries, grad_keys, grad_values], axis=-1)
    inward_weight_grad = jnp.einsum(
        "csd,cse->de", saved["lowered_first"], grad_project, preferred_element_type=jnp.float32
    )
    query_bias_grad = jnp.sum(grad_queries.astype(jnp.float32), axis=(0, 1))
    value_bias_grad = jnp.sum(grad_values.astype(jnp.float32), axis=(0, 1))
    grad_first = jnp.einsum(
        "cse,de->csd", grad_project, inward_weight, preferred_element_type=jnp.float32
    )
    first_gain_grad = jnp.sum(grad_first * saved["normed_first"], axis=(0, 1))
    first_shift_grad = jnp.sum(grad_first, axis=(0, 1))
    tokens_grad = grad_middle + norm_back(
        grad_first, saved["normed_first"], saved["inverse_first"], first_gain.astype(jnp.float32)
    )
    weight_shares = (
        lax.psum_scatter(first_gain_grad, ("fsdp", "seq"), scatter_dimension=0, tiled=True),
        lax.psum_scatter(first_shift_grad, ("fsdp", "seq"), scatter_dimension=0, tiled=True),
        lax.psum_scatter(inward_weight_grad, ("fsdp", "seq"), scatter_dimension=0, tiled=True),
        lax.psum_scatter(query_bias_grad, ("fsdp", "seq"), scatter_dimension=0, tiled=True),
        lax.psum_scatter(value_bias_grad, ("fsdp", "seq"), scatter_dimension=0, tiled=True),
        lax.psum_scatter(outward_weight_grad, ("fsdp", "seq"), scatter_dimension=0, tiled=True),
        lax.psum_scatter(outward_bias_grad, ("fsdp", "seq"), scatter_dimension=0, tiled=True),
        lax.psum_scatter(second_gain_grad, ("fsdp", "seq"), scatter_dimension=0, tiled=True),
        lax.psum_scatter(second_shift_grad, ("fsdp", "seq"), scatter_dimension=0, tiled=True),
        lax.psum_scatter(expand_weight_grad, ("fsdp", "seq"), scatter_dimension=0, tiled=True),
        lax.psum_scatter(expand_bias_grad, ("fsdp", "seq"), scatter_dimension=0, tiled=True),
        lax.psum_scatter(shrink_weight_grad, ("fsdp", "seq"), scatter_dimension=0, tiled=True),
        lax.psum_scatter(shrink_bias_grad, ("fsdp", "seq"), scatter_dimension=0, tiled=True),
    )
    return (tokens_grad, weight_shares)


def shards(
    tokens,
    visible,
    first_gain,
    first_shift,
    inward_weight,
    query_bias,
    value_bias,
    outward_weight,
    outward_bias,
    second_gain,
    second_shift,
    expand_weight,
    expand_bias,
    shrink_weight,
    shrink_bias,
    upstream,
):
    clip_count, seg_rows, model_width = tokens.shape
    slot_count = seg_rows * lax.axis_size("seq")
    local_start = lax.axis_index("seq") * seg_rows
    row_positions = local_start + jnp.arange(seg_rows, dtype=jnp.int32)
    row_valid = (row_positions[None, :] < visible[:, None])[..., None]
    key_valid = jnp.arange(slot_count, dtype=jnp.int32)[None, :] < visible[:, None]
    tokens32 = tokens.astype(jnp.float32)
    upstream32 = upstream.astype(jnp.float32)
    gathered = gather_weights(
        first_gain,
        first_shift,
        inward_weight,
        query_bias,
        value_bias,
        outward_weight,
        outward_bias,
        second_gain,
        second_shift,
        expand_weight,
        expand_bias,
        shrink_weight,
        shrink_bias,
    )
    saved = forward(tokens32, key_valid, row_valid, gathered)
    layer_out = saved["output"]
    gathered = gather_weights(
        first_gain,
        first_shift,
        inward_weight,
        query_bias,
        value_bias,
        outward_weight,
        outward_bias,
        second_gain,
        second_shift,
        expand_weight,
        expand_bias,
        shrink_weight,
        shrink_bias,
    )
    saved = forward(tokens32, key_valid, row_valid, gathered)
    tokens_grad, shares = backward(saved, gathered, upstream32, key_valid, row_valid)
    return (
        layer_out,
        tokens_grad,
        shares[0],
        shares[1],
        shares[2],
        shares[3],
        shares[4],
        shares[5],
        shares[6],
        shares[7],
        shares[8],
        shares[9],
        shares[10],
        shares[11],
        shares[12],
    )


F32 = jnp.float32
BF16 = jnp.bfloat16
MESH = pl.DeviceIdType.MESH
SENDS, RECVS, LOCALS = 43, 123, 19
SLAB = 8


def matmul(a, b):
    return lax.dot_general(a, b, (((1,), (0,)), ((), ())), preferred_element_type=F32)


def matmul_bt(a, b):
    return lax.dot_general(a, b, (((1,), (1,)), ((), ())), preferred_element_type=F32)


def matmul_at(a, b):
    return lax.dot_general(a, b, (((0,), (0,)), ((), ())), preferred_element_type=F32)


def row_stats(x):
    mean = jnp.mean(x, axis=-1, keepdims=True)
    centered = x - mean
    inverse = lax.rsqrt(jnp.mean(centered * centered, axis=-1, keepdims=True) + epsilon)
    return centered * inverse, inverse


def row_norm_back(grad, normed, inverse, gain):
    scaled = grad * gain
    first_mean = jnp.mean(scaled, axis=-1, keepdims=True)
    second_mean = jnp.mean(scaled * normed, axis=-1, keepdims=True)
    return inverse * (scaled - first_mean - normed * second_mean)


class Place:
    def __init__(self, groups):
        self.groups = groups
        self.f = lax.axis_index("fsdp")
        self.y = lax.axis_index("seq")
        self.r = self.f // 4
        self.xc = self.f % 4
        self.t = self.xc * 2 + self.y
        x, c = self.xc // 2, self.xc % 2
        self.step = {4: 4 - 8 * x, 2: 2 - 4 * c, 1: 1 - 2 * self.y}

    def peer(self, mask):
        at = self.t
        for bit in (4, 2, 1):
            if mask & bit:
                at = at + self.step[bit]
        return at

    def device(self, r, t):
        return (r * 4 + t // 2, t % 2)


def rows(ref, index, size):
    return ref.at[pl.ds(pl.multiple_of(index * size, size), size), :]


def cols(ref, index, size):
    return ref.at[:, pl.ds(pl.multiple_of(index * size, size), size)]


class Wire:
    def __init__(self, place, send_sems, recv_sems, local_sems):
        self.place = place
        self.send_sems, self.recv_sems, self.local_sems = send_sems, recv_sems, local_sems
        self.sends = self.recvs = self.locals = 0
        self.free, self.open_sends = [], []

    def recv_slots(self, count):
        first = self.recvs
        self.recvs += count
        return [self.recv_sems.at[first + i] for i in range(count)]

    def batch(self, whole, far=False):
        spot = self.take()
        self.open_sends.append((lambda: self.describe(whole, whole, spot, self.recv_sems.at[0], self.near()), None, spot, far))
        return spot

    def near(self):
        return (self.place.r, self.place.peer(2))

    def take(self):
        if not self.free:
            self.free.append(self.sends)
            self.sends += 1
        return self.free.pop()

    def describe(self, src, dst, spot, slot, to):
        return pltpu.make_async_remote_copy(
            src_ref=src,
            dst_ref=dst,
            send_sem=self.send_sems.at[spot],
            recv_sem=slot,
            device_id=self.place.device(*to),
            device_id_type=MESH,
        )

    def send(self, src, dst, slot, to, when=None, batch=None):
        spot = self.take() if batch is None else batch

        def make():
            return self.describe(src, dst, spot, slot, to)

        if when is None:
            make().start()
        else:
            pl.when(when)(lambda: make().start())
        if batch is None:
            self.open_sends.append((make, when, spot, to[0] is not self.place.r))

    def settle(self, count=None, slab_only=False):
        count = len(self.open_sends) if count is None else count
        kept = []
        for item in self.open_sends[:count]:
            make, when, spot, far = item
            if slab_only and far:
                kept.append(item)
                continue
            if when is None:
                make().wait_send()
            else:
                pl.when(when)(lambda make=make: make().wait_send())
            self.free.append(spot)
        self.open_sends = kept + self.open_sends[count:]

    def arrived(self, dst, slot, when=None):
        def wait():
            self.describe(dst, dst, 0, slot, self.near()).wait_recv()

        if when is None:
            wait()
        else:
            pl.when(when)(wait)

    def local(self, src, dst, more=()):
        sem = self.local_sems.at[self.locals]
        self.locals += 1
        for one in more or ((src, dst),):
            pltpu.make_async_copy(*one, sem).start()
        return pltpu.make_async_copy(dst, dst, sem)


class SlabGather:
    def __init__(self, wire, at, half, several, apart):
        self.wire, self.at, self.half, self.several, self.apart = wire, at, half, several, apart
        self.slots = wire.recv_slots(11 if apart else 7)
        if not apart:
            self.slots += self.slots[6:7] * 4

    def start(self, whole, halves):
        wire, place, slots = self.wire, self.wire.place, self.slots
        t, r = place.t, place.r
        batch = wire.batch(self.several(3))
        wire.send(halves[0], self.half(t, 0), slots[0], (r, place.peer(4)), batch=batch)
        wire.send(halves[1], self.half(t, 1), slots[3], (r, place.peer(1)), batch=batch)
        wire.send(halves[1], self.half(t, 1), slots[1], (r, place.peer(4)), batch=batch)
        wire.send(halves[0], self.half(t, 0), slots[2], (r, place.peer(1)), batch=batch)
        wire.send(whole, self.at(t), slots[6], (r, place.peer(2)), batch=batch)

    def relay(self):
        wire, place, slots = self.wire, self.wire.place, self.slots
        r, far, near = place.r, place.peer(4), place.peer(1)
        self.passed = wire.batch(self.several(4))
        wire.arrived(self.half(far, 0), slots[0])
        wire.send(self.half(far, 0), self.half(far, 0), slots[4], (r, near), batch=self.passed)
        wire.arrived(self.half(near, 1), slots[3])
        wire.send(self.half(near, 1), self.half(near, 1), slots[5], (r, far), batch=self.passed)
        wire.arrived(self.half(far, 1), slots[1])
        wire.send(self.at(far), self.at(far), slots[7], (r, place.peer(2)), batch=self.passed)
        wire.arrived(self.half(near, 0), slots[2])
        wire.send(self.at(near), self.at(near), slots[8], (r, place.peer(2)), batch=self.passed)

    def forward(self):
        wire, place, slots = self.wire, self.wire.place, self.slots
        across = place.peer(5)
        for h in range(2):
            block = self.half(across, h)
            wire.arrived(block, slots[4 + h])
            wire.send(block, block, slots[9 + h], (place.r, place.peer(2)), batch=self.passed)

    def wait_block(self, mask):
        wire, place, slots = self.wire, self.wire.place, self.slots
        if mask == 7:
            for h in range(2):
                wire.arrived(self.half(place.peer(7), h), slots[9 + h])
        else:
            wire.arrived(self.at(place.peer(mask)), slots[{2: 6, 6: 7, 3: 8}[mask]])

    def wait(self):
        self.wire.arrived(self.several(4), self.slots[6])


class SlabScatter:
    def __init__(self, wire, part, core_in, chip_in, block):
        self.wire, self.part, self.core_in, self.chip_in, self.block = wire, part, core_in, chip_in, block
        self.core_slots = wire.recv_slots(4)
        self.slots = wire.recv_slots(6)
        self.order = (5, 4, 1, 0)

    def cores(self):
        place = self.wire.place
        batch = self.wire.batch(self.core_in)
        for i, mask in enumerate(self.order):
            self.wire.send(
                rows(self.part, place.peer(mask ^ 2), self.block),
                self.core_in.at[i],
                self.core_slots[i],
                (place.r, place.peer(2)),
                batch=batch,
            )

    def half(self, mask, h):
        return rows(self.part, self.wire.place.peer(mask) * 2 + h, self.block // 2)

    def add_core(self, i):
        mask = self.order[i]
        self.wire.arrived(self.core_in.at[i], self.core_slots[i])
        mine = rows(self.part, self.wire.place.peer(mask), self.block)
        mine[...] = (mine[...].astype(F32) + self.core_in[i].astype(F32)).astype(BF16)

    def chips(self):
        wire, place = self.wire, self.wire.place
        far, near = (place.r, place.peer(4)), (place.r, place.peer(1))
        self.passed = wire.batch(self.chip_in)
        self.add_core(0)
        wire.send(self.half(5, 0), self.chip_in.at[0], self.slots[0], far, batch=self.passed)
        wire.send(self.half(5, 1), self.chip_in.at[1], self.slots[1], near, batch=self.passed)
        self.add_core(1)
        wire.send(self.half(4, 0), self.chip_in.at[2], self.slots[2], far, batch=self.passed)
        self.add_core(2)
        wire.send(self.half(1, 1), self.chip_in.at[3], self.slots[3], near, batch=self.passed)
        wire.arrived(self.core_in.at[3], self.core_slots[3])

    def relay(self):
        wire, place = self.wire, self.wire.place
        far, near = (place.r, place.peer(4)), (place.r, place.peer(1))
        for i, (block, to) in enumerate(((self.half(1, 0), near), (self.half(4, 1), far))):
            wire.arrived(self.chip_in.at[i], self.slots[i])
            block[...] = (block[...].astype(F32) + self.chip_in[i].astype(F32)).astype(BF16)
            wire.send(block, self.chip_in.at[4 + i], self.slots[4 + i], to, batch=self.passed)

    def wait(self):
        for i in range(2, 6):
            self.wire.arrived(self.chip_in.at[i], self.slots[i])

    def total(self, first, size):
        mine = self.part[pl.ds(pl.multiple_of(self.wire.place.t * self.block + first, size), size), :].astype(F32)
        mine = mine + self.core_in[3, pl.ds(pl.multiple_of(first, size), size), :].astype(F32)
        h = first // (self.block // 2)
        at = pl.ds(pl.multiple_of(first % (self.block // 2), size), size)
        return mine + self.chip_in[2 + h, at, :].astype(F32) + self.chip_in[4 + h, at, :].astype(F32)


class SlabSwap:
    def __init__(self, wire, source, target, seven):
        self.wire, self.source, self.target, self.seven = wire, source, target, seven
        (self.slot,) = wire.recv_slots(1)

    def start(self):
        place = self.wire.place
        self.own = self.wire.local(self.source(place.t), self.target(place.t))
        batch = self.wire.batch(self.seven)
        for i in (4, 5, 3, 6, 2, 7, 1):
            to = (place.t + i) % SLAB
            self.wire.send(self.source(to), self.target(place.t), self.slot, (place.r, to), batch=batch)

    def wait(self):
        self.wire.arrived(self.seven, self.slot)
        self.own.wait()


class GroupGather:
    def __init__(self, wire, at):
        self.wire, self.at = wire, at
        self.slots = [None] + wire.recv_slots(3)
        self.first = wire.recvs - 4
        r = wire.place.r
        self.inner, self.outer = (r + 1) // 2 == 1, (r + 1) // 2 != 1

    def start(self, src, dst=None):
        wire, place = self.wire, self.wire.place
        r = place.r
        dst = self.at(r) if dst is None else dst
        wire.send(src, dst, self.slots[1], ((r + 1) % 4, place.t), r != 3)
        wire.send(src, dst, self.slots[3], ((r + 3) % 4, place.t), r != 0)

    def pass_on(self):
        wire, place = self.wire, self.wire.place
        r = place.r
        below, above = (r + 3) % 4, (r + 1) % 4
        for block, slot, to in ((self.at(below), self.slots[1], above), (self.at(above), self.slots[3], below)):
            wire.arrived(block, slot, self.inner)
            wire.send(block, block, self.slots[2], (to, place.t), self.inner)

    def pass_far(self):
        wire, place = self.wire, self.wire.place
        r = place.r
        block = self.at((r + 2) % 4)
        wire.arrived(block, self.slots[2], self.inner)
        slot = wire.recv_sems.at[self.first + (2 * r + 3) % 4]
        wire.send(block, block, slot, ((3 * r + 1) % 4, place.t), self.inner)

    def wait(self):
        wire, r = self.wire, self.wire.place.r
        for i in (1, 2, 3):
            wire.arrived(self.at((r + 4 - i) % 4), self.slots[i], self.outer)


class GroupScatter:
    def __init__(self, wire, out, into, own):
        self.wire, self.out, self.into, self.own = wire, out, into, own
        self.slots = wire.recv_slots(5)
        self.spots = {}
        r = wire.place.r
        self.inner, self.outer = (r + 1) // 2 == 1, (r + 1) // 2 != 1
        low = 1 - r // 2
        self.far, self.next = (r + 1 + 2 * low) % 4, (r + 3 - 2 * low) % 4

        @pl.when(self.outer)
        def _():
            into[2] = jnp.zeros_like(into[2])

    def put(self, k, spot, to, when):
        if k not in self.spots:
            self.spots[k] = self.wire.batch(self.out.at[k], far=True)
        to = (to, self.wire.place.t)
        self.wire.send(self.out.at[k], self.into.at[spot], self.slots[spot], to, when, self.spots[k])

    def start(self, make, hold=False):
        r = self.wire.place.r
        for k, to in enumerate((self.far, (r + 2) % 4, self.next)):
            self.out[k] = make(to).astype(BF16)
            if k < 2 or not hold:
                self.put(k, k, self.next, self.outer)
        self.own[...] = make(r)

    def start_last(self):
        self.put(2, 2, self.next, self.outer)

    def add(self, k, spot):
        self.wire.arrived(self.into.at[spot], self.slots[spot], self.inner)

        @pl.when(self.inner)
        def _():
            self.out[k] = (self.out[k].astype(F32) + self.into[spot].astype(F32)).astype(BF16)

    def relay(self):
        self.add(1, 0)
        self.put(1, 3, self.next, self.inner)
        self.add(2, 1)
        self.put(2, 4, self.next, self.inner)

    def relay_end(self):
        self.add(0, 3)
        self.put(0, 4, self.far, self.inner)

    def total(self):
        self.wire.arrived(self.into.at[2], self.slots[2], self.inner)
        self.wire.arrived(self.into.at[4], self.slots[4])
        return self.own[...] + self.into[2].astype(F32) + self.into[4].astype(F32)


def layer_kernel(
    groups,
    scale,
    tokens,
    upstream,
    visible,
    first_gain,
    first_shift,
    query_bias,
    value_bias,
    outward_bias,
    second_gain,
    second_shift,
    shrink_bias,
    expand_bias,
    w_in,
    w_out,
    w_exp,
    w_shr,
    layer_hbm,
    tokens_hbm,
    in_hbm,
    out_hbm,
    exp_hbm,
    shr_hbm,
    vec_hbm,
    layer_out,
    tokens_grad,
    out_grad,
    shr_grad,
    vec_grad,
    pack,
    small,
    wide_small,
    packs,
    tok_all,
    first_all,
    win,
    wex,
    wsh,
    wo,
    gls,
    gls_all,
    vecs,
    ebias,
    qkv,
    gqkv,
    soft_all,
    blend_t,
    blend,
    middle,
    normed,
    inverses,
    second,
    second_all,
    active,
    ghid,
    slopes,
    part_a,
    part_b,
    part_c,
    part_d,
    core_a,
    core_b,
    core_c,
    core_d,
    chip_a,
    chip_b,
    chip_c,
    chip_d,
    gsec,
    glow,
    gblend,
    gblend_t,
    sh_out,
    sh_in,
    sh_own,
    ex_out,
    ex_in,
    ex_own,
    ex_sum,
    ex_all,
    in_out,
    in_in,
    in_own,
    in_sum,
    in_all,
    ou_out,
    ou_in,
    ou_own,
    gvec,
    gvec_exp,
    gvec_out,
    gvec_in,
    gvec_sum,
    gvec_far,
    send_sems,
    recv_sems,
    local_sems,
):
    place = Place(groups)
    wire = Wire(place, send_sems, recv_sems, local_sems)
    f, y, r, xc, t = place.f, place.y, place.r, place.xc, place.t
    devices = groups * SLAB
    me = r * SLAB + t
    seg, width = tokens.shape
    clips = SLAB // 2
    slots = seg * 2
    total_rows = SLAB * seg
    head2 = qkv.shape[1] // 3
    own_rows = w_in.shape[0]
    slab_rows = own_rows * 4
    share = width // devices
    chunk = wsh.shape[1]
    strip = 32
    tile = 256

    vectors = (
        first_gain,
        first_shift,
        query_bias,
        value_bias,
        outward_bias,
        second_gain,
        second_shift,
        shrink_bias,
    )
    loads = [wire.local(None, small, [(ref, small.at[k]) for k, ref in enumerate(vectors)])]
    loads.append(wire.local(expand_bias, wide_small))
    barrier = pltpu.get_barrier_semaphore()
    for i in range(1, devices):
        to = (me + i) % devices
        pl.semaphore_signal(barrier, inc=1, device_id=place.device(to // SLAB, to % SLAB), device_id_type=MESH)
    for copy in loads:
        copy.wait()
    per_lane = 128 // own_rows
    lines = [jnp.concatenate([small[k].astype(F32)] * per_lane, axis=1) for k in range(8)]
    lines.append(wide_small[...].astype(F32))
    count_here = jnp.full((6, 128), visible[0], jnp.int32).astype(F32)
    pack[...] = jnp.concatenate(lines + [count_here], axis=0).astype(BF16)
    pl.semaphore_wait(barrier, devices - 1)

    (pack_slot,) = wire.recv_slots(1)
    pack_batch = wire.batch(packs.at[pl.ds(0, groups * 4 - 1)])
    for i in range(1, groups * 4):
        to = (f + i) % (groups * 4)
        wire.send(pack, packs.at[f], pack_slot, (to // 4, (to % 4) * 2 + y), batch=pack_batch)
    own_pack = wire.local(pack, packs.at[f])

    in_slots = [None] + wire.recv_slots(3)
    ex_slots = [None] + wire.recv_slots(3)

    def in_piece(index, c):
        return win.at[pl.ds(pl.multiple_of(index * own_rows, own_rows), own_rows), pl.ds(c * head2, head2)]

    def ex_piece(index, c):
        return wex.at[pl.ds(pl.multiple_of(index * own_rows, own_rows), own_rows), pl.ds(c * chunk, chunk)]

    own_in = []
    in_batch = wire.batch(win.at[pl.ds(0, 3 * own_rows), :])
    for i in (2, 3, 1, 0):
        to = ((xc + i) % 4) * 2 + y
        for c in range(3):
            src = w_in.at[:, pl.ds(pl.multiple_of(c * width + to * head2, head2), head2)]
            if i == 0:
                own_in.append((src, in_piece(f, c)))
            else:
                wire.send(src, in_piece(f, c), in_slots[i], (r, to), batch=in_batch)
    own_in = wire.local(None, rows(win, f, own_rows), own_in)

    out_share = w_out.at[pl.ds(pl.multiple_of(y * share, share), share), :]
    own_out = wire.local(out_share, wo.at[r, t])
    group_wo = GroupGather(wire, lambda at: wo.at[at, t])
    group_wo.start(out_share)
    shr_share = w_shr.at[pl.ds(pl.multiple_of(y * chunk, chunk), chunk), :]
    own_shr = wire.local(shr_share, wsh.at[r])
    group_sh = GroupGather(wire, lambda at: wsh.at[at])

    def shr_half(h):
        at = pl.ds(h * (chunk // 2), chunk // 2)
        src = w_shr.at[pl.ds(pl.multiple_of(y * chunk + h * (chunk // 2), chunk // 2), chunk // 2), :]
        group_sh.start(src, wsh.at[r, at])

    shr_half(0)

    def slab_gather(ref, apart=True):
        return SlabGather(
            wire,
            lambda at: rows(ref, at, seg),
            lambda at, h: rows(ref, at * 2 + h, seg // 2),
            lambda count: ref.at[pl.ds(0, count * seg), :],
            apart,
        )

    gather_tok = slab_gather(tok_all)
    gather_tok.start(tokens, [rows(tokens, h, seg // 2) for h in range(2)])

    own_ex = []
    ex_batch = wire.batch(wex.at[pl.ds(0, 3 * own_rows), :])
    for i in (2, 3, 1, 0):
        to = ((xc + i) % 4) * 2 + y
        for c in range(groups):
            src = w_exp.at[:, pl.ds(pl.multiple_of((c * SLAB + to) * chunk, chunk), chunk)]
            if i == 0:
                own_ex.append((src, ex_piece(f, c)))
            else:
                wire.send(src, ex_piece(f, c), ex_slots[i], (r, to), batch=ex_batch)
    own_ex = wire.local(None, rows(wex, f, own_rows), own_ex)

    row_at = y * seg + lax.broadcasted_iota(jnp.int32, (seg, 1), 0)
    row_valid = row_at.astype(F32) < pack[10:11, 0:1].astype(F32)
    gls[...] = jnp.where(row_valid, upstream[...].astype(F32), 0.0).astype(BF16)
    gls_all[pl.ds(pl.multiple_of(t * seg, seg), seg), :] = gls[...]
    gvec[...] = jnp.zeros_like(gvec)
    gvec_exp[...] = jnp.zeros_like(gvec_exp)
    group_shr = GroupScatter(wire, sh_out, sh_in, sh_own)
    group_exp = GroupScatter(wire, ex_out, ex_in, ex_own)
    group_inw = GroupScatter(wire, in_out, in_in, in_own)
    group_out = GroupScatter(wire, ou_out, ou_in, ou_own)

    for i in range(1, 4):
        frm = r * 4 + (xc + 4 - i) % 4
        wire.arrived(rows(win, frm, own_rows), in_slots[i])
    own_in.wait()
    own_out.wait()
    group_wo.pass_on()
    group_in = GroupGather(wire, lambda at: rows(win, at, slab_rows))
    group_in.start(rows(win, r, slab_rows))
    shr_half(1)
    group_wo.pass_far()

    own_pack.wait()
    wire.arrived(packs.at[pl.ds(0, groups * 4 - 1)], pack_slot)
    lane = lax.broadcasted_iota(jnp.int32, (1, 128), 1)
    for j in range(width // 128):
        piece = packs[j * per_lane].astype(F32)
        for k in range(1, per_lane):
            piece = jnp.where(lane >= k * own_rows, packs[j * per_lane + k].astype(F32), piece)
        vecs[:, j * 128 : (j + 1) * 128] = piece
    for c in range(groups):
        both = packs[c * 4 + t // 2].astype(F32)
        ebias[0:1, c * chunk : (c + 1) * chunk] = jnp.where(y == 0, both[8:9], both[9:10])

    def first_norm(src, offset, block):
        def strip_norm(i, carry):
            at = pl.multiple_of(i * strip, strip)
            n, _ = row_stats(src[pl.ds(offset + at, strip), :].astype(F32))
            to = pl.multiple_of(block * seg + at, strip)
            first_all[pl.ds(to, strip), :] = (n * vecs[0:1, :] + vecs[1:2, :]).astype(BF16)
            return carry

        lax.fori_loop(0, seg // strip, strip_norm, 0)

    first_norm(tokens, 0, t)

    def norm_block(mask):
        block = place.peer(mask)
        first_norm(tok_all, pl.multiple_of(block * seg, seg), block)

    gather_tok.relay()
    group_wo.wait()
    gather_wo = SlabGather(
        wire,
        lambda at: wo.at[:, at],
        lambda at, h: wo.at[pl.ds(h * (groups // 2), groups // 2), at],
        lambda count: wo.at[:, pl.ds(0, count)],
        apart=False,
    )
    gather_wo.start(wo.at[:, t], [wo.at[pl.ds(h * (groups // 2), groups // 2), t] for h in range(2)])
    group_in.pass_on()
    norm_block(4)
    norm_block(1)

    gather_tok.forward()

    norm_block(5)
    group_in.pass_far()
    for i in range(1, 4):
        frm = r * 4 + (xc + 4 - i) % 4
        wire.arrived(rows(wex, frm, own_rows), ex_slots[i])
    own_ex.wait()
    group_ex = GroupGather(wire, lambda at: rows(wex, at, slab_rows))
    group_ex.start(rows(wex, r, slab_rows))


    for mask in (2, 6, 3, 7):
        gather_tok.wait_block(mask)
        norm_block(mask)

    gather_wo.relay()
    gather_gls = slab_gather(gls_all, apart=False)
    gather_gls.start(gls, [rows(gls, h, seg // 2) for h in range(2)])
    group_in.wait()
    at_head = pl.ds(pl.multiple_of(t * head2, head2), head2)
    bias = jnp.concatenate([vecs[2:3, at_head], jnp.zeros((1, head2), F32), vecs[3:4, at_head]], axis=1)

    def project(i, carry):
        at = pl.ds(pl.multiple_of(i * tile, tile), tile)
        qkv[at, :] = (matmul(first_all[at, :], win[...]) + bias).astype(BF16)
        return carry

    lax.fori_loop(0, total_rows // tile, project, 0)

    group_sh.pass_on()
    head_size = head2 // 2
    low_half = lane < head_size
    half_masks = [low_half.astype(F32).astype(BF16), (1.0 - low_half.astype(F32)).astype(BF16)]
    key_at = lax.broadcasted_iota(jnp.int32, (1, slots), 1).astype(F32)

    def attend(i, carry):
        at = pl.ds(pl.multiple_of(i * slots, slots), slots)
        q = qkv[at, 0:head2]
        k = qkv[at, head2 : 2 * head2]
        v = qkv[at, 2 * head2 : 3 * head2]
        count = packs[r * 4 + i].astype(F32)[10:11, 0:1]
        key_valid = key_at < count
        halves = []
        for h in range(2):
            scores = matmul_bt(q * half_masks[h], k) * scale
            scores = jnp.where(key_valid, scores, -1e30)
            top = jnp.max(scores, axis=-1, keepdims=True)
            soft = jnp.exp(scores - top)
            soft = soft * (1.0 / jnp.sum(soft, axis=-1, keepdims=True))
            soft_all[i * 2 + h] = soft
            halves.append(matmul(soft.astype(BF16), v))
        blend_t[at, :] = jnp.where(low_half, halves[0], halves[1]).astype(BF16)
        return carry

    lax.fori_loop(0, clips, attend, 0)

    group_ex.pass_on()
    swap_blend = SlabSwap(wire, lambda at: rows(blend_t, at, seg), lambda at: cols(blend, at, head2), blend.at[:, 0 : 7 * head2])
    swap_blend.start()
    gather_wo.forward()

    gather_gls.relay()
    gather_wo.wait()
    swap_blend.wait()
    group_ex.pass_far()
    wide = 256
    for j in range(width // wide):
        at = slice(j * wide, (j + 1) * wide)
        product = matmul(blend[...], wo[:, :, :, at].reshape(width, wide))
        middle[:, at] = tokens[:, at].astype(F32) + (product + vecs[4:5, at])

    own_second_rows = pl.multiple_of(t * seg, seg)

    def second_norm(i, carry):
        at = pl.ds(pl.multiple_of(i * strip, strip), strip)
        n, inverse = row_stats(middle[at, :])
        normed[at, :] = n
        inverses[at, :] = jnp.broadcast_to(inverse, (strip, 128))
        low = (n * vecs[5:6, :] + vecs[6:7, :]).astype(BF16)
        second[at, :] = low
        second_all[pl.ds(pl.multiple_of(own_second_rows + i * strip, strip), strip), :] = low
        return carry

    lax.fori_loop(0, seg // strip, second_norm, 0)

    gather_second = slab_gather(second_all)
    gather_second.start(second, [rows(second, h, seg // 2) for h in range(2)])
    gather_gls.forward()
    hidden_units = groups * chunk

    def feed(i, carry):
        at = pl.ds(pl.multiple_of(i * tile, tile), tile)
        hidden = matmul(second_all[at, :], wex[...]) + ebias[0:1, :]
        cdf = 0.5 * (1.0 + lax.erf(hidden * 0.7071067811865476))
        active[at, :] = (hidden * cdf).astype(BF16)
        slopes[at, :] = cdf + hidden * (0.3989422804014327 * jnp.exp(-0.5 * hidden * hidden))
        return carry

    gather_second.relay()
    group_sh.pass_far()
    group_ex.wait()
    core = xc % 2
    beside = xc + 1 - 2 * core
    across = (xc + 2) % 4
    feed(xc, 0)
    gather_second.forward()
    feed(across, 0)
    gather_second.wait_block(2)
    gather_second.wait_block(3)
    feed(beside, 0)
    gather_second.wait_block(6)
    gather_second.wait_block(7)
    feed((beside + 2) % 4, 0)
    gather_gls.wait()
    front_sends = len(wire.open_sends)

    group_shr.start(
        lambda c: matmul_at(active[:, pl.ds(pl.multiple_of(c * chunk, chunk), chunk)], gls_all[...]),
        hold=True,
    )
    group_sh.wait()
    own_shr.wait()

    def feed_back(i, carry):
        at = pl.ds(pl.multiple_of(i * tile, tile), tile)
        grad_active = matmul_bt(gls_all[at, :], wsh[...].reshape(hidden_units, width))
        grad_hidden = (grad_active * slopes[at, :]).astype(BF16)
        ghid[at, :] = grad_hidden
        gvec_exp[...] += jnp.sum(grad_hidden.astype(F32), axis=0, keepdims=True)
        part_a[at, :] = matmul_bt(grad_hidden, wex[...]).astype(BF16)
        return carry

    scatter_second = SlabScatter(wire, part_a, core_a, chip_a, seg)
    lax.fori_loop(0, 2, lambda k, carry: feed_back(1 - core + 2 * k, carry), 0)
    scatter_second.cores()
    lax.fori_loop(0, 2, lambda k, carry: feed_back(core + 2 * k, carry), 0)

    scatter_second.chips()
    group_exp.start(
        lambda c: matmul_at(second_all[:, pl.ds(pl.multiple_of(c * slab_rows, slab_rows), slab_rows)], ghid[...])
    )
    scatter_second.relay()
    group_shr.relay()

    def feed_out(i, carry):
        at = pl.ds(pl.multiple_of(i * tile, tile), tile)
        part_b[at, :] = matmul(active[at, :], wsh[...].reshape(hidden_units, width)).astype(BF16)
        return carry

    lax.fori_loop(0, total_rows // tile, feed_out, 0)
    scatter_result = SlabScatter(wire, part_b, core_b, chip_b, seg)
    scatter_result.cores()

    scatter_second.wait()
    wire.settle(front_sends)

    feed_sends = len(wire.open_sends)

    def second_back(i, carry):
        first = i * strip
        at = pl.ds(pl.multiple_of(first, strip), strip)
        grad = scatter_second.total(first, strip)
        n = normed[at, :]
        back = row_norm_back(grad, n, inverses[at, 0:1], vecs[5:6, :])
        grad_result = gls[at, :].astype(F32)
        grad_middle = grad_result + back
        gsec[at, :] = grad_middle
        low = grad_middle.astype(BF16)
        glow[at, :] = low
        gvec[4:5, :] += jnp.sum(low.astype(F32), axis=0, keepdims=True)
        gvec[5:6, :] += jnp.sum(grad * n, axis=0, keepdims=True)
        gvec[6:7, :] += jnp.sum(grad, axis=0, keepdims=True)
        gvec[7:8, :] += jnp.sum(grad_result, axis=0, keepdims=True)
        return carry

    lax.fori_loop(0, seg // strip, second_back, 0)

    for j in range(width // wide):
        rows_of = slice(j * (groups * wide // width), (j + 1) * (groups * wide // width))
        gblend[:, j * wide : (j + 1) * wide] = matmul_bt(
            glow[...], wo[rows_of].reshape(wide, width)
        ).astype(BF16)
    swap_gblend = SlabSwap(wire, lambda at: cols(gblend, at, head2), lambda at: rows(gblend_t, at, seg), gblend_t.at[pl.ds(0, 7 * seg), :])
    swap_gblend.start()

    for c in range(groups):
        product = matmul_at(blend[:, c * slab_rows : (c + 1) * slab_rows], glow[...])
        for to in range(SLAB):
            part_d[to * seg + c * share : to * seg + (c + 1) * share, :] = product[
                to * share : (to + 1) * share
            ].astype(BF16)
    scatter_out = SlabScatter(wire, part_d, core_d, chip_d, seg)
    scatter_out.cores()

    group_shr.relay_end()
    scatter_out.chips()
    swap_gblend.wait()

    def attend_back(i, carry):
        at = pl.ds(pl.multiple_of(i * slots, slots), slots)
        q = qkv[at, 0:head2]
        k = qkv[at, head2 : 2 * head2]
        v = qkv[at, 2 * head2 : 3 * head2]
        grad = gblend_t[at, :]
        parts = []
        for h in range(2):
            soft = soft_all[i * 2 + h]
            grad_soft = matmul_bt(grad * half_masks[h], v)
            inner = jnp.sum(grad_soft * soft, axis=-1, keepdims=True)
            grad_scores = (soft * (grad_soft - inner)).astype(BF16)
            parts.append(
                (
                    matmul(grad_scores, k) * scale,
                    matmul_at(grad_scores, q) * scale,
                    matmul_at(soft.astype(BF16), grad),
                )
            )
        for c in range(3):
            gqkv[at, c * head2 : (c + 1) * head2] = jnp.where(low_half, parts[0][c], parts[1][c]).astype(BF16)
        return carry

    lax.fori_loop(0, clips, attend_back, 0)

    scatter_out.relay()
    group_exp.relay()
    def project_back(i, carry):
        at = pl.ds(pl.multiple_of(i * tile, tile), tile)
        part_c[at, :] = matmul_bt(gqkv[at, :], win[...]).astype(BF16)
        return carry

    scatter_first = SlabScatter(wire, part_c, core_c, chip_c, seg)
    lax.fori_loop(0, 2, lambda k, carry: project_back(1 - core + 2 * k, carry), 0)
    scatter_first.cores()
    lax.fori_loop(0, 2, lambda k, carry: project_back(core + 2 * k, carry), 0)

    group_inw.start(
        lambda c: matmul_at(first_all[:, pl.ds(pl.multiple_of(c * slab_rows, slab_rows), slab_rows)], gqkv[...]),
        hold=True,
    )
    scatter_first.chips()
    gvec[2:3, at_head] = jnp.sum(gqkv[:, 0:head2].astype(F32), axis=0, keepdims=True)
    gvec[3:4, at_head] = jnp.sum(gqkv[:, 2 * head2 :].astype(F32), axis=0, keepdims=True)

    scatter_out.wait()
    group_out.start(lambda c: scatter_out.total(c * share, share), hold=True)
    group_inw.start_last()
    group_out.start_last()
    scatter_first.relay()
    group_exp.relay_end()
    scatter_result.chips()
    group_inw.relay()
    scatter_first.wait()
    wire.settle(feed_sends, slab_only=True)

    def first_back(i, carry):
        first = i * strip
        at = pl.ds(pl.multiple_of(first, strip), strip)
        grad = scatter_first.total(first, strip)
        n, inverse = row_stats(tokens[at, :].astype(F32))
        tokens_grad[at, :] = gsec[at, :] + row_norm_back(grad, n, inverse, vecs[0:1, :])
        gvec[0:1, :] += jnp.sum(grad * n, axis=0, keepdims=True)
        gvec[1:2, :] += jnp.sum(grad, axis=0, keepdims=True)
        return carry

    lax.fori_loop(0, seg // strip, first_back, 0)
    stores = [wire.local(tokens_grad, tokens_hbm)]

    group_out.relay()
    for to in range(SLAB):
        gvec_out[to] = jnp.concatenate(
            [gvec[:, (c * SLAB + to) * share : (c * SLAB + to + 1) * share] for c in range(groups)], axis=1
        )
    swap_vec = SlabSwap(wire, lambda at: gvec_out.at[at], lambda at: gvec_in.at[at], gvec_in.at[pl.ds(0, 7)])
    swap_vec.start()

    group_inw.relay_end()
    scatter_result.relay()
    ex_sum[...] = group_exp.total().astype(BF16)
    swap_exp = SlabSwap(wire, lambda at: rows(ex_sum, at, share), lambda at: ex_all.at[at], ex_all.at[pl.ds(0, 7)])
    swap_exp.start()
    swap_vec.wait()
    summed = gvec_in[0]
    for i in range(1, SLAB):
        summed = summed + gvec_in[i]
    gvec_sum[0:8] = summed
    for c in range(groups):
        gvec_sum[8 + c : 9 + c] = gvec_exp[0:1, c * chunk : (c + 1) * chunk]
    gvec_sum[8 + groups : 16] = jnp.zeros((8 - groups, 128), F32)
    vec_slots = wire.recv_slots(groups - 1)
    for i in range(1, groups):
        wire.send(gvec_sum, gvec_far.at[i - 1], vec_slots[i - 1], ((r + i) % groups, t))
    group_shr.start_last()
    group_out.relay_end()
    in_sum[...] = group_inw.total().astype(BF16)
    swap_in = SlabSwap(wire, lambda at: rows(in_sum, at, share), lambda at: in_all.at[at], in_all.at[pl.ds(0, 7)])
    swap_in.start()
    scatter_result.wait()

    def finish_out(i, carry):
        first = i * strip
        at = pl.ds(pl.multiple_of(first, strip), strip)
        result = middle[at, :] + (scatter_result.total(first, strip) + vecs[7:8, :])
        spot = y * seg + first + lax.broadcasted_iota(jnp.int32, (strip, 1), 0)
        valid = spot.astype(F32) < pack[10:11, 0:1].astype(F32)
        layer_out[at, :] = jnp.where(valid, result, 0.0).astype(BF16)
        return carry

    lax.fori_loop(0, seg // strip, finish_out, 0)
    stores.append(wire.local(layer_out, layer_hbm))

    out_grad[...] = group_out.total()
    stores.append(wire.local(out_grad, out_hbm))
    shr_grad[...] = group_shr.total()
    stores.append(wire.local(shr_grad, shr_hbm))
    for i in range(1, groups):
        wire.arrived(gvec_far.at[i - 1], vec_slots[i - 1])
    total = gvec_sum[...]
    for i in range(1, groups):
        total = total + gvec_far[i - 1]
    vec_grad[0:8, :] = pltpu.roll(total[0:8], (128 - share * r) % 128, 1)
    line = total[8:9]
    for c in range(1, groups):
        line = jnp.where(r == c, total[8 + c : 9 + c], line)
    vec_grad[8:16, :] = jnp.broadcast_to(line, (8, 128))
    stores.append(wire.local(vec_grad, vec_hbm))
    swap_exp.wait()
    stores.append(wire.local(ex_all, exp_hbm))
    swap_in.wait()
    stores.append(wire.local(in_all, in_hbm))
    for copy in stores:
        copy.wait()
    wire.settle()
    assert (wire.sends, wire.recvs, wire.locals) == (SENDS, RECVS, LOCALS), (wire.sends, wire.recvs, wire.locals)


def output_kernel(
    groups,
    layer_in,
    tokens_in,
    in_pieces,
    out_in,
    exp_pieces,
    shr_in,
    vec_in,
    layer_out,
    tokens_grad,
    first_gain_grad,
    first_shift_grad,
    in_grad,
    query_bias_grad,
    value_bias_grad,
    out_grad,
    outward_bias_grad,
    second_gain_grad,
    second_shift_grad,
    exp_grad,
    expand_bias_grad,
    shr_grad,
    shrink_bias_grad,
    layer_buf,
    tokens_buf,
    in_buf,
    out_buf,
    exp_buf,
    shr_buf,
    vec_buf,
    in_wide,
    exp_wide,
    lines,
    wide_line,
    load_sems,
    store_sems,
):
    share, width = out_buf.shape
    head2, chunk = in_buf.shape[2] // 3, exp_buf.shape[2] // groups
    loads = [
        pltpu.make_async_copy(src, dst, load_sems.at[i])
        for i, (src, dst) in enumerate(
            (
                (vec_in, vec_buf),
                (exp_pieces, exp_buf),
                (in_pieces, in_buf),
                (shr_in, shr_buf),
                (tokens_in, tokens_buf),
                (layer_in, layer_buf),
                (out_in, out_buf),
            )
        )
    ]
    for copy in loads:
        copy.start()
    stores = []

    def store(src, dst):
        stores.append(pltpu.make_async_copy(src, dst, store_sems.at[len(stores)]))
        stores[-1].start()

    loads[0].wait()
    vectors = (
        first_gain_grad,
        first_shift_grad,
        query_bias_grad,
        value_bias_grad,
        outward_bias_grad,
        second_gain_grad,
        second_shift_grad,
        shrink_bias_grad,
    )
    for k, ref in enumerate(vectors):
        lines[k] = vec_buf[k, 0:share]
        store(lines.at[k], ref)
    wide_line[...] = vec_buf[8, :]
    store(wide_line, expand_bias_grad)
    loads[1].wait()
    for frm in range(SLAB):
        for c in range(groups):
            at = (c * SLAB + frm) * chunk
            exp_wide[:, at : at + chunk] = exp_buf[frm, :, c * chunk : (c + 1) * chunk].astype(F32)
    store(exp_wide, exp_grad)
    loads[2].wait()
    for frm in range(SLAB):
        for c in range(3):
            at = c * width + frm * head2
            in_wide[:, at : at + head2] = in_buf[frm, :, c * head2 : (c + 1) * head2].astype(F32)
    store(in_wide, in_grad)
    for copy, src, dst in (
        (loads[3], shr_buf, shr_grad),
        (loads[4], tokens_buf, tokens_grad.at[0]),
        (loads[5], layer_buf, layer_out.at[0]),
        (loads[6], out_buf, out_grad),
    ):
        copy.wait()
        store(src, dst)
    for copy in stores:
        copy.wait()


def fused_shards(
    tokens,
    visible,
    first_gain,
    first_shift,
    inward_weight,
    query_bias,
    value_bias,
    outward_weight,
    outward_bias,
    second_gain,
    second_shift,
    expand_weight,
    expand_bias,
    shrink_weight,
    shrink_bias,
    upstream,
):
    seg, width = tokens.shape[1:]
    groups = lax.axis_size("fsdp") // 4
    devices = groups * SLAB
    own_rows = inward_weight.shape[0]
    hidden = expand_weight.shape[1]
    share = width // devices
    chunk = hidden // devices
    units = groups * chunk
    head2 = width // SLAB
    scale = (width // HEADS) ** (-0.5)
    total_rows = SLAB * seg
    slab_rows = 4 * own_rows
    vmem = pl.BlockSpec(memory_space=pltpu.VMEM)
    anywhere = pl.BlockSpec(memory_space=pl.ANY)
    outs = pl.pallas_call(
        functools.partial(layer_kernel, groups, scale),
        out_shape=(
            jax.ShapeDtypeStruct((seg, width), BF16),
            jax.ShapeDtypeStruct((seg, width), F32),
            jax.ShapeDtypeStruct((SLAB, share, 3 * head2), BF16),
            jax.ShapeDtypeStruct((share, width), F32),
            jax.ShapeDtypeStruct((SLAB, share, units), BF16),
            jax.ShapeDtypeStruct((chunk, width), F32),
            jax.ShapeDtypeStruct((16, 128), F32),
        ),
        in_specs=[vmem, vmem, pl.BlockSpec(memory_space=pltpu.SMEM)] + [anywhere] * 13,
        out_specs=[anywhere] * 7,
        scratch_shapes=[
            pltpu.VMEM((seg, width), BF16),
            pltpu.VMEM((seg, width), F32),
            pltpu.VMEM((share, width), F32),
            pltpu.VMEM((chunk, width), F32),
            pltpu.VMEM((16, 128), F32),
            pltpu.VMEM((16, 128), BF16),
            pltpu.VMEM((8, 1, own_rows), BF16),
            pltpu.VMEM((2, 128), BF16),
            pltpu.VMEM((groups * 4, 16, 128), BF16),
            pltpu.VMEM((total_rows, width), BF16),
            pltpu.VMEM((total_rows, width), BF16),
            pltpu.VMEM((width, 3 * head2), BF16),
            pltpu.VMEM((width, units), BF16),
            pltpu.VMEM((groups, chunk, width), BF16),
            pltpu.VMEM((groups, SLAB, share, width), BF16),
            pltpu.VMEM((seg, width), BF16),
            pltpu.VMEM((total_rows, width), BF16),
            pltpu.VMEM((16, width), F32),
            pltpu.VMEM((8, units), F32),
            pltpu.VMEM((total_rows, 3 * head2), BF16),
            pltpu.VMEM((total_rows, 3 * head2), BF16),
            pltpu.VMEM((SLAB, 2 * seg, 2 * seg), F32),
            pltpu.VMEM((total_rows, head2), BF16),
            pltpu.VMEM((seg, width), BF16),
            pltpu.VMEM((seg, width), F32),
            pltpu.VMEM((seg, width), F32),
            pltpu.VMEM((seg, 128), F32),
            pltpu.VMEM((seg, width), BF16),
            pltpu.VMEM((total_rows, width), BF16),
            pltpu.VMEM((total_rows, units), BF16),
            pltpu.VMEM((total_rows, units), BF16),
            pltpu.VMEM((total_rows, units), F32),
        ]
        + [pltpu.VMEM((total_rows, width), BF16)] * 4
        + [pltpu.VMEM((4, seg, width), BF16)] * 4
        + [pltpu.VMEM((6, seg // 2, width), BF16)] * 4
        + [
            pltpu.VMEM((seg, width), F32),
            pltpu.VMEM((seg, width), BF16),
            pltpu.VMEM((seg, width), BF16),
            pltpu.VMEM((total_rows, head2), BF16),
            pltpu.VMEM((groups - 1, chunk, width), BF16),
            pltpu.VMEM((5, chunk, width), BF16),
            pltpu.VMEM((chunk, width), F32),
            pltpu.VMEM((groups - 1, slab_rows, units), BF16),
            pltpu.VMEM((5, slab_rows, units), BF16),
            pltpu.VMEM((slab_rows, units), F32),
            pltpu.VMEM((slab_rows, units), BF16),
            pltpu.VMEM((SLAB, share, units), BF16),
            pltpu.VMEM((groups - 1, slab_rows, 3 * head2), BF16),
            pltpu.VMEM((5, slab_rows, 3 * head2), BF16),
            pltpu.VMEM((slab_rows, 3 * head2), F32),
            pltpu.VMEM((slab_rows, 3 * head2), BF16),
            pltpu.VMEM((SLAB, share, 3 * head2), BF16),
            pltpu.VMEM((groups - 1, share, width), BF16),
            pltpu.VMEM((5, share, width), BF16),
            pltpu.VMEM((share, width), F32),
            pltpu.VMEM((8, width), F32),
            pltpu.VMEM((1, units), F32),
            pltpu.VMEM((SLAB, 8, 128), F32),
            pltpu.VMEM((SLAB, 8, 128), F32),
            pltpu.VMEM((16, 128), F32),
            pltpu.VMEM((groups - 1, 16, 128), F32),
            pltpu.SemaphoreType.DMA((SENDS,)),
            pltpu.SemaphoreType.DMA((RECVS,)),
            pltpu.SemaphoreType.DMA((LOCALS,)),
        ],
        compiler_params=pltpu.CompilerParams(
            collective_id=0, has_side_effects=True, vmem_limit_bytes=67043328
        ),
        name="layer",
    )(
        tokens.reshape(seg, width),
        upstream.reshape(seg, width),
        visible,
        *(
            vector.reshape(1, own_rows)
            for vector in (
                first_gain,
                first_shift,
                query_bias,
                value_bias,
                outward_bias,
                second_gain,
                second_shift,
                shrink_bias,
            )
        ),
        expand_bias.reshape(2, 128),
        inward_weight,
        outward_weight,
        expand_weight,
        shrink_weight,
    )
    vector = jax.ShapeDtypeStruct((share,), F32)
    return pl.pallas_call(
        functools.partial(output_kernel, groups),
        out_shape=(
            jax.ShapeDtypeStruct((1, seg, width), BF16),
            jax.ShapeDtypeStruct((1, seg, width), F32),
            vector,
            vector,
            jax.ShapeDtypeStruct((share, 3 * width), F32),
            vector,
            vector,
            jax.ShapeDtypeStruct((share, width), F32),
            vector,
            vector,
            vector,
            jax.ShapeDtypeStruct((share, hidden), F32),
            jax.ShapeDtypeStruct((chunk,), F32),
            jax.ShapeDtypeStruct((chunk, width), F32),
            vector,
        ),
        in_specs=[anywhere] * 7,
        out_specs=[anywhere] * 15,
        scratch_shapes=[
            pltpu.VMEM((seg, width), BF16),
            pltpu.VMEM((seg, width), F32),
            pltpu.VMEM((SLAB, share, 3 * head2), BF16),
            pltpu.VMEM((share, width), F32),
            pltpu.VMEM((SLAB, share, units), BF16),
            pltpu.VMEM((chunk, width), F32),
            pltpu.VMEM((16, 128), F32),
            pltpu.VMEM((share, 3 * width), F32),
            pltpu.VMEM((share, hidden), F32),
            pltpu.VMEM((8, share), F32),
            pltpu.VMEM((chunk,), F32),
            pltpu.SemaphoreType.DMA((7,)),
            pltpu.SemaphoreType.DMA((15,)),
        ],
        name="outputs",
    )(*outs)


def fits_fused(mesh, tokens, inward_weight, expand_weight):
    fsdp, seq = mesh.shape["fsdp"], mesh.shape["seq"]
    clips, slots, width = tokens.shape
    devices = fsdp * seq
    return (
        seq == 2
        and clips == fsdp
        and fsdp == 16
        and width // HEADS * 2 == 128
        and width == SLAB * 128
        and slots % 64 == 0
        and width % (16 * devices) == 0
        and 128 % (width // fsdp) == 0
        and width // devices * 4 == 128
        and expand_weight.shape[1] == 128 * devices
    )


def solution(mesh):
    in_specs = (
        P("fsdp", "seq", None),
        P("fsdp"),
        P("fsdp"),
        P("fsdp"),
        P("fsdp", None),
        P("fsdp"),
        P("fsdp"),
        P("fsdp", None),
        P("fsdp"),
        P("fsdp"),
        P("fsdp"),
        P("fsdp", None),
        P("fsdp"),
        P("fsdp", None),
        P("fsdp"),
        P("fsdp", "seq", None),
    )
    out_specs = (
        P("fsdp", "seq", None),
        P("fsdp", "seq", None),
        P(("fsdp", "seq")),
        P(("fsdp", "seq")),
        P(("fsdp", "seq"), None),
        P(("fsdp", "seq")),
        P(("fsdp", "seq")),
        P(("fsdp", "seq"), None),
        P(("fsdp", "seq")),
        P(("fsdp", "seq")),
        P(("fsdp", "seq")),
        P(("fsdp", "seq"), None),
        P(("fsdp", "seq")),
        P(("fsdp", "seq"), None),
        P(("fsdp", "seq")),
    )

    def step(*args):
        body = fused_shards if fits_fused(mesh, args[0], args[4], args[11]) else shards
        return jax.shard_map(body, mesh=mesh, in_specs=in_specs, out_specs=out_specs, check_vma=False)(*args)

    return step
```

```python
import functools

import jax
import jax.numpy as jnp
from jax import lax
from jax.experimental import pallas as pl
from jax.experimental.pallas import tpu as pltpu
from jax.sharding import PartitionSpec as P

HEADS = 16


epsilon = 1e-06


def norm_rows(inputs, norm_gain, norm_shift):
    row_mean = jnp.mean(inputs, axis=-1, keepdims=True)
    centered = inputs - row_mean
    variance = jnp.mean(centered * centered, axis=-1, keepdims=True)
    inverse = lax.rsqrt(variance + epsilon)
    normed = centered * inverse
    return (normed * norm_gain + norm_shift, normed, inverse)


def norm_back(grad_out, normed, inverse, norm_gain):
    scaled = grad_out * norm_gain
    first_mean = jnp.mean(scaled, axis=-1, keepdims=True)
    second_mean = jnp.mean(scaled * normed, axis=-1, keepdims=True)
    return inverse * (scaled - first_mean - normed * second_mean)


def gather_weights(
    first_gain,
    first_shift,
    inward_weight,
    query_bias,
    value_bias,
    outward_weight,
    outward_bias,
    second_gain,
    second_shift,
    expand_weight,
    expand_bias,
    shrink_weight,
    shrink_bias,
):
    return (
        lax.all_gather(first_gain, "fsdp", axis=0, tiled=True),
        lax.all_gather(first_shift, "fsdp", axis=0, tiled=True),
        lax.all_gather(inward_weight, "fsdp", axis=0, tiled=True),
        lax.all_gather(query_bias, "fsdp", axis=0, tiled=True),
        lax.all_gather(value_bias, "fsdp", axis=0, tiled=True),
        lax.all_gather(outward_weight, "fsdp", axis=0, tiled=True),
        lax.all_gather(outward_bias, "fsdp", axis=0, tiled=True),
        lax.all_gather(second_gain, "fsdp", axis=0, tiled=True),
        lax.all_gather(second_shift, "fsdp", axis=0, tiled=True),
        lax.all_gather(expand_weight, "fsdp", axis=0, tiled=True),
        lax.all_gather(expand_bias, "fsdp", axis=0, tiled=True),
        lax.all_gather(shrink_weight, "fsdp", axis=0, tiled=True),
        lax.all_gather(shrink_bias, "fsdp", axis=0, tiled=True),
    )


def attend_scores(query_heads, key_heads, key_valid, scale):
    scores = (
        jnp.einsum("cqhe,ckhe->chqk", query_heads, key_heads, preferred_element_type=jnp.float32)
        * scale
    )
    return jnp.where(key_valid[:, None, None, :], scores, -1e30)


def forward(tokens32, key_valid, row_valid, gathered):
    (
        first_gain,
        first_shift,
        inward_weight,
        query_bias,
        value_bias,
        outward_weight,
        outward_bias,
        second_gain,
        second_shift,
        expand_weight,
        expand_bias,
        shrink_weight,
        shrink_bias,
    ) = gathered
    clip_count, seg_rows, model_width = tokens32.shape
    head_size = model_width // HEADS
    scale = head_size ** (-0.5)
    affine_first, normed_first, inverse_first = norm_rows(
        tokens32, first_gain.astype(jnp.float32), first_shift.astype(jnp.float32)
    )
    lowered_first = affine_first.astype(jnp.bfloat16)
    merged_bias = jnp.concatenate([query_bias, jnp.zeros_like(query_bias), value_bias]).astype(
        jnp.float32
    )
    project = (
        jnp.einsum("csd,de->cse", lowered_first, inward_weight, preferred_element_type=jnp.float32)
        + merged_bias
    )
    queries = project[..., :model_width].astype(jnp.bfloat16)
    key_local = project[..., model_width : 2 * model_width].astype(jnp.bfloat16)
    value_local = project[..., 2 * model_width :].astype(jnp.bfloat16)
    key_all, value_all = (
        lax.all_gather(key_local, "seq", axis=1, tiled=True),
        lax.all_gather(value_local, "seq", axis=1, tiled=True),
    )
    slot_count = key_all.shape[1]
    query_heads = queries.reshape(clip_count, seg_rows, HEADS, head_size)
    key_heads = key_all.reshape(clip_count, slot_count, HEADS, head_size)
    value_heads = value_all.reshape(clip_count, slot_count, HEADS, head_size)
    scores = attend_scores(query_heads, key_heads, key_valid, scale)
    row_top = jnp.max(scores, axis=-1, keepdims=True)
    row_total = jnp.sum(jnp.exp(scores - row_top), axis=-1, keepdims=True)
    log_total = row_top + jnp.log(row_total)
    soft_low = jnp.exp(scores - log_total).astype(jnp.bfloat16)
    blended = jnp.einsum(
        "chqk,ckhe->cqhe", soft_low, value_heads, preferred_element_type=jnp.float32
    )
    blended = blended.reshape(clip_count, seg_rows, model_width).astype(jnp.bfloat16)
    branch = jnp.einsum(
        "csd,de->cse", blended, outward_weight, preferred_element_type=jnp.float32
    ) + outward_bias.astype(jnp.float32)
    middle = tokens32 + branch
    affine_second, normed_second, inverse_second = norm_rows(
        middle, second_gain.astype(jnp.float32), second_shift.astype(jnp.float32)
    )
    lowered_second = affine_second.astype(jnp.bfloat16)
    hidden = jnp.einsum(
        "csd,df->csf", lowered_second, expand_weight, preferred_element_type=jnp.float32
    ) + expand_bias.astype(jnp.float32)
    active = jax.nn.gelu(hidden, approximate=False).astype(jnp.bfloat16)
    branch_second = jnp.einsum(
        "csf,fd->csd", active, shrink_weight, preferred_element_type=jnp.float32
    ) + shrink_bias.astype(jnp.float32)
    result = middle + branch_second
    output = jnp.where(row_valid, result, 0.0).astype(jnp.bfloat16)
    return {
        "normed_first": normed_first,
        "inverse_first": inverse_first,
        "lowered_first": lowered_first,
        "query_heads": query_heads,
        "key_heads": key_heads,
        "value_heads": value_heads,
        "log_total": log_total,
        "blended": blended,
        "normed_second": normed_second,
        "inverse_second": inverse_second,
        "lowered_second": lowered_second,
        "hidden": hidden,
        "active": active,
        "output": output,
    }


def gelu_exact(inputs):
    return jax.nn.gelu(inputs, approximate=False)


def backward(saved, gathered, upstream32, key_valid, row_valid):
    (
        first_gain,
        first_shift,
        inward_weight,
        query_bias,
        value_bias,
        outward_weight,
        outward_bias,
        second_gain,
        second_shift,
        expand_weight,
        expand_bias,
        shrink_weight,
        shrink_bias,
    ) = gathered
    clip_count, seg_rows, model_width = upstream32.shape
    head_size = model_width // HEADS
    scale = head_size ** (-0.5)
    grad_result = jnp.where(row_valid, upstream32, 0.0)
    grad_low_second = grad_result.astype(jnp.bfloat16)
    shrink_weight_grad = jnp.einsum(
        "csf,csd->fd", saved["active"], grad_low_second, preferred_element_type=jnp.float32
    )
    shrink_bias_grad = jnp.sum(grad_low_second.astype(jnp.float32), axis=(0, 1))
    grad_active = jnp.einsum(
        "csd,fd->csf", grad_low_second, shrink_weight, preferred_element_type=jnp.float32
    )
    gelu_value, gelu_pull = jax.vjp(gelu_exact, saved["hidden"])
    grad_hidden = gelu_pull(grad_active)[0].astype(jnp.bfloat16)
    expand_weight_grad = jnp.einsum(
        "csd,csf->df", saved["lowered_second"], grad_hidden, preferred_element_type=jnp.float32
    )
    expand_bias_grad = jnp.sum(grad_hidden.astype(jnp.float32), axis=(0, 1))
    grad_second = jnp.einsum(
        "csf,df->csd", grad_hidden, expand_weight, preferred_element_type=jnp.float32
    )
    second_gain_grad = jnp.sum(grad_second * saved["normed_second"], axis=(0, 1))
    second_shift_grad = jnp.sum(grad_second, axis=(0, 1))
    grad_middle = grad_result + norm_back(
        grad_second,
        saved["normed_second"],
        saved["inverse_second"],
        second_gain.astype(jnp.float32),
    )
    grad_low_first = grad_middle.astype(jnp.bfloat16)
    outward_weight_grad = jnp.einsum(
        "csd,cse->de", saved["blended"], grad_low_first, preferred_element_type=jnp.float32
    )
    outward_bias_grad = jnp.sum(grad_low_first.astype(jnp.float32), axis=(0, 1))
    grad_blended = jnp.einsum(
        "cse,de->csd", grad_low_first, outward_weight, preferred_element_type=jnp.float32
    )
    grad_blended = grad_blended.astype(jnp.bfloat16).reshape(clip_count, seg_rows, HEADS, head_size)
    query_heads = saved["query_heads"]
    key_heads = saved["key_heads"]
    value_heads = saved["value_heads"]
    slot_count = key_heads.shape[1]
    scores = attend_scores(query_heads, key_heads, key_valid, scale)
    soft = jnp.exp(scores - saved["log_total"])
    soft_low = soft.astype(jnp.bfloat16)
    grad_soft = jnp.einsum(
        "cqhe,ckhe->chqk", grad_blended, value_heads, preferred_element_type=jnp.float32
    )
    grad_scores = soft * (grad_soft - jnp.sum(grad_soft * soft, axis=-1, keepdims=True))
    grad_scores = grad_scores.astype(jnp.bfloat16)
    grad_queries = (
        jnp.einsum("chqk,ckhe->cqhe", grad_scores, key_heads, preferred_element_type=jnp.float32)
        * scale
    )
    grad_queries = grad_queries.astype(jnp.bfloat16).reshape(clip_count, seg_rows, model_width)
    grad_keys_part = (
        jnp.einsum("chqk,cqhe->ckhe", grad_scores, query_heads, preferred_element_type=jnp.float32)
        * scale
    )
    grad_values_part = jnp.einsum(
        "chqk,cqhe->ckhe", soft_low, grad_blended, preferred_element_type=jnp.float32
    )
    grad_keys_part = grad_keys_part.reshape(clip_count, slot_count, model_width)
    grad_values_part = grad_values_part.reshape(clip_count, slot_count, model_width)
    grad_keys, grad_values = (
        lax.psum_scatter(
            grad_keys_part.astype(jnp.bfloat16), "seq", scatter_dimension=1, tiled=True
        ).astype(jnp.float32),
        lax.psum_scatter(
            grad_values_part.astype(jnp.bfloat16), "seq", scatter_dimension=1, tiled=True
        ).astype(jnp.float32),
    )
    grad_keys = grad_keys.astype(jnp.bfloat16)
    grad_values = grad_values.astype(jnp.bfloat16)
    grad_project = jnp.concatenate([grad_queries, grad_keys, grad_values], axis=-1)
    inward_weight_grad = jnp.einsum(
        "csd,cse->de", saved["lowered_first"], grad_project, preferred_element_type=jnp.float32
    )
    query_bias_grad = jnp.sum(grad_queries.astype(jnp.float32), axis=(0, 1))
    value_bias_grad = jnp.sum(grad_values.astype(jnp.float32), axis=(0, 1))
    grad_first = jnp.einsum(
        "cse,de->csd", grad_project, inward_weight, preferred_element_type=jnp.float32
    )
    first_gain_grad = jnp.sum(grad_first * saved["normed_first"], axis=(0, 1))
    first_shift_grad = jnp.sum(grad_first, axis=(0, 1))
    tokens_grad = grad_middle + norm_back(
        grad_first, saved["normed_first"], saved["inverse_first"], first_gain.astype(jnp.float32)
    )
    weight_shares = (
        lax.psum_scatter(first_gain_grad, ("fsdp", "seq"), scatter_dimension=0, tiled=True),
        lax.psum_scatter(first_shift_grad, ("fsdp", "seq"), scatter_dimension=0, tiled=True),
        lax.psum_scatter(inward_weight_grad, ("fsdp", "seq"), scatter_dimension=0, tiled=True),
        lax.psum_scatter(query_bias_grad, ("fsdp", "seq"), scatter_dimension=0, tiled=True),
        lax.psum_scatter(value_bias_grad, ("fsdp", "seq"), scatter_dimension=0, tiled=True),
        lax.psum_scatter(outward_weight_grad, ("fsdp", "seq"), scatter_dimension=0, tiled=True),
        lax.psum_scatter(outward_bias_grad, ("fsdp", "seq"), scatter_dimension=0, tiled=True),
        lax.psum_scatter(second_gain_grad, ("fsdp", "seq"), scatter_dimension=0, tiled=True),
        lax.psum_scatter(second_shift_grad, ("fsdp", "seq"), scatter_dimension=0, tiled=True),
        lax.psum_scatter(expand_weight_grad, ("fsdp", "seq"), scatter_dimension=0, tiled=True),
        lax.psum_scatter(expand_bias_grad, ("fsdp", "seq"), scatter_dimension=0, tiled=True),
        lax.psum_scatter(shrink_weight_grad, ("fsdp", "seq"), scatter_dimension=0, tiled=True),
        lax.psum_scatter(shrink_bias_grad, ("fsdp", "seq"), scatter_dimension=0, tiled=True),
    )
    return (tokens_grad, weight_shares)


def shards(
    tokens,
    visible,
    first_gain,
    first_shift,
    inward_weight,
    query_bias,
    value_bias,
    outward_weight,
    outward_bias,
    second_gain,
    second_shift,
    expand_weight,
    expand_bias,
    shrink_weight,
    shrink_bias,
    upstream,
):
    clip_count, seg_rows, model_width = tokens.shape
    slot_count = seg_rows * lax.axis_size("seq")
    local_start = lax.axis_index("seq") * seg_rows
    row_positions = local_start + jnp.arange(seg_rows, dtype=jnp.int32)
    row_valid = (row_positions[None, :] < visible[:, None])[..., None]
    key_valid = jnp.arange(slot_count, dtype=jnp.int32)[None, :] < visible[:, None]
    tokens32 = tokens.astype(jnp.float32)
    upstream32 = upstream.astype(jnp.float32)
    gathered = gather_weights(
        first_gain,
        first_shift,
        inward_weight,
        query_bias,
        value_bias,
        outward_weight,
        outward_bias,
        second_gain,
        second_shift,
        expand_weight,
        expand_bias,
        shrink_weight,
        shrink_bias,
    )
    saved = forward(tokens32, key_valid, row_valid, gathered)
    layer_out = saved["output"]
    gathered = gather_weights(
        first_gain,
        first_shift,
        inward_weight,
        query_bias,
        value_bias,
        outward_weight,
        outward_bias,
        second_gain,
        second_shift,
        expand_weight,
        expand_bias,
        shrink_weight,
        shrink_bias,
    )
    saved = forward(tokens32, key_valid, row_valid, gathered)
    tokens_grad, shares = backward(saved, gathered, upstream32, key_valid, row_valid)
    return (
        layer_out,
        tokens_grad,
        shares[0],
        shares[1],
        shares[2],
        shares[3],
        shares[4],
        shares[5],
        shares[6],
        shares[7],
        shares[8],
        shares[9],
        shares[10],
        shares[11],
        shares[12],
    )


F32 = jnp.float32
BF16 = jnp.bfloat16
MESH = pl.DeviceIdType.MESH
SENDS, RECVS, LOCALS = 42, 123, 22
SLAB = 8


def matmul(a, b):
    return lax.dot_general(a, b, (((1,), (0,)), ((), ())), preferred_element_type=F32)


def matmul_bt(a, b):
    return lax.dot_general(a, b, (((1,), (1,)), ((), ())), preferred_element_type=F32)


def matmul_at(a, b):
    return lax.dot_general(a, b, (((0,), (0,)), ((), ())), preferred_element_type=F32)


def row_stats(x):
    mean = jnp.mean(x, axis=-1, keepdims=True)
    centered = x - mean
    inverse = lax.rsqrt(jnp.mean(centered * centered, axis=-1, keepdims=True) + epsilon)
    return centered * inverse, inverse


def row_norm_back(grad, normed, inverse, gain):
    scaled = grad * gain
    first_mean = jnp.mean(scaled, axis=-1, keepdims=True)
    second_mean = jnp.mean(scaled * normed, axis=-1, keepdims=True)
    return inverse * (scaled - first_mean - normed * second_mean)


class Place:
    def __init__(self, groups):
        self.groups = groups
        self.f = lax.axis_index("fsdp")
        self.y = lax.axis_index("seq")
        self.r = self.f // 4
        self.xc = self.f % 4
        self.t = self.xc * 2 + self.y
        x, c = self.xc // 2, self.xc % 2
        self.step = {4: 4 - 8 * x, 2: 2 - 4 * c, 1: 1 - 2 * self.y}

    def peer(self, mask):
        at = self.t
        for bit in (4, 2, 1):
            if mask & bit:
                at = at + self.step[bit]
        return at

    def device(self, r, t):
        return (r * 4 + t // 2, t % 2)


def rows(ref, index, size):
    return ref.at[pl.ds(pl.multiple_of(index * size, size), size), :]


def cols(ref, index, size):
    return ref.at[:, pl.ds(pl.multiple_of(index * size, size), size)]


class Wire:
    def __init__(self, place, send_sems, recv_sems, local_sems):
        self.place = place
        self.send_sems, self.recv_sems, self.local_sems = send_sems, recv_sems, local_sems
        self.sends = self.recvs = self.locals = 0
        self.free, self.open_sends = [], []

    def recv_slots(self, count):
        first = self.recvs
        self.recvs += count
        return [self.recv_sems.at[first + i] for i in range(count)]

    def batch(self, whole, far=False):
        spot = self.take()
        self.open_sends.append((lambda: self.describe(whole, whole, spot, self.recv_sems.at[0], self.near()), None, spot, far))
        return spot

    def near(self):
        return (self.place.r, self.place.peer(2))

    def take(self):
        if not self.free:
            self.free.append(self.sends)
            self.sends += 1
        return self.free.pop()

    def describe(self, src, dst, spot, slot, to):
        return pltpu.make_async_remote_copy(
            src_ref=src,
            dst_ref=dst,
            send_sem=self.send_sems.at[spot],
            recv_sem=slot,
            device_id=self.place.device(*to),
            device_id_type=MESH,
        )

    def send(self, src, dst, slot, to, when=None, batch=None):
        spot = self.take() if batch is None else batch

        def make():
            return self.describe(src, dst, spot, slot, to)

        if when is None:
            make().start()
        else:
            pl.when(when)(lambda: make().start())
        if batch is None:
            self.open_sends.append((make, when, spot, to[0] is not self.place.r))

    def settle(self, count=None, slab_only=False):
        count = len(self.open_sends) if count is None else count
        kept = []
        for item in self.open_sends[:count]:
            make, when, spot, far = item
            if slab_only and far:
                kept.append(item)
                continue
            if when is None:
                make().wait_send()
            else:
                pl.when(when)(lambda make=make: make().wait_send())
            self.free.append(spot)
        self.open_sends = kept + self.open_sends[count:]

    def arrived(self, dst, slot, when=None):
        def wait():
            self.describe(dst, dst, 0, slot, self.near()).wait_recv()

        if when is None:
            wait()
        else:
            pl.when(when)(wait)

    def local(self, src, dst, more=()):
        sem = self.local_sems.at[self.locals]
        self.locals += 1
        for one in more or ((src, dst),):
            pltpu.make_async_copy(*one, sem).start()
        return pltpu.make_async_copy(dst, dst, sem)


class SlabGather:
    def __init__(self, wire, at, half, several, apart):
        self.wire, self.at, self.half, self.several, self.apart = wire, at, half, several, apart
        self.slots = wire.recv_slots(11 if apart else 7)
        if not apart:
            self.slots += self.slots[6:7] * 4

    def start(self, whole, halves):
        wire, place, slots = self.wire, self.wire.place, self.slots
        t, r = place.t, place.r
        batch = wire.batch(self.several(3))
        wire.send(halves[0], self.half(t, 0), slots[0], (r, place.peer(4)), batch=batch)
        wire.send(halves[1], self.half(t, 1), slots[3], (r, place.peer(1)), batch=batch)
        wire.send(halves[1], self.half(t, 1), slots[1], (r, place.peer(4)), batch=batch)
        wire.send(halves[0], self.half(t, 0), slots[2], (r, place.peer(1)), batch=batch)
        wire.send(whole, self.at(t), slots[6], (r, place.peer(2)), batch=batch)

    def relay(self):
        wire, place, slots = self.wire, self.wire.place, self.slots
        r, far, near = place.r, place.peer(4), place.peer(1)
        self.passed = wire.batch(self.several(4))
        wire.arrived(self.half(far, 0), slots[0])
        wire.send(self.half(far, 0), self.half(far, 0), slots[4], (r, near), batch=self.passed)
        wire.arrived(self.half(near, 1), slots[3])
        wire.send(self.half(near, 1), self.half(near, 1), slots[5], (r, far), batch=self.passed)
        wire.arrived(self.half(far, 1), slots[1])
        wire.send(self.at(far), self.at(far), slots[7], (r, place.peer(2)), batch=self.passed)
        wire.arrived(self.half(near, 0), slots[2])
        wire.send(self.at(near), self.at(near), slots[8], (r, place.peer(2)), batch=self.passed)

    def forward(self):
        wire, place, slots = self.wire, self.wire.place, self.slots
        across = place.peer(5)
        for h in range(2):
            block = self.half(across, h)
            wire.arrived(block, slots[4 + h])
            wire.send(block, block, slots[9 + h], (place.r, place.peer(2)), batch=self.passed)

    def wait_block(self, mask):
        wire, place, slots = self.wire, self.wire.place, self.slots
        if mask == 7:
            for h in range(2):
                wire.arrived(self.half(place.peer(7), h), slots[9 + h])
        else:
            wire.arrived(self.at(place.peer(mask)), slots[{2: 6, 6: 7, 3: 8}[mask]])

    def wait(self):
        self.wire.arrived(self.several(4), self.slots[6])


class SlabScatter:
    def __init__(self, wire, part, core_in, chip_in, block):
        self.wire, self.part, self.core_in, self.chip_in, self.block = wire, part, core_in, chip_in, block
        self.core_slots = wire.recv_slots(4)
        self.slots = wire.recv_slots(6)
        self.order = (5, 4, 1, 0)

    def cores(self):
        place = self.wire.place
        batch = self.wire.batch(self.core_in)
        for i, mask in enumerate(self.order):
            self.wire.send(
                rows(self.part, place.peer(mask ^ 2), self.block),
                self.core_in.at[i],
                self.core_slots[i],
                (place.r, place.peer(2)),
                batch=batch,
            )

    def half(self, mask, h):
        return rows(self.part, self.wire.place.peer(mask) * 2 + h, self.block // 2)

    def add_core(self, i):
        mask = self.order[i]
        self.wire.arrived(self.core_in.at[i], self.core_slots[i])
        mine = rows(self.part, self.wire.place.peer(mask), self.block)
        mine[...] = (mine[...].astype(F32) + self.core_in[i].astype(F32)).astype(BF16)

    def chips(self):
        wire, place = self.wire, self.wire.place
        far, near = (place.r, place.peer(4)), (place.r, place.peer(1))
        self.passed = wire.batch(self.chip_in)
        self.add_core(0)
        wire.send(self.half(5, 0), self.chip_in.at[0], self.slots[0], far, batch=self.passed)
        wire.send(self.half(5, 1), self.chip_in.at[1], self.slots[1], near, batch=self.passed)
        self.add_core(1)
        wire.send(self.half(4, 0), self.chip_in.at[2], self.slots[2], far, batch=self.passed)
        self.add_core(2)
        wire.send(self.half(1, 1), self.chip_in.at[3], self.slots[3], near, batch=self.passed)
        wire.arrived(self.core_in.at[3], self.core_slots[3])

    def relay(self):
        wire, place = self.wire, self.wire.place
        far, near = (place.r, place.peer(4)), (place.r, place.peer(1))
        for i, (block, to) in enumerate(((self.half(1, 0), near), (self.half(4, 1), far))):
            wire.arrived(self.chip_in.at[i], self.slots[i])
            block[...] = (block[...].astype(F32) + self.chip_in[i].astype(F32)).astype(BF16)
            wire.send(block, self.chip_in.at[4 + i], self.slots[4 + i], to, batch=self.passed)

    def wait(self):
        for i in range(2, 6):
            self.wire.arrived(self.chip_in.at[i], self.slots[i])

    def total(self, first, size):
        mine = self.part[pl.ds(pl.multiple_of(self.wire.place.t * self.block + first, size), size), :].astype(F32)
        mine = mine + self.core_in[3, pl.ds(pl.multiple_of(first, size), size), :].astype(F32)
        h = first // (self.block // 2)
        at = pl.ds(pl.multiple_of(first % (self.block // 2), size), size)
        return mine + self.chip_in[2 + h, at, :].astype(F32) + self.chip_in[4 + h, at, :].astype(F32)


class SlabSwap:
    def __init__(self, wire, source, target, seven):
        self.wire, self.source, self.target, self.seven = wire, source, target, seven
        (self.slot,) = wire.recv_slots(1)

    def start(self):
        place = self.wire.place
        self.own = self.wire.local(self.source(place.t), self.target(place.t))
        batch = self.wire.batch(self.seven)
        for i in (4, 5, 3, 6, 2, 7, 1):
            to = (place.t + i) % SLAB
            self.wire.send(self.source(to), self.target(place.t), self.slot, (place.r, to), batch=batch)

    def wait(self):
        self.wire.arrived(self.seven, self.slot)
        self.own.wait()


class GroupGather:
    def __init__(self, wire, at):
        self.wire, self.at = wire, at
        self.slots = [None] + wire.recv_slots(3)
        self.first = wire.recvs - 4
        r = wire.place.r
        self.inner, self.outer = (r + 1) // 2 == 1, (r + 1) // 2 != 1

    def start(self, src, dst=None):
        wire, place = self.wire, self.wire.place
        r = place.r
        dst = self.at(r) if dst is None else dst
        wire.send(src, dst, self.slots[1], ((r + 1) % 4, place.t), r != 3)
        wire.send(src, dst, self.slots[3], ((r + 3) % 4, place.t), r != 0)

    def pass_on(self):
        wire, place = self.wire, self.wire.place
        r = place.r
        below, above = (r + 3) % 4, (r + 1) % 4
        for block, slot, to in ((self.at(below), self.slots[1], above), (self.at(above), self.slots[3], below)):
            wire.arrived(block, slot, self.inner)
            wire.send(block, block, self.slots[2], (to, place.t), self.inner)

    def pass_far(self):
        wire, place = self.wire, self.wire.place
        r = place.r
        block = self.at((r + 2) % 4)
        wire.arrived(block, self.slots[2], self.inner)
        slot = wire.recv_sems.at[self.first + (2 * r + 3) % 4]
        wire.send(block, block, slot, ((3 * r + 1) % 4, place.t), self.inner)

    def wait(self):
        wire, r = self.wire, self.wire.place.r
        for i in (1, 2, 3):
            wire.arrived(self.at((r + 4 - i) % 4), self.slots[i], self.outer)


class GroupScatter:
    def __init__(self, wire, out, into, own):
        self.wire, self.out, self.into, self.own = wire, out, into, own
        self.slots = wire.recv_slots(5)
        self.spots = {}
        r = wire.place.r
        self.inner, self.outer = (r + 1) // 2 == 1, (r + 1) // 2 != 1
        low = 1 - r // 2
        self.far, self.next = (r + 1 + 2 * low) % 4, (r + 3 - 2 * low) % 4

        @pl.when(self.outer)
        def _():
            into[2] = jnp.zeros_like(into[2])

    def put(self, k, spot, to, when):
        if k not in self.spots:
            self.spots[k] = self.wire.batch(self.out.at[k], far=True)
        to = (to, self.wire.place.t)
        self.wire.send(self.out.at[k], self.into.at[spot], self.slots[spot], to, when, self.spots[k])

    def start(self, make, hold=False):
        r = self.wire.place.r
        for k, to in enumerate((self.far, (r + 2) % 4, self.next)):
            self.out[k] = make(to).astype(BF16)
            if k < 2 or not hold:
                self.put(k, k, self.next, self.outer)
        self.own[...] = make(r)

    def start_last(self):
        self.put(2, 2, self.next, self.outer)

    def add(self, k, spot):
        self.wire.arrived(self.into.at[spot], self.slots[spot], self.inner)

        @pl.when(self.inner)
        def _():
            self.out[k] = (self.out[k].astype(F32) + self.into[spot].astype(F32)).astype(BF16)

    def relay_far(self):
        self.add(1, 0)
        self.put(1, 3, self.next, self.inner)

    def relay_next(self):
        self.add(2, 1)
        self.put(2, 4, self.next, self.inner)

    def relay_end(self):
        self.add(0, 3)
        self.put(0, 4, self.far, self.inner)

    def total(self):
        self.wire.arrived(self.into.at[2], self.slots[2], self.inner)
        self.wire.arrived(self.into.at[4], self.slots[4])
        return self.own[...] + self.into[2].astype(F32) + self.into[4].astype(F32)


def layer_kernel(
    groups,
    scale,
    tokens_hbm_in,
    upstream_hbm_in,
    visible_hbm,
    first_gain,
    first_shift,
    query_bias,
    value_bias,
    outward_bias,
    second_gain,
    second_shift,
    shrink_bias,
    expand_bias,
    w_in,
    w_out,
    w_exp,
    w_shr,
    layer_hbm,
    tokens_hbm,
    in_hbm,
    out_hbm,
    exp_hbm,
    shr_hbm,
    vec_hbm,
    layer_out,
    tokens_grad,
    out_grad,
    shr_grad,
    vec_grad,
    tokens,
    upstream,
    visible,
    pack,
    small,
    wide_small,
    packs,
    tok_all,
    first_all,
    win,
    wex,
    wsh,
    wo,
    gls,
    gls_all,
    vecs,
    ebias,
    qkv,
    gqkv,
    soft_all,
    blend_t,
    blend,
    middle,
    normed,
    inverses,
    second,
    second_all,
    active,
    ghid,
    slopes,
    part_a,
    part_b,
    part_c,
    part_d,
    core_a,
    core_b,
    core_c,
    core_d,
    chip_a,
    chip_b,
    chip_c,
    chip_d,
    gsec,
    glow,
    gblend,
    gblend_t,
    sh_out,
    sh_in,
    sh_own,
    ex_out,
    ex_in,
    ex_own,
    ex_sum,
    ex_all,
    in_out,
    in_in,
    in_own,
    in_sum,
    in_all,
    ou_out,
    ou_in,
    ou_own,
    gvec,
    gvec_exp,
    gvec_out,
    gvec_in,
    gvec_sum,
    gvec_far,
    send_sems,
    recv_sems,
    local_sems,
):
    place = Place(groups)
    wire = Wire(place, send_sems, recv_sems, local_sems)
    f, y, r, xc, t = place.f, place.y, place.r, place.xc, place.t
    devices = groups * SLAB
    me = r * SLAB + t
    seg, width = tokens.shape
    clips = SLAB // 2
    slots = seg * 2
    total_rows = SLAB * seg
    head2 = qkv.shape[1] // 3
    own_rows = w_in.shape[0]
    slab_rows = own_rows * 4
    share = width // devices
    chunk = wsh.shape[1]
    strip = 32
    tile = 256

    vectors = (
        first_gain,
        first_shift,
        query_bias,
        value_bias,
        outward_bias,
        second_gain,
        second_shift,
        shrink_bias,
    )
    loads = [wire.local(None, small, [(ref, small.at[k]) for k, ref in enumerate(vectors)])]
    loads.append(wire.local(expand_bias, wide_small))
    loads.append(wire.local(visible_hbm, visible))
    early = wire.local(tokens_hbm_in, tokens)
    late = wire.local(upstream_hbm_in, upstream)
    barrier = pltpu.get_barrier_semaphore()
    for i in range(1, devices):
        to = (me + i) % devices
        pl.semaphore_signal(barrier, inc=1, device_id=place.device(to // SLAB, to % SLAB), device_id_type=MESH)
    for copy in loads:
        copy.wait()
    per_lane = 128 // own_rows
    lines = [jnp.concatenate([small[k].astype(F32)] * per_lane, axis=1) for k in range(8)]
    lines.append(wide_small[...].astype(F32))
    count_here = jnp.full((6, 128), visible[0], jnp.int32).astype(F32)
    pack[...] = jnp.concatenate(lines + [count_here], axis=0).astype(BF16)
    pl.semaphore_wait(barrier, devices - 1)

    (pack_slot,) = wire.recv_slots(1)
    pack_batch = wire.batch(packs.at[pl.ds(0, groups * 4 - 1)])
    for i in range(1, groups * 4):
        to = (f + i) % (groups * 4)
        wire.send(pack, packs.at[f], pack_slot, (to // 4, (to % 4) * 2 + y), batch=pack_batch)
    own_pack = wire.local(pack, packs.at[f])

    in_slots = [None] + wire.recv_slots(3)
    ex_slots = [None] + wire.recv_slots(3)

    def in_piece(index, c):
        return win.at[pl.ds(pl.multiple_of(index * own_rows, own_rows), own_rows), pl.ds(c * head2, head2)]

    def ex_piece(index, c):
        return wex.at[pl.ds(pl.multiple_of(index * own_rows, own_rows), own_rows), pl.ds(c * chunk, chunk)]

    own_in = []
    in_batch = wire.batch(win.at[pl.ds(0, 3 * own_rows), :])
    for i in (2, 3, 1, 0):
        to = ((xc + i) % 4) * 2 + y
        for c in range(3):
            src = w_in.at[:, pl.ds(pl.multiple_of(c * width + to * head2, head2), head2)]
            if i == 0:
                own_in.append((src, in_piece(f, c)))
            else:
                wire.send(src, in_piece(f, c), in_slots[i], (r, to), batch=in_batch)
    own_in = wire.local(None, rows(win, f, own_rows), own_in)

    out_share = w_out.at[pl.ds(pl.multiple_of(y * share, share), share), :]
    own_out = wire.local(out_share, wo.at[r, t])
    group_wo = GroupGather(wire, lambda at: wo.at[at, t])
    group_wo.start(out_share)
    shr_share = w_shr.at[pl.ds(pl.multiple_of(y * chunk, chunk), chunk), :]
    own_shr = wire.local(shr_share, wsh.at[r])
    group_sh = GroupGather(wire, lambda at: wsh.at[at])

    def shr_half(h):
        at = pl.ds(h * (chunk // 2), chunk // 2)
        src = w_shr.at[pl.ds(pl.multiple_of(y * chunk + h * (chunk // 2), chunk // 2), chunk // 2), :]
        group_sh.start(src, wsh.at[r, at])

    shr_half(0)

    def slab_gather(ref, apart=True):
        return SlabGather(
            wire,
            lambda at: rows(ref, at, seg),
            lambda at, h: rows(ref, at * 2 + h, seg // 2),
            lambda count: ref.at[pl.ds(0, count * seg), :],
            apart,
        )

    early.wait()
    gather_tok = slab_gather(tok_all)
    gather_tok.start(tokens, [rows(tokens, h, seg // 2) for h in range(2)])

    own_ex = []
    ex_batch = wire.batch(wex.at[pl.ds(0, 3 * own_rows), :])
    for i in (2, 3, 1, 0):
        to = ((xc + i) % 4) * 2 + y
        for c in range(groups):
            src = w_exp.at[:, pl.ds(pl.multiple_of((c * SLAB + to) * chunk, chunk), chunk)]
            if i == 0:
                own_ex.append((src, ex_piece(f, c)))
            else:
                wire.send(src, ex_piece(f, c), ex_slots[i], (r, to), batch=ex_batch)
    own_ex = wire.local(None, rows(wex, f, own_rows), own_ex)

    late.wait()
    row_at = y * seg + lax.broadcasted_iota(jnp.int32, (seg, 1), 0)
    row_valid = row_at.astype(F32) < pack[10:11, 0:1].astype(F32)
    gls[...] = jnp.where(row_valid, upstream[...].astype(F32), 0.0).astype(BF16)
    gls_all[pl.ds(pl.multiple_of(t * seg, seg), seg), :] = gls[...]
    gvec[...] = jnp.zeros_like(gvec)
    gvec_exp[...] = jnp.zeros_like(gvec_exp)
    group_shr = GroupScatter(wire, sh_out, sh_in, sh_own)
    group_exp = GroupScatter(wire, ex_out, ex_in, ex_own)
    group_inw = GroupScatter(wire, in_out, in_in, in_own)
    group_out = GroupScatter(wire, ou_out, ou_in, ou_own)

    for i in range(1, 4):
        frm = r * 4 + (xc + 4 - i) % 4
        wire.arrived(rows(win, frm, own_rows), in_slots[i])
    own_in.wait()
    own_out.wait()
    group_wo.pass_on()
    group_in = GroupGather(wire, lambda at: rows(win, at, slab_rows))
    group_in.start(rows(win, r, slab_rows))
    shr_half(1)
    group_wo.pass_far()

    own_pack.wait()
    wire.arrived(packs.at[pl.ds(0, groups * 4 - 1)], pack_slot)
    lane = lax.broadcasted_iota(jnp.int32, (1, 128), 1)
    for j in range(width // 128):
        piece = packs[j * per_lane].astype(F32)
        for k in range(1, per_lane):
            piece = jnp.where(lane >= k * own_rows, packs[j * per_lane + k].astype(F32), piece)
        vecs[:, j * 128 : (j + 1) * 128] = piece
    for c in range(groups):
        both = packs[c * 4 + t // 2].astype(F32)
        ebias[0:1, c * chunk : (c + 1) * chunk] = jnp.where(y == 0, both[8:9], both[9:10])

    def first_norm(src, offset, block):
        def strip_norm(i, carry):
            at = pl.multiple_of(i * strip, strip)
            n, _ = row_stats(src[pl.ds(offset + at, strip), :].astype(F32))
            to = pl.multiple_of(block * seg + at, strip)
            first_all[pl.ds(to, strip), :] = (n * vecs[0:1, :] + vecs[1:2, :]).astype(BF16)
            return carry

        lax.fori_loop(0, seg // strip, strip_norm, 0)

    first_norm(tokens, 0, t)

    def norm_block(mask):
        block = place.peer(mask)
        first_norm(tok_all, pl.multiple_of(block * seg, seg), block)

    gather_tok.relay()
    group_wo.wait()
    gather_wo = SlabGather(
        wire,
        lambda at: wo.at[:, at],
        lambda at, h: wo.at[pl.ds(h * (groups // 2), groups // 2), at],
        lambda count: wo.at[:, pl.ds(0, count)],
        apart=False,
    )
    gather_wo.start(wo.at[:, t], [wo.at[pl.ds(h * (groups // 2), groups // 2), t] for h in range(2)])
    group_in.pass_on()
    norm_block(4)
    norm_block(1)

    gather_tok.forward()

    norm_block(5)
    group_in.pass_far()
    for i in range(1, 4):
        frm = r * 4 + (xc + 4 - i) % 4
        wire.arrived(rows(wex, frm, own_rows), ex_slots[i])
    own_ex.wait()
    group_ex = GroupGather(wire, lambda at: rows(wex, at, slab_rows))
    group_ex.start(rows(wex, r, slab_rows))


    for mask in (2, 6, 3, 7):
        gather_tok.wait_block(mask)
        norm_block(mask)

    gather_wo.relay()
    gather_gls = slab_gather(gls_all, apart=False)
    gather_gls.start(gls, [rows(gls, h, seg // 2) for h in range(2)])
    group_in.wait()
    at_head = pl.ds(pl.multiple_of(t * head2, head2), head2)
    bias = jnp.concatenate([vecs[2:3, at_head], jnp.zeros((1, head2), F32), vecs[3:4, at_head]], axis=1)

    def project(i, carry):
        at = pl.ds(pl.multiple_of(i * tile, tile), tile)
        qkv[at, :] = (matmul(first_all[at, :], win[...]) + bias).astype(BF16)
        return carry

    lax.fori_loop(0, total_rows // tile, project, 0)

    group_sh.pass_on()
    head_size = head2 // 2
    low_half = lane < head_size
    half_masks = [low_half.astype(F32).astype(BF16), (1.0 - low_half.astype(F32)).astype(BF16)]
    key_at = lax.broadcasted_iota(jnp.int32, (1, slots), 1).astype(F32)

    def attend(i, carry):
        at = pl.ds(pl.multiple_of(i * slots, slots), slots)
        q = qkv[at, 0:head2]
        k = qkv[at, head2 : 2 * head2]
        v = qkv[at, 2 * head2 : 3 * head2]
        count = packs[r * 4 + i].astype(F32)[10:11, 0:1]
        key_valid = key_at < count
        halves = []
        for h in range(2):
            scores = matmul_bt(q * half_masks[h], k) * scale
            scores = jnp.where(key_valid, scores, -1e30)
            top = jnp.max(scores, axis=-1, keepdims=True)
            soft = jnp.exp(scores - top)
            soft = soft * (1.0 / jnp.sum(soft, axis=-1, keepdims=True))
            soft_all[i * 2 + h] = soft
            halves.append(matmul(soft.astype(BF16), v))
        blend_t[at, :] = jnp.where(low_half, halves[0], halves[1]).astype(BF16)
        return carry

    lax.fori_loop(0, clips, attend, 0)

    group_ex.pass_on()
    swap_blend = SlabSwap(wire, lambda at: rows(blend_t, at, seg), lambda at: cols(blend, at, head2), blend.at[:, 0 : 7 * head2])
    swap_blend.start()
    gather_wo.forward()

    gather_gls.relay()
    gather_wo.wait()
    swap_blend.wait()
    group_ex.pass_far()
    wide = 256
    for j in range(width // wide):
        at = slice(j * wide, (j + 1) * wide)
        product = matmul(blend[...], wo[:, :, :, at].reshape(width, wide))
        middle[:, at] = tokens[:, at].astype(F32) + (product + vecs[4:5, at])

    own_second_rows = pl.multiple_of(t * seg, seg)

    def second_norm(i, carry):
        at = pl.ds(pl.multiple_of(i * strip, strip), strip)
        n, inverse = row_stats(middle[at, :])
        normed[at, :] = n
        inverses[at, :] = jnp.broadcast_to(inverse, (strip, 128))
        low = (n * vecs[5:6, :] + vecs[6:7, :]).astype(BF16)
        second[at, :] = low
        second_all[pl.ds(pl.multiple_of(own_second_rows + i * strip, strip), strip), :] = low
        return carry

    lax.fori_loop(0, seg // strip, second_norm, 0)

    gather_second = slab_gather(second_all)
    gather_second.start(second, [rows(second, h, seg // 2) for h in range(2)])
    gather_gls.forward()
    hidden_units = groups * chunk

    def feed(i, carry):
        at = pl.ds(pl.multiple_of(i * tile, tile), tile)
        hidden = matmul(second_all[at, :], wex[...]) + ebias[0:1, :]
        cdf = 0.5 * (1.0 + lax.erf(hidden * 0.7071067811865476))
        active[at, :] = (hidden * cdf).astype(BF16)
        slopes[at, :] = cdf + hidden * (0.3989422804014327 * jnp.exp(-0.5 * hidden * hidden))
        return carry

    gather_second.relay()
    group_sh.pass_far()
    group_ex.wait()
    core = xc % 2
    beside = xc + 1 - 2 * core
    across = (xc + 2) % 4
    feed(xc, 0)
    gather_second.forward()
    feed(across, 0)
    gather_second.wait_block(2)
    gather_second.wait_block(3)
    feed(beside, 0)
    gather_second.wait_block(6)
    gather_second.wait_block(7)
    feed((beside + 2) % 4, 0)
    gather_gls.wait()
    front_sends = len(wire.open_sends)

    group_shr.start(
        lambda c: matmul_at(active[:, pl.ds(pl.multiple_of(c * chunk, chunk), chunk)], gls_all[...]),
        hold=True,
    )
    group_sh.wait()
    own_shr.wait()

    def feed_back(i, carry):
        at = pl.ds(pl.multiple_of(i * tile, tile), tile)
        grad_active = matmul_bt(gls_all[at, :], wsh[...].reshape(hidden_units, width))
        grad_hidden = (grad_active * slopes[at, :]).astype(BF16)
        ghid[at, :] = grad_hidden
        gvec_exp[...] += jnp.sum(grad_hidden.astype(F32), axis=0, keepdims=True)
        part_a[at, :] = matmul_bt(grad_hidden, wex[...]).astype(BF16)
        return carry

    scatter_second = SlabScatter(wire, part_a, core_a, chip_a, seg)
    lax.fori_loop(0, 2, lambda k, carry: feed_back(1 - core + 2 * k, carry), 0)
    scatter_second.cores()
    lax.fori_loop(0, 2, lambda k, carry: feed_back(core + 2 * k, carry), 0)

    scatter_second.chips()
    group_exp.start(
        lambda c: matmul_at(second_all[:, pl.ds(pl.multiple_of(c * slab_rows, slab_rows), slab_rows)], ghid[...])
    )
    scatter_second.relay()
    group_shr.relay_far()

    def feed_out(i, carry):
        at = pl.ds(pl.multiple_of(i * tile, tile), tile)
        part_b[at, :] = matmul(active[at, :], wsh[...].reshape(hidden_units, width)).astype(BF16)
        return carry

    lax.fori_loop(0, total_rows // tile, feed_out, 0)
    scatter_result = SlabScatter(wire, part_b, core_b, chip_b, seg)
    scatter_result.cores()

    scatter_second.wait()
    wire.settle(front_sends)

    feed_sends = len(wire.open_sends)

    def second_back(i, carry):
        first = i * strip
        at = pl.ds(pl.multiple_of(first, strip), strip)
        grad = scatter_second.total(first, strip)
        n = normed[at, :]
        back = row_norm_back(grad, n, inverses[at, 0:1], vecs[5:6, :])
        grad_result = gls[at, :].astype(F32)
        grad_middle = grad_result + back
        gsec[at, :] = grad_middle
        low = grad_middle.astype(BF16)
        glow[at, :] = low
        gvec[4:5, :] += jnp.sum(low.astype(F32), axis=0, keepdims=True)
        gvec[5:6, :] += jnp.sum(grad * n, axis=0, keepdims=True)
        gvec[6:7, :] += jnp.sum(grad, axis=0, keepdims=True)
        gvec[7:8, :] += jnp.sum(grad_result, axis=0, keepdims=True)
        return carry

    lax.fori_loop(0, seg // strip, second_back, 0)

    for j in range(width // wide):
        rows_of = slice(j * (groups * wide // width), (j + 1) * (groups * wide // width))
        gblend[:, j * wide : (j + 1) * wide] = matmul_bt(
            glow[...], wo[rows_of].reshape(wide, width)
        ).astype(BF16)
    swap_gblend = SlabSwap(wire, lambda at: cols(gblend, at, head2), lambda at: rows(gblend_t, at, seg), gblend_t.at[pl.ds(0, 7 * seg), :])
    swap_gblend.start()

    for c in range(groups):
        product = matmul_at(blend[:, c * slab_rows : (c + 1) * slab_rows], glow[...])
        for to in range(SLAB):
            part_d[to * seg + c * share : to * seg + (c + 1) * share, :] = product[
                to * share : (to + 1) * share
            ].astype(BF16)
    scatter_out = SlabScatter(wire, part_d, core_d, chip_d, seg)
    scatter_out.cores()

    group_shr.relay_next()
    scatter_out.chips()
    swap_gblend.wait()

    group_shr.relay_end()
    group_exp.relay_far()
    def attend_back(i, carry):
        at = pl.ds(pl.multiple_of(i * slots, slots), slots)
        q = qkv[at, 0:head2]
        k = qkv[at, head2 : 2 * head2]
        v = qkv[at, 2 * head2 : 3 * head2]
        grad = gblend_t[at, :]
        parts = []
        for h in range(2):
            soft = soft_all[i * 2 + h]
            grad_soft = matmul_bt(grad * half_masks[h], v)
            inner = jnp.sum(grad_soft * soft, axis=-1, keepdims=True)
            grad_scores = (soft * (grad_soft - inner)).astype(BF16)
            parts.append(
                (
                    matmul(grad_scores, k) * scale,
                    matmul_at(grad_scores, q) * scale,
                    matmul_at(soft.astype(BF16), grad),
                )
            )
        for c in range(3):
            gqkv[at, c * head2 : (c + 1) * head2] = jnp.where(low_half, parts[0][c], parts[1][c]).astype(BF16)
        return carry

    lax.fori_loop(0, clips, attend_back, 0)

    scatter_out.relay()
    group_exp.relay_next()
    def project_back(i, carry):
        at = pl.ds(pl.multiple_of(i * tile, tile), tile)
        part_c[at, :] = matmul_bt(gqkv[at, :], win[...]).astype(BF16)
        return carry

    scatter_first = SlabScatter(wire, part_c, core_c, chip_c, seg)
    lax.fori_loop(0, 2, lambda k, carry: project_back(1 - core + 2 * k, carry), 0)
    scatter_first.cores()
    lax.fori_loop(0, 2, lambda k, carry: project_back(core + 2 * k, carry), 0)

    group_inw.start(
        lambda c: matmul_at(first_all[:, pl.ds(pl.multiple_of(c * slab_rows, slab_rows), slab_rows)], gqkv[...]),
        hold=True,
    )
    scatter_first.chips()
    gvec[2:3, at_head] = jnp.sum(gqkv[:, 0:head2].astype(F32), axis=0, keepdims=True)
    gvec[3:4, at_head] = jnp.sum(gqkv[:, 2 * head2 :].astype(F32), axis=0, keepdims=True)

    scatter_out.wait()
    group_out.start(lambda c: scatter_out.total(c * share, share), hold=True)
    group_inw.start_last()
    group_out.start_last()
    scatter_first.relay()
    group_exp.relay_end()
    scatter_result.chips()
    group_inw.relay_far()
    scatter_first.wait()
    wire.settle(feed_sends, slab_only=True)

    group_inw.relay_next()
    group_out.relay_far()
    group_out.relay_next()
    group_inw.relay_end()
    def first_back(i, carry):
        first = i * strip
        at = pl.ds(pl.multiple_of(first, strip), strip)
        grad = scatter_first.total(first, strip)
        n, inverse = row_stats(tokens[at, :].astype(F32))
        tokens_grad[at, :] = gsec[at, :] + row_norm_back(grad, n, inverse, vecs[0:1, :])
        gvec[0:1, :] += jnp.sum(grad * n, axis=0, keepdims=True)
        gvec[1:2, :] += jnp.sum(grad, axis=0, keepdims=True)
        return carry

    lax.fori_loop(0, seg // strip, first_back, 0)
    stores = [wire.local(tokens_grad, tokens_hbm)]

    for to in range(SLAB):
        gvec_out[to] = jnp.concatenate(
            [gvec[:, (c * SLAB + to) * share : (c * SLAB + to + 1) * share] for c in range(groups)], axis=1
        )
    swap_vec = SlabSwap(wire, lambda at: gvec_out.at[at], lambda at: gvec_in.at[at], gvec_in.at[pl.ds(0, 7)])
    swap_vec.start()

    scatter_result.relay()
    ex_sum[...] = group_exp.total().astype(BF16)
    swap_exp = SlabSwap(wire, lambda at: rows(ex_sum, at, share), lambda at: ex_all.at[at], ex_all.at[pl.ds(0, 7)])
    swap_exp.start()
    swap_vec.wait()
    summed = gvec_in[0]
    for i in range(1, SLAB):
        summed = summed + gvec_in[i]
    gvec_sum[0:8] = summed
    for c in range(groups):
        gvec_sum[8 + c : 9 + c] = gvec_exp[0:1, c * chunk : (c + 1) * chunk]
    gvec_sum[8 + groups : 16] = jnp.zeros((8 - groups, 128), F32)
    vec_slots = wire.recv_slots(groups - 1)
    for i in range(1, groups):
        wire.send(gvec_sum, gvec_far.at[i - 1], vec_slots[i - 1], ((r + i) % groups, t))
    group_shr.start_last()
    group_out.relay_end()
    in_sum[...] = group_inw.total().astype(BF16)
    swap_in = SlabSwap(wire, lambda at: rows(in_sum, at, share), lambda at: in_all.at[at], in_all.at[pl.ds(0, 7)])
    swap_in.start()
    scatter_result.wait()

    def finish_out(i, carry):
        first = i * strip
        at = pl.ds(pl.multiple_of(first, strip), strip)
        result = middle[at, :] + (scatter_result.total(first, strip) + vecs[7:8, :])
        spot = y * seg + first + lax.broadcasted_iota(jnp.int32, (strip, 1), 0)
        valid = spot.astype(F32) < pack[10:11, 0:1].astype(F32)
        layer_out[at, :] = jnp.where(valid, result, 0.0).astype(BF16)
        return carry

    lax.fori_loop(0, seg // strip, finish_out, 0)
    stores.append(wire.local(layer_out, layer_hbm))

    out_grad[...] = group_out.total()
    stores.append(wire.local(out_grad, out_hbm))
    shr_grad[...] = group_shr.total()
    stores.append(wire.local(shr_grad, shr_hbm))
    for i in range(1, groups):
        wire.arrived(gvec_far.at[i - 1], vec_slots[i - 1])
    total = gvec_sum[...]
    for i in range(1, groups):
        total = total + gvec_far[i - 1]
    vec_grad[0:8, :] = pltpu.roll(total[0:8], (128 - share * r) % 128, 1)
    line = total[8:9]
    for c in range(1, groups):
        line = jnp.where(r == c, total[8 + c : 9 + c], line)
    vec_grad[8:16, :] = jnp.broadcast_to(line, (8, 128))
    stores.append(wire.local(vec_grad, vec_hbm))
    swap_exp.wait()
    stores.append(wire.local(ex_all, exp_hbm))
    swap_in.wait()
    stores.append(wire.local(in_all, in_hbm))
    for copy in stores:
        copy.wait()
    wire.settle()
    assert (wire.sends, wire.recvs, wire.locals) == (SENDS, RECVS, LOCALS), (wire.sends, wire.recvs, wire.locals)


def output_kernel(
    groups,
    layer_in,
    tokens_in,
    in_pieces,
    out_in,
    exp_pieces,
    shr_in,
    vec_in,
    layer_out,
    tokens_grad,
    first_gain_grad,
    first_shift_grad,
    in_grad,
    query_bias_grad,
    value_bias_grad,
    out_grad,
    outward_bias_grad,
    second_gain_grad,
    second_shift_grad,
    exp_grad,
    expand_bias_grad,
    shr_grad,
    shrink_bias_grad,
    layer_buf,
    tokens_buf,
    in_buf,
    out_buf,
    exp_buf,
    shr_buf,
    vec_buf,
    in_wide,
    exp_wide,
    lines,
    wide_line,
    load_sems,
    store_sems,
):
    share, width = out_buf.shape
    head2, chunk = in_buf.shape[2] // 3, exp_buf.shape[2] // groups
    loads = [
        pltpu.make_async_copy(src, dst, load_sems.at[i])
        for i, (src, dst) in enumerate(
            (
                (vec_in, vec_buf),
                (exp_pieces, exp_buf),
                (in_pieces, in_buf),
                (shr_in, shr_buf),
                (tokens_in, tokens_buf),
                (layer_in, layer_buf),
                (out_in, out_buf),
            )
        )
    ]
    for copy in loads:
        copy.start()
    stores = []

    def store(src, dst):
        stores.append(pltpu.make_async_copy(src, dst, store_sems.at[len(stores)]))
        stores[-1].start()

    loads[0].wait()
    vectors = (
        first_gain_grad,
        first_shift_grad,
        query_bias_grad,
        value_bias_grad,
        outward_bias_grad,
        second_gain_grad,
        second_shift_grad,
        shrink_bias_grad,
    )
    for k, ref in enumerate(vectors):
        lines[k] = vec_buf[k, 0:share]
        store(lines.at[k], ref)
    wide_line[...] = vec_buf[8, :]
    store(wide_line, expand_bias_grad)
    loads[1].wait()
    for frm in range(SLAB):
        for c in range(groups):
            at = (c * SLAB + frm) * chunk
            exp_wide[:, at : at + chunk] = exp_buf[frm, :, c * chunk : (c + 1) * chunk].astype(F32)
    store(exp_wide, exp_grad)
    loads[2].wait()
    for frm in range(SLAB):
        for c in range(3):
            at = c * width + frm * head2
            in_wide[:, at : at + head2] = in_buf[frm, :, c * head2 : (c + 1) * head2].astype(F32)
    store(in_wide, in_grad)
    for copy, src, dst in (
        (loads[3], shr_buf, shr_grad),
        (loads[4], tokens_buf, tokens_grad.at[0]),
        (loads[5], layer_buf, layer_out.at[0]),
        (loads[6], out_buf, out_grad),
    ):
        copy.wait()
        store(src, dst)
    for copy in stores:
        copy.wait()


def fused_shards(
    tokens,
    visible,
    first_gain,
    first_shift,
    inward_weight,
    query_bias,
    value_bias,
    outward_weight,
    outward_bias,
    second_gain,
    second_shift,
    expand_weight,
    expand_bias,
    shrink_weight,
    shrink_bias,
    upstream,
):
    seg, width = tokens.shape[1:]
    groups = lax.axis_size("fsdp") // 4
    devices = groups * SLAB
    own_rows = inward_weight.shape[0]
    hidden = expand_weight.shape[1]
    share = width // devices
    chunk = hidden // devices
    units = groups * chunk
    head2 = width // SLAB
    scale = (width // HEADS) ** (-0.5)
    total_rows = SLAB * seg
    slab_rows = 4 * own_rows
    vmem = pl.BlockSpec(memory_space=pltpu.VMEM)
    anywhere = pl.BlockSpec(memory_space=pl.ANY)
    outs = pl.pallas_call(
        functools.partial(layer_kernel, groups, scale),
        out_shape=(
            jax.ShapeDtypeStruct((seg, width), BF16),
            jax.ShapeDtypeStruct((seg, width), F32),
            jax.ShapeDtypeStruct((SLAB, share, 3 * head2), BF16),
            jax.ShapeDtypeStruct((share, width), F32),
            jax.ShapeDtypeStruct((SLAB, share, units), BF16),
            jax.ShapeDtypeStruct((chunk, width), F32),
            jax.ShapeDtypeStruct((16, 128), F32),
        ),
        in_specs=[anywhere] * 2 + [pl.BlockSpec(memory_space=pltpu.HBM)] + [anywhere] * 13,
        out_specs=[anywhere] * 7,
        scratch_shapes=[
            pltpu.VMEM((seg, width), BF16),
            pltpu.VMEM((seg, width), F32),
            pltpu.VMEM((share, width), F32),
            pltpu.VMEM((chunk, width), F32),
            pltpu.VMEM((16, 128), F32),
            pltpu.VMEM((seg, width), BF16),
            pltpu.VMEM((seg, width), BF16),
            pltpu.SMEM((1,), jnp.int32),
            pltpu.VMEM((16, 128), BF16),
            pltpu.VMEM((8, 1, own_rows), BF16),
            pltpu.VMEM((2, 128), BF16),
            pltpu.VMEM((groups * 4, 16, 128), BF16),
            pltpu.VMEM((total_rows, width), BF16),
            pltpu.VMEM((total_rows, width), BF16),
            pltpu.VMEM((width, 3 * head2), BF16),
            pltpu.VMEM((width, units), BF16),
            pltpu.VMEM((groups, chunk, width), BF16),
            pltpu.VMEM((groups, SLAB, share, width), BF16),
            pltpu.VMEM((seg, width), BF16),
            pltpu.VMEM((total_rows, width), BF16),
            pltpu.VMEM((16, width), F32),
            pltpu.VMEM((8, units), F32),
            pltpu.VMEM((total_rows, 3 * head2), BF16),
            pltpu.VMEM((total_rows, 3 * head2), BF16),
            pltpu.VMEM((SLAB, 2 * seg, 2 * seg), F32),
            pltpu.VMEM((total_rows, head2), BF16),
            pltpu.VMEM((seg, width), BF16),
            pltpu.VMEM((seg, width), F32),
            pltpu.VMEM((seg, width), F32),
            pltpu.VMEM((seg, 128), F32),
            pltpu.VMEM((seg, width), BF16),
            pltpu.VMEM((total_rows, width), BF16),
            pltpu.VMEM((total_rows, units), BF16),
            pltpu.VMEM((total_rows, units), BF16),
            pltpu.VMEM((total_rows, units), F32),
        ]
        + [pltpu.VMEM((total_rows, width), BF16)] * 4
        + [pltpu.VMEM((4, seg, width), BF16)] * 4
        + [pltpu.VMEM((6, seg // 2, width), BF16)] * 4
        + [
            pltpu.VMEM((seg, width), F32),
            pltpu.VMEM((seg, width), BF16),
            pltpu.VMEM((seg, width), BF16),
            pltpu.VMEM((total_rows, head2), BF16),
            pltpu.VMEM((groups - 1, chunk, width), BF16),
            pltpu.VMEM((5, chunk, width), BF16),
            pltpu.VMEM((chunk, width), F32),
            pltpu.VMEM((groups - 1, slab_rows, units), BF16),
            pltpu.VMEM((5, slab_rows, units), BF16),
            pltpu.VMEM((slab_rows, units), F32),
            pltpu.VMEM((slab_rows, units), BF16),
            pltpu.VMEM((SLAB, share, units), BF16),
            pltpu.VMEM((groups - 1, slab_rows, 3 * head2), BF16),
            pltpu.VMEM((5, slab_rows, 3 * head2), BF16),
            pltpu.VMEM((slab_rows, 3 * head2), F32),
            pltpu.VMEM((slab_rows, 3 * head2), BF16),
            pltpu.VMEM((SLAB, share, 3 * head2), BF16),
            pltpu.VMEM((groups - 1, share, width), BF16),
            pltpu.VMEM((5, share, width), BF16),
            pltpu.VMEM((share, width), F32),
            pltpu.VMEM((8, width), F32),
            pltpu.VMEM((1, units), F32),
            pltpu.VMEM((SLAB, 8, 128), F32),
            pltpu.VMEM((SLAB, 8, 128), F32),
            pltpu.VMEM((16, 128), F32),
            pltpu.VMEM((groups - 1, 16, 128), F32),
            pltpu.SemaphoreType.DMA((SENDS,)),
            pltpu.SemaphoreType.DMA((RECVS,)),
            pltpu.SemaphoreType.DMA((LOCALS,)),
        ],
        compiler_params=pltpu.CompilerParams(
            collective_id=0, has_side_effects=True, vmem_limit_bytes=67043328
        ),
        name="layer",
    )(
        tokens.reshape(seg, width),
        upstream.reshape(seg, width),
        visible,
        *(
            vector.reshape(1, own_rows)
            for vector in (
                first_gain,
                first_shift,
                query_bias,
                value_bias,
                outward_bias,
                second_gain,
                second_shift,
                shrink_bias,
            )
        ),
        expand_bias.reshape(2, 128),
        inward_weight,
        outward_weight,
        expand_weight,
        shrink_weight,
    )
    vector = jax.ShapeDtypeStruct((share,), F32)
    return pl.pallas_call(
        functools.partial(output_kernel, groups),
        out_shape=(
            jax.ShapeDtypeStruct((1, seg, width), BF16),
            jax.ShapeDtypeStruct((1, seg, width), F32),
            vector,
            vector,
            jax.ShapeDtypeStruct((share, 3 * width), F32),
            vector,
            vector,
            jax.ShapeDtypeStruct((share, width), F32),
            vector,
            vector,
            vector,
            jax.ShapeDtypeStruct((share, hidden), F32),
            jax.ShapeDtypeStruct((chunk,), F32),
            jax.ShapeDtypeStruct((chunk, width), F32),
            vector,
        ),
        in_specs=[anywhere] * 7,
        out_specs=[anywhere] * 15,
        scratch_shapes=[
            pltpu.VMEM((seg, width), BF16),
            pltpu.VMEM((seg, width), F32),
            pltpu.VMEM((SLAB, share, 3 * head2), BF16),
            pltpu.VMEM((share, width), F32),
            pltpu.VMEM((SLAB, share, units), BF16),
            pltpu.VMEM((chunk, width), F32),
            pltpu.VMEM((16, 128), F32),
            pltpu.VMEM((share, 3 * width), F32),
            pltpu.VMEM((share, hidden), F32),
            pltpu.VMEM((8, share), F32),
            pltpu.VMEM((chunk,), F32),
            pltpu.SemaphoreType.DMA((7,)),
            pltpu.SemaphoreType.DMA((15,)),
        ],
        name="outputs",
    )(*outs)


def fits_fused(mesh, tokens, inward_weight, expand_weight):
    fsdp, seq = mesh.shape["fsdp"], mesh.shape["seq"]
    clips, slots, width = tokens.shape
    devices = fsdp * seq
    return (
        seq == 2
        and clips == fsdp
        and fsdp == 16
        and width // HEADS * 2 == 128
        and width == SLAB * 128
        and slots % 64 == 0
        and width % (16 * devices) == 0
        and 128 % (width // fsdp) == 0
        and width // devices * 4 == 128
        and expand_weight.shape[1] == 128 * devices
    )


def solution(mesh):
    in_specs = (
        P("fsdp", "seq", None),
        P("fsdp"),
        P("fsdp"),
        P("fsdp"),
        P("fsdp", None),
        P("fsdp"),
        P("fsdp"),
        P("fsdp", None),
        P("fsdp"),
        P("fsdp"),
        P("fsdp"),
        P("fsdp", None),
        P("fsdp"),
        P("fsdp", None),
        P("fsdp"),
        P("fsdp", "seq", None),
    )
    out_specs = (
        P("fsdp", "seq", None),
        P("fsdp", "seq", None),
        P(("fsdp", "seq")),
        P(("fsdp", "seq")),
        P(("fsdp", "seq"), None),
        P(("fsdp", "seq")),
        P(("fsdp", "seq")),
        P(("fsdp", "seq"), None),
        P(("fsdp", "seq")),
        P(("fsdp", "seq")),
        P(("fsdp", "seq")),
        P(("fsdp", "seq"), None),
        P(("fsdp", "seq")),
        P(("fsdp", "seq"), None),
        P(("fsdp", "seq")),
    )

    def step(*args):
        body = fused_shards if fits_fused(mesh, args[0], args[4], args[11]) else shards
        return jax.shard_map(body, mesh=mesh, in_specs=in_specs, out_specs=out_specs, check_vma=False)(*args)

    return step
```
